32 devices in a mesh: pipe: 2 (over core), grp: 4 (over z), dp: 4 (over y, x).
Axes of the slice: x: 2, y: 2, z: 4, core: 2. Of those that a mesh axis runs over, the one named last changes fastest.
Arguments:
- block_input: bfloat16 [2, 16, 512, 512], P(None, ('grp', 'dp')), may hold values from -6 to 6
- cotangent: bfloat16 [2, 16, 512, 512], P(None, ('grp', 'dp')), may hold values from -6 to 6
- segments: int32 [2, 16, 512], P(None, ('grp', 'dp')), may hold values from 0 to 7, never falling along the last dimension, each value on 1 to 256 neighbouring positions
- ln1_gain: float32 [2, 512], P('pipe'), may hold values from 0.5 to 1.5
- ln1_shift: float32 [2, 512], P('pipe'), may hold values from -1.25 to 1.25
- qkv_weight: bfloat16 [2, 512, 1536], P('pipe'), may hold values from -0.25 to 0.25
- qkv_bias: float32 [2, 1536], P('pipe'), may hold values from -1.25 to 1.25
- attn_weight: bfloat16 [2, 512, 512], P('pipe'), may hold values from -1.5 to 1.5
- attn_bias: float32 [2, 512], P('pipe'), may hold values from -1.25 to 1.25
- ln2_gain: float32 [2, 512], P('pipe'), may hold values from 0.5 to 1.5
- ln2_shift: float32 [2, 512], P('pipe'), may hold values from -1.25 to 1.25
- ff_in_weight: bfloat16 [2, 512, 2048], P('pipe'), may hold values from -0.25 to 0.25
- ff_in_bias: float32 [2, 2048], P('pipe'), may hold values from -1.25 to 1.25
- ff_out_weight: bfloat16 [2, 2048, 512], P('pipe'), may hold values from -0.125 to 0.125
- ff_out_bias: float32 [2, 512], P('pipe'), may hold values from -1.25 to 1.25
- prefix_embed: float32 [10, 512], replicated, may hold values from -6 to 6
- up_weight: float32 [512, 512], replicated, may hold values from -0.25 to 0.25
- up_bias: float32 [512], replicated, may hold values from -3 to 3
- out_weight: float32 [512, 2048], replicated, may hold values from -0.375 to 0.375
- out_bias: float32 [2048], replicated, may hold values from -1.75 to 1.75
Outputs:
- activations: bfloat16 [2, 2, 16, 512, 512], P('pipe', None, ('grp', 'dp'))
- input_grads: float32 [2, 2, 16, 512, 512], P('pipe', None, ('grp', 'dp'))
- grad_embed: float32 [10, 512], replicated
- grad_up_weight: float32 [512, 512], replicated
- grad_up_bias: float32 [512], replicated
- grad_out_weight: float32 [512, 2048], P(None, ('pipe', 'dp'))
- grad_out_bias: float32 [2048], P(('pipe', 'dp'))
The draws below stay inside these ranges and needn't reach their ends.
Inputs may be any that keep to these rules, and one draw needn't show every extreme that they name: `segments`: within a packed row segment numbers never fall, and every segment holds 1 to 256 tokens.
All inputs are finite; a program needn't handle non-finite values.
Results may differ from the reference program's by a relative error of at most 0.019.
Values may be sent and summed in bfloat16 or wider, within the bound.
No kernel may reach another device: no remote copies, remote signals or barrier semaphores. Data moves between devices by JAX's collectives and lax.ppermute only.
A program may use at most 192 MiB of HBM per device.

```python
import math
import jax
import jax.numpy as jnp
import numpy as np
from jax import lax

D = 512
HEADS = 8
HD = 64
FF = 2048
ROT = 16
PREFIX = 10
REPARAM = 512
SEQ = 512
MICRO = 2
SEGS = 8
LAYERS = 2
BATCH = 16


def steps_of(rng, shape, shards, low, largest):
    def one(dim, blocks):
        steps = jax.random.uniform(jax.random.fold_in(jax.random.fold_in(rng, 6), dim), (blocks,), jnp.float32, low / len(shards), largest / len(shards))
        return jnp.repeat(jnp.exp(steps), shape[dim] // blocks).reshape((-1,) + (1,) * (len(shape) - dim - 1))

    loudness = one(*shards[0])
    for cut in shards[1:]:
        loudness = loudness * one(*cut)
    return loudness


def length_profile(amount, total, bound, skew):
    weights = [(1 << 20) // math.isqrt(standing ** skew) + 1 for standing in range(2, amount + 1)]
    surplus, given = total - bound - (amount - 1), [1] * (amount - 1)
    while surplus > 0:
        free = [i for i in range(amount - 1) if given[i] < bound]
        pool, budget = sum([weights[i] for i in free]), surplus
        for i in free:
            addition = min(bound - given[i], max(1, budget * weights[i] // pool), surplus)
            given[i] = given[i] + addition
            surplus = surplus - addition
    return np.array([bound] + given)


def ragged(rng, count, total, limit, lean):
    if count == 2:
        one = jax.random.randint(rng, (), max(1, total - limit), min(limit, total - 1) + 1)
        return jnp.stack([one, total - one])
    sizes = jnp.asarray(length_profile(count, total, limit, lean), jnp.int32)
    couples = (count - 1) // 2
    giver, receiver = sizes[1:1 + 2 * couples:2], sizes[2:2 + 2 * couples:2]
    slack = jnp.minimum(giver - 1, limit - receiver)
    shifted = jax.random.randint(jax.random.fold_in(rng, 1), (couples,), 0, 1 << 20) % (slack + 1)
    sizes = sizes.at[1:1 + 2 * couples:2].set(giver - shifted).at[2:2 + 2 * couples:2].set(receiver + shifted)
    return sizes[jax.random.permutation(jax.random.fold_in(rng, 2), count)]


def scatter_about(key, shape, deviation, bound, shards=(), kind=jnp.bfloat16):
    values = deviation * jax.random.normal(key, shape, jnp.float32)
    if shards:
        values = values * steps_of(key, shape, shards, -0.22, 0.18)
    return jnp.clip(values, -bound, bound).astype(kind)


def setup_inputs(seed: int = 0) -> dict:
    splits = jax.random.split(jax.random.key(seed), 21)
    return {
        "block_input": scatter_about(splits[0], (MICRO, BATCH, SEQ, D), 1.0, 6.0, ((1, 16),)),
        "cotangent": scatter_about(splits[1], (MICRO, BATCH, SEQ, D), 1.0, 6.0, ((1, 16),)),
        "segments": jax.vmap(lambda own: jnp.searchsorted(jnp.cumsum(ragged(own, SEGS, SEQ, SEQ // 2, 0)), jnp.arange(SEQ), side="right"))(jax.random.split(splits[2], MICRO * BATCH)).reshape((MICRO, BATCH, SEQ)).astype(jnp.int32),
        "ln1_gain": jnp.clip(1.0 + 0.1 * jax.random.normal(splits[3], (LAYERS, D), jnp.float32), 0.5, 1.5),
        "ln1_shift": scatter_about(splits[4], (LAYERS, D), 0.2, 1.25, ((0, 2),), jnp.float32),
        "qkv_weight": scatter_about(splits[5], (LAYERS, D, 3 * D), D ** -0.5, 0.25, ((0, 2),)),
        "qkv_bias": scatter_about(splits[6], (LAYERS, 3 * D), 0.2, 1.25, ((0, 2),), jnp.float32),
        "attn_weight": scatter_about(splits[7], (LAYERS, D, D), (D // 32) ** -0.5, 1.5, ((0, 2),)),
        "attn_bias": scatter_about(splits[8], (LAYERS, D), 0.2, 1.25, ((0, 2),), jnp.float32),
        "ln2_gain": jnp.clip(1.0 + 0.1 * jax.random.normal(splits[9], (LAYERS, D), jnp.float32), 0.5, 1.5),
        "ln2_shift": scatter_about(splits[10], (LAYERS, D), 0.2, 1.25, ((0, 2),), jnp.float32),
        "ff_in_weight": scatter_about(splits[11], (LAYERS, D, FF), D ** -0.5, 0.25, ((0, 2),)),
        "ff_in_bias": scatter_about(splits[12], (LAYERS, FF), 0.2, 1.25, ((0, 2),), jnp.float32),
        "ff_out_weight": scatter_about(splits[13], (LAYERS, FF, D), FF ** -0.5, 0.125, ((0, 2),)),
        "ff_out_bias": scatter_about(splits[14], (LAYERS, D), 0.2, 1.25, ((0, 2),), jnp.float32),
        "prefix_embed": scatter_about(splits[15], (PREFIX, D), 1.0, 6.0, (), jnp.float32),
        "up_weight": scatter_about(splits[16], (D, REPARAM), D ** -0.5, 0.25, (), jnp.float32),
        "up_bias": scatter_about(splits[17], (REPARAM,), 0.5, 3.0, (), jnp.float32),
        "out_weight": scatter_about(splits[18], (REPARAM, 4 * D), (REPARAM // 2) ** -0.5, 0.375, (), jnp.float32),
        "out_bias": scatter_about(splits[19], (4 * D,), 0.3, 1.75, (), jnp.float32),
    }


@jax.custom_vjp
def low(v):
    return lax.optimization_barrier(v.astype(jnp.bfloat16)).astype(jnp.float32)

@jax.custom_vjp
def low_back(v):
    return v

def low_keep(v):
    return (low(v), None)

def low_pass(kept, grad):
    return (grad,)

def back_keep(v):
    return (v, None)

def back_low(kept, grad):
    return (low(grad),)
low.defvjp(low_keep, low_pass)
low_back.defvjp(back_keep, back_low)

def matmul_hi(left_mat, right_mat):
    return jnp.dot(left_mat, right_mat, precision=lax.Precision.HIGHEST, preferred_element_type=jnp.float32)

def layer_norm(values, gain_vec, shift_vec):
    row_mean = lax.optimization_barrier(jnp.mean(values, axis=-1, keepdims=True))
    centered = values - row_mean
    variance = lax.optimization_barrier(jnp.mean(centered * centered, axis=-1, keepdims=True))
    return centered * lax.rsqrt(variance + 1e-05) * gain_vec + shift_vec

def rotate_heads(head_rows):
    half_rot = ROT // 2
    positions = jnp.arange(head_rows.shape[0]).astype(head_rows.dtype)
    inv_freq = jnp.exp(jnp.arange(half_rot).astype(head_rows.dtype) * (-2.0 * math.log(10000.0) / ROT))
    angles = positions[:, None] * inv_freq[None, :]
    cosine = jnp.cos(angles)[:, None, :]
    sine_val = jnp.sin(angles)[:, None, :]
    lead_part = head_rows[..., :half_rot]
    tail_part = head_rows[..., half_rot:ROT]
    return jnp.concatenate([lead_part * cosine - tail_part * sine_val, tail_part * cosine + lead_part * sine_val, head_rows[..., ROT:]], axis=-1)

def seen_mask(seg_row):
    seq_len = seg_row.shape[0]
    key_pos = jnp.arange(seq_len)
    causal = key_pos[None, :] <= key_pos[:, None]
    same_seg = seg_row[None, :] == seg_row[:, None]
    return jnp.concatenate([jnp.ones((seq_len, PREFIX), dtype=jnp.bool_), causal & same_seg], axis=1)

def block_layer(hidden, prefix_keys, prefix_values, seg_row, params):
    gain_one, shift_one, w_qkv, b_qkv, w_attn, b_attn, gain_two, shift_two, w_in, bias_in, w_back, bias_back = params
    seq_len = hidden.shape[0]
    normed_one = low(layer_norm(hidden, gain_one, shift_one))
    packed = low_back(matmul_hi(normed_one, w_qkv) + b_qkv)
    queries = low(rotate_heads(packed[:, :D].reshape(seq_len, HEADS, HD)))
    key_rows = low(rotate_heads(packed[:, D:2 * D].reshape(seq_len, HEADS, HD)))
    value_rows = low(packed[:, 2 * D:].reshape(seq_len, HEADS, HD))
    key_list = jnp.concatenate([low(prefix_keys).reshape(PREFIX, HEADS, HD), key_rows], axis=0)
    value_list = jnp.concatenate([low(prefix_values).reshape(PREFIX, HEADS, HD), value_rows], axis=0)
    scores = low_back(jnp.einsum('qhd,khd->hqk', queries, key_list, precision=lax.Precision.HIGHEST) * HD ** (-0.5))
    scores = jnp.where(seen_mask(seg_row)[None], scores, -1e+30)
    probs = low(jax.nn.softmax(scores, axis=-1))
    mixed = jnp.einsum('hqk,khd->qhd', probs, value_list, precision=lax.Precision.HIGHEST).reshape(seq_len, D)
    mixed = low_back(low(mixed))
    attn_out = matmul_hi(mixed, w_attn) + b_attn
    normed_two = low(layer_norm(hidden, gain_two, shift_two))
    before = low_back(matmul_hi(normed_two, w_in) + bias_in)
    activated = low(jax.nn.gelu(before, approximate=False))
    return hidden + attn_out + matmul_hi(activated, w_back) + bias_back

def reparam(prefix_embed, up_weight, up_bias, out_weight, out_bias):
    hidden_units = jnp.tanh(matmul_hi(prefix_embed, up_weight) + up_bias)
    return matmul_hi(hidden_units, out_weight) + out_bias

def reference(block_input, cotangent, segments, ln1_gain, ln1_shift, qkv_weight, qkv_bias, attn_weight, attn_bias, ln2_gain, ln2_shift, ff_in_weight, ff_in_bias, ff_out_weight, ff_out_bias, prefix_embed, up_weight, up_bias, out_weight, out_bias):
    stacked = (ln1_gain, ln1_shift, qkv_weight, qkv_bias, attn_weight, attn_bias, ln2_gain, ln2_shift, ff_in_weight, ff_in_bias, ff_out_weight, ff_out_bias)
    layer_params = [tuple((array_in[layer_idx].astype(jnp.float32) for array_in in stacked)) for layer_idx in range(LAYERS)]
    prefix_states, reparam_back = jax.vjp(reparam, prefix_embed, up_weight, up_bias, out_weight, out_bias)

    def row_step(carry_sum, row_data):
        row_in, row_cot, seg_row = row_data

        def two_layers(start_rows, probe_rows, states_all):
            first_out = block_layer(start_rows, states_all[:, :D], states_all[:, D:2 * D], seg_row, layer_params[0])
            passed = low_back(low(first_out)) + probe_rows
            second_out = block_layer(passed, states_all[:, 2 * D:3 * D], states_all[:, 3 * D:], seg_row, layer_params[1])
            return (second_out, first_out)
        second_out, row_back, first_out = jax.vjp(two_layers, row_in.astype(jnp.float32), jnp.zeros((SEQ, D), jnp.float32), prefix_states, has_aux=True)
        grad_in, grad_probe, grad_states = row_back(row_cot.astype(jnp.float32))
        return (carry_sum + grad_states, (first_out.astype(jnp.bfloat16), second_out.astype(jnp.bfloat16), grad_in, grad_probe))
    rows_in = block_input.reshape(MICRO * BATCH, SEQ, D)
    rows_cot = cotangent.reshape(MICRO * BATCH, SEQ, D)
    rows_seg = segments.reshape(MICRO * BATCH, SEQ)
    prefix_grad, (firsts, seconds, grads_in, grads_probe) = lax.scan(row_step, jnp.zeros((PREFIX, 4 * D), jnp.float32), (rows_in, rows_cot, rows_seg))
    grad_embed, grad_up_weight, grad_up_bias, grad_out_weight, grad_out_bias = reparam_back(prefix_grad)
    activations = jnp.stack([firsts, seconds]).reshape(LAYERS, MICRO, BATCH, SEQ, D)
    input_grads = jnp.stack([grads_in, grads_probe]).reshape(LAYERS, MICRO, BATCH, SEQ, D)
    return (activations, input_grads, grad_embed, grad_up_weight, grad_up_bias, grad_out_weight, grad_out_bias)
```

```python
import math

import jax
import jax.numpy as jnp
import numpy as np
from jax import lax
from jax.experimental import pallas as pl
from jax.experimental.pallas import tpu as pltpu
from jax.sharding import PartitionSpec as P

D = 512
SEQ = 512
HEADS = 8
HD = 64
FF = 2048
ROT = 16
PREFIX = 10
PAD = 16
BLK = 128
BLOCKS = SEQ // BLK
PAIRS = HEADS // 2
LIVE = (1, 2, 3, 3)
P_ROWS = BLK * sum(LIVE)
P_START = (0, 128, 384, 768)

f32 = jnp.float32
bf16 = jnp.bfloat16
LOG2E = math.log2(math.e)
Q_SCALE = LOG2E * HD**-0.5
K_BACK = 1.0 / LOG2E
Q_BACK = HD**-0.5
NEG = -1e30

NN = (((1,), (0,)), ((), ()))
NT = (((1,), (1,)), ((), ()))
TN = (((0,), (0,)), ((), ()))

VMEM = pl.BlockSpec(memory_space=pltpu.VMEM)
ANY = pl.BlockSpec(memory_space=pl.ANY)
MIB = 1024 * 1024

G1, B1, G2, B2, B_ATTN, B_OUT, B_QKV, B_IN = 0, 1, 2, 3, 4, 5, 6, 9
SMALL_ROWS = 16


def dot(left, right, dims):
    return lax.dot_general(left, right, dims, preferred_element_type=f32)


def shape_of(shape, dtype):
    return jax.ShapeDtypeStruct(shape, dtype)


def params_of(mib):
    return pltpu.CompilerParams(vmem_limit_bytes=mib * MIB)


def rope_tables():
    inv_freq = 10000.0 ** (-2.0 * np.arange(ROT // 2) / ROT)
    angles = inv_freq[:, None] * np.arange(SEQ)[None, :]
    return np.concatenate([np.cos(angles), np.sin(angles)], axis=0).astype(np.float32)


def start_of_layer(section, layer, own, other, dst, sem):
    @pl.when(section == layer)
    def _():
        pltpu.make_async_copy(own, dst, sem).start()

    @pl.when(section != layer)
    def _():
        pltpu.make_async_copy(other, dst, sem).start()


def wait_for(src, dst, sem):
    pltpu.make_async_copy(src, dst, sem).wait()


def normalized(hidden):
    mean = jnp.mean(hidden, axis=-1, keepdims=True)
    centered = hidden - mean
    variance = jnp.mean(centered * centered, axis=-1, keepdims=True)
    scale = lax.rsqrt(variance + 1e-05)
    return centered * scale, scale


def rope_heads(rows, cos, sin):
    parts = []
    for head in range(rows.shape[0] // HD):
        base = head * HD
        lead = rows[base : base + 8]
        tail = rows[base + 8 : base + 16]
        parts += [lead * cos - tail * sin, tail * cos + lead * sin, rows[base + 16 : base + HD]]
    return jnp.concatenate(parts, axis=0)


def fill_mask(seg_ref, section, mask_ref):
    seg_row = seg_ref[pl.ds(section, 1), :].astype(f32)
    seg_col = jnp.transpose(jnp.broadcast_to(seg_row, (8, SEQ)))[:, 0:1]
    for block in range(BLOCKS):
        for key_block in range(block + 1 - LIVE[block], block + 1):
            seen = seg_col[key_block * BLK : (key_block + 1) * BLK] == (
                seg_row[:, block * BLK : (block + 1) * BLK]
            )
            if key_block == block:
                key_pos = lax.broadcasted_iota(jnp.int32, (BLK, BLK), 0)
                query_pos = lax.broadcasted_iota(jnp.int32, (BLK, BLK), 1)
                seen = seen & (key_pos <= query_pos)
            start = P_START[block] + (key_block - (block + 1 - LIVE[block])) * BLK
            mask_ref[start : start + BLK, :] = jnp.where(seen, 0.0, NEG)


def project_heads(normed, w_ref, small_ref, cos, sin, q_t, k_t, k_m, v_m, v_t):
    bias = small_ref[B_QKV : B_QKV + 1, :]
    rows = dot(normed, w_ref[:, :D], NN) + bias
    q_t[...] = (rope_heads(jnp.transpose(rows), cos, sin) * Q_SCALE).astype(bf16)
    bias = small_ref[B_QKV + 1 : B_QKV + 2, :]
    rows = dot(normed, w_ref[:, D : 2 * D], NN) + bias
    keys = rope_heads(jnp.transpose(rows), cos, sin).astype(bf16)
    k_t[...] = keys
    k_m[...] = jnp.transpose(keys)
    bias = small_ref[B_QKV + 2 : B_QKV + 3, :]
    values = (dot(normed, w_ref[:, 2 * D :], NN) + bias).astype(bf16)
    v_m[...] = values
    v_t[...] = jnp.transpose(values)


def block_diagonal(pair_rows):
    zeros = jnp.zeros((HD, BLK), pair_rows.dtype)
    return jnp.concatenate(
        [
            jnp.concatenate([pair_rows[:HD], zeros], axis=1),
            jnp.concatenate([zeros, pair_rows[HD:]], axis=1),
        ],
        axis=0,
    )


def from_diagonal(both):
    return jnp.concatenate([both[:HD, :BLK], both[HD:, BLK:]], axis=0)


def per_head(row, rows=HD):
    return jnp.concatenate(
        [
            jnp.broadcast_to(row[:, :BLK], (rows, BLK)),
            jnp.broadcast_to(row[:, BLK:], (rows, BLK)),
        ],
        axis=0,
    )


def attend(q_t, k_m, v_t, pre_k, pre_v_t, mask_ref, p_ref, pp_ref, inv_ref, mixed_ref):
    pad_mask = jnp.where(lax.broadcasted_iota(jnp.int32, (PAD, 1), 0) < PREFIX, 0.0, NEG)

    def one_pair(pair, carry):
        feats = pl.ds(pl.multiple_of(pair * BLK, BLK), BLK)
        prefix_keys = pre_k[:, feats]
        prefix_values = pre_v_t[feats, :]
        for block in range(BLOCKS):
            live = LIVE[block] * BLK
            key_start = (block + 1) * BLK - live
            tokens = slice(block * BLK, (block + 1) * BLK)
            queries = block_diagonal(q_t[feats, tokens])
            mask = mask_ref[P_START[block] : P_START[block] + live, :]
            scores = dot(k_m[key_start : key_start + live, feats], queries, NN)
            scores = scores + jnp.concatenate([mask, mask], axis=1)
            pre_scores = dot(prefix_keys, queries, NN) + pad_mask
            peak = jnp.maximum(
                jnp.max(scores, axis=0, keepdims=True), jnp.max(pre_scores, axis=0, keepdims=True)
            )
            expo = jnp.exp2(scores - peak)
            pre_expo = jnp.exp2(pre_scores - peak)
            total = jnp.sum(expo, axis=0, keepdims=True) + jnp.sum(pre_expo, axis=0, keepdims=True)
            inverse = 1.0 / total
            expo = expo.astype(bf16)
            pre_expo = pre_expo.astype(bf16)
            mixed = dot(v_t[feats, key_start : key_start + live], expo, NN) + dot(
                prefix_values, pre_expo, NN
            )
            mixed_ref[feats, tokens] = (from_diagonal(mixed) * per_head(inverse)).astype(bf16)
            p_ref[pair, P_START[block] : P_START[block] + live, :] = expo
            pp_ref[pair, block] = pre_expo
            inv_ref[pair, block] = jnp.broadcast_to(inverse, (8, 2 * BLK))
        return carry

    lax.fori_loop(0, PAIRS, one_pair, 0)


def attend_back(grad_t, q_t, k_t, v_m, pre_k_t, pre_v, p_ref, pp_ref, inv_ref, mixed_ref,
                dq_ref, dk_ref, dv_ref, pre_grad, pre_row):
    def one_pair(pair, carry):
        feats = pl.ds(pl.multiple_of(pair * BLK, BLK), BLK)
        prefix_values = pre_v[:, feats]
        prefix_keys_t = pre_k_t[feats, :]
        pre_dk = jnp.zeros((PAD, BLK), f32)
        pre_dv = jnp.zeros((PAD, BLK), f32)
        for block in range(BLOCKS):
            live = LIVE[block] * BLK
            key_start = (block + 1) * BLK - live
            keys = slice(key_start, key_start + live)
            tokens = slice(block * BLK, (block + 1) * BLK)
            scaled = (grad_t[feats, tokens] * per_head(inv_ref[pair, block][0:1, :])).astype(bf16)
            products = scaled.astype(f32) * mixed_ref[feats, tokens].astype(f32)
            inner = jnp.concatenate(
                [
                    jnp.sum(products[:HD], axis=0, keepdims=True),
                    jnp.sum(products[HD:], axis=0, keepdims=True),
                ],
                axis=1,
            )
            grads = block_diagonal(scaled)
            queries = block_diagonal(q_t[feats, tokens])
            probs = p_ref[pair, P_START[block] : P_START[block] + live, :]
            pre_probs = pp_ref[pair, block]
            grad_probs = dot(v_m[keys, feats], grads, NN)
            pre_grad_probs = dot(prefix_values, grads, NN)
            grad_scores = (probs.astype(f32) * (grad_probs - inner)).astype(bf16)
            pre_scores = (pre_probs.astype(f32) * (pre_grad_probs - inner)).astype(bf16)
            dq = dot(k_t[feats, keys], grad_scores, NN) + dot(prefix_keys_t, pre_scores, NN)
            dq_ref[feats, tokens] = from_diagonal(dq)
            dv = dot(grads, probs, NT)
            dk = dot(queries, grad_scores, NT)
            if live > BLK:
                old = slice(key_start, block * BLK)
                dv_ref[feats, old] += dv[:, : live - BLK]
                dk_ref[feats, old] += dk[:, : live - BLK]
            dv_ref[feats, tokens] = dv[:, live - BLK :]
            dk_ref[feats, tokens] = dk[:, live - BLK :]
            pre_dk = pre_dk + dot(pre_scores, queries, NT)
            pre_dv = pre_dv + dot(pre_probs, grads, NT)
        pre_grad[pre_row : pre_row + PAD, feats] = pre_dk * K_BACK
        pre_grad[pre_row + PAD : pre_row + 2 * PAD, feats] = pre_dv
        return carry

    lax.fori_loop(0, PAIRS, one_pair, 0)


def pack_grads(dq_ref, dk_ref, dv_ref, cos, sin, packed_t):
    packed_t[:D, :] = (rope_heads(dq_ref[...], cos, -sin) * Q_BACK).astype(bf16)
    packed_t[D : 2 * D, :] = (rope_heads(dk_ref[...], cos, -sin) * K_BACK).astype(bf16)
    packed_t[2 * D :, :] = dv_ref[...].astype(bf16)


def gelu_both(before):
    cdf = 0.5 + 0.5 * lax.erf(before * (0.5**0.5))
    density = jnp.exp2(before * before * (-0.5 * LOG2E)) * (1.0 / math.sqrt(2.0 * math.pi))
    return before * cdf, cdf + before * density


FF_CHUNK = 512


def feed_in(normed, w_ref, small_ref, act_ref, slope_ref):
    for chunk in range(FF // FF_CHUNK):
        cols = slice(chunk * FF_CHUNK, (chunk + 1) * FF_CHUNK)
        before = dot(normed, w_ref[:, cols], NN) + small_ref[B_IN + chunk : B_IN + chunk + 1, :]
        act, slope = gelu_both(before)
        act_ref[:, cols] = act.astype(bf16)
        slope_ref[:, cols] = slope.astype(bf16)


def layer_result(hidden, mixed_t, w_attn, act_ref, w_out, small_ref):
    attn_out = dot(jnp.transpose(mixed_t), w_attn, NN) + small_ref[B_ATTN : B_ATTN + 1, :]
    ff_out = dot(act_ref[...], w_out, NN) + small_ref[B_OUT : B_OUT + 1, :]
    return hidden + attn_out + ff_out


def feed_back(grad, w_out, w_in, slope_ref):
    total = jnp.zeros((SEQ, D), f32)
    for chunk in range(FF // FF_CHUNK):
        cols = slice(chunk * FF_CHUNK, (chunk + 1) * FF_CHUNK)
        grad_act = dot(grad, w_out[cols, :], NT)
        grad_before = (grad_act * slope_ref[:, cols].astype(f32)).astype(bf16)
        total = total + dot(grad_before, w_in[:, cols], NT)
    return total


def norms_back(grad, hidden, grad_two, packed_t, w_qkv, small_ref):
    grad_one = jnp.transpose(dot(w_qkv, packed_t, NN))
    grad_hat = (
        grad_one * small_ref[G1 : G1 + 1, :] + grad_two * small_ref[G2 : G2 + 1, :]
    )
    hat, scale = normalized(hidden)
    mean_one = jnp.mean(grad_hat, axis=-1, keepdims=True)
    mean_two = jnp.mean(grad_hat * hat, axis=-1, keepdims=True)
    return grad.astype(f32) + scale * (grad_hat - mean_one - hat * mean_two)


def prefix_kernel(embed, up_w, up_b, out_w, out_b, hidden_ref, low_ref, low_t_ref):
    high = lax.Precision.HIGHEST
    units = jnp.tanh(
        jnp.dot(embed[...], up_w[...], precision=high, preferred_element_type=f32) + up_b[...]
    )
    hidden_ref[...] = units
    for part in range(4):
        cols = slice(part * D, (part + 1) * D)
        states = (
            jnp.dot(units, out_w[:, cols], precision=high, preferred_element_type=f32)
            + out_b[:, cols]
        )
        padded = jnp.concatenate([states, jnp.zeros((BLK - PREFIX, D), f32)], axis=0)
        low_ref[part] = padded[:PAD].astype(bf16)
        low_t_ref[part] = jnp.transpose(padded)[:, :PAD].astype(bf16)


def prefix_call(embed, up_w, up_b, out_w, out_b):
    return pl.pallas_call(
        prefix_kernel,
        name="prefix",
        out_shape=[
            shape_of((PREFIX, D), f32),
            shape_of((4, PAD, D), bf16),
            shape_of((4, D, PAD), bf16),
        ],
        compiler_params=params_of(32),
    )(embed, up_w, up_b.reshape(1, D), out_w, out_b.reshape(1, 4 * D))


def head_outputs():
    return [
        shape_of((D, SEQ), bf16),
        shape_of((D, SEQ), bf16),
        shape_of((SEQ, D), bf16),
        shape_of((PAIRS, P_ROWS, 2 * BLK), bf16),
        shape_of((PAIRS, BLOCKS, PAD, 2 * BLK), bf16),
        shape_of((PAIRS, BLOCKS, 8, 2 * BLK), f32),
        shape_of((D, SEQ), bf16),
    ]


def first_kernel(x_hbm, seg, own_small, other_small, own_qkv, other_qkv, low, low_t, tables,
                 q_t, k_t, v_m, p_ref, pp_ref, inv_ref, mixed_ref, two_ref, mask_ref,
                 x_ref, w_ref, small_ref, k_m, v_t, sems):
    section = lax.axis_index("pipe")
    x_copy = pltpu.make_async_copy(x_hbm.at[section, 0], x_ref, sems.at[0])
    x_copy.start()
    start_of_layer(section, 0, own_small, other_small, small_ref, sems.at[1])
    start_of_layer(section, 0, own_qkv.at[0], other_qkv.at[0], w_ref, sems.at[2])
    fill_mask(seg, section, mask_ref)
    x_copy.wait()
    wait_for(own_small, small_ref, sems.at[1])
    hat, _ = normalized(x_ref[...].astype(f32))
    normed = (hat * small_ref[G1 : G1 + 1, :] + small_ref[B1 : B1 + 1, :]).astype(bf16)
    two_ref[...] = (hat * small_ref[G2 : G2 + 1, :] + small_ref[B2 : B2 + 1, :]).astype(bf16)
    wait_for(own_qkv.at[0], w_ref, sems.at[2])
    cos, sin = tables[:8, :], tables[8:, :]
    project_heads(normed, w_ref, small_ref, cos, sin, q_t, k_t, k_m, v_m, v_t)
    attend(q_t, k_m, v_t, low.at[0], low_t.at[1], mask_ref, p_ref, pp_ref, inv_ref, mixed_ref)


def first_call(block_input, seg, own_small, other_small, own_qkv, other_qkv, low, low_t, tables):
    return pl.pallas_call(
        first_kernel,
        name="first_attention",
        out_shape=head_outputs() + [shape_of((SEQ, D), bf16), shape_of((P_ROWS, BLK), f32)],
        in_specs=[ANY, VMEM, ANY, ANY, ANY, ANY, VMEM, VMEM, VMEM],
        out_specs=[VMEM] * 9,
        scratch_shapes=[
            pltpu.VMEM((SEQ, D), bf16),
            pltpu.VMEM((D, 3 * D), bf16),
            pltpu.VMEM((SMALL_ROWS, D), f32),
            pltpu.VMEM((SEQ, D), bf16),
            pltpu.VMEM((D, SEQ), bf16),
            pltpu.SemaphoreType.DMA((3,)),
        ],
        compiler_params=params_of(48),
    )(block_input, seg, own_small, other_small, own_qkv, other_qkv, low, low_t, tables)


def feed_kernel(two_ref, own_small, other_small, own_in, other_in, act_ref, slope_ref,
                w_ref, small_ref, sems):
    section = lax.axis_index("pipe")
    start_of_layer(section, 0, own_small, other_small, small_ref, sems.at[0])
    start_of_layer(section, 0, own_in.at[0], other_in.at[0], w_ref, sems.at[1])
    wait_for(own_small, small_ref, sems.at[0])
    wait_for(own_in.at[0], w_ref, sems.at[1])
    feed_in(two_ref[...], w_ref, small_ref, act_ref, slope_ref)


def feed_call(normed_two, own_small, other_small, own_in, other_in):
    return pl.pallas_call(
        feed_kernel,
        name="first_feed",
        out_shape=[shape_of((SEQ, FF), bf16)] * 2,
        in_specs=[VMEM, ANY, ANY, ANY, ANY],
        out_specs=[VMEM] * 2,
        scratch_shapes=[
            pltpu.VMEM((D, FF), bf16),
            pltpu.VMEM((SMALL_ROWS, D), f32),
            pltpu.SemaphoreType.DMA((2,)),
        ],
        compiler_params=params_of(32),
    )(normed_two, own_small, other_small, own_in, other_in)


def middle_kernel(x_hbm, cot_hbm, mask_ref, own_small, other_small, own_qkv, other_qkv,
                  own_attn, other_attn, own_in, other_in, own_out, other_out, low, low_t, tables,
                  q0_hbm, k0_hbm, v0_hbm, p0_hbm, pp0_ref, inv0_ref, mixed0_ref, act0_hbm,
                  h_one, act_one, mixed_one, grad_one, grad_low, packed_zero, prefix_grad,
                  x_ref, cot_ref, small_zero, small_one, w_qkv, w_attn_zero, w_attn, w_in, w_out_zero, w_out,
                  act_ref, q_t, k_t, k_m, v_m, v_t, p_ref, pp_ref, inv_ref, slope_ref,
                  q0, k0, v0, p0, dq, dk, dv, packed, pre_grad, sems):
    section = lax.axis_index("pipe")
    copies = []

    def fetch(src, dst, sem):
        copy = pltpu.make_async_copy(src, dst, sems.at[sem])
        copy.start()
        return copy

    start_of_layer(section, 0, own_small, other_small, small_zero, sems.at[0])
    start_of_layer(section, 0, own_attn.at[0], other_attn.at[0], w_attn_zero, sems.at[1])
    x_copy = fetch(x_hbm.at[section, 0], x_ref, 2)
    start_of_layer(section, 0, own_out.at[0], other_out.at[0], w_out_zero, sems.at[3])
    act_copy = fetch(act0_hbm, act_ref, 4)
    start_of_layer(section, 1, own_small, other_small, small_one, sems.at[5])
    start_of_layer(section, 1, own_qkv.at[0], other_qkv.at[0], w_qkv, sems.at[6])
    start_of_layer(section, 1, own_in.at[0], other_in.at[0], w_in, sems.at[7])
    cot_copy = fetch(cot_hbm.at[section, 0], cot_ref, 8)
    start_of_layer(section, 1, own_out.at[0], other_out.at[0], w_out, sems.at[9])
    start_of_layer(section, 1, own_attn.at[0], other_attn.at[0], w_attn, sems.at[10])
    late = [
        fetch(src, dst, 11 + i)
        for i, (src, dst) in enumerate(((q0_hbm, q0), (k0_hbm, k0), (v0_hbm, v0), (p0_hbm, p0)))
    ]
    cos, sin = tables[:8, :], tables[8:, :]

    wait_for(own_small, small_zero, sems.at[0])
    wait_for(own_attn.at[0], w_attn_zero, sems.at[1])
    x_copy.wait()
    wait_for(own_out.at[0], w_out_zero, sems.at[3])
    act_copy.wait()
    h_one[...] = layer_result(
        x_ref[...].astype(f32), mixed0_ref[...], w_attn_zero[...], act_ref, w_out_zero[...], small_zero
    ).astype(bf16)

    hidden = h_one[...].astype(f32)
    hat, _ = normalized(hidden)
    wait_for(own_small, small_one, sems.at[5])
    normed = (hat * small_one[G1 : G1 + 1, :] + small_one[B1 : B1 + 1, :]).astype(bf16)
    two = (hat * small_one[G2 : G2 + 1, :] + small_one[B2 : B2 + 1, :]).astype(bf16)
    wait_for(own_qkv.at[0], w_qkv, sems.at[6])
    project_heads(normed, w_qkv, small_one, cos, sin, q_t, k_t, k_m, v_m, v_t)
    attend(q_t, k_m, v_t, low.at[2], low_t.at[3], mask_ref, p_ref, pp_ref, inv_ref, mixed_one)
    wait_for(own_in.at[0], w_in, sems.at[7])
    feed_in(two, w_in, small_one, act_one, slope_ref)

    cot_copy.wait()
    wait_for(own_out.at[0], w_out, sems.at[9])
    grad = cot_ref[...]
    grad_two = feed_back(grad, w_out, w_in, slope_ref)
    wait_for(own_attn.at[0], w_attn, sems.at[10])
    dq[...] = dot(w_attn[...], grad, NT)
    attend_back(dq, q_t, k_t, v_m, low_t.at[2], low.at[3], p_ref, pp_ref, inv_ref, mixed_one,
                dq, dk, dv, pre_grad, 2 * PAD)
    pack_grads(dq, dk, dv, cos, sin, packed)
    result = norms_back(grad, hidden, grad_two, packed[...], w_qkv[...], small_one)
    grad_one[...] = result
    grad_low[...] = result.astype(bf16)

    dq[...] = dot(w_attn_zero[...], grad_low[...], NT)
    for copy in late:
        copy.wait()
    attend_back(dq, q0, k0, v0, low_t.at[0], low.at[1], p0, pp0_ref, inv0_ref, mixed0_ref,
                dq, dk, dv, pre_grad, 0)
    pack_grads(dq, dk, dv, cos, sin, packed_zero)
    for part in range(4):
        prefix_grad[part * PREFIX : (part + 1) * PREFIX, :] = pre_grad[
            part * PAD : part * PAD + PREFIX, :
        ]


def middle_call(block_input, cotangent, mask, own_small, other_small, own, other, low, low_t, tables,
                heads_zero, act_zero):
    q0, k0, v0, p0, pp0, inv0, mixed0 = heads_zero
    own_qkv, own_attn, own_in, own_out = own
    other_qkv, other_attn, other_in, other_out = other
    return pl.pallas_call(
        middle_kernel,
        name="middle",
        out_shape=[
            shape_of((SEQ, D), bf16),
            shape_of((SEQ, FF), bf16),
            shape_of((D, SEQ), bf16),
            shape_of((SEQ, D), f32),
            shape_of((SEQ, D), bf16),
            shape_of((3 * D, SEQ), bf16),
            shape_of((4 * PREFIX, D), f32),
        ],
        in_specs=[ANY, ANY, VMEM] + [ANY] * 10 + [VMEM] * 3 + [ANY] * 4 + [VMEM] * 3 + [ANY],
        out_specs=[VMEM] * 7,
        scratch_shapes=[
            pltpu.VMEM((SEQ, D), bf16),
            pltpu.VMEM((SEQ, D), bf16),
            pltpu.VMEM((SMALL_ROWS, D), f32),
            pltpu.VMEM((SMALL_ROWS, D), f32),
            pltpu.VMEM((D, 3 * D), bf16),
            pltpu.VMEM((D, D), bf16),
            pltpu.VMEM((D, D), bf16),
            pltpu.VMEM((D, FF), bf16),
            pltpu.VMEM((FF, D), bf16),
            pltpu.VMEM((FF, D), bf16),
            pltpu.VMEM((SEQ, FF), bf16),
            pltpu.VMEM((D, SEQ), bf16),
            pltpu.VMEM((D, SEQ), bf16),
            pltpu.VMEM((SEQ, D), bf16),
            pltpu.VMEM((SEQ, D), bf16),
            pltpu.VMEM((D, SEQ), bf16),
            pltpu.VMEM((PAIRS, P_ROWS, 2 * BLK), bf16),
            pltpu.VMEM((PAIRS, BLOCKS, PAD, 2 * BLK), bf16),
            pltpu.VMEM((PAIRS, BLOCKS, 8, 2 * BLK), f32),
            pltpu.VMEM((SEQ, FF), bf16),
            pltpu.VMEM((D, SEQ), bf16),
            pltpu.VMEM((D, SEQ), bf16),
            pltpu.VMEM((SEQ, D), bf16),
            pltpu.VMEM((PAIRS, P_ROWS, 2 * BLK), bf16),
            pltpu.VMEM((D, SEQ), f32),
            pltpu.VMEM((D, SEQ), f32),
            pltpu.VMEM((D, SEQ), f32),
            pltpu.VMEM((3 * D, SEQ), bf16),
            pltpu.VMEM((4 * PAD, D), f32),
            pltpu.SemaphoreType.DMA((15,)),
        ],
        compiler_params=params_of(60),
    )(
        block_input, cotangent, mask, own_small, other_small, own_qkv, other_qkv, own_attn,
        other_attn, own_in, other_in, own_out, other_out, low, low_t, tables, q0, k0, v0, p0, pp0,
        inv0, mixed0, act_zero,
    )


def late_kernel(x_hbm, own_small, other_small, own_qkv, other_qkv, own_attn, other_attn, own_in,
                other_in, own_out, other_out, h_one, act_one, mixed_one, grad_one, grad_low,
                packed_zero, slope_zero, act_keep, act_send, grad_keep, grad_send,
                x_ref, small_zero, small_one, w_qkv, w_attn, w_in, w_out_zero, w_out, sems):
    section = lax.axis_index("pipe")
    start_of_layer(section, 0, own_small, other_small, small_zero, sems.at[0])
    start_of_layer(section, 0, own_out.at[0], other_out.at[0], w_out_zero, sems.at[1])
    start_of_layer(section, 0, own_in.at[0], other_in.at[0], w_in, sems.at[2])
    start_of_layer(section, 0, own_qkv.at[0], other_qkv.at[0], w_qkv, sems.at[3])
    x_copy = pltpu.make_async_copy(x_hbm.at[section, 0], x_ref, sems.at[4])
    x_copy.start()
    start_of_layer(section, 1, own_small, other_small, small_one, sems.at[5])
    start_of_layer(section, 1, own_attn.at[0], other_attn.at[0], w_attn, sems.at[6])
    start_of_layer(section, 1, own_out.at[0], other_out.at[0], w_out, sems.at[7])

    wait_for(own_small, small_zero, sems.at[0])
    wait_for(own_out.at[0], w_out_zero, sems.at[1])
    wait_for(own_in.at[0], w_in, sems.at[2])
    grad_two = feed_back(grad_low[...], w_out_zero, w_in, slope_zero)
    wait_for(own_qkv.at[0], w_qkv, sems.at[3])
    x_copy.wait()
    grad_zero = norms_back(
        grad_low[...], x_ref[...].astype(f32), grad_two, packed_zero[...], w_qkv[...], small_zero
    )

    wait_for(own_small, small_one, sems.at[5])
    wait_for(own_attn.at[0], w_attn, sems.at[6])
    wait_for(own_out.at[0], w_out, sems.at[7])
    h_two = layer_result(
        h_one[...].astype(f32), mixed_one[...], w_attn[...], act_one, w_out[...], small_one
    ).astype(bf16)

    @pl.when(section == 0)
    def _():
        act_keep[...] = h_one[...]
        act_send[...] = h_two
        grad_keep[...] = grad_zero
        grad_send[...] = grad_one[...].astype(grad_send.dtype)

    @pl.when(section != 0)
    def _():
        act_keep[...] = h_two
        act_send[...] = h_one[...]
        grad_keep[...] = grad_one[...]
        grad_send[...] = grad_zero.astype(grad_send.dtype)


def late_call(block_input, own_small, other_small, own, other, middle, slope_zero):
    h_one, act_one, mixed_one, grad_one, grad_low, packed_zero = middle
    own_qkv, own_attn, own_in, own_out = own
    other_qkv, other_attn, other_in, other_out = other
    return pl.pallas_call(
        late_kernel,
        name="late",
        out_shape=[
            shape_of((SEQ, D), bf16),
            shape_of((SEQ, D), bf16),
            shape_of((SEQ, D), f32),
            shape_of((SEQ, D), f32),
        ],
        in_specs=[ANY] * 11 + [VMEM] * 7,
        out_specs=[VMEM] * 4,
        scratch_shapes=[
            pltpu.VMEM((SEQ, D), bf16),
            pltpu.VMEM((SMALL_ROWS, D), f32),
            pltpu.VMEM((SMALL_ROWS, D), f32),
            pltpu.VMEM((D, 3 * D), bf16),
            pltpu.VMEM((D, D), bf16),
            pltpu.VMEM((D, FF), bf16),
            pltpu.VMEM((FF, D), bf16),
            pltpu.VMEM((FF, D), bf16),
            pltpu.SemaphoreType.DMA((8,)),
        ],
        compiler_params=params_of(48),
    )(
        block_input, own_small, other_small, own_qkv, other_qkv, own_attn, other_attn, own_in,
        other_in, own_out, other_out, h_one, act_one, mixed_one, grad_one, grad_low, packed_zero,
        slope_zero,
    )


def final_kernel(col_width, grads_ref, hidden_ref, embed, up_w, out_w, act_keep, act_other, grad_keep,
                 grad_other, d_embed, d_up, d_up_b, d_out, d_out_b, act_out, grad_out, sems):
    section = lax.axis_index("pipe")
    shard = lax.axis_index("dp")
    copies = [
        pltpu.make_async_copy(act_keep, act_out.at[0, section, 0], sems.at[0]),
        pltpu.make_async_copy(act_other, act_out.at[0, 1 - section, 0], sems.at[1]),
        pltpu.make_async_copy(grad_keep, grad_out.at[0, section, 0], sems.at[2]),
        pltpu.make_async_copy(grad_other, grad_out.at[0, 1 - section, 0], sems.at[3]),
    ]
    for copy in copies:
        copy.start()
    high = lax.Precision.HIGHEST
    units = hidden_ref[...]
    grad_units = jnp.zeros((PREFIX, D), f32)
    for part in range(4):
        grad_units = grad_units + lax.dot_general(
            grads_ref[part * PREFIX : (part + 1) * PREFIX, :], out_w[:, part * D : (part + 1) * D],
            NT, precision=high, preferred_element_type=f32,
        )
    grad_pre = grad_units * (1.0 - units * units)
    d_up_b[...] = jnp.sum(grad_pre, axis=0, keepdims=True)
    d_up[...] = lax.dot_general(embed[...], grad_pre, TN, precision=high, preferred_element_type=f32)
    d_embed[...] = lax.dot_general(grad_pre, up_w[...], NT, precision=high, preferred_element_type=f32)
    column = section * (2 * D) + shard * col_width
    own_part = column // D
    own_cols = jnp.zeros((PREFIX, col_width), f32)
    for part in range(4):
        for piece in range(D // col_width):
            here = (column == part * D + piece * col_width).astype(f32)
            own_cols = own_cols + here * grads_ref[
                part * PREFIX : (part + 1) * PREFIX, piece * col_width : (piece + 1) * col_width
            ]
    d_out[...] = lax.dot_general(units, own_cols, TN, precision=high, preferred_element_type=f32)
    d_out_b[...] = jnp.sum(own_cols, axis=0, keepdims=True)
    for copy in copies:
        copy.wait()


def final_call(col_width, prefix_grad, hidden_units, embed, up_w, out_w, act_keep, act_other, grad_keep, grad_other):
    def body(*refs):
        final_kernel(col_width, *refs)

    return pl.pallas_call(
        body,
        name="reparam",
        out_shape=[
            shape_of((PREFIX, D), f32),
            shape_of((D, D), f32),
            shape_of((1, D), f32),
            shape_of((D, col_width), f32),
            shape_of((1, col_width), f32),
            shape_of((1, 2, 1, SEQ, D), bf16),
            shape_of((1, 2, 1, SEQ, D), f32),
        ],
        in_specs=[VMEM] * 5 + [ANY] * 4,
        out_specs=[VMEM] * 5 + [ANY] * 2,
        scratch_shapes=[pltpu.SemaphoreType.DMA((4,))],
        compiler_params=params_of(48),
    )(prefix_grad, hidden_units, embed, up_w, out_w, act_keep, act_other, grad_keep, grad_other)


def swapped(array_in):
    return lax.ppermute(array_in, "pipe", [(0, 1), (1, 0)])


def summed(array_in, axis):
    size = lax.axis_size(axis)
    if size & (size - 1):
        return lax.psum(array_in, axis)
    step = 1
    while step < size:
        array_in = array_in + lax.ppermute(array_in, axis, [(i, i ^ step) for i in range(size)])
        step *= 2
    return array_in


def local(
    block_input,
    cotangent,
    segments,
    ln1_gain,
    ln1_shift,
    qkv_weight,
    qkv_bias,
    attn_weight,
    attn_bias,
    ln2_gain,
    ln2_shift,
    ff_in_weight,
    ff_in_bias,
    ff_out_weight,
    ff_out_bias,
    prefix_embed,
    up_weight,
    up_bias,
    out_weight,
    out_bias,
):
    small = jnp.concatenate(
        [ln1_gain, ln1_shift, ln2_gain, ln2_shift, attn_bias, ff_out_bias]
        + [qkv_bias.reshape(3, D), ff_in_bias.reshape(4, D), jnp.zeros((3, D), f32)],
        axis=0,
    )
    own = (qkv_weight, attn_weight, ff_in_weight, ff_out_weight)
    other_small = swapped(small)
    other_qkv = swapped(qkv_weight)
    other_in = swapped(ff_in_weight)
    other_out = swapped(ff_out_weight)
    other_attn = swapped(attn_weight)
    other = (other_qkv, other_attn, other_in, other_out)
    tables = jnp.asarray(rope_tables())
    hidden_units, low, low_t = prefix_call(prefix_embed, up_weight, up_bias, out_weight, out_bias)
    *heads_zero, normed_two, mask = first_call(
        block_input, segments[:, 0], small, other_small, qkv_weight, other_qkv, low, low_t, tables
    )
    act_zero, slope_zero = feed_call(normed_two, small, other_small, ff_in_weight, other_in)
    *middle, prefix_grad = middle_call(
        block_input, cotangent, mask, small, other_small, own, other, low, low_t, tables,
        heads_zero, act_zero,
    )
    act_keep, act_send, grad_keep, grad_send = late_call(
        block_input, small, other_small, own, other, middle, slope_zero
    )
    act_other = swapped(act_send)
    grad_other = swapped(grad_send)
    for axis in ("pipe", "dp", "grp"):
        prefix_grad = summed(prefix_grad, axis)
    col_width = 2 * D // lax.axis_size("dp")
    grad_embed, grad_up, grad_up_b, grad_out, grad_out_b, activations, input_grads = final_call(
        col_width, prefix_grad, hidden_units, prefix_embed, up_weight, out_weight,
        act_keep, act_other, grad_keep, grad_other,
    )
    return (
        activations,
        input_grads,
        grad_embed,
        grad_up,
        grad_up_b[0],
        grad_out,
        grad_out_b[0],
    )


def solution(mesh):
    return jax.shard_map(
        local,
        mesh=mesh,
        in_specs=(
            P(None, ("grp", "dp"), None, None),
            P(None, ("grp", "dp"), None, None),
            P(None, ("grp", "dp"), None),
            P("pipe", None),
            P("pipe", None),
            P("pipe", None, None),
            P("pipe", None),
            P("pipe", None, None),
            P("pipe", None),
            P("pipe", None),
            P("pipe", None),
            P("pipe", None, None),
            P("pipe", None),
            P("pipe", None, None),
            P("pipe", None),
            P(),
            P(),
            P(),
            P(),
            P(),
        ),
        out_specs=(
            P("pipe", None, ("grp", "dp"), None, None),
            P("pipe", None, ("grp", "dp"), None, None),
            P(),
            P(),
            P(),
            P(None, ("pipe", "dp")),
            P(("pipe", "dp")),
        ),
        check_vma=False,
    )
```

```python
import math

import jax
import jax.numpy as jnp
import numpy as np
from jax import lax
from jax.experimental import pallas as pl
from jax.experimental.pallas import tpu as pltpu
from jax.sharding import PartitionSpec as P

D = 512
SEQ = 512
HEADS = 8
HD = 64
FF = 2048
ROT = 16
PREFIX = 10
PAD = 16
BLK = 128
BLOCKS = SEQ // BLK
PAIRS = HEADS // 2
LIVE = (1, 2, 3, 3)
P_ROWS = BLK * sum(LIVE)
P_START = (0, 128, 384, 768)

f32 = jnp.float32
bf16 = jnp.bfloat16
LOG2E = math.log2(math.e)
Q_SCALE = LOG2E * HD**-0.5
K_BACK = 1.0 / LOG2E
Q_BACK = HD**-0.5
NEG = -1e30

NN = (((1,), (0,)), ((), ()))
NT = (((1,), (1,)), ((), ()))
TN = (((0,), (0,)), ((), ()))

VMEM = pl.BlockSpec(memory_space=pltpu.VMEM)
NO_COPIES = ((),) * 4
ANY = pl.BlockSpec(memory_space=pltpu.HBM)
MIB = 1024 * 1024
LATE_MIB = 16

G1, B1, G2, B2, B_ATTN, B_OUT, B_QKV, B_IN = 0, 1, 2, 3, 4, 5, 6, 9
SMALL = 13 * D


def dot(left, right, dims):
    return lax.dot_general(left, right, dims, preferred_element_type=f32)


def shape_of(shape, dtype):
    return jax.ShapeDtypeStruct(shape, dtype)


def params_of(mib):
    return pltpu.CompilerParams(vmem_limit_bytes=mib * MIB)


def all_vmem():
    return pltpu.CompilerParams(vmem_limit_bytes=64 * MIB - 64 * 1024)


def small_row(small_ref, place):
    return small_ref[:, place * D : (place + 1) * D]


def estimate(flops, bytes_accessed):
    return pl.CostEstimate(flops=flops, bytes_accessed=bytes_accessed, transcendentals=0)


def rope_tables():
    inv_freq = 10000.0 ** (-2.0 * np.arange(ROT // 2) / ROT)
    angles = inv_freq[:, None] * np.arange(SEQ)[None, :]
    return np.concatenate([np.cos(angles), np.sin(angles)], axis=0).astype(np.float32)


class Copies:
    def __init__(self, sems):
        self.sems = sems
        self.count = 0

    def start(self, src, dst):
        copy = pltpu.make_async_copy(src, dst, self.sems.at[self.count])
        self.count += 1
        copy.start()
        return copy

    def of_layer(self, here, own, other, dst):
        sem = self.sems.at[self.count]
        self.count += 1
        copy = pltpu.make_async_copy(own, dst, sem)

        @pl.when(here)
        def _():
            copy.start()

        @pl.when(jnp.logical_not(here))
        def _():
            pltpu.make_async_copy(other, dst, sem).start()

        return copy


def wait_all(*copies):
    for copy in copies:
        copy.wait()


def normalized(hidden):
    mean = jnp.mean(hidden, axis=-1, keepdims=True)
    centered = hidden - mean
    variance = jnp.mean(centered * centered, axis=-1, keepdims=True)
    scale = lax.rsqrt(variance + 1e-05)
    return centered * scale, scale


def rope_heads(rows, cos, sin):
    parts = []
    for head in range(rows.shape[0] // HD):
        base = head * HD
        lead = rows[base : base + 8]
        tail = rows[base + 8 : base + 16]
        parts += [lead * cos - tail * sin, tail * cos + lead * sin, rows[base + 16 : base + HD]]
    return jnp.concatenate(parts, axis=0)


def fill_mask(seg_ref, mask_ref):
    seg_row = seg_ref[...].astype(f32)
    seg_col = jnp.transpose(jnp.broadcast_to(seg_row, (8, SEQ)))[:, 0:1]
    for block in range(BLOCKS):
        for key_block in range(block + 1 - LIVE[block], block + 1):
            seen = seg_col[key_block * BLK : (key_block + 1) * BLK] == (
                seg_row[:, block * BLK : (block + 1) * BLK]
            )
            if key_block == block:
                key_pos = lax.broadcasted_iota(jnp.int32, (BLK, BLK), 0)
                query_pos = lax.broadcasted_iota(jnp.int32, (BLK, BLK), 1)
                seen = seen & (key_pos <= query_pos)
            start = P_START[block] + (key_block - (block + 1 - LIVE[block])) * BLK
            mask_ref[start : start + BLK, :] = jnp.where(seen, 0.0, NEG)


def project_heads(normed, w_ref, small_ref, cos, sin, q_t, k_t, k_m, v_m, v_t):
    bias = small_row(small_ref, B_QKV)
    rows = dot(normed, w_ref[:, :D], NN) + bias
    q_t[...] = (rope_heads(jnp.transpose(rows), cos, sin) * Q_SCALE).astype(bf16)
    bias = small_row(small_ref, B_QKV + 1)
    rows = dot(normed, w_ref[:, D : 2 * D], NN) + bias
    keys = rope_heads(jnp.transpose(rows), cos, sin).astype(bf16)
    k_t[...] = keys
    k_m[...] = jnp.transpose(keys)
    bias = small_row(small_ref, B_QKV + 2)
    values = (dot(normed, w_ref[:, 2 * D :], NN) + bias).astype(bf16)
    v_m[...] = values
    v_t[...] = jnp.transpose(values)


def block_diagonal(pair_rows):
    zeros = jnp.zeros((HD, BLK), pair_rows.dtype)
    return jnp.concatenate(
        [
            jnp.concatenate([pair_rows[:HD], zeros], axis=1),
            jnp.concatenate([zeros, pair_rows[HD:]], axis=1),
        ],
        axis=0,
    )


def from_diagonal(both):
    return jnp.concatenate([both[:HD, :BLK], both[HD:, BLK:]], axis=0)


def per_head(row, rows=HD):
    return jnp.concatenate(
        [
            jnp.broadcast_to(row[:, :BLK], (rows, BLK)),
            jnp.broadcast_to(row[:, BLK:], (rows, BLK)),
        ],
        axis=0,
    )


def geometry(block):
    live = LIVE[block] * BLK
    end = (block + 1) * BLK
    start = P_START[block]
    return slice(end - live, end), slice(block * BLK, end), slice(start, start + live)


def attend(q_t, k_m, v_t, pre_k, pre_v_t, mask_ref, p_ref, pp_ref, inv_ref, mixed_ref, then=None):
    pad_mask = jnp.where(lax.broadcasted_iota(jnp.int32, (PAD, 1), 0) < PREFIX, 0.0, NEG)

    def score(feats, block):
        keys, tokens, rows = geometry(block)
        queries = block_diagonal(q_t[feats, tokens])
        mask = mask_ref[rows, :]
        scores = dot(k_m[keys, feats], queries, NN) + jnp.concatenate([mask, mask], axis=1)
        return scores, dot(pre_k[:, feats], queries, NN) + pad_mask

    def soften(pair, block, scores, pre_scores):
        _, _, rows = geometry(block)
        peak = jnp.maximum(
            jnp.max(scores, axis=0, keepdims=True), jnp.max(pre_scores, axis=0, keepdims=True)
        )
        expo = jnp.exp2(scores - peak)
        pre_expo = jnp.exp2(pre_scores - peak)
        total = jnp.sum(expo, axis=0, keepdims=True) + jnp.sum(pre_expo, axis=0, keepdims=True)
        inverse = 1.0 / total
        expo = expo.astype(bf16)
        pre_expo = pre_expo.astype(bf16)
        p_ref[pair, rows, :] = expo
        pp_ref[pair, block] = pre_expo
        inv_ref[pair, block] = jnp.broadcast_to(inverse, (8, 2 * BLK))
        return expo, pre_expo, inverse

    def mix(feats, block, expo, pre_expo, inverse):
        keys, tokens, _ = geometry(block)
        mixed = dot(v_t[feats, keys], expo, NN) + dot(pre_v_t[feats, :], pre_expo, NN)
        mixed_ref[feats, tokens] = (from_diagonal(mixed) * per_head(inverse)).astype(bf16)

    for pair in range(PAIRS):
        feats = slice(pair * BLK, (pair + 1) * BLK)
        scores = [score(feats, block) for block in range(BLOCKS)]
        soft = [soften(pair, block, *scores[block]) for block in range(BLOCKS)]
        for block in range(BLOCKS):
            mix(feats, block, *soft[block])
        if then is not None:
            then(pair)


def attend_back(grad_t, q_t, k_t, v_m, pre_k_t, pre_v, p_ref, pp_ref, inv_ref, mixed_ref,
                dq_ref, dk_ref, dv_ref, pre_grad, pre_row):
    def value_grads(pair, feats, block):
        keys, tokens, _ = geometry(block)
        scaled = (grad_t[feats, tokens] * per_head(inv_ref[pair, block][0:1, :])).astype(bf16)
        products = scaled.astype(f32) * mixed_ref[feats, tokens].astype(f32)
        inner = jnp.concatenate(
            [
                jnp.sum(products[:HD], axis=0, keepdims=True),
                jnp.sum(products[HD:], axis=0, keepdims=True),
            ],
            axis=1,
        )
        grads = block_diagonal(scaled)
        return grads, inner, dot(v_m[keys, feats], grads, NN), dot(pre_v[:, feats], grads, NN)

    def score_grads(pair, block, inner, grad_probs, pre_grad_probs):
        _, _, rows = geometry(block)
        probs = p_ref[pair, rows, :].astype(f32)
        pre_probs = pp_ref[pair, block].astype(f32)
        return (
            (probs * (grad_probs - inner)).astype(bf16),
            (pre_probs * (pre_grad_probs - inner)).astype(bf16),
        )

    def out_grads(pair, feats, block, grads, grad_scores, pre_scores):
        keys, tokens, rows = geometry(block)
        queries = block_diagonal(q_t[feats, tokens])
        dq = dot(k_t[feats, keys], grad_scores, NN) + dot(pre_k_t[feats, :], pre_scores, NN)
        dq_ref[feats, tokens] = from_diagonal(dq)
        return (
            dot(queries, grad_scores, NT),
            dot(grads, p_ref[pair, rows, :], NT),
            dot(pre_scores, queries, NT),
            dot(pp_ref[pair, block], grads, NT),
        )

    def by_keys(outs, which, key_block):
        total = None
        for block in range(BLOCKS):
            place = key_block - (block + 1 - LIVE[block])
            if 0 <= place < LIVE[block]:
                part = outs[block][which][:, place * BLK : (place + 1) * BLK]
                total = part if total is None else total + part
        return total

    for pair in range(PAIRS):
        feats = slice(pair * BLK, (pair + 1) * BLK)
        first = [value_grads(pair, feats, block) for block in range(BLOCKS)]
        second = [score_grads(pair, block, *first[block][1:]) for block in range(BLOCKS)]
        outs = [
            out_grads(pair, feats, block, first[block][0], *second[block])
            for block in range(BLOCKS)
        ]
        for key_block in range(BLOCKS):
            keys = slice(key_block * BLK, (key_block + 1) * BLK)
            dk_ref[feats, keys] = by_keys(outs, 0, key_block)
            dv_ref[feats, keys] = by_keys(outs, 1, key_block)
        pre_dk = outs[0][2] + outs[1][2] + outs[2][2] + outs[3][2]
        pre_dv = outs[0][3] + outs[1][3] + outs[2][3] + outs[3][3]
        pre_grad[pre_row : pre_row + PAD, feats] = pre_dk * K_BACK
        pre_grad[pre_row + PAD : pre_row + 2 * PAD, feats] = pre_dv


def pack_grads(dq_ref, dk_ref, dv_ref, cos, sin, packed_t):
    packed_t[:D, :] = (rope_heads(dq_ref[...], cos, -sin) * Q_BACK).astype(bf16)
    packed_t[D : 2 * D, :] = (rope_heads(dk_ref[...], cos, -sin) * K_BACK).astype(bf16)
    packed_t[2 * D :, :] = dv_ref[...].astype(bf16)


def gelu_both(before):
    cdf = 0.5 + 0.5 * lax.erf(before * (0.5**0.5))
    density = jnp.exp2(before * before * (-0.5 * LOG2E)) * (1.0 / math.sqrt(2.0 * math.pi))
    return before * cdf, cdf + before * density


FF_CHUNK = 512


def chunk_of(index):
    return slice(index * FF_CHUNK, (index + 1) * FF_CHUNK)


def feed_in(normed, w_ref, small_ref, act_ref, slope_ref, arrivals):
    for chunk in range(FF // FF_CHUNK):
        cols = chunk_of(chunk)
        wait_all(*arrivals[chunk])
        before = dot(normed, w_ref[:, cols], NN) + small_row(small_ref, B_IN + chunk)
        act, slope = gelu_both(before)
        act_ref[:, cols] = act.astype(bf16)
        slope_ref[:, cols] = slope.astype(bf16)


def layer_result(hidden, mixed_t, w_attn, act_ref, w_out, small_ref):
    attn_out = dot(jnp.transpose(mixed_t), w_attn, NN) + small_row(small_ref, B_ATTN)
    ff_out = dot(act_ref[...], w_out, NN) + small_row(small_ref, B_OUT)
    return hidden + attn_out + ff_out


def feed_back(grad, w_out, w_in, slope_ref, arrivals):
    total = jnp.zeros((SEQ, D), f32)
    for chunk in range(FF // FF_CHUNK):
        cols = chunk_of(chunk)
        wait_all(*arrivals[chunk])
        grad_act = dot(grad, w_out[cols, :], NT)
        grad_before = (grad_act * slope_ref[:, cols].astype(f32)).astype(bf16)
        total = total + dot(grad_before, w_in[:, cols], NT)
    return total


def norms_back(grad, hidden, grad_two, packed_t, w_qkv, small_ref):
    grad_one = jnp.transpose(dot(w_qkv, packed_t, NN))
    grad_hat = (
        grad_one * small_row(small_ref, G1) + grad_two * small_row(small_ref, G2)
    )
    hat, scale = normalized(hidden)
    mean_one = jnp.mean(grad_hat, axis=-1, keepdims=True)
    mean_two = jnp.mean(grad_hat * hat, axis=-1, keepdims=True)
    return grad.astype(f32) + scale * (grad_hat - mean_one - hat * mean_two)


def halves(values):
    high = values.astype(bf16)
    return high, (values - high.astype(f32)).astype(bf16)


def padded(values):
    return jnp.concatenate([values, jnp.zeros((PAD - PREFIX, values.shape[1]), f32)], axis=0)


def few_rows_dot(left, right):
    left_high, left_rest = halves(padded(left))
    right_high, right_rest = halves(right)
    both = dot(jnp.concatenate([left_high, left_rest], axis=0), right_high, NN)
    return both[:PAD] + both[PAD:] + dot(left_high, right_rest, NN)


def stacked_dot(left, right):
    left_high, left_rest = halves(padded(left))
    right_high, right_rest = halves(padded(right))
    return dot(
        jnp.concatenate([left_high, left_high, left_rest], axis=0),
        jnp.concatenate([right_high, right_rest, right_high], axis=0),
        TN,
    )


def small_kernel(gain_one, shift_one, gain_two, shift_two, attn_b, out_b, qkv_b, in_b, packed_out, packed, sems):
    copies = Copies(sems)
    places = [(gain_one, 0), (shift_one, 1), (gain_two, 2), (shift_two, 3), (attn_b, 4), (out_b, 5)]
    places += [(qkv_b, 6), (in_b, 9)]
    wait_all(
        *[
            copies.start(row, packed.at[:, place * D : place * D + row.shape[1]])
            for row, place in places
        ]
    )
    wait_all(copies.start(packed, packed_out))


def small_call(*arrays):
    return pl.pallas_call(
        small_kernel,
        name="small_parameters",
        cost_estimate=estimate(SMALL, 8 * SMALL),
        out_shape=shape_of((1, SMALL), f32),
        in_specs=[ANY] * 8,
        out_specs=ANY,
        scratch_shapes=[pltpu.VMEM((1, SMALL), f32), pltpu.SemaphoreType.DMA((9,))],
        compiler_params=all_vmem(),
    )(*arrays)


def prefix_kernel(embed_hbm, up_hbm, up_b_hbm, out_hbm, out_b_hbm, hidden_out, low_out, low_t_out,
                  hidden, low, low_t, embed, up_w, up_b, out_w, out_b, sems):
    copies = Copies(sems)
    early = [
        copies.start(src, dst)
        for src, dst in ((embed_hbm, embed), (up_hbm, up_w), (up_b_hbm, up_b.at[0]))
    ]
    parts = [
        copies.start(out_hbm.at[:, i * D : (i + 1) * D], out_w.at[:, i * D : (i + 1) * D])
        for i in range(4)
    ]
    late = [copies.start(out_b_hbm, out_b.at[0])]
    wait_all(*early)
    units = jnp.tanh(few_rows_dot(embed[...], up_w[...])[:PREFIX] + up_b[...])
    hidden[...] = units
    wait_all(*late)
    real = lax.broadcasted_iota(jnp.int32, (PAD, 1), 0) < PREFIX
    for part in range(4):
        cols = slice(part * D, (part + 1) * D)
        parts[part].wait()
        states = jnp.where(real, few_rows_dot(units, out_w[:, cols]) + out_b[:, cols], 0.0)
        low[part] = states.astype(bf16)
        tall = jnp.concatenate([states, jnp.zeros((BLK - PAD, D), f32)], axis=0)
        low_t[part] = jnp.transpose(tall)[:, :PAD].astype(bf16)
    wait_all(
        copies.start(low, low_out), copies.start(low_t, low_t_out), copies.start(hidden, hidden_out)
    )


def prefix_call(*arrays):
    shapes = (((PREFIX, D), f32), ((4, PAD, D), bf16), ((4, D, PAD), bf16))
    return pl.pallas_call(
        prefix_kernel,
        name="prefix",
        cost_estimate=estimate(2 * 6 * PAD * D * 5 * D, 6 * MIB),
        out_shape=[shape_of(*pair) for pair in shapes],
        in_specs=[ANY] * 5,
        out_specs=[ANY] * 3,
        scratch_shapes=[pltpu.VMEM(*pair) for pair in shapes]
        + [
            pltpu.VMEM((PREFIX, D), f32),
            pltpu.VMEM((D, D), f32),
            pltpu.VMEM((1, D), f32),
            pltpu.VMEM((D, 4 * D), f32),
            pltpu.VMEM((1, 4 * D), f32),
            pltpu.SemaphoreType.DMA((11,)),
        ],
        compiler_params=all_vmem(),
    )(*arrays)


HEAD_SHAPES = (
    ((D, SEQ), bf16),
    ((D, SEQ), bf16),
    ((SEQ, D), bf16),
    ((PAIRS, P_ROWS, 2 * BLK), bf16),
    ((PAIRS, BLOCKS, PAD, 2 * BLK), bf16),
    ((PAIRS, BLOCKS, 8, 2 * BLK), f32),
    ((D, SEQ), bf16),
)
FIRST_SHAPES = HEAD_SHAPES + (((SEQ, D), bf16),)


def first_kernel(x_hbm, seg_hbm, own_small, other_small, own_qkv, other_qkv, low_hbm, low_t_hbm, tables_hbm,
                 *refs):
    outs, (q_t, k_t, v_m, p_ref, pp_ref, inv_ref, mixed_ref, two_ref), rest = refs[:8], refs[8:16], refs[16:]
    mask_ref, x_ref, small_ref, w_ref, low, low_t, tables, seg, k_m, v_t, sems = rest
    section = lax.axis_index("pipe")
    here = section == 0
    copies = Copies(sems)
    x_copy = copies.start(x_hbm.at[section, 0], x_ref)
    seg_copy = copies.start(seg_hbm.at[section], seg)
    small_copy = copies.of_layer(here, own_small, other_small, small_ref)
    late = [
        copies.of_layer(here, own_qkv.at[0, rows], other_qkv.at[0, rows], w_ref.at[rows])
        for rows in (slice(i * BLK, (i + 1) * BLK) for i in range(4))
    ]
    late += [
        copies.start(src, dst)
        for src, dst in ((tables_hbm, tables), (low_hbm, low), (low_t_hbm, low_t))
    ]
    seg_copy.wait()
    fill_mask(seg, mask_ref)
    wait_all(x_copy, small_copy)
    hat, _ = normalized(x_ref[...].astype(f32))
    normed = (hat * small_row(small_ref, G1) + small_row(small_ref, B1)).astype(bf16)
    two_ref[...] = (hat * small_row(small_ref, G2) + small_row(small_ref, B2)).astype(bf16)
    done = [copies.start(two_ref, outs[7])]
    wait_all(*late)
    project_heads(normed, w_ref, small_ref, tables[:8, :], tables[8:, :], q_t, k_t, k_m, v_m, v_t)
    done += [copies.start(*pair) for pair in zip((q_t, k_t, v_m), outs[:3])]

    def then(pair):
        done.append(copies.start(p_ref.at[pair], outs[3].at[pair]))

    attend(q_t, k_m, v_t, low.at[0], low_t.at[1], mask_ref, p_ref, pp_ref, inv_ref, mixed_ref, then)
    done += [copies.start(*pair) for pair in zip((pp_ref, inv_ref, mixed_ref), outs[4:7])]
    wait_all(*done)


def first_call(*arrays):
    return pl.pallas_call(
        first_kernel,
        name="first_attention",
        cost_estimate=estimate(200 * SEQ * D * 3 * D, 40 * MIB),
        out_shape=[shape_of(*pair) for pair in FIRST_SHAPES],
        in_specs=[ANY] * 9,
        out_specs=[ANY] * 8,
        scratch_shapes=[pltpu.VMEM(*pair) for pair in FIRST_SHAPES]
        + [
            pltpu.VMEM((P_ROWS, BLK), f32),
            pltpu.VMEM((SEQ, D), bf16),
            pltpu.VMEM((1, SMALL), f32),
            pltpu.VMEM((D, 3 * D), bf16),
            pltpu.VMEM((4, PAD, D), bf16),
            pltpu.VMEM((4, D, PAD), bf16),
            pltpu.VMEM((2 * 8, SEQ), f32),
            pltpu.VMEM((1, SEQ), jnp.int32),
            pltpu.VMEM((SEQ, D), bf16),
            pltpu.VMEM((D, SEQ), bf16),
            pltpu.SemaphoreType.DMA((21,)),
        ],
        compiler_params=all_vmem(),
    )(*arrays)


WEIGHT_SHAPES = (((D, 3 * D), bf16), ((D, D), bf16), ((D, FF), bf16), ((FF, D), bf16))


def middle_kernel(*refs):
    def take(count):
        nonlocal refs
        taken, refs = refs[:count], refs[count:]
        return taken

    x_hbm, cot_hbm, seg_hbm, own_small, other_small = take(5)
    own, other = take(4), take(4)
    low_hbm, low_t_hbm, tables_hbm = take(3)
    saved_hbm = take(8)
    act_out, act_send, grad_out, grad_send, prefix_out = take(5)
    q0, k0, v0, p0, pp0, inv0, mixed0, two0 = take(8)
    w_qkv_zero, w_attn_zero, w_in_zero, w_out_zero = take(4)
    w_qkv, w_attn, w_in, w_out = take(4)
    q_t, k_t, v_m, p_ref, pp_ref, inv_ref, mixed_one = take(7)
    (x_ref, cot_ref, seg, mask, small_zero, small_one, low, low_t, tables, h_one, h_two, act_zero, slope_zero,
     act_one, slope_one, k_m, v_t, dq, dk, dv, packed, pre_grad, prefix_grad, grad_one, grad_low, grad_zero,
     sems) = refs
    section = lax.axis_index("pipe")
    zero, one = section == 0, section == 1
    copies = Copies(sems)

    def fetch_saved(which, dst):
        return copies.start(saved_hbm[which], dst)

    def weights(here, which, dst, index=()):
        index = (0,) + index
        view = dst.at[index[1:]] if len(index) > 1 else dst
        return copies.of_layer(here, own[which].at[index], other[which].at[index], view)

    def hand_over(layer, value, whole, send):
        sem = copies.sems.at[copies.count]
        copies.count += 1

        @pl.when(section == layer)
        def _():
            pltpu.make_async_copy(value, whole.at[0, section, 0], sem).start()

        @pl.when(section != layer)
        def _():
            pltpu.make_async_copy(value, send, sem).start()

        done.append(pltpu.make_async_copy(value, send, sem))

    everything = slice(None)
    done = []
    small_copy = copies.of_layer(zero, own_small, other_small, small_zero)
    two_copy = fetch_saved(7, two0)
    in_zero = [[weights(zero, 2, w_in_zero, (everything, chunk_of(i)))] for i in range(4)]
    out_copies = [
        fetch_saved(6, mixed0),
        weights(zero, 1, w_attn_zero),
        copies.start(x_hbm.at[section, 0], x_ref),
    ]
    out_copies += [weights(zero, 3, w_out_zero, (chunk_of(i),)) for i in range(4)]
    seg_copy = copies.start(seg_hbm.at[section], seg)
    wait_all(small_copy, two_copy)
    feed_in(two0[...], w_in_zero, small_zero, act_zero, slope_zero, in_zero)
    head_copies = [
        copies.of_layer(one, own_small, other_small, small_one),
        weights(one, 0, w_qkv),
        copies.start(tables_hbm, tables),
        copies.start(low_hbm, low),
        copies.start(low_t_hbm, low_t),
    ]
    in_one = [[weights(one, 2, w_in, (everything, chunk_of(i)))] for i in range(4)]
    seg_copy.wait()
    fill_mask(seg, mask)
    wait_all(*out_copies)
    h_one[...] = layer_result(
        x_ref[...].astype(f32), mixed0[...], w_attn_zero[...], act_zero, w_out_zero[...], small_zero
    ).astype(bf16)
    hand_over(0, h_one, act_out, act_send)

    back_copies = [copies.start(cot_hbm.at[section, 0], cot_ref)]
    back_copies += [weights(one, 3, w_out, (chunk_of(i),)) for i in range(4)]
    attn_copy = weights(one, 1, w_attn)
    late = [
        fetch_saved(which, dst)
        for which, dst in ((0, q0), (1, k0), (2, v0), (3, p0), (4, pp0), (5, inv0))
    ]
    qkv_copy = weights(zero, 0, w_qkv_zero)
    wait_all(*head_copies)
    cos, sin = tables[:8, :], tables[8:, :]
    hat, _ = normalized(h_one[...].astype(f32))
    normed = (hat * small_row(small_one, G1) + small_row(small_one, B1)).astype(bf16)
    two = (hat * small_row(small_one, G2) + small_row(small_one, B2)).astype(bf16)
    project_heads(normed, w_qkv, small_one, cos, sin, q_t, k_t, k_m, v_m, v_t)
    attend(q_t, k_m, v_t, low.at[2], low_t.at[3], mask, p_ref, pp_ref, inv_ref, mixed_one)
    feed_in(two, w_in, small_one, act_one, slope_one, in_one)
    wait_all(*back_copies)
    attn_copy.wait()
    h_two[...] = layer_result(
        h_one[...].astype(f32), mixed_one[...], w_attn[...], act_one, w_out[...], small_one
    ).astype(bf16)
    hand_over(1, h_two, act_out, act_send)

    grad = cot_ref[...]
    grad_two = feed_back(grad, w_out, w_in, slope_one, NO_COPIES)
    dq[...] = dot(w_attn[...], grad, NT)
    attend_back(dq, q_t, k_t, v_m, low_t.at[2], low.at[3], p_ref, pp_ref, inv_ref, mixed_one,
                dq, dk, dv, pre_grad, 2 * PAD)
    pack_grads(dq, dk, dv, cos, sin, packed)
    result = norms_back(grad, h_one[...].astype(f32), grad_two, packed[...], w_qkv[...], small_one)
    grad_one[...] = result
    grad_low[...] = result.astype(bf16)
    hand_over(1, grad_one, grad_out, grad_send)

    grad = grad_low[...]
    dq[...] = dot(w_attn_zero[...], grad, NT)
    wait_all(*late)
    attend_back(dq, q0, k0, v0, low_t.at[0], low.at[1], p0, pp0, inv0, mixed0,
                dq, dk, dv, pre_grad, 0)
    for part in range(4):
        prefix_grad[part * PREFIX : (part + 1) * PREFIX, :] = pre_grad[
            part * PAD : part * PAD + PREFIX, :
        ]
    done.append(copies.start(prefix_grad, prefix_out))
    pack_grads(dq, dk, dv, cos, sin, packed)
    grad_two = feed_back(grad, w_out_zero, w_in_zero, slope_zero, NO_COPIES)
    qkv_copy.wait()
    grad_zero[...] = norms_back(
        grad, x_ref[...].astype(f32), grad_two, packed[...], w_qkv_zero[...], small_zero
    )
    hand_over(0, grad_zero, grad_out, grad_send)
    wait_all(*done)


def middle_call(*arrays):
    scratch = FIRST_SHAPES + WEIGHT_SHAPES + WEIGHT_SHAPES + HEAD_SHAPES
    scratch += (
        ((SEQ, D), bf16),
        ((SEQ, D), bf16),
        ((1, SEQ), jnp.int32),
        ((P_ROWS, BLK), f32),
        ((1, SMALL), f32),
        ((1, SMALL), f32),
        ((4, PAD, D), bf16),
        ((4, D, PAD), bf16),
        ((2 * 8, SEQ), f32),
        ((SEQ, D), bf16),
        ((SEQ, D), bf16),
        ((SEQ, FF), bf16),
        ((SEQ, FF), bf16),
        ((SEQ, FF), bf16),
        ((SEQ, FF), bf16),
        ((SEQ, D), bf16),
        ((D, SEQ), bf16),
        ((D, SEQ), f32),
        ((D, SEQ), f32),
        ((D, SEQ), f32),
        ((3 * D, SEQ), bf16),
        ((4 * PAD, D), f32),
        ((4 * PREFIX, D), f32),
        ((SEQ, D), f32),
        ((SEQ, D), bf16),
        ((SEQ, D), f32),
    )
    return pl.pallas_call(
        middle_kernel,
        name="middle",
        cost_estimate=estimate(20 * SEQ * D * 6 * D, 20 * MIB),
        out_shape=[
            shape_of((1, 2, 1, SEQ, D), bf16),
            shape_of((SEQ, D), bf16),
            shape_of((1, 2, 1, SEQ, D), f32),
            shape_of((SEQ, D), f32),
            shape_of((4 * PREFIX, D), f32),
        ],
        in_specs=[ANY] * 24,
        out_specs=[ANY] * 5,
        scratch_shapes=[pltpu.VMEM(*pair) for pair in scratch] + [pltpu.SemaphoreType.DMA((44,))],
        compiler_params=all_vmem(),
    )(*arrays)


def turn_kernel(out_hbm, up_hbm, wide, up_high, up_rest, out_w, up_w, sems):
    copies = Copies(sems)
    up = copies.start(up_hbm, up_w)
    parts = [
        copies.start(out_hbm.at[:, i * D : (i + 1) * D], out_w.at[:, i * D : (i + 1) * D])
        for i in range(4)
    ]
    up.wait()
    up_high[...], up_rest[...] = halves(jnp.transpose(up_w[...]))
    for part in range(4):
        cols = slice(part * D, (part + 1) * D)
        parts[part].wait()
        wide[cols, :] = jnp.transpose(out_w[:, cols].astype(bf16))


def turn_call(*arrays):
    return pl.pallas_call(
        turn_kernel,
        name="turned_matrices",
        out_shape=[shape_of((4 * D, D), bf16), shape_of((D, D), bf16), shape_of((D, D), bf16)],
        in_specs=[ANY] * 2,
        out_specs=[VMEM] * 3,
        scratch_shapes=[
            pltpu.VMEM((D, 4 * D), f32),
            pltpu.VMEM((D, D), f32),
            pltpu.SemaphoreType.DMA((5,)),
        ],
        compiler_params=params_of(LATE_MIB),
        cost_estimate=estimate(SEQ * D * D, 8 * MIB),
    )(*arrays)


def final_kernel(col_width, grads_ref, hidden, embed, wide, up_high, up_rest, act_other, grad_other,
                 act_in, grad_in, d_embed, d_up, d_up_b, d_out, d_out_b, act_out, grad_out, sems):
    section = lax.axis_index("pipe")
    shard = lax.axis_index("dp")
    copies = Copies(sems)
    placed = [
        copies.start(act_other, act_out.at[0, 1 - section, 0]),
        copies.start(grad_other, grad_out.at[0, 1 - section, 0]),
    ]
    units = hidden[...]
    both = jnp.zeros((2 * PAD, D), f32)
    for part in range(4):
        high, rest = halves(padded(grads_ref[part * PREFIX : (part + 1) * PREFIX, :]))
        both = both + dot(
            jnp.concatenate([high, rest], axis=0), wide[part * D : (part + 1) * D, :], NN
        )
    grad_units = (both[:PAD] + both[PAD:])[:PREFIX]
    grad_pre = grad_units * (1.0 - units * units)
    d_up_b[...] = jnp.sum(grad_pre, axis=0, keepdims=True)
    d_up[...] = stacked_dot(embed[...], grad_pre)
    high, rest = halves(padded(grad_pre))
    both = dot(jnp.concatenate([high, rest], axis=0), up_high[...], NN)
    both = both[:PAD] + both[PAD:] + dot(high, up_rest[...], NN)
    d_embed[...] = both[:PREFIX]
    column = section * (2 * D) + shard * col_width
    own_cols = jnp.zeros((PREFIX, col_width), f32)
    for part in range(4):
        for piece in range(D // col_width):
            here = column == part * D + piece * col_width
            cols = slice(piece * col_width, (piece + 1) * col_width)
            rows = slice(part * PREFIX, (part + 1) * PREFIX)
            own_cols = jnp.where(here, grads_ref[rows, cols], own_cols)
    d_out[...] = stacked_dot(units, own_cols)
    d_out_b[...] = jnp.sum(own_cols, axis=0, keepdims=True)
    wait_all(*placed)


def final_call(col_width, *arrays):
    def body(*refs):
        final_kernel(col_width, *refs)

    return pl.pallas_call(
        body,
        name="reparam",
        out_shape=[
            shape_of((PREFIX, D), f32),
            shape_of((D, D), f32),
            shape_of((1, D), f32),
            shape_of((D, col_width), f32),
            shape_of((1, col_width), f32),
            shape_of((1, 2, 1, SEQ, D), bf16),
            shape_of((1, 2, 1, SEQ, D), f32),
        ],
        in_specs=[VMEM] * 8 + [ANY] * 2,
        out_specs=[VMEM] * 5 + [ANY] * 2,
        scratch_shapes=[pltpu.SemaphoreType.DMA((2,))],
        input_output_aliases={8: 5, 9: 6},
        compiler_params=params_of(LATE_MIB),
    )(*arrays)


def swapped(array_in):
    return lax.ppermute(array_in, "pipe", [(0, 1), (1, 0)])


def hops(axis):
    size = lax.axis_size(axis)
    steps = []
    step = 1
    while step < size:
        steps.append((axis, [(i, i ^ step) for i in range(size)]))
        step *= 2
    assert step == size
    return steps


def local(
    block_input,
    cotangent,
    segments,
    ln1_gain,
    ln1_shift,
    qkv_weight,
    qkv_bias,
    attn_weight,
    attn_bias,
    ln2_gain,
    ln2_shift,
    ff_in_weight,
    ff_in_bias,
    ff_out_weight,
    ff_out_bias,
    prefix_embed,
    up_weight,
    up_bias,
    out_weight,
    out_bias,
):
    other_qkv = swapped(qkv_weight)
    small = small_call(
        ln1_gain, ln1_shift, ln2_gain, ln2_shift, attn_bias, ff_out_bias, qkv_bias, ff_in_bias
    )
    other_small = swapped(small)
    small, prefix_embed = lax.optimization_barrier((small, prefix_embed))
    tables = jnp.asarray(rope_tables())
    hidden_units, low, low_t = prefix_call(prefix_embed, up_weight, up_bias, out_weight, out_bias)
    _, *later = lax.optimization_barrier((small, attn_weight, ff_in_weight, ff_out_weight))
    own = (qkv_weight, attn_weight, ff_in_weight, ff_out_weight)
    other = (other_qkv,) + tuple(swapped(weight) for weight in later)
    saved = first_call(
        block_input, segments, small, other_small, qkv_weight, other_qkv, low, low_t, tables
    )
    act, act_send, grad, grad_send, prefix_grad = middle_call(
        block_input, cotangent, segments, small, other_small, *own, *other, low, low_t, tables, *saved
    )

    def swap_acts(state):
        return dict(state, act=swapped(state["act"]))

    def swap_grads(state):
        return dict(state, grad=swapped(state["grad"]))

    def turn(state):
        return dict(state, turned=turn_call(state["out_weight"], up_weight))

    works = [None, swap_acts, swap_grads, turn]
    state = {"act": act_send, "grad": grad_send, "out_weight": out_weight}
    for axis, pairs in hops("pipe") + hops("dp") + hops("grp"):
        moved = lax.ppermute(prefix_grad, axis, pairs)
        work = works.pop(0) if works else None
        if work:
            state = work(state)
        prefix_grad, moved, state = lax.optimization_barrier((prefix_grad, moved, state))
        prefix_grad = prefix_grad + moved
    for work in works:
        state = work(state)
    col_width = 2 * D // lax.axis_size("dp")
    grad_embed, grad_up, grad_up_b, grad_out, grad_out_b, activations, input_grads = final_call(
        col_width, prefix_grad, hidden_units, prefix_embed, *state["turned"], state["act"], state["grad"],
        act, grad,
    )
    return (
        activations,
        input_grads,
        grad_embed,
        grad_up,
        grad_up_b[0],
        grad_out,
        grad_out_b[0],
    )


def solution(mesh):
    return jax.shard_map(
        local,
        mesh=mesh,
        in_specs=(
            P(None, ("grp", "dp"), None, None),
            P(None, ("grp", "dp"), None, None),
            P(None, ("grp", "dp"), None),
            P("pipe", None),
            P("pipe", None),
            P("pipe", None, None),
            P("pipe", None),
            P("pipe", None, None),
            P("pipe", None),
            P("pipe", None),
            P("pipe", None),
            P("pipe", None, None),
            P("pipe", None),
            P("pipe", None, None),
            P("pipe", None),
            P(),
            P(),
            P(),
            P(),
            P(),
        ),
        out_specs=(
            P("pipe", None, ("grp", "dp"), None, None),
            P("pipe", None, ("grp", "dp"), None, None),
            P(),
            P(),
            P(),
            P(None, ("pipe", "dp")),
            P(("pipe", "dp")),
        ),
        check_vma=False,
    )
```

```python
import math

import jax
import jax.numpy as jnp
import numpy as np
from jax import lax
from jax.experimental import pallas as pl
from jax.experimental.pallas import tpu as pltpu
from jax.sharding import PartitionSpec as P

D = 512
SEQ = 512
HEADS = 8
HD = 64
FF = 2048
ROT = 16
PREFIX = 10
PAD = 16
BLK = 128
BLOCKS = SEQ // BLK
PAIRS = HEADS // 2
LIVE = (1, 2, 3, 3)
P_ROWS = BLK * sum(LIVE)
P_START = (0, 128, 384, 768)

f32 = jnp.float32
bf16 = jnp.bfloat16
LOG2E = math.log2(math.e)
Q_SCALE = LOG2E * HD**-0.5
K_BACK = 1.0 / LOG2E
Q_BACK = HD**-0.5
NEG = -1e30

NN = (((1,), (0,)), ((), ()))
NT = (((1,), (1,)), ((), ()))
TN = (((0,), (0,)), ((), ()))

NO_COPIES = ((),) * 4
MIB = 1024 * 1024
FIRST_MIB = 40
MIDDLE_MIB = 34
LATE_MIB = 16

G1, B1, G2, B2, B_ATTN, B_OUT, B_QKV, B_IN = 0, 1, 2, 3, 4, 5, 6, 9
SMALL = 13 * D


def dot(left, right, dims):
    return lax.dot_general(left, right, dims, preferred_element_type=f32)


def call_kernel(kernel, name, ins, outs, scratch, sems, mib, cost, aliases=None):
    operands = [pltpu.with_memory_space_constraint(array, space) for array, space in ins]
    return pl.pallas_call(
        kernel,
        name=name,
        out_shape=[space(shape, dtype) for space, shape, dtype in outs],
        in_specs=[pl.BlockSpec(memory_space=space) for _, space in ins],
        out_specs=[pl.BlockSpec(memory_space=space) for space, _, _ in outs],
        scratch_shapes=[pltpu.VMEM(*pair) for pair in scratch]
        + ([pltpu.SemaphoreType.DMA((sems,))] if sems else []),
        input_output_aliases=aliases or {},
        compiler_params=pltpu.CompilerParams(vmem_limit_bytes=mib * MIB),
        cost_estimate=pl.CostEstimate(flops=cost, bytes_accessed=8 * MIB, transcendentals=0),
    )(*operands)


def in_hbm(*arrays):
    return [(array, pltpu.HBM) for array in arrays]


def anywhere(*arrays):
    return [(array, pl.ANY) for array in arrays]


def in_vmem(*arrays):
    return [(array, pltpu.VMEM) for array in arrays]


def vmem(shapes):
    return [(pltpu.VMEM, *pair) for pair in shapes]


def small_row(small_ref, place):
    return small_ref[:, place * D : (place + 1) * D]


def rope_tables():
    inv_freq = 10000.0 ** (-2.0 * np.arange(ROT // 2) / ROT)
    angles = inv_freq[:, None] * np.arange(SEQ)[None, :]
    return np.concatenate([np.cos(angles), np.sin(angles)], axis=0).astype(np.float32)


class Copies:
    def __init__(self, sems):
        self.sems = sems
        self.count = 0

    def start(self, src, dst):
        copy = pltpu.make_async_copy(src, dst, self.sems.at[self.count])
        self.count += 1
        copy.start()
        return copy

    def of_layer(self, here, own, other, dst):
        sem = self.sems.at[self.count]
        self.count += 1
        copy = pltpu.make_async_copy(own, dst, sem)

        @pl.when(here)
        def _():
            copy.start()

        @pl.when(jnp.logical_not(here))
        def _():
            pltpu.make_async_copy(other, dst, sem).start()

        return copy


def wait_all(*copies):
    for copy in copies:
        copy.wait()


def normalized(hidden):
    mean = jnp.mean(hidden, axis=-1, keepdims=True)
    centered = hidden - mean
    variance = jnp.mean(centered * centered, axis=-1, keepdims=True)
    scale = lax.rsqrt(variance + 1e-05)
    return centered * scale, scale


def rope_heads(rows, cos, sin):
    parts = []
    for head in range(rows.shape[0] // HD):
        base = head * HD
        lead = rows[base : base + 8]
        tail = rows[base + 8 : base + 16]
        parts += [lead * cos - tail * sin, tail * cos + lead * sin, rows[base + 16 : base + HD]]
    return jnp.concatenate(parts, axis=0)


def fill_mask(seg_ref, mask_ref):
    seg_row = seg_ref[...].astype(f32)
    seg_col = jnp.transpose(jnp.broadcast_to(seg_row, (8, SEQ)))[:, 0:1]
    for block in range(BLOCKS):
        for key_block in range(block + 1 - LIVE[block], block + 1):
            seen = seg_col[key_block * BLK : (key_block + 1) * BLK] == (
                seg_row[:, block * BLK : (block + 1) * BLK]
            )
            if key_block == block:
                key_pos = lax.broadcasted_iota(jnp.int32, (BLK, BLK), 0)
                query_pos = lax.broadcasted_iota(jnp.int32, (BLK, BLK), 1)
                seen = seen & (key_pos <= query_pos)
            start = P_START[block] + (key_block - (block + 1 - LIVE[block])) * BLK
            mask_ref[start : start + BLK, :] = jnp.where(seen, 0.0, NEG)


def project_heads(normed, w_ref, small_ref, cos, sin, q_t, k_t, k_m, v_m, v_t):
    bias = small_row(small_ref, B_QKV)
    rows = dot(normed, w_ref[:, :D], NN) + bias
    q_t[...] = (rope_heads(jnp.transpose(rows), cos, sin) * Q_SCALE).astype(bf16)
    bias = small_row(small_ref, B_QKV + 1)
    rows = dot(normed, w_ref[:, D : 2 * D], NN) + bias
    keys = rope_heads(jnp.transpose(rows), cos, sin).astype(bf16)
    k_t[...] = keys
    k_m[...] = jnp.transpose(keys)
    bias = small_row(small_ref, B_QKV + 2)
    values = (dot(normed, w_ref[:, 2 * D :], NN) + bias).astype(bf16)
    v_m[...] = values
    v_t[...] = jnp.transpose(values)


def block_diagonal(pair_rows):
    zeros = jnp.zeros((HD, BLK), pair_rows.dtype)
    return jnp.concatenate(
        [
            jnp.concatenate([pair_rows[:HD], zeros], axis=1),
            jnp.concatenate([zeros, pair_rows[HD:]], axis=1),
        ],
        axis=0,
    )


def from_diagonal(both):
    return jnp.concatenate([both[:HD, :BLK], both[HD:, BLK:]], axis=0)


def per_head(row, rows=HD):
    return jnp.concatenate(
        [
            jnp.broadcast_to(row[:, :BLK], (rows, BLK)),
            jnp.broadcast_to(row[:, BLK:], (rows, BLK)),
        ],
        axis=0,
    )


def geometry(block):
    live = LIVE[block] * BLK
    end = (block + 1) * BLK
    start = P_START[block]
    return slice(end - live, end), slice(block * BLK, end), slice(start, start + live)


def attend(q_t, k_m, v_t, pre_k, pre_v, mask_ref, p_ref, pp_ref, inv_ref, mixed_ref):
    pad_mask = jnp.where(lax.broadcasted_iota(jnp.int32, (PAD, 1), 0) < PREFIX, 0.0, NEG)

    def score(feats, block):
        keys, tokens, rows = geometry(block)
        queries = block_diagonal(q_t[feats, tokens])
        mask = mask_ref[rows, :]
        scores = dot(k_m[keys, feats], queries, NN) + jnp.concatenate([mask, mask], axis=1)
        return scores, dot(pre_k[:, feats], queries, NN) + pad_mask

    def soften(pair, block, scores, pre_scores):
        _, _, rows = geometry(block)
        peak = jnp.maximum(
            jnp.max(scores, axis=0, keepdims=True), jnp.max(pre_scores, axis=0, keepdims=True)
        )
        expo = jnp.exp2(scores - peak)
        pre_expo = jnp.exp2(pre_scores - peak)
        total = jnp.sum(expo, axis=0, keepdims=True) + jnp.sum(pre_expo, axis=0, keepdims=True)
        inverse = 1.0 / total
        expo = expo.astype(bf16)
        pre_expo = pre_expo.astype(bf16)
        p_ref[pair, rows, :] = expo
        pp_ref[pair, block] = pre_expo
        inv_ref[pair, block] = jnp.broadcast_to(inverse, (8, 2 * BLK))
        return expo, pre_expo, inverse

    def mix(feats, block, expo, pre_expo, inverse):
        keys, tokens, _ = geometry(block)
        mixed = dot(v_t[feats, keys], expo, NN) + dot(pre_v[:, feats], pre_expo, TN)
        mixed_ref[feats, tokens] = (from_diagonal(mixed) * per_head(inverse)).astype(bf16)

    for pair in range(PAIRS):
        feats = slice(pair * BLK, (pair + 1) * BLK)
        scores = [score(feats, block) for block in range(BLOCKS)]
        soft = [soften(pair, block, *scores[block]) for block in range(BLOCKS)]
        for block in range(BLOCKS):
            mix(feats, block, *soft[block])


def attend_back(grad_t, q_t, k_t, v_m, pre_k, pre_v, p_ref, pp_ref, inv_ref, mixed_ref,
                dq_ref, dk_ref, dv_ref, pre_grad, pre_row):
    def value_grads(pair, feats, block):
        keys, tokens, _ = geometry(block)
        scaled = (grad_t[feats, tokens] * per_head(inv_ref[pair, block][0:1, :])).astype(bf16)
        products = scaled.astype(f32) * mixed_ref[feats, tokens].astype(f32)
        inner = jnp.concatenate(
            [
                jnp.sum(products[:HD], axis=0, keepdims=True),
                jnp.sum(products[HD:], axis=0, keepdims=True),
            ],
            axis=1,
        )
        grads = block_diagonal(scaled)
        return grads, inner, dot(v_m[keys, feats], grads, NN), dot(pre_v[:, feats], grads, NN)

    def score_grads(pair, block, inner, grad_probs, pre_grad_probs):
        _, _, rows = geometry(block)
        probs = p_ref[pair, rows, :].astype(f32)
        pre_probs = pp_ref[pair, block].astype(f32)
        return (
            (probs * (grad_probs - inner)).astype(bf16),
            (pre_probs * (pre_grad_probs - inner)).astype(bf16),
        )

    def out_grads(pair, feats, block, grads, grad_scores, pre_scores):
        keys, tokens, rows = geometry(block)
        queries = block_diagonal(q_t[feats, tokens])
        dq = dot(k_t[feats, keys], grad_scores, NN) + dot(pre_k[:, feats], pre_scores, TN)
        dq_ref[feats, tokens] = from_diagonal(dq)
        return (
            dot(queries, grad_scores, NT),
            dot(grads, p_ref[pair, rows, :], NT),
            dot(pre_scores, queries, NT),
            dot(pp_ref[pair, block], grads, NT),
        )

    def by_keys(outs, which, key_block):
        total = None
        for block in range(BLOCKS):
            place = key_block - (block + 1 - LIVE[block])
            if 0 <= place < LIVE[block]:
                part = outs[block][which][:, place * BLK : (place + 1) * BLK]
                total = part if total is None else total + part
        return total

    for pair in range(PAIRS):
        feats = slice(pair * BLK, (pair + 1) * BLK)
        first = [value_grads(pair, feats, block) for block in range(BLOCKS)]
        second = [score_grads(pair, block, *first[block][1:]) for block in range(BLOCKS)]
        outs = [
            out_grads(pair, feats, block, first[block][0], *second[block])
            for block in range(BLOCKS)
        ]
        for key_block in range(BLOCKS):
            keys = slice(key_block * BLK, (key_block + 1) * BLK)
            dk_ref[feats, keys] = by_keys(outs, 0, key_block)
            dv_ref[feats, keys] = by_keys(outs, 1, key_block)
        pre_dk = outs[0][2] + outs[1][2] + outs[2][2] + outs[3][2]
        pre_dv = outs[0][3] + outs[1][3] + outs[2][3] + outs[3][3]
        pre_grad[pre_row : pre_row + PAD, feats] = pre_dk * K_BACK
        pre_grad[pre_row + PAD : pre_row + 2 * PAD, feats] = pre_dv


def pack_grads(dq_ref, dk_ref, dv_ref, cos, sin, packed_t):
    packed_t[:D, :] = (rope_heads(dq_ref[...], cos, -sin) * Q_BACK).astype(bf16)
    packed_t[D : 2 * D, :] = (rope_heads(dk_ref[...], cos, -sin) * K_BACK).astype(bf16)
    packed_t[2 * D :, :] = dv_ref[...].astype(bf16)


def gelu_both(before):
    cdf = 0.5 + 0.5 * lax.erf(before * (0.5**0.5))
    density = jnp.exp2(before * before * (-0.5 * LOG2E)) * (1.0 / math.sqrt(2.0 * math.pi))
    return before * cdf, cdf + before * density


FF_CHUNK = 512


def chunk_of(index):
    return slice(index * FF_CHUNK, (index + 1) * FF_CHUNK)


def feed_in(normed, w_ref, small_ref, act_ref, slope_ref, arrivals):
    for chunk in range(FF // FF_CHUNK):
        cols = chunk_of(chunk)
        wait_all(*arrivals[chunk])
        before = dot(normed, w_ref[:, cols], NN) + small_row(small_ref, B_IN + chunk)
        act, slope = gelu_both(before)
        act_ref[:, cols] = act.astype(bf16)
        slope_ref[:, cols] = slope.astype(bf16)


def layer_result(hidden, mixed_t, w_attn, act_ref, w_out, small_ref):
    attn_out = dot(jnp.transpose(mixed_t), w_attn, NN) + small_row(small_ref, B_ATTN)
    ff_out = dot(act_ref[...], w_out, NN) + small_row(small_ref, B_OUT)
    return hidden + attn_out + ff_out


def feed_back(grad, w_out, w_in, slope_ref, arrivals):
    total = jnp.zeros((SEQ, D), f32)
    for chunk in range(FF // FF_CHUNK):
        cols = chunk_of(chunk)
        wait_all(*arrivals[chunk])
        grad_act = dot(grad, w_out[cols, :], NT)
        grad_before = (grad_act * slope_ref[:, cols].astype(f32)).astype(bf16)
        total = total + dot(grad_before, w_in[:, cols], NT)
    return total


def norms_back(grad, hidden, grad_two, packed_t, w_qkv, small_ref):
    grad_one = jnp.transpose(dot(w_qkv, packed_t, NN))
    grad_hat = (
        grad_one * small_row(small_ref, G1) + grad_two * small_row(small_ref, G2)
    )
    hat, scale = normalized(hidden)
    mean_one = jnp.mean(grad_hat, axis=-1, keepdims=True)
    mean_two = jnp.mean(grad_hat * hat, axis=-1, keepdims=True)
    return grad.astype(f32) + scale * (grad_hat - mean_one - hat * mean_two)


def halves(values):
    high = values.astype(bf16)
    return high, (values - high.astype(f32)).astype(bf16)


def padded(values):
    return jnp.concatenate([values, jnp.zeros((PAD - PREFIX, values.shape[1]), f32)], axis=0)


def few_rows_dot(left, right):
    left_high, left_rest = halves(padded(left))
    right_high, right_rest = halves(right)
    both = dot(jnp.concatenate([left_high, left_rest], axis=0), right_high, NN)
    return both[:PAD] + both[PAD:] + dot(left_high, right_rest, NN)


def stacked_dot(left, right):
    left_high, left_rest = halves(padded(left))
    right_high, right_rest = halves(padded(right))
    return dot(
        jnp.concatenate([left_high, left_high, left_rest], axis=0),
        jnp.concatenate([right_high, right_rest, right_high], axis=0),
        TN,
    )


def small_kernel(gain_one, shift_one, gain_two, shift_two, attn_b, out_b, qkv_b, in_b, packed, sems):
    copies = Copies(sems)
    places = [(gain_one, 0), (shift_one, 1), (gain_two, 2), (shift_two, 3), (attn_b, 4), (out_b, 5)]
    places += [(qkv_b, 6), (in_b, 9)]
    wait_all(
        *[
            copies.start(row, packed.at[:, place * D : place * D + row.shape[1]])
            for row, place in places
        ]
    )


def small_call(*arrays):
    (packed,) = call_kernel(
        small_kernel, "small_parameters", in_hbm(*arrays), vmem([((1, SMALL), f32)]), [], 8, 8, SMALL
    )
    return packed


def prefix_states(embed, up_w, up_b, out_w, out_b, arrivals, hidden, low):
    units = jnp.tanh(few_rows_dot(embed[...], up_w[...])[:PREFIX] + up_b[...])
    hidden[...] = units
    real = lax.broadcasted_iota(jnp.int32, (PAD, 1), 0) < PREFIX
    for part in range(4):
        cols = slice(part * D, (part + 1) * D)
        arrivals[part].wait()
        states = few_rows_dot(units, out_w[:, cols]) + out_b[:, cols]
        low[part] = jnp.where(real, states, 0.0).astype(bf16)


HEAD_SHAPES = (
    ((D, SEQ), bf16),
    ((D, SEQ), bf16),
    ((SEQ, D), bf16),
    ((PAIRS, P_ROWS, 2 * BLK), bf16),
    ((PAIRS, BLOCKS, PAD, 2 * BLK), bf16),
    ((PAIRS, BLOCKS, 8, 2 * BLK), f32),
    ((D, SEQ), bf16),
)
FIRST_SHAPES = HEAD_SHAPES + (
    ((SEQ, D), bf16),
    ((4, PAD, D), bf16),
    ((P_ROWS, BLK), f32),
    ((SEQ, D), bf16),
    ((1, SMALL), f32),
    ((D, 3 * D), bf16),
    ((PREFIX, D), f32),
)


def first_kernel(own_small, other_small, other_qkv, x_hbm, seg_hbm, own_qkv, embed_hbm, up_hbm, up_b_hbm,
                 out_hbm, out_b_hbm, tables_hbm, *refs):
    q_t, k_t, v_m, p_ref, pp_ref, inv_ref, mixed_ref, two_ref, low, mask_ref, x_ref, small_ref = refs[:12]
    w_ref, hidden, embed, up_w, up_b, out_w, out_b, tables, seg, k_m, v_t, sems = refs[12:]
    section = lax.axis_index("pipe")
    here = section == 0
    copies = Copies(sems)
    x_copy = copies.start(x_hbm.at[section, 0], x_ref)
    seg_copy = copies.start(seg_hbm.at[section], seg)
    small_copy = copies.of_layer(here, own_small, other_small, small_ref)
    late = [
        copies.of_layer(here, own_qkv.at[0, rows], other_qkv.at[0, rows], w_ref.at[rows])
        for rows in (slice(i * BLK, (i + 1) * BLK) for i in range(4))
    ]
    late.append(copies.start(tables_hbm, tables))
    prefix_copies = [
        copies.start(src, dst)
        for src, dst in ((embed_hbm, embed), (up_hbm, up_w), (up_b_hbm, up_b.at[0]), (out_b_hbm, out_b.at[0]))
    ]
    parts = [
        copies.start(out_hbm.at[:, i * D : (i + 1) * D], out_w.at[:, i * D : (i + 1) * D])
        for i in range(4)
    ]
    seg_copy.wait()
    fill_mask(seg, mask_ref)
    wait_all(x_copy, small_copy)
    hat, _ = normalized(x_ref[...].astype(f32))
    normed = (hat * small_row(small_ref, G1) + small_row(small_ref, B1)).astype(bf16)
    two_ref[...] = (hat * small_row(small_ref, G2) + small_row(small_ref, B2)).astype(bf16)
    wait_all(*late)
    project_heads(normed, w_ref, small_ref, tables[:8, :], tables[8:, :], q_t, k_t, k_m, v_m, v_t)
    wait_all(*prefix_copies)
    prefix_states(embed, up_w, up_b, out_w, out_b, parts, hidden, low)
    attend(q_t, k_m, v_t, low.at[0], low.at[1], mask_ref, p_ref, pp_ref, inv_ref, mixed_ref)


def first_call(smalls, other_qkv, *arrays):
    scratch = [
        ((PREFIX, D), f32),
        ((D, D), f32),
        ((1, D), f32),
        ((D, 4 * D), f32),
        ((1, 4 * D), f32),
        ((2 * 8, SEQ), f32),
        ((1, SEQ), jnp.int32),
        ((SEQ, D), bf16),
        ((D, SEQ), bf16),
    ]
    return call_kernel(
        first_kernel, "first_attention", in_vmem(*smalls) + anywhere(other_qkv) + in_hbm(*arrays),
        vmem(FIRST_SHAPES), scratch, 16, FIRST_MIB, 200 * SEQ * D * 3 * D,
    )


WEIGHT_SHAPES = (((D, 3 * D), bf16), ((D, D), bf16), ((D, FF), bf16), ((FF, D), bf16))


MIDDLE_OUTS = (
    ((SEQ, D), bf16),
    ((SEQ, FF), bf16),
    ((D, SEQ), bf16),
    ((SEQ, D), f32),
    ((SEQ, D), bf16),
    ((SEQ, FF), bf16),
    ((3 * D, SEQ), bf16),
    ((4 * PREFIX, D), f32),
    ((1, SMALL), f32),
    ((D, FF), bf16),
    ((FF, D), bf16),
    ((D, D), bf16),
    ((FF, D), bf16),
)


def middle_kernel(*refs):
    def take(count):
        nonlocal refs
        taken, refs = refs[:count], refs[count:]
        return taken

    own_small, other_small, q0, k0, v0, p0, pp0, inv0, mixed0, two0, low, mask, x_ref, small_zero = take(14)
    other = take(4)
    (cot_hbm,) = take(1)
    own = take(4)
    (tables_hbm,) = take(1)
    (h_one, act_one, mixed_one, grad_one, grad_low, slope_zero, packed_zero, prefix_grad,
     small_one, w_in_zero, w_out_zero, w_attn, w_out) = take(13)
    w_attn_zero, w_qkv, w_in = take(3)
    q_t, k_t, v_m, p_ref, pp_ref, inv_ref = take(6)
    cot_ref, tables, act_zero, slope_one, k_m, v_t, dq, dk, dv, packed, pre_grad, sems = refs
    section = lax.axis_index("pipe")
    zero, one = section == 0, section == 1
    copies = Copies(sems)

    def weights(here, which, dst, index=()):
        index = (0,) + index
        view = dst.at[index[1:]] if len(index) > 1 else dst
        return copies.of_layer(here, own[which].at[index], other[which].at[index], view)

    everything = slice(None)
    in_zero = [[weights(zero, 2, w_in_zero, (everything, chunk_of(i)))] for i in range(4)]
    out_copies = [weights(zero, 1, w_attn_zero)]
    out_copies += [weights(zero, 3, w_out_zero, (chunk_of(i),)) for i in range(4)]
    feed_in(two0[...], w_in_zero, small_zero, act_zero, slope_zero, in_zero)
    head_copies = [
        copies.of_layer(one, own_small, other_small, small_one),
        weights(one, 0, w_qkv),
        copies.start(tables_hbm, tables),
    ]
    in_one = [[weights(one, 2, w_in, (everything, chunk_of(i)))] for i in range(4)]
    wait_all(*out_copies)
    h_one[...] = layer_result(
        x_ref[...].astype(f32), mixed0[...], w_attn_zero[...], act_zero, w_out_zero[...], small_zero
    ).astype(bf16)

    back_copies = [copies.start(cot_hbm.at[section, 0], cot_ref)]
    back_copies += [weights(one, 3, w_out, (chunk_of(i),)) for i in range(4)]
    attn_copy = weights(one, 1, w_attn)
    wait_all(*head_copies)
    cos, sin = tables[:8, :], tables[8:, :]
    hat, _ = normalized(h_one[...].astype(f32))
    normed = (hat * small_row(small_one, G1) + small_row(small_one, B1)).astype(bf16)
    two = (hat * small_row(small_one, G2) + small_row(small_one, B2)).astype(bf16)
    project_heads(normed, w_qkv, small_one, cos, sin, q_t, k_t, k_m, v_m, v_t)
    attend(q_t, k_m, v_t, low.at[2], low.at[3], mask, p_ref, pp_ref, inv_ref, mixed_one)
    feed_in(two, w_in, small_one, act_one, slope_one, in_one)

    wait_all(*back_copies)
    grad = cot_ref[...]
    grad_two = feed_back(grad, w_out, w_in, slope_one, NO_COPIES)
    attn_copy.wait()
    dq[...] = dot(w_attn[...], grad, NT)
    attend_back(dq, q_t, k_t, v_m, low.at[2], low.at[3], p_ref, pp_ref, inv_ref, mixed_one,
                dq, dk, dv, pre_grad, 2 * PAD)
    pack_grads(dq, dk, dv, cos, sin, packed)
    result = norms_back(grad, h_one[...].astype(f32), grad_two, packed[...], w_qkv[...], small_one)
    grad_one[...] = result
    grad_low[...] = result.astype(bf16)

    dq[...] = dot(w_attn_zero[...], grad_low[...], NT)
    attend_back(dq, q0, k0, v0, low.at[0], low.at[1], p0, pp0, inv0, mixed0,
                dq, dk, dv, pre_grad, 0)
    for part in range(4):
        prefix_grad[part * PREFIX : (part + 1) * PREFIX, :] = pre_grad[
            part * PAD : part * PAD + PREFIX, :
        ]
    pack_grads(dq, dk, dv, cos, sin, packed_zero)


def middle_call(saved, other, *arrays):
    scratch = (((D, D), bf16), ((D, 3 * D), bf16), ((D, FF), bf16)) + HEAD_SHAPES[:6]
    scratch += (
        ((SEQ, D), bf16),
        ((2 * 8, SEQ), f32),
        ((SEQ, FF), bf16),
        ((SEQ, FF), bf16),
        ((SEQ, D), bf16),
        ((D, SEQ), bf16),
        ((D, SEQ), f32),
        ((D, SEQ), f32),
        ((D, SEQ), f32),
        ((3 * D, SEQ), bf16),
        ((4 * PAD, D), f32),
    )
    return call_kernel(
        middle_kernel, "middle", in_vmem(*saved) + anywhere(*other) + in_hbm(*arrays),
        vmem(MIDDLE_OUTS), scratch, 24, MIDDLE_MIB, 20 * SEQ * D * 6 * D,
    )


def hand_over(section, values, keep, send_ref, whole, sem):
    @pl.when(section == 0)
    def _():
        keep[...] = values[0]
        send_ref[...] = values[1]

    @pl.when(section != 0)
    def _():
        keep[...] = values[1]
        send_ref[...] = values[0]

    wait_all(Copies(sem).start(keep, whole.at[0, section, 0]))


def result_kernel(h_one, act, mixed, small, w_attn, w_out, whole, send_ref, keep, sem):
    result = layer_result(
        h_one[...].astype(f32), mixed[...], w_attn[...], act, w_out[...], small
    ).astype(bf16)
    hand_over(lax.axis_index("pipe"), (h_one[...], result), keep, send_ref, whole, sem)


def result_call(*arrays):
    return call_kernel(
        result_kernel, "layer_one_out", in_vmem(*arrays),
        [(pltpu.HBM, (1, 2, 1, SEQ, D), bf16), (pltpu.VMEM, (SEQ, D), bf16)],
        [((SEQ, D), bf16)], 1, LATE_MIB, 2 * SEQ * D * (D + FF),
    )


def feed_back_kernel(grad, slope, w_in, w_out, total):
    total[...] = feed_back(grad[...], w_out, w_in, slope, NO_COPIES)


def feed_back_call(*arrays):
    (total,) = call_kernel(
        feed_back_kernel, "layer_zero_feed_back", in_vmem(*arrays), vmem([((SEQ, D), f32)]), [], 0,
        LATE_MIB, 4 * SEQ * D * FF,
    )
    return total


def norms_kernel(x_ref, grad, two, packed, grad_one, small, w_qkv, whole, send_ref, keep, sem):
    result = norms_back(
        grad[...], x_ref[...].astype(f32), two[...], packed[...], w_qkv[...], small
    )
    hand_over(lax.axis_index("pipe"), (result, grad_one[...]), keep, send_ref, whole, sem)


def norms_call(*arrays):
    return call_kernel(
        norms_kernel, "layer_zero_norms", in_vmem(*arrays),
        [(pltpu.HBM, (1, 2, 1, SEQ, D), f32), (pltpu.VMEM, (SEQ, D), f32)],
        [((SEQ, D), f32)], 1, LATE_MIB, 6 * SEQ * D * D,
    )


def turn_kernel(out_hbm, up_hbm, wide, up_high, up_rest, out_w, up_w, sems):
    copies = Copies(sems)
    up = copies.start(up_hbm, up_w)
    parts = [
        copies.start(out_hbm.at[:, i * D : (i + 1) * D], out_w.at[:, i * D : (i + 1) * D])
        for i in range(4)
    ]
    up.wait()
    up_high[...], up_rest[...] = halves(jnp.transpose(up_w[...]))
    for part in range(4):
        cols = slice(part * D, (part + 1) * D)
        parts[part].wait()
        wide[cols, :] = jnp.transpose(out_w[:, cols].astype(bf16))


def turn_call(*arrays):
    return call_kernel(
        turn_kernel, "turned_matrices", in_hbm(*arrays),
        vmem([((4 * D, D), bf16), ((D, D), bf16), ((D, D), bf16)]),
        [((D, 4 * D), f32), ((D, D), f32)], 5, LATE_MIB, SEQ * D * D,
    )


def final_kernel(col_width, grads_ref, hidden, embed, wide, up_high, up_rest, act_other, grad_other,
                 act_in, grad_in, *refs):
    results, (act_out, grad_out, d_embed, d_up, d_up_b, d_out, d_out_b, sems) = refs[:5], refs[5:]
    section = lax.axis_index("pipe")
    shard = lax.axis_index("dp")
    copies = Copies(sems)
    placed = [
        copies.start(act_other, act_out.at[0, 1 - section, 0]),
        copies.start(grad_other, grad_out.at[0, 1 - section, 0]),
    ]
    units = hidden[...]
    both = jnp.zeros((2 * PAD, D), f32)
    for part in range(4):
        high, rest = halves(padded(grads_ref[part * PREFIX : (part + 1) * PREFIX, :]))
        both = both + dot(
            jnp.concatenate([high, rest], axis=0), wide[part * D : (part + 1) * D, :], NN
        )
    grad_units = (both[:PAD] + both[PAD:])[:PREFIX]
    grad_pre = grad_units * (1.0 - units * units)
    d_up_b[...] = jnp.sum(grad_pre, axis=0, keepdims=True)
    d_up[...] = stacked_dot(embed[...], grad_pre)
    placed += [copies.start(d_up_b, results[2]), copies.start(d_up, results[1])]
    high, rest = halves(padded(grad_pre))
    both = dot(jnp.concatenate([high, rest], axis=0), up_high[...], NN)
    both = both[:PAD] + both[PAD:] + dot(high, up_rest[...], NN)
    d_embed[...] = both[:PREFIX]
    placed.append(copies.start(d_embed, results[0]))
    column = section * (2 * D) + shard * col_width
    own_cols = jnp.zeros((PREFIX, col_width), f32)
    for part in range(4):
        for piece in range(D // col_width):
            here = column == part * D + piece * col_width
            cols = slice(piece * col_width, (piece + 1) * col_width)
            rows = slice(part * PREFIX, (part + 1) * PREFIX)
            own_cols = jnp.where(here, grads_ref[rows, cols], own_cols)
    d_out[...] = stacked_dot(units, own_cols)
    d_out_b[...] = jnp.sum(own_cols, axis=0, keepdims=True)
    placed += [copies.start(d_out, results[3]), copies.start(d_out_b, results[4])]
    wait_all(*placed)


def final_call(col_width, wholes, *arrays):
    def body(*refs):
        final_kernel(col_width, *refs)

    shapes = [((PREFIX, D), f32), ((D, D), f32), ((1, D), f32), ((D, col_width), f32), ((1, col_width), f32)]
    whole_shapes = [((1, 2, 1, SEQ, D), bf16), ((1, 2, 1, SEQ, D), f32)]
    return call_kernel(
        body, "reparam", in_vmem(*arrays) + in_hbm(*wholes),
        [(pltpu.HBM, *pair) for pair in shapes + whole_shapes], shapes, 7, LATE_MIB, SEQ * D * D,
        {8: 5, 9: 6},
    )


def swapped(array_in):
    return lax.ppermute(array_in, "pipe", [(0, 1), (1, 0)])


def hops(axis):
    size = lax.axis_size(axis)
    steps = []
    step = 1
    while step < size:
        steps.append((axis, [(i, i ^ step) for i in range(size)]))
        step *= 2
    assert step == size
    return steps


def local(
    block_input,
    cotangent,
    segments,
    ln1_gain,
    ln1_shift,
    qkv_weight,
    qkv_bias,
    attn_weight,
    attn_bias,
    ln2_gain,
    ln2_shift,
    ff_in_weight,
    ff_in_bias,
    ff_out_weight,
    ff_out_bias,
    prefix_embed,
    up_weight,
    up_bias,
    out_weight,
    out_bias,
):
    other_qkv = swapped(qkv_weight)
    small = small_call(
        ln1_gain, ln1_shift, ln2_gain, ln2_shift, attn_bias, ff_out_bias, qkv_bias, ff_in_bias
    )
    other_small = swapped(small)
    small, prefix_embed = lax.optimization_barrier((small, prefix_embed))
    tables = jnp.asarray(rope_tables())
    _, *later = lax.optimization_barrier((small, attn_weight, ff_in_weight, ff_out_weight))
    own = (qkv_weight, attn_weight, ff_in_weight, ff_out_weight)
    other = (other_qkv,) + tuple(swapped(weight) for weight in later)
    *saved, qkv_zero, hidden_units = first_call(
        (small, other_small), other_qkv, block_input, segments, qkv_weight, prefix_embed, up_weight,
        up_bias, out_weight, out_bias, tables,
    )
    x_zero, small_zero = saved[10:]
    (h_one, act_one, mixed_one, grad_one, grad_low, slope_zero, packed_zero, prefix_grad, small_one,
     in_zero, out_zero, attn_one, out_one) = middle_call(
        (small, other_small, *saved), other, cotangent, *own, tables
    )

    def layer_one_out(state):
        keep, send = result_call(state["h_one"], act_one, mixed_one, small_one, attn_one, out_one)
        return dict(state, act=keep, act_send=send)

    def layer_zero_feed(state):
        two = feed_back_call(state["grad_low"], slope_zero, in_zero, out_zero)
        return dict(state, grad_two=two, act_other=swapped(state["act_send"]))

    def layer_zero_norms(state):
        keep, send = norms_call(
            x_zero, grad_low, state["grad_two"], packed_zero, grad_one, small_zero, qkv_zero
        )
        return dict(state, grad=keep, grad_send=send)

    def swap_grads(state):
        turned = turn_call(state["out_weight"], up_weight)
        return dict(state, grad_other=swapped(state["grad_send"]), turned=turned)

    works = [layer_one_out, layer_zero_feed, layer_zero_norms, swap_grads]
    state = {"h_one": h_one, "grad_low": grad_low, "out_weight": out_weight}
    for axis, pairs in hops("pipe") + hops("dp") + hops("grp"):
        moved = lax.ppermute(prefix_grad, axis, pairs)
        if works:
            state = works.pop(0)(state)
        prefix_grad, moved, state = lax.optimization_barrier((prefix_grad, moved, state))
        prefix_grad = prefix_grad + moved
    for work in works:
        state = work(state)
    col_width = 2 * D // lax.axis_size("dp")
    grad_embed, grad_up, grad_up_b, grad_out, grad_out_b, activations, input_grads = final_call(
        col_width, (state["act"], state["grad"]), prefix_grad, hidden_units, prefix_embed,
        *state["turned"], state["act_other"], state["grad_other"],
    )
    return (
        activations,
        input_grads,
        grad_embed,
        grad_up,
        grad_up_b[0],
        grad_out,
        grad_out_b[0],
    )


def solution(mesh):
    return jax.shard_map(
        local,
        mesh=mesh,
        in_specs=(
            P(None, ("grp", "dp"), None, None),
            P(None, ("grp", "dp"), None, None),
            P(None, ("grp", "dp"), None),
            P("pipe", None),
            P("pipe", None),
            P("pipe", None, None),
            P("pipe", None),
            P("pipe", None, None),
            P("pipe", None),
            P("pipe", None),
            P("pipe", None),
            P("pipe", None, None),
            P("pipe", None),
            P("pipe", None, None),
            P("pipe", None),
            P(),
            P(),
            P(),
            P(),
            P(),
        ),
        out_specs=(
            P("pipe", None, ("grp", "dp"), None, None),
            P("pipe", None, ("grp", "dp"), None, None),
            P(),
            P(),
            P(),
            P(None, ("pipe", "dp")),
            P(("pipe", "dp")),
        ),
        check_vma=False,
    )
```

```python
import math

import jax
import jax.numpy as jnp
import numpy as np
from jax import lax
from jax.experimental import pallas as pl
from jax.experimental.pallas import tpu as pltpu
from jax.sharding import PartitionSpec as P

D = 512
SEQ = 512
HEADS = 8
HD = 64
FF = 2048
ROT = 16
PREFIX = 10
PAD = 16
BLK = 128
BLOCKS = SEQ // BLK
PAIRS = HEADS // 2
LIVE = (1, 2, 3, 3)
P_ROWS = BLK * sum(LIVE)
P_START = (0, 128, 384, 768)

f32 = jnp.float32
bf16 = jnp.bfloat16
LOG2E = math.log2(math.e)
Q_SCALE = LOG2E * HD**-0.5
K_BACK = 1.0 / LOG2E
Q_BACK = HD**-0.5
NEG = -1e30

NN = (((1,), (0,)), ((), ()))
NT = (((1,), (1,)), ((), ()))
TN = (((0,), (0,)), ((), ()))

NO_COPIES = ((),) * 4
MIB = 1024 * 1024
EARLY_MIB = 24
MIDDLE_MIB = 22
LATE_MIB = 12

G1, B1, G2, B2, B_ATTN, B_OUT, B_QKV, B_IN = 0, 1, 2, 3, 4, 5, 6, 9
SMALL = 13 * D


def dot(left, right, dims):
    return lax.dot_general(left, right, dims, preferred_element_type=f32)


def call_kernel(kernel, name, ins, outs, scratch, sems, mib, cost, aliases=None):
    operands = [pltpu.with_memory_space_constraint(array, space) for array, space in ins]
    return pl.pallas_call(
        kernel,
        name=name,
        out_shape=[space(shape, dtype) for space, shape, dtype in outs],
        in_specs=[pl.BlockSpec(memory_space=space) for _, space in ins],
        out_specs=[pl.BlockSpec(memory_space=space) for space, _, _ in outs],
        scratch_shapes=[pltpu.VMEM(*pair) for pair in scratch]
        + ([pltpu.SemaphoreType.DMA((sems,))] if sems else []),
        input_output_aliases=aliases or {},
        compiler_params=pltpu.CompilerParams(vmem_limit_bytes=mib * MIB),
        cost_estimate=pl.CostEstimate(flops=cost, bytes_accessed=8 * MIB, transcendentals=0),
    )(*operands)


def in_hbm(*arrays):
    return [(array, pltpu.HBM) for array in arrays]


def anywhere(*arrays):
    return [(array, pl.ANY) for array in arrays]


def in_vmem(*arrays):
    return [(array, pltpu.VMEM) for array in arrays]


def vmem(shapes):
    return [(pltpu.VMEM, *pair) for pair in shapes]


def small_row(small_ref, place):
    return small_ref[:, place * D : (place + 1) * D]


def rope_tables():
    inv_freq = 10000.0 ** (-2.0 * np.arange(ROT // 2) / ROT)
    angles = inv_freq[:, None] * np.arange(SEQ)[None, :]
    return np.concatenate([np.cos(angles), np.sin(angles)], axis=0).astype(np.float32)


class Copies:
    def __init__(self, sems):
        self.sems = sems
        self.count = 0

    def start(self, src, dst):
        copy = pltpu.make_async_copy(src, dst, self.sems.at[self.count])
        self.count += 1
        copy.start()
        return copy

    def of_layer(self, here, own, other, dst):
        sem = self.sems.at[self.count]
        self.count += 1
        copy = pltpu.make_async_copy(own, dst, sem)

        @pl.when(here)
        def _():
            copy.start()

        @pl.when(jnp.logical_not(here))
        def _():
            pltpu.make_async_copy(other, dst, sem).start()

        return copy


def wait_all(*copies):
    for copy in copies:
        copy.wait()


def normalized(hidden):
    mean = jnp.mean(hidden, axis=-1, keepdims=True)
    centered = hidden - mean
    variance = jnp.mean(centered * centered, axis=-1, keepdims=True)
    scale = lax.rsqrt(variance + 1e-05)
    return centered * scale, scale


def rope_heads(rows, cos, sin):
    parts = []
    for head in range(rows.shape[0] // HD):
        base = head * HD
        lead = rows[base : base + 8]
        tail = rows[base + 8 : base + 16]
        parts += [lead * cos - tail * sin, tail * cos + lead * sin, rows[base + 16 : base + HD]]
    return jnp.concatenate(parts, axis=0)


def fill_mask(seg_ref, mask_ref):
    seg_row = seg_ref[...].astype(f32)
    seg_col = jnp.transpose(jnp.broadcast_to(seg_row, (8, SEQ)))[:, 0:1]
    for block in range(BLOCKS):
        for key_block in range(block + 1 - LIVE[block], block + 1):
            seen = seg_col[key_block * BLK : (key_block + 1) * BLK] == (
                seg_row[:, block * BLK : (block + 1) * BLK]
            )
            if key_block == block:
                key_pos = lax.broadcasted_iota(jnp.int32, (BLK, BLK), 0)
                query_pos = lax.broadcasted_iota(jnp.int32, (BLK, BLK), 1)
                seen = seen & (key_pos <= query_pos)
            start = P_START[block] + (key_block - (block + 1 - LIVE[block])) * BLK
            mask_ref[start : start + BLK, :] = jnp.where(seen, 0.0, NEG)


def project_heads(normed, w_ref, small_ref, cos, sin, q_t, k_t, k_m, v_m, v_t):
    bias = small_row(small_ref, B_QKV)
    rows = dot(normed, w_ref[:, :D], NN) + bias
    q_t[...] = (rope_heads(jnp.transpose(rows), cos, sin) * Q_SCALE).astype(bf16)
    bias = small_row(small_ref, B_QKV + 1)
    rows = dot(normed, w_ref[:, D : 2 * D], NN) + bias
    keys = rope_heads(jnp.transpose(rows), cos, sin).astype(bf16)
    k_t[...] = keys
    k_m[...] = jnp.transpose(keys)
    bias = small_row(small_ref, B_QKV + 2)
    values = (dot(normed, w_ref[:, 2 * D :], NN) + bias).astype(bf16)
    v_m[...] = values
    v_t[...] = jnp.transpose(values)


def block_diagonal(pair_rows):
    zeros = jnp.zeros((HD, BLK), pair_rows.dtype)
    return jnp.concatenate(
        [
            jnp.concatenate([pair_rows[:HD], zeros], axis=1),
            jnp.concatenate([zeros, pair_rows[HD:]], axis=1),
        ],
        axis=0,
    )


def from_diagonal(both):
    return jnp.concatenate([both[:HD, :BLK], both[HD:, BLK:]], axis=0)


def per_head(row, rows=HD):
    return jnp.concatenate(
        [
            jnp.broadcast_to(row[:, :BLK], (rows, BLK)),
            jnp.broadcast_to(row[:, BLK:], (rows, BLK)),
        ],
        axis=0,
    )


def geometry(block):
    live = LIVE[block] * BLK
    end = (block + 1) * BLK
    start = P_START[block]
    return slice(end - live, end), slice(block * BLK, end), slice(start, start + live)


def attend(q_t, k_m, v_t, pre_k, pre_v, mask_ref, p_ref, pp_ref, inv_ref, mixed_ref):
    pad_mask = jnp.where(lax.broadcasted_iota(jnp.int32, (PAD, 1), 0) < PREFIX, 0.0, NEG)

    def score(feats, block):
        keys, tokens, rows = geometry(block)
        queries = block_diagonal(q_t[feats, tokens])
        mask = mask_ref[rows, :]
        scores = dot(k_m[keys, feats], queries, NN) + jnp.concatenate([mask, mask], axis=1)
        return scores, dot(pre_k[:, feats], queries, NN) + pad_mask

    def soften(pair, block, scores, pre_scores):
        _, _, rows = geometry(block)
        peak = jnp.maximum(
            jnp.max(scores, axis=0, keepdims=True), jnp.max(pre_scores, axis=0, keepdims=True)
        )
        expo = jnp.exp2(scores - peak)
        pre_expo = jnp.exp2(pre_scores - peak)
        total = jnp.sum(expo, axis=0, keepdims=True) + jnp.sum(pre_expo, axis=0, keepdims=True)
        inverse = 1.0 / total
        expo = expo.astype(bf16)
        pre_expo = pre_expo.astype(bf16)
        p_ref[pair, rows, :] = expo
        pp_ref[pair, block] = pre_expo
        inv_ref[pair, block] = jnp.broadcast_to(inverse, (8, 2 * BLK))
        return expo, pre_expo, inverse

    def mix(feats, block, expo, pre_expo, inverse):
        keys, tokens, _ = geometry(block)
        mixed = dot(v_t[feats, keys], expo, NN) + dot(pre_v[:, feats], pre_expo, TN)
        mixed_ref[feats, tokens] = (from_diagonal(mixed) * per_head(inverse)).astype(bf16)

    for pair in range(PAIRS):
        feats = slice(pair * BLK, (pair + 1) * BLK)
        scores = [score(feats, block) for block in range(BLOCKS)]
        soft = [soften(pair, block, *scores[block]) for block in range(BLOCKS)]
        for block in range(BLOCKS):
            mix(feats, block, *soft[block])


def attend_back(grad_t, q_t, k_t, v_m, pre_k, pre_v, p_ref, pp_ref, inv_ref, mixed_ref,
                dq_ref, dk_ref, dv_ref, pre_grad, pre_row):
    def value_grads(pair, feats, block):
        keys, tokens, _ = geometry(block)
        scaled = (grad_t[feats, tokens] * per_head(inv_ref[pair, block][0:1, :])).astype(bf16)
        products = scaled.astype(f32) * mixed_ref[feats, tokens].astype(f32)
        inner = jnp.concatenate(
            [
                jnp.sum(products[:HD], axis=0, keepdims=True),
                jnp.sum(products[HD:], axis=0, keepdims=True),
            ],
            axis=1,
        )
        grads = block_diagonal(scaled)
        return grads, inner, dot(v_m[keys, feats], grads, NN), dot(pre_v[:, feats], grads, NN)

    def score_grads(pair, block, inner, grad_probs, pre_grad_probs):
        _, _, rows = geometry(block)
        probs = p_ref[pair, rows, :].astype(f32)
        pre_probs = pp_ref[pair, block].astype(f32)
        return (
            (probs * (grad_probs - inner)).astype(bf16),
            (pre_probs * (pre_grad_probs - inner)).astype(bf16),
        )

    def out_grads(pair, feats, block, grads, grad_scores, pre_scores):
        keys, tokens, rows = geometry(block)
        queries = block_diagonal(q_t[feats, tokens])
        dq = dot(k_t[feats, keys], grad_scores, NN) + dot(pre_k[:, feats], pre_scores, TN)
        dq_ref[feats, tokens] = from_diagonal(dq)
        return (
            dot(queries, grad_scores, NT),
            dot(grads, p_ref[pair, rows, :], NT),
            dot(pre_scores, queries, NT),
            dot(pp_ref[pair, block], grads, NT),
        )

    def by_keys(outs, which, key_block):
        total = None
        for block in range(BLOCKS):
            place = key_block - (block + 1 - LIVE[block])
            if 0 <= place < LIVE[block]:
                part = outs[block][which][:, place * BLK : (place + 1) * BLK]
                total = part if total is None else total + part
        return total

    for pair in range(PAIRS):
        feats = slice(pair * BLK, (pair + 1) * BLK)
        first = [value_grads(pair, feats, block) for block in range(BLOCKS)]
        second = [score_grads(pair, block, *first[block][1:]) for block in range(BLOCKS)]
        outs = [
            out_grads(pair, feats, block, first[block][0], *second[block])
            for block in range(BLOCKS)
        ]
        for key_block in range(BLOCKS):
            keys = slice(key_block * BLK, (key_block + 1) * BLK)
            dk_ref[feats, keys] = by_keys(outs, 0, key_block)
            dv_ref[feats, keys] = by_keys(outs, 1, key_block)
        pre_dk = outs[0][2] + outs[1][2] + outs[2][2] + outs[3][2]
        pre_dv = outs[0][3] + outs[1][3] + outs[2][3] + outs[3][3]
        pre_grad[pre_row : pre_row + PAD, feats] = pre_dk * K_BACK
        pre_grad[pre_row + PAD : pre_row + 2 * PAD, feats] = pre_dv


def pack_grads(dq_ref, dk_ref, dv_ref, cos, sin, packed_t):
    packed_t[:D, :] = (rope_heads(dq_ref[...], cos, -sin) * Q_BACK).astype(bf16)
    packed_t[D : 2 * D, :] = (rope_heads(dk_ref[...], cos, -sin) * K_BACK).astype(bf16)
    packed_t[2 * D :, :] = dv_ref[...].astype(bf16)


def gelu_both(before):
    cdf = 0.5 + 0.5 * lax.erf(before * (0.5**0.5))
    density = jnp.exp2(before * before * (-0.5 * LOG2E)) * (1.0 / math.sqrt(2.0 * math.pi))
    return before * cdf, cdf + before * density


FF_CHUNK = 512


def chunk_of(index):
    return slice(index * FF_CHUNK, (index + 1) * FF_CHUNK)


def feed_in(normed, w_ref, small_ref, act_ref, slope_ref, arrivals):
    for chunk in range(FF // FF_CHUNK):
        cols = chunk_of(chunk)
        wait_all(*arrivals[chunk])
        before = dot(normed, w_ref[:, cols], NN) + small_row(small_ref, B_IN + chunk)
        act, slope = gelu_both(before)
        act_ref[:, cols] = act.astype(bf16)
        slope_ref[:, cols] = slope.astype(bf16)


def layer_result(hidden, mixed_t, w_attn, act_ref, w_out, small_ref):
    attn_out = dot(jnp.transpose(mixed_t), w_attn, NN) + small_row(small_ref, B_ATTN)
    ff_out = dot(act_ref[...], w_out, NN) + small_row(small_ref, B_OUT)
    return hidden + attn_out + ff_out


def feed_back(grad, w_out, w_in, slope_ref, arrivals):
    total = jnp.zeros((SEQ, D), f32)
    for chunk in range(FF // FF_CHUNK):
        cols = chunk_of(chunk)
        wait_all(*arrivals[chunk])
        grad_act = dot(grad, w_out[cols, :], NT)
        grad_before = (grad_act * slope_ref[:, cols].astype(f32)).astype(bf16)
        total = total + dot(grad_before, w_in[:, cols], NT)
    return total


def norms_back(grad, hidden, grad_two, packed_t, w_qkv, small_ref):
    grad_one = jnp.transpose(dot(w_qkv, packed_t, NN))
    grad_hat = (
        grad_one * small_row(small_ref, G1) + grad_two * small_row(small_ref, G2)
    )
    hat, scale = normalized(hidden)
    mean_one = jnp.mean(grad_hat, axis=-1, keepdims=True)
    mean_two = jnp.mean(grad_hat * hat, axis=-1, keepdims=True)
    return grad.astype(f32) + scale * (grad_hat - mean_one - hat * mean_two)


def halves(values):
    high = values.astype(bf16)
    return high, (values - high.astype(f32)).astype(bf16)


def padded(values):
    return jnp.concatenate([values, jnp.zeros((PAD - PREFIX, values.shape[1]), f32)], axis=0)


def few_rows_dot(left, right):
    left_high, left_rest = halves(padded(left))
    right_high, right_rest = halves(right)
    both = dot(jnp.concatenate([left_high, left_rest], axis=0), right_high, NN)
    return both[:PAD] + both[PAD:] + dot(left_high, right_rest, NN)


def stacked_dot(left, right):
    left_high, left_rest = halves(padded(left))
    right_high, right_rest = halves(padded(right))
    return dot(
        jnp.concatenate([left_high, left_high, left_rest], axis=0),
        jnp.concatenate([right_high, right_rest, right_high], axis=0),
        TN,
    )


def small_kernel(gain_one, shift_one, gain_two, shift_two, attn_b, out_b, qkv_b, in_b, packed, sems):
    copies = Copies(sems)
    places = [(gain_one, 0), (shift_one, 1), (gain_two, 2), (shift_two, 3), (attn_b, 4), (out_b, 5)]
    places += [(qkv_b, 6), (in_b, 9)]
    wait_all(
        *[
            copies.start(row, packed.at[:, place * D : place * D + row.shape[1]])
            for row, place in places
        ]
    )


def small_call(*arrays):
    (packed,) = call_kernel(
        small_kernel, "small_parameters", in_hbm(*arrays), vmem([((1, SMALL), f32)]), [], 8, LATE_MIB, SMALL
    )
    return packed


def prefix_states(embed, up_w, up_b, out_w, out_b, arrivals, hidden, low):
    units = jnp.tanh(few_rows_dot(embed[...], up_w[...])[:PREFIX] + up_b[...])
    hidden[...] = units
    real = lax.broadcasted_iota(jnp.int32, (PAD, 1), 0) < PREFIX
    for part in range(4):
        cols = slice(part * D, (part + 1) * D)
        arrivals[part].wait()
        states = few_rows_dot(units, out_w[:, cols]) + out_b[:, cols]
        low[part] = jnp.where(real, states, 0.0).astype(bf16)


OPENING_SHAPES = (
    ((SEQ, D), bf16),
    ((SEQ, D), f32),
    ((P_ROWS, BLK), f32),
    ((4, PAD, D), bf16),
    ((PREFIX, D), f32),
    ((2 * 8, SEQ), f32),
    ((D, 3 * D), bf16),
)


def opening_kernel(x_hbm, seg_hbm, embed_hbm, up_hbm, up_b_hbm, out_hbm, out_b_hbm, tables_hbm, qkv_hbm,
                   x_ref, hat, mask, low, hidden, tables, own_qkv, seg, embed, up_w, up_b, out_w, out_b, sems):
    section = lax.axis_index("pipe")
    copies = Copies(sems)
    x_copy = copies.start(x_hbm.at[section, 0], x_ref)
    seg_copy = copies.start(seg_hbm.at[section], seg)
    prefix_copies = [
        copies.start(src, dst)
        for src, dst in ((embed_hbm, embed), (up_hbm, up_w), (up_b_hbm, up_b.at[0]), (out_b_hbm, out_b.at[0]))
    ]
    parts = [
        copies.start(out_hbm.at[:, i * D : (i + 1) * D], out_w.at[:, i * D : (i + 1) * D])
        for i in range(4)
    ]
    late = [copies.start(tables_hbm, tables), copies.start(qkv_hbm.at[0], own_qkv)]
    seg_copy.wait()
    fill_mask(seg, mask)
    x_copy.wait()
    hat[...], _ = normalized(x_ref[...].astype(f32))
    wait_all(*prefix_copies)
    prefix_states(embed, up_w, up_b, out_w, out_b, parts, hidden, low)
    wait_all(*late)


def opening_call(*arrays):
    scratch = [
        ((1, SEQ), jnp.int32),
        ((PREFIX, D), f32),
        ((D, D), f32),
        ((1, D), f32),
        ((D, 4 * D), f32),
        ((1, 4 * D), f32),
    ]
    return call_kernel(
        opening_kernel, "opening", in_hbm(*arrays), vmem(OPENING_SHAPES), scratch, 12, EARLY_MIB,
        2 * 6 * PAD * D * 5 * D,
    )


HEAD_SHAPES = (
    ((D, SEQ), bf16),
    ((D, SEQ), bf16),
    ((SEQ, D), bf16),
    ((PAIRS, P_ROWS, 2 * BLK), bf16),
    ((PAIRS, BLOCKS, PAD, 2 * BLK), bf16),
    ((PAIRS, BLOCKS, 8, 2 * BLK), f32),
    ((D, SEQ), bf16),
)
FIRST_SHAPES = HEAD_SHAPES + (
    ((SEQ, D), bf16),
    ((2, 1, SMALL), f32),
    ((2, D, 3 * D), bf16),
    ((2, D, D), bf16),
    ((2, D, FF), bf16),
    ((2, FF, D), bf16),
    ((SEQ, D), bf16),
)


def first_kernel(own_small, other_small, own_qkv, other_qkv, hat_ref, mask, low, tables,
                 attn_hbm, ff_in_hbm, ff_out_hbm, cot_hbm,
                 q_t, k_t, v_m, p_ref, pp_ref, inv_ref, mixed_ref, two_ref, small, w_qkv, w_attn, w_in,
                 w_out, cot_ref, k_m, v_t, sems):
    section = lax.axis_index("pipe")
    copies = Copies(sems)
    now = [
        copies.start(own_small, small.at[section]),
        copies.start(other_small, small.at[1 - section]),
        copies.start(own_qkv, w_qkv.at[section]),
        copies.start(other_qkv.at[0], w_qkv.at[1 - section]),
    ]
    later = [
        copies.start(ff_in_hbm.at[0], w_in.at[section]),
        copies.start(attn_hbm.at[0], w_attn.at[section]),
        copies.start(ff_out_hbm.at[0], w_out.at[section]),
        copies.start(cot_hbm.at[section, 0], cot_ref),
    ]
    wait_all(*now)
    hat = hat_ref[...]
    zero = small.at[0]
    normed = (hat * small_row(zero, G1) + small_row(zero, B1)).astype(bf16)
    two_ref[...] = (hat * small_row(zero, G2) + small_row(zero, B2)).astype(bf16)
    project_heads(normed, w_qkv.at[0], zero, tables[:8, :], tables[8:, :], q_t, k_t, k_m, v_m, v_t)
    attend(q_t, k_m, v_t, low.at[0], low.at[1], mask, p_ref, pp_ref, inv_ref, mixed_ref)
    wait_all(*later)


def first_call(ready, *arrays):
    return call_kernel(
        first_kernel, "first_attention", in_vmem(*ready) + in_hbm(*arrays), vmem(FIRST_SHAPES),
        [((SEQ, D), bf16), ((D, SEQ), bf16)], 8, EARLY_MIB, 200 * SEQ * D * 3 * D,
    )


def feed_kernel(two, small, other_in, w_in_before, act_ref, slope_ref, w_in, sems):
    wait_all(Copies(sems).start(other_in.at[0], w_in.at[1 - lax.axis_index("pipe")]))
    feed_in(two[...], w_in.at[0], small.at[0], act_ref, slope_ref, NO_COPIES)


def feed_call(*arrays):
    shapes = [((SEQ, FF), bf16), ((SEQ, FF), bf16), ((2, D, FF), bf16)]
    return call_kernel(
        feed_kernel, "first_feed", in_vmem(*arrays), vmem(shapes), [], 1, LATE_MIB, 2 * SEQ * D * FF,
        {3: 2},
    )


WEIGHT_SHAPES = (((D, 3 * D), bf16), ((D, D), bf16), ((D, FF), bf16), ((FF, D), bf16))


MIDDLE_OUTS = (
    ((SEQ, D), bf16),
    ((SEQ, FF), bf16),
    ((D, SEQ), bf16),
    ((SEQ, D), f32),
    ((SEQ, D), bf16),
    ((3 * D, SEQ), bf16),
    ((4 * PREFIX, D), f32),
    ((2, D, D), bf16),
    ((2, FF, D), bf16),
)


def middle_kernel(w_attn_before, w_out_before, q0, k0, v0, p0, pp0, inv0, mixed0, small, w_qkv, w_in,
                  other_attn, other_out, cot_ref, x_ref, act_zero, low, mask, tables,
                  h_one, act_one, mixed_one, grad_one, grad_low, packed_zero, prefix_grad, w_attn, w_out,
                  q_t, k_t, v_m, p_ref, pp_ref, inv_ref, slope_one, k_m, v_t, dq, dk, dv, packed, pre_grad,
                  sems):
    section = lax.axis_index("pipe")
    copies = Copies(sems)
    wait_all(
        copies.start(other_attn.at[0], w_attn.at[1 - section]),
        copies.start(other_out.at[0], w_out.at[1 - section]),
    )
    small_one = small.at[1]
    h_one[...] = layer_result(
        x_ref[...].astype(f32), mixed0[...], w_attn[0], act_zero, w_out[0], small.at[0]
    ).astype(bf16)

    cos, sin = tables[:8, :], tables[8:, :]
    hat, _ = normalized(h_one[...].astype(f32))
    normed = (hat * small_row(small_one, G1) + small_row(small_one, B1)).astype(bf16)
    two = (hat * small_row(small_one, G2) + small_row(small_one, B2)).astype(bf16)
    project_heads(normed, w_qkv.at[1], small_one, cos, sin, q_t, k_t, k_m, v_m, v_t)
    attend(q_t, k_m, v_t, low.at[2], low.at[3], mask, p_ref, pp_ref, inv_ref, mixed_one)
    feed_in(two, w_in.at[1], small_one, act_one, slope_one, NO_COPIES)

    grad = cot_ref[...]
    grad_two = feed_back(grad, w_out.at[1], w_in.at[1], slope_one, NO_COPIES)
    dq[...] = dot(w_attn[1], grad, NT)
    attend_back(dq, q_t, k_t, v_m, low.at[2], low.at[3], p_ref, pp_ref, inv_ref, mixed_one,
                dq, dk, dv, pre_grad, 2 * PAD)
    pack_grads(dq, dk, dv, cos, sin, packed)
    result = norms_back(grad, h_one[...].astype(f32), grad_two, packed[...], w_qkv[1], small_one)
    grad_one[...] = result
    grad_low[...] = result.astype(bf16)

    dq[...] = dot(w_attn[0], grad_low[...], NT)
    attend_back(dq, q0, k0, v0, low.at[0], low.at[1], p0, pp0, inv0, mixed0,
                dq, dk, dv, pre_grad, 0)
    for part in range(4):
        prefix_grad[part * PREFIX : (part + 1) * PREFIX, :] = pre_grad[
            part * PAD : part * PAD + PREFIX, :
        ]
    pack_grads(dq, dk, dv, cos, sin, packed_zero)


def middle_call(*arrays):
    scratch = HEAD_SHAPES[:6] + (
        ((SEQ, FF), bf16),
        ((SEQ, D), bf16),
        ((D, SEQ), bf16),
        ((D, SEQ), f32),
        ((D, SEQ), f32),
        ((D, SEQ), f32),
        ((3 * D, SEQ), bf16),
        ((4 * PAD, D), f32),
    )
    return call_kernel(
        middle_kernel, "middle", in_vmem(*arrays), vmem(MIDDLE_OUTS), scratch, 2, MIDDLE_MIB,
        20 * SEQ * D * 6 * D, {0: 7, 1: 8},
    )


def hand_over(section, values, send_ref, whole, sems):
    copies = Copies(sems)
    wait_all(
        copies.of_layer(section == 0, values[0], values[1], whole.at[0, section, 0]),
        copies.of_layer(section == 0, values[1], values[0], send_ref),
    )


def result_kernel(h_one, act, mixed, small, w_attn, w_out, whole, send_ref, result, sems):
    result[...] = layer_result(
        h_one[...].astype(f32), mixed[...], w_attn[1], act, w_out[1], small.at[1]
    ).astype(bf16)
    hand_over(lax.axis_index("pipe"), (h_one, result), send_ref, whole, sems)


def result_call(*arrays):
    return call_kernel(
        result_kernel, "layer_one_out", in_vmem(*arrays),
        [(pltpu.HBM, (1, 2, 1, SEQ, D), bf16), (pltpu.VMEM, (SEQ, D), bf16)],
        [((SEQ, D), bf16)], 2, LATE_MIB, 2 * SEQ * D * (D + FF),
    )


def feed_back_kernel(grad, slope, w_in, w_out, total):
    total[...] = feed_back(grad[...], w_out.at[0], w_in.at[0], slope, NO_COPIES)


def feed_back_call(*arrays):
    (total,) = call_kernel(
        feed_back_kernel, "layer_zero_feed_back", in_vmem(*arrays), vmem([((SEQ, D), f32)]), [], 0,
        LATE_MIB, 4 * SEQ * D * FF,
    )
    return total


def norms_kernel(x_ref, grad, two, packed, grad_one, small, w_qkv, whole, send_ref, result, sems):
    result[...] = norms_back(
        grad[...], x_ref[...].astype(f32), two[...], packed[...], w_qkv[0], small.at[0]
    )
    hand_over(lax.axis_index("pipe"), (result, grad_one), send_ref, whole, sems)


def norms_call(*arrays):
    return call_kernel(
        norms_kernel, "layer_zero_norms", in_vmem(*arrays),
        [(pltpu.HBM, (1, 2, 1, SEQ, D), f32), (pltpu.VMEM, (SEQ, D), f32)],
        [((SEQ, D), f32)], 2, LATE_MIB, 6 * SEQ * D * D,
    )


def turn_kernel(out_hbm, up_hbm, wide, up_high, up_rest, out_w, up_w, sems):
    copies = Copies(sems)
    up = copies.start(up_hbm, up_w)
    parts = [
        copies.start(out_hbm.at[:, i * D : (i + 1) * D], out_w.at[:, i * D : (i + 1) * D])
        for i in range(4)
    ]
    up.wait()
    up_high[...], up_rest[...] = halves(jnp.transpose(up_w[...]))
    for part in range(4):
        cols = slice(part * D, (part + 1) * D)
        parts[part].wait()
        wide[cols, :] = jnp.transpose(out_w[:, cols].astype(bf16))


def turn_call(*arrays):
    return call_kernel(
        turn_kernel, "turned_matrices", in_hbm(*arrays),
        vmem([((4 * D, D), bf16), ((D, D), bf16), ((D, D), bf16)]),
        [((D, 4 * D), f32), ((D, D), f32)], 5, LATE_MIB, SEQ * D * D,
    )


def final_kernel(col_width, grads_ref, hidden, embed, wide, up_high, up_rest, act_other, grad_other,
                 act_in, grad_in, *refs):
    results, (act_out, grad_out, d_embed, d_up, d_up_b, d_out, d_out_b, sems) = refs[:5], refs[5:]
    section = lax.axis_index("pipe")
    shard = lax.axis_index("dp")
    copies = Copies(sems)
    placed = [
        copies.start(act_other, act_out.at[0, 1 - section, 0]),
        copies.start(grad_other, grad_out.at[0, 1 - section, 0]),
    ]
    units = hidden[...]
    both = jnp.zeros((2 * PAD, D), f32)
    for part in range(4):
        high, rest = halves(padded(grads_ref[part * PREFIX : (part + 1) * PREFIX, :]))
        both = both + dot(
            jnp.concatenate([high, rest], axis=0), wide[part * D : (part + 1) * D, :], NN
        )
    grad_units = (both[:PAD] + both[PAD:])[:PREFIX]
    grad_pre = grad_units * (1.0 - units * units)
    d_up_b[...] = jnp.sum(grad_pre, axis=0, keepdims=True)
    d_up[...] = stacked_dot(embed[...], grad_pre)
    placed += [copies.start(d_up_b, results[2]), copies.start(d_up, results[1])]
    high, rest = halves(padded(grad_pre))
    both = dot(jnp.concatenate([high, rest], axis=0), up_high[...], NN)
    both = both[:PAD] + both[PAD:] + dot(high, up_rest[...], NN)
    d_embed[...] = both[:PREFIX]
    placed.append(copies.start(d_embed, results[0]))
    column = section * (2 * D) + shard * col_width
    own_cols = jnp.zeros((PREFIX, col_width), f32)
    for part in range(4):
        for piece in range(D // col_width):
            here = column == part * D + piece * col_width
            cols = slice(piece * col_width, (piece + 1) * col_width)
            rows = slice(part * PREFIX, (part + 1) * PREFIX)
            own_cols = jnp.where(here, grads_ref[rows, cols], own_cols)
    d_out[...] = stacked_dot(units, own_cols)
    d_out_b[...] = jnp.sum(own_cols, axis=0, keepdims=True)
    placed += [copies.start(d_out, results[3]), copies.start(d_out_b, results[4])]
    wait_all(*placed)


def final_call(col_width, wholes, *arrays):
    def body(*refs):
        final_kernel(col_width, *refs)

    shapes = [((PREFIX, D), f32), ((D, D), f32), ((1, D), f32), ((D, col_width), f32), ((1, col_width), f32)]
    whole_shapes = [((1, 2, 1, SEQ, D), bf16), ((1, 2, 1, SEQ, D), f32)]
    return call_kernel(
        body, "reparam", in_vmem(*arrays) + in_hbm(*wholes),
        [(pltpu.HBM, *pair) for pair in shapes + whole_shapes], shapes, 7, LATE_MIB, SEQ * D * D,
        {8: 5, 9: 6},
    )


def swapped(array_in):
    return lax.ppermute(array_in, "pipe", [(0, 1), (1, 0)])


def hops(axis):
    size = lax.axis_size(axis)
    steps = []
    step = 1
    while step < size:
        steps.append((axis, [(i, i ^ step) for i in range(size)]))
        step *= 2
    assert step == size
    return steps


def local(
    block_input,
    cotangent,
    segments,
    ln1_gain,
    ln1_shift,
    qkv_weight,
    qkv_bias,
    attn_weight,
    attn_bias,
    ln2_gain,
    ln2_shift,
    ff_in_weight,
    ff_in_bias,
    ff_out_weight,
    ff_out_bias,
    prefix_embed,
    up_weight,
    up_bias,
    out_weight,
    out_bias,
):
    other_qkv = swapped(qkv_weight)
    small = small_call(
        ln1_gain, ln1_shift, ln2_gain, ln2_shift, attn_bias, ff_out_bias, qkv_bias, ff_in_bias
    )
    other_small = swapped(small)
    small, prefix_embed = lax.optimization_barrier((small, prefix_embed))
    tables = jnp.asarray(rope_tables())
    _, *later = lax.optimization_barrier((small, attn_weight, ff_in_weight, ff_out_weight))
    other_attn, other_in, other_out = (swapped(weight) for weight in later)
    x_zero, hat_zero, mask, low, hidden_units, tables, own_qkv = opening_call(
        block_input, segments, prefix_embed, up_weight, up_bias, out_weight, out_bias, tables, qkv_weight
    )
    *heads, two_zero, small, w_qkv, w_attn, w_in, w_out, cot = first_call(
        (small, other_small, own_qkv, other_qkv, hat_zero, mask, low, tables),
        attn_weight, ff_in_weight, ff_out_weight, cotangent,
    )
    act_zero, slope_zero, w_in = feed_call(two_zero, small, other_in, w_in)
    h_one, act_one, mixed_one, grad_one, grad_low, packed_zero, prefix_grad, w_attn, w_out = middle_call(
        w_attn, w_out, *heads, small, w_qkv, w_in, other_attn, other_out, cot, x_zero, act_zero, low, mask,
        tables,
    )

    def layer_one_out(state):
        keep, send = result_call(state["h_one"], act_one, mixed_one, small, w_attn, w_out)
        return dict(state, act=keep, act_send=send)

    def layer_zero_feed(state):
        two = feed_back_call(state["grad_low"], slope_zero, w_in, w_out)
        return dict(state, grad_two=two, act_other=swapped(state["act_send"]))

    def layer_zero_norms(state):
        keep, send = norms_call(
            x_zero, grad_low, state["grad_two"], packed_zero, grad_one, small, w_qkv
        )
        return dict(state, grad=keep, grad_send=send)

    def swap_grads(state):
        turned = turn_call(state["out_weight"], up_weight)
        return dict(state, grad_other=swapped(state["grad_send"]), turned=turned)

    works = [None, layer_one_out, layer_zero_feed, layer_zero_norms, swap_grads]
    state = {"h_one": h_one, "grad_low": grad_low, "out_weight": out_weight}
    for axis, pairs in hops("pipe") + hops("dp") + hops("grp"):
        if axis == "pipe":
            moved = lax.ppermute(prefix_grad, axis, pairs)
        else:
            prefix_grad = lax.reduce_precision(prefix_grad, 8, 7)
            moved = lax.ppermute(prefix_grad.astype(bf16), axis, pairs)
        work = works.pop(0) if works else None
        if work:
            state = work(state)
        prefix_grad, moved, state = lax.optimization_barrier((prefix_grad, moved, state))
        prefix_grad = prefix_grad + moved.astype(f32)
    for work in works:
        state = work(state)
    col_width = 2 * D // lax.axis_size("dp")
    grad_embed, grad_up, grad_up_b, grad_out, grad_out_b, activations, input_grads = final_call(
        col_width, (state["act"], state["grad"]), prefix_grad, hidden_units, prefix_embed,
        *state["turned"], state["act_other"], state["grad_other"],
    )
    return (
        activations,
        input_grads,
        grad_embed,
        grad_up,
        grad_up_b[0],
        grad_out,
        grad_out_b[0],
    )


def solution(mesh):
    return jax.shard_map(
        local,
        mesh=mesh,
        in_specs=(
            P(None, ("grp", "dp"), None, None),
            P(None, ("grp", "dp"), None, None),
            P(None, ("grp", "dp"), None),
            P("pipe", None),
            P("pipe", None),
            P("pipe", None, None),
            P("pipe", None),
            P("pipe", None, None),
            P("pipe", None),
            P("pipe", None),
            P("pipe", None),
            P("pipe", None, None),
            P("pipe", None),
            P("pipe", None, None),
            P("pipe", None),
            P(),
            P(),
            P(),
            P(),
            P(),
        ),
        out_specs=(
            P("pipe", None, ("grp", "dp"), None, None),
            P("pipe", None, ("grp", "dp"), None, None),
            P(),
            P(),
            P(),
            P(None, ("pipe", "dp")),
            P(("pipe", "dp")),
        ),
        check_vma=False,
    )
```

```python
import math

import jax
import jax.numpy as jnp
import numpy as np
from jax import lax
from jax.experimental import pallas as pl
from jax.experimental.pallas import tpu as pltpu
from jax.sharding import PartitionSpec as P

D = 512
SEQ = 512
HEADS = 8
HD = 64
FF = 2048
ROT = 16
PREFIX = 10
PAD = 16
BLK = 128
BLOCKS = SEQ // BLK
PAIRS = HEADS // 2
LIVE = (1, 2, 3, 3)
P_ROWS = BLK * sum(LIVE)
P_START = (0, 128, 384, 768)

f32 = jnp.float32
bf16 = jnp.bfloat16
LOG2E = math.log2(math.e)
Q_SCALE = LOG2E * HD**-0.5
K_BACK = 1.0 / LOG2E
Q_BACK = HD**-0.5
NEG = -1e30

NN = (((1,), (0,)), ((), ()))
NT = (((1,), (1,)), ((), ()))
TN = (((0,), (0,)), ((), ()))

NO_COPIES = ((),) * 4
MIB = 1024 * 1024
EARLY_MIB = 24
MIDDLE_MIB = 22
LATE_MIB = 12

G1, B1, G2, B2, B_ATTN, B_OUT, B_QKV, B_IN = 0, 1, 2, 3, 4, 5, 6, 9
SMALL = 13 * D


def dot(left, right, dims):
    return lax.dot_general(left, right, dims, preferred_element_type=f32)


def call_kernel(kernel, name, ins, outs, scratch, sems, mib, cost, aliases=None):
    operands = [pltpu.with_memory_space_constraint(array, space) for array, space in ins]
    return pl.pallas_call(
        kernel,
        name=name,
        out_shape=[space(shape, dtype) for space, shape, dtype in outs],
        in_specs=[pl.BlockSpec(memory_space=space) for _, space in ins],
        out_specs=[pl.BlockSpec(memory_space=space) for space, _, _ in outs],
        scratch_shapes=[pltpu.VMEM(*pair) for pair in scratch]
        + ([pltpu.SemaphoreType.DMA((sems,))] if sems else []),
        input_output_aliases=aliases or {},
        compiler_params=pltpu.CompilerParams(vmem_limit_bytes=mib * MIB),
        cost_estimate=pl.CostEstimate(flops=cost, bytes_accessed=8 * MIB, transcendentals=0),
    )(*operands)


def in_hbm(*arrays):
    return [(array, pltpu.HBM) for array in arrays]


def anywhere(*arrays):
    return [(array, pl.ANY) for array in arrays]


def in_vmem(*arrays):
    return [(array, pltpu.VMEM) for array in arrays]


def vmem(shapes):
    return [(pltpu.VMEM, *pair) for pair in shapes]


def small_row(small_ref, place):
    return small_ref[:, place * D : (place + 1) * D]


def rope_tables():
    inv_freq = 10000.0 ** (-2.0 * np.arange(ROT // 2) / ROT)
    angles = inv_freq[:, None] * np.arange(SEQ)[None, :]
    return np.concatenate([np.cos(angles), np.sin(angles)], axis=0).astype(np.float32)


class Copies:
    def __init__(self, sems):
        self.sems = sems
        self.count = 0

    def start(self, src, dst):
        copy = pltpu.make_async_copy(src, dst, self.sems.at[self.count])
        self.count += 1
        copy.start()
        return copy

    def of_layer(self, here, own, other, dst):
        sem = self.sems.at[self.count]
        self.count += 1
        copy = pltpu.make_async_copy(own, dst, sem)

        @pl.when(here)
        def _():
            copy.start()

        @pl.when(jnp.logical_not(here))
        def _():
            pltpu.make_async_copy(other, dst, sem).start()

        return copy


def wait_all(*copies):
    for copy in copies:
        copy.wait()


def normalized(hidden):
    mean = jnp.mean(hidden, axis=-1, keepdims=True)
    centered = hidden - mean
    variance = jnp.mean(centered * centered, axis=-1, keepdims=True)
    scale = lax.rsqrt(variance + 1e-05)
    return centered * scale, scale


def rope_heads(rows, cos, sin):
    parts = []
    for head in range(rows.shape[0] // HD):
        base = head * HD
        lead = rows[base : base + 8]
        tail = rows[base + 8 : base + 16]
        parts += [lead * cos - tail * sin, tail * cos + lead * sin, rows[base + 16 : base + HD]]
    return jnp.concatenate(parts, axis=0)


def fill_mask(seg_ref, mask_ref):
    seg_row = seg_ref[...].astype(f32)
    seg_col = jnp.transpose(jnp.broadcast_to(seg_row, (8, SEQ)))[:, 0:1]
    for block in range(BLOCKS):
        for key_block in range(block + 1 - LIVE[block], block + 1):
            seen = seg_col[key_block * BLK : (key_block + 1) * BLK] == (
                seg_row[:, block * BLK : (block + 1) * BLK]
            )
            if key_block == block:
                key_pos = lax.broadcasted_iota(jnp.int32, (BLK, BLK), 0)
                query_pos = lax.broadcasted_iota(jnp.int32, (BLK, BLK), 1)
                seen = seen & (key_pos <= query_pos)
            start = P_START[block] + (key_block - (block + 1 - LIVE[block])) * BLK
            mask_ref[start : start + BLK, :] = jnp.where(seen, 0.0, NEG)


def project_heads(normed, w_ref, small_ref, cos, sin, q_t, k_t, k_m, v_m, v_t):
    bias = small_row(small_ref, B_QKV)
    rows = dot(normed, w_ref[:, :D], NN) + bias
    q_t[...] = (rope_heads(jnp.transpose(rows), cos, sin) * Q_SCALE).astype(bf16)
    bias = small_row(small_ref, B_QKV + 1)
    rows = dot(normed, w_ref[:, D : 2 * D], NN) + bias
    keys = rope_heads(jnp.transpose(rows), cos, sin).astype(bf16)
    k_t[...] = keys
    k_m[...] = jnp.transpose(keys)
    bias = small_row(small_ref, B_QKV + 2)
    values = (dot(normed, w_ref[:, 2 * D :], NN) + bias).astype(bf16)
    v_m[...] = values
    v_t[...] = jnp.transpose(values)


def block_diagonal(pair_rows):
    zeros = jnp.zeros((HD, BLK), pair_rows.dtype)
    return jnp.concatenate(
        [
            jnp.concatenate([pair_rows[:HD], zeros], axis=1),
            jnp.concatenate([zeros, pair_rows[HD:]], axis=1),
        ],
        axis=0,
    )


def from_diagonal(both):
    return jnp.concatenate([both[:HD, :BLK], both[HD:, BLK:]], axis=0)


def per_head(row, rows=HD):
    return jnp.concatenate(
        [
            jnp.broadcast_to(row[:, :BLK], (rows, BLK)),
            jnp.broadcast_to(row[:, BLK:], (rows, BLK)),
        ],
        axis=0,
    )


def geometry(block):
    live = LIVE[block] * BLK
    end = (block + 1) * BLK
    start = P_START[block]
    return slice(end - live, end), slice(block * BLK, end), slice(start, start + live)


def pair_rows(pair):
    return slice(pair * BLK, (pair + 1) * BLK)


def both_heads(rows, tokens):
    return jnp.concatenate([rows[:PAD, tokens], rows[PAD:, tokens]], axis=1)


def attend(q_t, k_m, v_t, pre_k, pre_v, mask_ref, p_ref, pp_ref, inv_ref, mixed_ref):
    real = lax.rem(lax.broadcasted_iota(jnp.int32, (2 * PAD, 1), 0), PAD) < PREFIX
    pad_mask = jnp.where(real, 0.0, NEG)

    def score(feats, block):
        keys, tokens, rows = geometry(block)
        queries = block_diagonal(q_t[feats, tokens])
        mask = mask_ref[rows, :]
        return dot(k_m[keys, feats], queries, NN) + jnp.concatenate([mask, mask], axis=1)

    def soften(pair, block, scores, pre_scores):
        _, tokens, rows = geometry(block)
        pre_scores = both_heads(pre_scores, tokens)
        peak = jnp.maximum(
            jnp.max(scores, axis=0, keepdims=True), jnp.max(pre_scores, axis=0, keepdims=True)
        )
        expo = jnp.exp2(scores - peak)
        pre_expo = jnp.exp2(pre_scores - peak)
        total = jnp.sum(expo, axis=0, keepdims=True) + jnp.sum(pre_expo, axis=0, keepdims=True)
        inverse = 1.0 / total
        expo = expo.astype(bf16)
        pre_expo = pre_expo.astype(bf16)
        p_ref[pair, rows, :] = expo
        pp_ref[pair, :PAD, tokens] = pre_expo[:, :BLK]
        pp_ref[pair, PAD:, tokens] = pre_expo[:, BLK:]
        inv_ref[2 * pair : 2 * pair + 1, tokens] = inverse[:, :BLK]
        inv_ref[2 * pair + 1 : 2 * pair + 2, tokens] = inverse[:, BLK:]
        return expo, inverse

    def mix(feats, block, pre_mixed, expo, inverse):
        keys, tokens, _ = geometry(block)
        mixed = from_diagonal(dot(v_t[feats, keys], expo, NN)) + pre_mixed[:, tokens]
        mixed_ref[feats, tokens] = (mixed * per_head(inverse)).astype(bf16)

    for pair in range(PAIRS):
        feats = pair_rows(pair)
        pre_scores = dot(pre_k[:, feats], q_t[feats, :], NN) + pad_mask
        scores = [score(feats, block) for block in range(BLOCKS)]
        soft = [soften(pair, block, scores[block], pre_scores) for block in range(BLOCKS)]
        pre_mixed = dot(pre_v[:, feats], pp_ref[pair], TN)
        for block in range(BLOCKS):
            mix(feats, block, pre_mixed, *soft[block])


def prefix_back(grad_t, q_t, pre_v, pp_ref, inv_ref, mixed_ref, scaled_ref, inner_ref, pre_ds_ref, pre_grad, pre_row):
    first_half = lax.broadcasted_iota(jnp.int32, (1, BLK), 1) < HD

    def own_head(both):
        return jnp.where(first_half, both[:PAD], both[PAD:])

    for pair in range(PAIRS):
        feats = pair_rows(pair)
        inner = []
        for head in (2 * pair, 2 * pair + 1):
            rows = slice(head * HD, (head + 1) * HD)
            scaled = (grad_t[rows, :] * inv_ref[head : head + 1, :]).astype(bf16)
            scaled_ref[rows, :] = scaled
            products = scaled.astype(f32) * mixed_ref[rows, :].astype(f32)
            inner.append(jnp.sum(products, axis=0, keepdims=True))
            inner_ref[head : head + 1, :] = inner[-1]
        inner = jnp.concatenate([jnp.broadcast_to(row, (PAD, SEQ)) for row in inner], axis=0)
        grads = scaled_ref[feats, :]
        probs = pp_ref[pair]
        grad_probs = dot(pre_v[:, feats], grads, NN)
        grad_scores = (probs.astype(f32) * (grad_probs - inner)).astype(bf16)
        pre_ds_ref[pair] = grad_scores
        pre_grad[pre_row : pre_row + PREFIX, feats] = (
            own_head(dot(grad_scores, q_t[feats, :], NT))[:PREFIX] * K_BACK
        )
        pre_grad[pre_row + PREFIX : pre_row + 2 * PREFIX, feats] = own_head(dot(probs, grads, NT))[:PREFIX]


def attend_back(scaled_ref, inner_ref, pre_ds_ref, q_t, k_t, v_m, pre_k, p_ref, dq_ref, dk_ref, dv_ref):
    def value_grads(feats, block):
        keys, tokens, _ = geometry(block)
        grads = block_diagonal(scaled_ref[feats, tokens])
        return grads, dot(v_m[keys, feats], grads, NN)

    def score_grads(pair, block, grad_probs):
        _, tokens, rows = geometry(block)
        inner = jnp.concatenate(
            [inner_ref[2 * pair : 2 * pair + 1, tokens], inner_ref[2 * pair + 1 : 2 * pair + 2, tokens]],
            axis=1,
        )
        return (p_ref[pair, rows, :].astype(f32) * (grad_probs - inner)).astype(bf16)

    def out_grads(pair, feats, block, pre_dq, grads, grad_scores):
        keys, tokens, rows = geometry(block)
        queries = block_diagonal(q_t[feats, tokens])
        dq_ref[feats, tokens] = (
            from_diagonal(dot(k_t[feats, keys], grad_scores, NN)) + pre_dq[:, tokens]
        )
        return dot(queries, grad_scores, NT), dot(grads, p_ref[pair, rows, :], NT)

    def by_keys(outs, which, key_block):
        total = None
        for block in range(BLOCKS):
            place = key_block - (block + 1 - LIVE[block])
            if 0 <= place < LIVE[block]:
                part = outs[block][which][:, place * BLK : (place + 1) * BLK]
                total = part if total is None else total + part
        return total

    for pair in range(PAIRS):
        feats = pair_rows(pair)
        first = [value_grads(feats, block) for block in range(BLOCKS)]
        second = [score_grads(pair, block, first[block][1]) for block in range(BLOCKS)]
        pre_dq = dot(pre_k[:, feats], pre_ds_ref[pair], TN)
        outs = [
            out_grads(pair, feats, block, pre_dq, first[block][0], second[block])
            for block in range(BLOCKS)
        ]
        for key_block in range(BLOCKS):
            keys = slice(key_block * BLK, (key_block + 1) * BLK)
            dk_ref[feats, keys] = by_keys(outs, 0, key_block)
            dv_ref[feats, keys] = by_keys(outs, 1, key_block)


def pack_grads(dq_ref, dk_ref, dv_ref, cos, sin, packed_t):
    packed_t[:D, :] = (rope_heads(dq_ref[...], cos, -sin) * Q_BACK).astype(bf16)
    packed_t[D : 2 * D, :] = (rope_heads(dk_ref[...], cos, -sin) * K_BACK).astype(bf16)
    packed_t[2 * D :, :] = dv_ref[...].astype(bf16)


def gelu_both(before):
    cdf = 0.5 + 0.5 * lax.erf(before * (0.5**0.5))
    density = jnp.exp2(before * before * (-0.5 * LOG2E)) * (1.0 / math.sqrt(2.0 * math.pi))
    return before * cdf, cdf + before * density


FF_CHUNK = 512


def chunk_of(index):
    return slice(index * FF_CHUNK, (index + 1) * FF_CHUNK)


def feed_in(normed, w_ref, small_ref, act_ref, slope_ref, arrivals):
    for chunk in range(FF // FF_CHUNK):
        cols = chunk_of(chunk)
        wait_all(*arrivals[chunk])
        before = dot(normed, w_ref[:, cols], NN) + small_row(small_ref, B_IN + chunk)
        act, slope = gelu_both(before)
        act_ref[:, cols] = act.astype(bf16)
        slope_ref[:, cols] = slope.astype(bf16)


def layer_result(hidden, mixed_t, w_attn, act_ref, w_out, small_ref):
    attn_out = dot(jnp.transpose(mixed_t), w_attn, NN) + small_row(small_ref, B_ATTN)
    ff_out = dot(act_ref[...], w_out, NN) + small_row(small_ref, B_OUT)
    return hidden + attn_out + ff_out


def feed_back(grad, w_out, w_in, slope_ref, arrivals):
    total = jnp.zeros((SEQ, D), f32)
    for chunk in range(FF // FF_CHUNK):
        cols = chunk_of(chunk)
        wait_all(*arrivals[chunk])
        grad_act = dot(grad, w_out[cols, :], NT)
        grad_before = (grad_act * slope_ref[:, cols].astype(f32)).astype(bf16)
        total = total + dot(grad_before, w_in[:, cols], NT)
    return total


def norms_back(grad, hidden, grad_two, packed_t, w_qkv, small_ref):
    grad_one = jnp.transpose(dot(w_qkv, packed_t, NN))
    grad_hat = (
        grad_one * small_row(small_ref, G1) + grad_two * small_row(small_ref, G2)
    )
    hat, scale = normalized(hidden)
    mean_one = jnp.mean(grad_hat, axis=-1, keepdims=True)
    mean_two = jnp.mean(grad_hat * hat, axis=-1, keepdims=True)
    return grad.astype(f32) + scale * (grad_hat - mean_one - hat * mean_two)


def halves(values):
    high = values.astype(bf16)
    return high, (values - high.astype(f32)).astype(bf16)


def padded(values):
    return jnp.concatenate([values, jnp.zeros((PAD - PREFIX, values.shape[1]), f32)], axis=0)


def few_rows_dot(left, right):
    left_high, left_rest = halves(padded(left))
    right_high, right_rest = halves(right)
    both = dot(jnp.concatenate([left_high, left_rest], axis=0), right_high, NN)
    return both[:PAD] + both[PAD:] + dot(left_high, right_rest, NN)


def stacked_dot(left, right):
    left_high, left_rest = halves(padded(left))
    right_high, right_rest = halves(padded(right))
    return dot(
        jnp.concatenate([left_high, left_high, left_rest], axis=0),
        jnp.concatenate([right_high, right_rest, right_high], axis=0),
        TN,
    )


def small_kernel(gain_one, shift_one, gain_two, shift_two, attn_b, out_b, qkv_b, in_b, packed, sems):
    copies = Copies(sems)
    places = [(gain_one, 0), (shift_one, 1), (gain_two, 2), (shift_two, 3), (attn_b, 4), (out_b, 5)]
    places += [(qkv_b, 6), (in_b, 9)]
    wait_all(
        *[
            copies.start(row, packed.at[:, place * D : place * D + row.shape[1]])
            for row, place in places
        ]
    )


def small_call(*arrays):
    (packed,) = call_kernel(
        small_kernel, "small_parameters", in_hbm(*arrays), vmem([((1, SMALL), f32)]), [], 8, LATE_MIB, SMALL
    )
    return packed


def prefix_states(embed, up_w, up_b, out_w, out_b, arrivals, hidden, low, wide, up_high, up_rest):
    units = jnp.tanh(few_rows_dot(embed[...], up_w[...])[:PREFIX] + up_b[...])
    hidden[...] = units
    up_high[...], up_rest[...] = halves(jnp.transpose(up_w[...]))
    real = lax.broadcasted_iota(jnp.int32, (PAD, 1), 0) < PREFIX
    first_head = lax.rem(lax.broadcasted_iota(jnp.int32, (1, D), 1), BLK) < HD
    for part in range(4):
        cols = slice(part * D, (part + 1) * D)
        arrivals[part].wait()
        states = jnp.where(real, few_rows_dot(units, out_w[:, cols]) + out_b[:, cols], 0.0)
        low[part, :PAD, :] = jnp.where(first_head, states, 0.0).astype(bf16)
        low[part, PAD:, :] = jnp.where(first_head, 0.0, states).astype(bf16)
        wide[cols, :] = jnp.transpose(out_w[:, cols].astype(bf16))


OPENING_SHAPES = (
    ((SEQ, D), bf16),
    ((SEQ, D), f32),
    ((P_ROWS, BLK), f32),
    ((4, 2 * PAD, D), bf16),
    ((PREFIX, D), f32),
    ((4 * D, D), bf16),
    ((D, D), bf16),
    ((D, D), bf16),
    ((2 * 8, SEQ), f32),
    ((D, 3 * D), bf16),
)


def opening_kernel(x_hbm, seg_hbm, embed_hbm, up_hbm, up_b_hbm, out_hbm, out_b_hbm, tables_hbm, qkv_hbm,
                   x_ref, hat, mask, low, hidden, wide, up_high, up_rest, tables, own_qkv, seg, embed, up_w, up_b,
                   out_w, out_b, sems):
    section = lax.axis_index("pipe")
    copies = Copies(sems)
    x_copy = copies.start(x_hbm.at[section, 0], x_ref)
    seg_copy = copies.start(seg_hbm.at[section], seg)
    prefix_copies = [
        copies.start(src, dst)
        for src, dst in ((embed_hbm, embed), (up_hbm, up_w), (up_b_hbm, up_b.at[0]), (out_b_hbm, out_b.at[0]))
    ]
    parts = [
        copies.start(out_hbm.at[:, i * D : (i + 1) * D], out_w.at[:, i * D : (i + 1) * D])
        for i in range(4)
    ]
    late = [copies.start(tables_hbm, tables), copies.start(qkv_hbm.at[0], own_qkv)]
    seg_copy.wait()
    fill_mask(seg, mask)
    x_copy.wait()
    hat[...], _ = normalized(x_ref[...].astype(f32))
    wait_all(*prefix_copies)
    prefix_states(embed, up_w, up_b, out_w, out_b, parts, hidden, low, wide, up_high, up_rest)
    wait_all(*late)


def opening_call(*arrays):
    scratch = [
        ((1, SEQ), jnp.int32),
        ((PREFIX, D), f32),
        ((D, D), f32),
        ((1, D), f32),
        ((D, 4 * D), f32),
        ((1, 4 * D), f32),
    ]
    return call_kernel(
        opening_kernel, "opening", in_hbm(*arrays), vmem(OPENING_SHAPES), scratch, 12, EARLY_MIB,
        2 * 6 * PAD * D * 5 * D,
    )


HEAD_SHAPES = (
    ((D, SEQ), bf16),
    ((D, SEQ), bf16),
    ((SEQ, D), bf16),
    ((PAIRS, P_ROWS, 2 * BLK), bf16),
    ((PAIRS, 2 * PAD, SEQ), bf16),
    ((HEADS, SEQ), f32),
    ((D, SEQ), bf16),
)
FIRST_SHAPES = HEAD_SHAPES + (
    ((SEQ, D), bf16),
    ((2, 1, SMALL), f32),
    ((2, D, 3 * D), bf16),
    ((2, D, D), bf16),
    ((2, D, FF), bf16),
    ((2, FF, D), bf16),
    ((SEQ, D), bf16),
)


def first_kernel(own_small, other_small, own_qkv, other_qkv, hat_ref, mask, low, tables,
                 attn_hbm, ff_in_hbm, ff_out_hbm, cot_hbm,
                 q_t, k_t, v_m, p_ref, pp_ref, inv_ref, mixed_ref, two_ref, small, w_qkv, w_attn, w_in,
                 w_out, cot_ref, k_m, v_t, sems):
    section = lax.axis_index("pipe")
    copies = Copies(sems)
    now = [
        copies.start(own_small, small.at[section]),
        copies.start(other_small, small.at[1 - section]),
        copies.start(own_qkv, w_qkv.at[section]),
        copies.start(other_qkv.at[0], w_qkv.at[1 - section]),
    ]
    later = [
        copies.start(ff_in_hbm.at[0], w_in.at[section]),
        copies.start(attn_hbm.at[0], w_attn.at[section]),
        copies.start(ff_out_hbm.at[0], w_out.at[section]),
        copies.start(cot_hbm.at[section, 0], cot_ref),
    ]
    wait_all(*now)
    hat = hat_ref[...]
    zero = small.at[0]
    normed = (hat * small_row(zero, G1) + small_row(zero, B1)).astype(bf16)
    two_ref[...] = (hat * small_row(zero, G2) + small_row(zero, B2)).astype(bf16)
    project_heads(normed, w_qkv.at[0], zero, tables[:8, :], tables[8:, :], q_t, k_t, k_m, v_m, v_t)
    attend(q_t, k_m, v_t, low.at[0], low.at[1], mask, p_ref, pp_ref, inv_ref, mixed_ref)
    wait_all(*later)


def first_call(ready, *arrays):
    return call_kernel(
        first_kernel, "first_attention", in_vmem(*ready) + in_hbm(*arrays), vmem(FIRST_SHAPES),
        [((SEQ, D), bf16), ((D, SEQ), bf16)], 8, EARLY_MIB, 200 * SEQ * D * 3 * D,
    )


def feed_kernel(two, small, other_in, w_in_before, act_ref, slope_ref, w_in, sems):
    wait_all(Copies(sems).start(other_in.at[0], w_in.at[1 - lax.axis_index("pipe")]))
    feed_in(two[...], w_in.at[0], small.at[0], act_ref, slope_ref, NO_COPIES)


def feed_call(*arrays):
    shapes = [((SEQ, FF), bf16), ((SEQ, FF), bf16), ((2, D, FF), bf16)]
    return call_kernel(
        feed_kernel, "first_feed", in_vmem(*arrays), vmem(shapes), [], 1, LATE_MIB, 2 * SEQ * D * FF,
        {3: 2},
    )


WEIGHT_SHAPES = (((D, 3 * D), bf16), ((D, D), bf16), ((D, FF), bf16), ((FF, D), bf16))


MIDDLE_OUTS = (
    ((SEQ, D), bf16),
    ((SEQ, FF), bf16),
    ((D, SEQ), bf16),
    ((SEQ, D), f32),
    ((SEQ, D), bf16),
    ((D, SEQ), bf16),
    ((HEADS, SEQ), f32),
    ((PAIRS, 2 * PAD, SEQ), bf16),
    ((4 * PREFIX, D), f32),
    ((2, D, D), bf16),
    ((2, FF, D), bf16),
)


def middle_kernel(w_attn_before, w_out_before, q0, pp0, inv0, mixed0, small, w_qkv, w_in,
                  other_attn, other_out, cot_ref, x_ref, act_zero, low, mask, tables,
                  h_one, act_one, mixed_one, grad_one, grad_low, scaled_zero, inner_zero, pre_ds_zero,
                  prefix_grad, w_attn, w_out,
                  q_t, k_t, v_m, p_ref, pp_ref, inv_ref, scaled, inner, pre_ds, slope_one, k_m, v_t,
                  dq, dk, dv, packed, sems):
    section = lax.axis_index("pipe")
    copies = Copies(sems)
    wait_all(
        copies.start(other_attn.at[0], w_attn.at[1 - section]),
        copies.start(other_out.at[0], w_out.at[1 - section]),
    )
    small_one = small.at[1]
    h_one[...] = layer_result(
        x_ref[...].astype(f32), mixed0[...], w_attn[0], act_zero, w_out[0], small.at[0]
    ).astype(bf16)

    cos, sin = tables[:8, :], tables[8:, :]
    hat, _ = normalized(h_one[...].astype(f32))
    normed = (hat * small_row(small_one, G1) + small_row(small_one, B1)).astype(bf16)
    two = (hat * small_row(small_one, G2) + small_row(small_one, B2)).astype(bf16)
    project_heads(normed, w_qkv.at[1], small_one, cos, sin, q_t, k_t, k_m, v_m, v_t)
    attend(q_t, k_m, v_t, low.at[2], low.at[3], mask, p_ref, pp_ref, inv_ref, mixed_one)
    feed_in(two, w_in.at[1], small_one, act_one, slope_one, NO_COPIES)

    grad = cot_ref[...]
    grad_two = feed_back(grad, w_out.at[1], w_in.at[1], slope_one, NO_COPIES)
    dq[...] = dot(w_attn[1], grad, NT)
    prefix_back(dq, q_t, low.at[3], pp_ref, inv_ref, mixed_one, scaled, inner, pre_ds, prefix_grad, 2 * PREFIX)
    attend_back(scaled, inner, pre_ds, q_t, k_t, v_m, low.at[2], p_ref, dq, dk, dv)
    pack_grads(dq, dk, dv, cos, sin, packed)
    result = norms_back(grad, h_one[...].astype(f32), grad_two, packed[...], w_qkv[1], small_one)
    grad_one[...] = result
    grad_low[...] = result.astype(bf16)

    dq[...] = dot(w_attn[0], grad_low[...], NT)
    prefix_back(dq, q0, low.at[1], pp0, inv0, mixed0, scaled_zero, inner_zero, pre_ds_zero, prefix_grad, 0)


def middle_call(*arrays):
    scratch = HEAD_SHAPES[:6] + (
        ((D, SEQ), bf16),
        ((HEADS, SEQ), f32),
        ((PAIRS, 2 * PAD, SEQ), bf16),
        ((SEQ, FF), bf16),
        ((SEQ, D), bf16),
        ((D, SEQ), bf16),
        ((D, SEQ), f32),
        ((D, SEQ), f32),
        ((D, SEQ), f32),
        ((3 * D, SEQ), bf16),
    )
    return call_kernel(
        middle_kernel, "middle", in_vmem(*arrays), vmem(MIDDLE_OUTS), scratch, 2, MIDDLE_MIB,
        20 * SEQ * D * 6 * D, {0: 9, 1: 10},
    )


def hand_over(values, keep, send, sems):
    here = lax.axis_index("pipe") == 0
    copies = Copies(sems)
    wait_all(
        copies.of_layer(here, values[0], values[1], keep),
        copies.of_layer(here, values[1], values[0], send),
    )


def result_kernel(h_one, act, mixed, small, w_attn, w_out, keep, send, result, sems):
    result[...] = layer_result(
        h_one[...].astype(f32), mixed[...], w_attn[1], act, w_out[1], small.at[1]
    ).astype(bf16)
    hand_over((h_one, result), keep, send, sems)


def result_call(*arrays):
    return call_kernel(
        result_kernel, "layer_one_out", in_vmem(*arrays), vmem([((SEQ, D), bf16)] * 2),
        [((SEQ, D), bf16)], 2, LATE_MIB, 2 * SEQ * D * (D + FF),
    )


def heads_back_kernel(scaled, inner, pre_ds, q_t, k_t, v_m, low, p_ref, tables, packed, dq, dk, dv):
    attend_back(scaled, inner, pre_ds, q_t, k_t, v_m, low.at[0], p_ref, dq, dk, dv)
    pack_grads(dq, dk, dv, tables[:8, :], tables[8:, :], packed)


def heads_back_call(*arrays):
    return call_kernel(
        heads_back_kernel, "layer_zero_attention_back", in_vmem(*arrays), vmem([((3 * D, SEQ), bf16)]),
        [((D, SEQ), f32)] * 3, 0, LATE_MIB, 10 * SEQ * SEQ * D,
    )[0]


def feed_back_kernel(grad, slope, w_in, w_out, total):
    total[...] = feed_back(grad[...], w_out.at[0], w_in.at[0], slope, NO_COPIES)


def feed_back_call(*arrays):
    (total,) = call_kernel(
        feed_back_kernel, "layer_zero_feed_back", in_vmem(*arrays), vmem([((SEQ, D), f32)]), [], 0,
        LATE_MIB, 4 * SEQ * D * FF,
    )
    return total


def norms_kernel(x_ref, grad, two, packed, grad_one, small, w_qkv, keep, send, result, sems):
    result[...] = norms_back(
        grad[...], x_ref[...].astype(f32), two[...], packed[...], w_qkv[0], small.at[0]
    )
    hand_over((result, grad_one), keep, send, sems)


def norms_call(*arrays):
    return call_kernel(
        norms_kernel, "layer_zero_norms", in_vmem(*arrays), vmem([((SEQ, D), f32)] * 2),
        [((SEQ, D), f32)], 2, LATE_MIB, 6 * SEQ * D * D,
    )


def place_kernel(act, grad, act_out, grad_out, sems):
    section = lax.axis_index("pipe")
    copies = Copies(sems)
    wait_all(
        copies.start(grad, grad_out.at[0, section, 0]), copies.start(act, act_out.at[0, section, 0])
    )


def place_call(act, grad):
    wholes = [(pltpu.HBM, (1, 2, 1, SEQ, D), bf16), (pltpu.HBM, (1, 2, 1, SEQ, D), f32)]
    return call_kernel(
        place_kernel, "place_own", in_vmem(act, grad), wholes, [], 2, LATE_MIB, 2 * SEQ * D
    )


def final_kernel(col_width, grads_ref, hidden, embed, wide, up_high, up_rest, act_other, grad_other,
                 act_in, grad_in, *refs):
    results, (act_out, grad_out, d_embed, d_up, d_up_b, d_out, d_out_b, sems) = refs[:5], refs[5:]
    section = lax.axis_index("pipe")
    shard = lax.axis_index("dp")
    copies = Copies(sems)
    placed = [
        copies.start(grad_other, grad_out.at[0, 1 - section, 0]),
        copies.start(act_other, act_out.at[0, 1 - section, 0]),
    ]
    units = hidden[...]
    both = jnp.zeros((2 * PAD, D), f32)
    for part in range(4):
        high, rest = halves(padded(grads_ref[part * PREFIX : (part + 1) * PREFIX, :]))
        both = both + dot(
            jnp.concatenate([high, rest], axis=0), wide[part * D : (part + 1) * D, :], NN
        )
    grad_units = (both[:PAD] + both[PAD:])[:PREFIX]
    grad_pre = grad_units * (1.0 - units * units)
    d_up_b[...] = jnp.sum(grad_pre, axis=0, keepdims=True)
    d_up[...] = stacked_dot(embed[...], grad_pre)
    placed += [copies.start(d_up, results[1]), copies.start(d_up_b, results[2])]
    column = section * (2 * D) + shard * col_width
    own_cols = jnp.zeros((PREFIX, col_width), f32)
    for part in range(4):
        for piece in range(D // col_width):
            here = column == part * D + piece * col_width
            cols = slice(piece * col_width, (piece + 1) * col_width)
            rows = slice(part * PREFIX, (part + 1) * PREFIX)
            own_cols = jnp.where(here, grads_ref[rows, cols], own_cols)
    d_out[...] = stacked_dot(units, own_cols)
    d_out_b[...] = jnp.sum(own_cols, axis=0, keepdims=True)
    placed += [copies.start(d_out, results[3]), copies.start(d_out_b, results[4])]
    high, rest = halves(padded(grad_pre))
    both = dot(jnp.concatenate([high, rest], axis=0), up_high[...], NN)
    both = both[:PAD] + both[PAD:] + dot(high, up_rest[...], NN)
    d_embed[...] = both[:PREFIX]
    placed.append(copies.start(d_embed, results[0]))
    wait_all(*placed)


def final_call(col_width, wholes, *arrays):
    def body(*refs):
        final_kernel(col_width, *refs)

    shapes = [((PREFIX, D), f32), ((D, D), f32), ((1, D), f32), ((D, col_width), f32), ((1, col_width), f32)]
    whole_shapes = [((1, 2, 1, SEQ, D), bf16), ((1, 2, 1, SEQ, D), f32)]
    return call_kernel(
        body, "reparam", in_vmem(*arrays) + in_hbm(*wholes),
        [(pltpu.HBM, *pair) for pair in shapes + whole_shapes], shapes, 7, LATE_MIB, SEQ * D * D,
        {8: 5, 9: 6},
    )


def swapped(array_in):
    return lax.ppermute(array_in, "pipe", [(0, 1), (1, 0)])


def hops(axis):
    size = lax.axis_size(axis)
    steps = []
    step = 1
    while step < size:
        steps.append((axis, [(i, i ^ step) for i in range(size)]))
        step *= 2
    assert step == size
    return steps


def local(
    block_input,
    cotangent,
    segments,
    ln1_gain,
    ln1_shift,
    qkv_weight,
    qkv_bias,
    attn_weight,
    attn_bias,
    ln2_gain,
    ln2_shift,
    ff_in_weight,
    ff_in_bias,
    ff_out_weight,
    ff_out_bias,
    prefix_embed,
    up_weight,
    up_bias,
    out_weight,
    out_bias,
):
    other_qkv = swapped(qkv_weight)
    small = small_call(
        ln1_gain, ln1_shift, ln2_gain, ln2_shift, attn_bias, ff_out_bias, qkv_bias, ff_in_bias
    )
    other_small = swapped(small)
    small, prefix_embed = lax.optimization_barrier((small, prefix_embed))
    tables = jnp.asarray(rope_tables())
    _, *later = lax.optimization_barrier((small, attn_weight, ff_in_weight, ff_out_weight))
    other_attn, other_in, other_out = (swapped(weight) for weight in later)
    x_zero, hat_zero, mask, low, hidden_units, wide, up_high, up_rest, tables, own_qkv = opening_call(
        block_input, segments, prefix_embed, up_weight, up_bias, out_weight, out_bias, tables, qkv_weight
    )
    q0, k0, v0, p0, pp0, inv0, mixed0, two_zero, small, w_qkv, w_attn, w_in, w_out, cot = first_call(
        (small, other_small, own_qkv, other_qkv, hat_zero, mask, low, tables),
        attn_weight, ff_in_weight, ff_out_weight, cotangent,
    )
    act_zero, slope_zero, w_in = feed_call(two_zero, small, other_in, w_in)
    (h_one, act_one, mixed_one, grad_one, grad_low, scaled_zero, inner_zero, pre_ds_zero, prefix_grad,
     w_attn, w_out) = middle_call(
        w_attn, w_out, q0, pp0, inv0, mixed0, small, w_qkv, w_in, other_attn, other_out, cot, x_zero,
        act_zero, low, mask, tables,
    )

    def layer_one_out(state):
        own, send = result_call(state["h_one"], act_one, mixed_one, small, w_attn, w_out)
        return dict(state, act_own=own, act_send=send)

    def layer_zero_attention(state):
        packed = heads_back_call(
            state["scaled"], inner_zero, pre_ds_zero, q0, k0, v0, low, p0, tables
        )
        return dict(state, packed=packed, act_other=swapped(state["act_send"]))

    def layer_zero_feed(state):
        return dict(state, two=feed_back_call(state["grad_low"], slope_zero, w_in, w_out))

    def layer_zero_norms(state):
        own, send = norms_call(x_zero, grad_low, state["two"], state["packed"], grad_one, small, w_qkv)
        return dict(state, grad_own=own, grad_send=send)

    def swap_grads(state):
        wholes = place_call(state["act_own"], state["grad_own"])
        return dict(state, grad_other=swapped(state["grad_send"]), wholes=wholes)

    works = [layer_one_out, layer_zero_attention, layer_zero_feed, layer_zero_norms, swap_grads]
    state = {"h_one": h_one, "grad_low": grad_low, "scaled": scaled_zero}
    for axis, pairs in hops("pipe") + hops("dp") + hops("grp"):
        if axis == "pipe":
            moved = lax.ppermute(prefix_grad, axis, pairs)
        else:
            prefix_grad = lax.reduce_precision(prefix_grad, 8, 7)
            moved = lax.ppermute(prefix_grad.astype(bf16), axis, pairs)
        if works:
            state = works.pop(0)(state)
        prefix_grad, moved, state = lax.optimization_barrier((prefix_grad, moved, state))
        prefix_grad = prefix_grad + moved.astype(f32)
    for work in works:
        state = work(state)
    col_width = 2 * D // lax.axis_size("dp")
    grad_embed, grad_up, grad_up_b, grad_out, grad_out_b, activations, input_grads = final_call(
        col_width, state["wholes"], prefix_grad, hidden_units, prefix_embed, wide, up_high, up_rest,
        state["act_other"], state["grad_other"],
    )
    return (
        activations,
        input_grads,
        grad_embed,
        grad_up,
        grad_up_b[0],
        grad_out,
        grad_out_b[0],
    )


def solution(mesh):
    return jax.shard_map(
        local,
        mesh=mesh,
        in_specs=(
            P(None, ("grp", "dp"), None, None),
            P(None, ("grp", "dp"), None, None),
            P(None, ("grp", "dp"), None),
            P("pipe", None),
            P("pipe", None),
            P("pipe", None, None),
            P("pipe", None),
            P("pipe", None, None),
            P("pipe", None),
            P("pipe", None),
            P("pipe", None),
            P("pipe", None, None),
            P("pipe", None),
            P("pipe", None, None),
            P("pipe", None),
            P(),
            P(),
            P(),
            P(),
            P(),
        ),
        out_specs=(
            P("pipe", None, ("grp", "dp"), None, None),
            P("pipe", None, ("grp", "dp"), None, None),
            P(),
            P(),
            P(),
            P(None, ("pipe", "dp")),
            P(("pipe", "dp")),
        ),
        check_vma=False,
    )
```

```python
import math

import jax
import jax.numpy as jnp
import numpy as np
from jax import lax
from jax.experimental import pallas as pl
from jax.experimental.pallas import tpu as pltpu
from jax.sharding import PartitionSpec as P

D = 512
SEQ = 512
HEADS = 8
HD = 64
FF = 2048
ROT = 16
PREFIX = 10
PAD = 16
BLK = 128
BLOCKS = SEQ // BLK
PAIRS = HEADS // 2
LIVE = (1, 2, 3, 3)
P_ROWS = BLK * sum(LIVE)
P_START = (0, 128, 384, 768)

f32 = jnp.float32
bf16 = jnp.bfloat16
LOG2E = math.log2(math.e)
Q_SCALE = LOG2E * HD**-0.5
K_BACK = 1.0 / LOG2E
Q_BACK = HD**-0.5
NEG = -1e30

NN = (((1,), (0,)), ((), ()))
NT = (((1,), (1,)), ((), ()))
TN = (((0,), (0,)), ((), ()))

NO_COPIES = ((),) * 4
MIB = 1024 * 1024
EARLY_MIB = 24
MIDDLE_MIB = 22
LATE_MIB = 12

G1, B1, G2, B2, B_ATTN, B_OUT, B_QKV, B_IN = 0, 1, 2, 3, 4, 5, 6, 9
SMALL = 13 * D


def dot(left, right, dims):
    return lax.dot_general(left, right, dims, preferred_element_type=f32)


def call_kernel(kernel, name, ins, outs, scratch, sems, mib, cost, aliases=None):
    operands = [pltpu.with_memory_space_constraint(array, space) for array, space in ins]
    return pl.pallas_call(
        kernel,
        name=name,
        out_shape=[space(shape, dtype) for space, shape, dtype in outs],
        in_specs=[pl.BlockSpec(memory_space=space) for _, space in ins],
        out_specs=[pl.BlockSpec(memory_space=space) for space, _, _ in outs],
        scratch_shapes=[pltpu.VMEM(*pair) for pair in scratch]
        + ([pltpu.SemaphoreType.DMA((sems,))] if sems else []),
        input_output_aliases=aliases or {},
        compiler_params=pltpu.CompilerParams(vmem_limit_bytes=mib * MIB),
        cost_estimate=pl.CostEstimate(flops=cost, bytes_accessed=8 * MIB, transcendentals=0),
    )(*operands)


def in_hbm(*arrays):
    return [(array, pltpu.HBM) for array in arrays]


def anywhere(*arrays):
    return [(array, pl.ANY) for array in arrays]


def in_vmem(*arrays):
    return [(array, pltpu.VMEM) for array in arrays]


def vmem(shapes):
    return [(pltpu.VMEM, *pair) for pair in shapes]


def small_row(small_ref, place):
    return small_ref[:, place * D : (place + 1) * D]


def rope_tables():
    inv_freq = 10000.0 ** (-2.0 * np.arange(ROT // 2) / ROT)
    angles = inv_freq[:, None] * np.arange(SEQ)[None, :]
    return np.concatenate([np.cos(angles), np.sin(angles)], axis=0).astype(np.float32)


class Copies:
    def __init__(self, sems):
        self.sems = sems
        self.count = 0

    def start(self, src, dst):
        copy = pltpu.make_async_copy(src, dst, self.sems.at[self.count])
        self.count += 1
        copy.start()
        return copy

    def of_layer(self, here, own, other, dst):
        sem = self.sems.at[self.count]
        self.count += 1
        copy = pltpu.make_async_copy(own, dst, sem)

        @pl.when(here)
        def _():
            copy.start()

        @pl.when(jnp.logical_not(here))
        def _():
            pltpu.make_async_copy(other, dst, sem).start()

        return copy


def wait_all(*copies):
    for copy in copies:
        copy.wait()


def normalized(hidden):
    mean = jnp.mean(hidden, axis=-1, keepdims=True)
    centered = hidden - mean
    variance = jnp.mean(centered * centered, axis=-1, keepdims=True)
    scale = lax.rsqrt(variance + 1e-05)
    return centered * scale, scale


def rope_heads(rows, cos, sin):
    parts = []
    for head in range(rows.shape[0] // HD):
        base = head * HD
        lead = rows[base : base + 8]
        tail = rows[base + 8 : base + 16]
        parts += [lead * cos - tail * sin, tail * cos + lead * sin, rows[base + 16 : base + HD]]
    return jnp.concatenate(parts, axis=0)


def fill_mask(seg_ref, mask_ref):
    seg_row = seg_ref[...].astype(f32)
    seg_col = jnp.transpose(jnp.broadcast_to(seg_row, (8, SEQ)))[:, 0:1]
    for block in range(BLOCKS):
        for key_block in range(block + 1 - LIVE[block], block + 1):
            seen = seg_col[key_block * BLK : (key_block + 1) * BLK] == (
                seg_row[:, block * BLK : (block + 1) * BLK]
            )
            if key_block == block:
                key_pos = lax.broadcasted_iota(jnp.int32, (BLK, BLK), 0)
                query_pos = lax.broadcasted_iota(jnp.int32, (BLK, BLK), 1)
                seen = seen & (key_pos <= query_pos)
            start = P_START[block] + (key_block - (block + 1 - LIVE[block])) * BLK
            mask_ref[start : start + BLK, :] = jnp.where(seen, 0.0, NEG)


def project_heads(normed, w_ref, small_ref, cos, sin, q_t, k_t, k_m, v_m, v_t):
    bias = small_row(small_ref, B_QKV)
    rows = dot(normed, w_ref[:, :D], NN) + bias
    q_t[...] = (rope_heads(jnp.transpose(rows), cos, sin) * Q_SCALE).astype(bf16)
    bias = small_row(small_ref, B_QKV + 1)
    rows = dot(normed, w_ref[:, D : 2 * D], NN) + bias
    keys = rope_heads(jnp.transpose(rows), cos, sin).astype(bf16)
    k_t[...] = keys
    k_m[...] = jnp.transpose(keys)
    bias = small_row(small_ref, B_QKV + 2)
    values = (dot(normed, w_ref[:, 2 * D :], NN) + bias).astype(bf16)
    v_m[...] = values
    v_t[...] = jnp.transpose(values)


def block_diagonal(pair_rows):
    zeros = jnp.zeros((HD, BLK), pair_rows.dtype)
    return jnp.concatenate(
        [
            jnp.concatenate([pair_rows[:HD], zeros], axis=1),
            jnp.concatenate([zeros, pair_rows[HD:]], axis=1),
        ],
        axis=0,
    )


def from_diagonal(both):
    return jnp.concatenate([both[:HD, :BLK], both[HD:, BLK:]], axis=0)


def per_head(row, rows=HD):
    return jnp.concatenate(
        [
            jnp.broadcast_to(row[:, :BLK], (rows, BLK)),
            jnp.broadcast_to(row[:, BLK:], (rows, BLK)),
        ],
        axis=0,
    )


def geometry(block):
    live = LIVE[block] * BLK
    end = (block + 1) * BLK
    start = P_START[block]
    return slice(end - live, end), slice(block * BLK, end), slice(start, start + live)


def pair_rows(pair):
    return slice(pair * BLK, (pair + 1) * BLK)


def both_heads(rows, tokens):
    return jnp.concatenate([rows[:PAD, tokens], rows[PAD:, tokens]], axis=1)


def attend(q_t, k_m, v_t, pre_k, pre_v, mask_ref, p_ref, pp_ref, inv_ref, mixed_ref):
    real = lax.rem(lax.broadcasted_iota(jnp.int32, (2 * PAD, 1), 0), PAD) < PREFIX
    pad_mask = jnp.where(real, 0.0, NEG)

    def score(feats, block):
        keys, tokens, rows = geometry(block)
        queries = block_diagonal(q_t[feats, tokens])
        mask = mask_ref[rows, :]
        return dot(k_m[keys, feats], queries, NN) + jnp.concatenate([mask, mask], axis=1)

    def soften(pair, block, scores, pre_scores):
        _, tokens, rows = geometry(block)
        pre_scores = both_heads(pre_scores, tokens)
        peak = jnp.maximum(
            jnp.max(scores, axis=0, keepdims=True), jnp.max(pre_scores, axis=0, keepdims=True)
        )
        expo = jnp.exp2(scores - peak).astype(bf16)
        pre_expo = jnp.exp2(pre_scores - peak)
        p_ref[pair, rows, :] = expo
        pp_ref[pair, :PAD, tokens] = pre_expo[:, :BLK].astype(bf16)
        pp_ref[pair, PAD:, tokens] = pre_expo[:, BLK:].astype(bf16)
        return expo, jnp.sum(pre_expo, axis=0, keepdims=True)

    def mix(pair, block, pre_mixed, expo, pre_total):
        feats = pair_rows(pair)
        keys, tokens, _ = geometry(block)
        ones = jnp.ones((PAD, expo.shape[0]), bf16)
        mixed = dot(jnp.concatenate([v_t[feats, keys], ones], axis=0), expo, NN)
        inverse = 1.0 / (mixed[BLK : BLK + 1] + pre_total)
        inv_ref[2 * pair : 2 * pair + 1, tokens] = inverse[:, :BLK]
        inv_ref[2 * pair + 1 : 2 * pair + 2, tokens] = inverse[:, BLK:]
        mixed = from_diagonal(mixed[:BLK]) + pre_mixed[:, tokens]
        mixed_ref[feats, tokens] = (mixed * per_head(inverse)).astype(bf16)

    def score_all(pair):
        feats = pair_rows(pair)
        pre_scores = dot(pre_k[:, feats], q_t[feats, :], NN) + pad_mask
        return pre_scores, [score(feats, block) for block in range(BLOCKS)]

    def mix_all(pair, soft):
        pre_mixed = dot(pre_v[:, pair_rows(pair)], pp_ref[pair], TN)
        for block in range(BLOCKS):
            mix(pair, block, pre_mixed, *soft[block])

    ahead, behind = score_all(0), None
    for pair in range(PAIRS):
        pre_scores, scores = ahead
        if pair + 1 < PAIRS:
            ahead = score_all(pair + 1)
        soft = [soften(pair, block, scores[block], pre_scores) for block in range(BLOCKS)]
        if behind is not None:
            mix_all(*behind)
        behind = (pair, soft)
    mix_all(*behind)


def prefix_back(w_attn, grad, q_t, pre_v, pp_ref, inv_ref, mixed_ref, scaled_ref, inner_ref, pre_ds_ref, turned,
                pre_grad, pre_row):
    turned[...] = jnp.transpose(grad)

    def scale(pair):
        grad_mixed = dot(w_attn[pair_rows(pair), :], turned[...], NN)
        inner = []
        for place in range(2):
            head = 2 * pair + place
            rows = slice(head * HD, (head + 1) * HD)
            scaled = grad_mixed[place * HD : (place + 1) * HD] * inv_ref[head : head + 1, :]
            scaled = scaled.astype(bf16)
            scaled_ref[rows, :] = scaled
            products = scaled.astype(f32) * mixed_ref[rows, :].astype(f32)
            inner.append(jnp.sum(products, axis=0, keepdims=True))
            inner_ref[head : head + 1, :] = inner[-1]
        return jnp.concatenate([jnp.broadcast_to(row, (PAD, SEQ)) for row in inner], axis=0)

    pairs = range(PAIRS)
    inner = [scale(pair) for pair in pairs]
    grad_probs = [dot(pre_v[:, pair_rows(pair)], scaled_ref[pair_rows(pair), :], NN) for pair in pairs]
    for pair in pairs:
        probs = pp_ref[pair].astype(f32)
        pre_ds_ref[pair] = (probs * (grad_probs[pair] - inner[pair])).astype(bf16)
    keys = [dot(q_t[pair_rows(pair), :], pre_ds_ref[pair], NT) for pair in pairs]
    values = [dot(scaled_ref[pair_rows(pair), :], pp_ref[pair], NT) for pair in pairs]
    first_head = lax.rem(lax.broadcasted_iota(jnp.int32, (1, D), 1), BLK) < HD

    def own_head(parts):
        both = jnp.transpose(jnp.concatenate(parts, axis=0))
        return jnp.where(first_head, both[:PREFIX], both[PAD : PAD + PREFIX])

    pre_grad[pre_row : pre_row + PREFIX, :] = own_head(keys) * K_BACK
    pre_grad[pre_row + PREFIX : pre_row + 2 * PREFIX, :] = own_head(values)


def attend_back(scaled_ref, inner_ref, pre_ds_ref, q_t, k_t, v_m, pre_k, p_ref, dq_ref, dk_ref, dv_ref):
    def value_grads(feats, block):
        keys, tokens, _ = geometry(block)
        grads = block_diagonal(scaled_ref[feats, tokens])
        return grads, dot(v_m[keys, feats], grads, NN)

    def score_grads(pair, block, grad_probs):
        _, tokens, rows = geometry(block)
        inner = jnp.concatenate(
            [inner_ref[2 * pair : 2 * pair + 1, tokens], inner_ref[2 * pair + 1 : 2 * pair + 2, tokens]],
            axis=1,
        )
        return (p_ref[pair, rows, :].astype(f32) * (grad_probs - inner)).astype(bf16)

    def out_grads(pair, feats, block, pre_dq, grads, grad_scores):
        keys, tokens, rows = geometry(block)
        queries = block_diagonal(q_t[feats, tokens])
        dq_ref[feats, tokens] = (
            from_diagonal(dot(k_t[feats, keys], grad_scores, NN)) + pre_dq[:, tokens]
        )
        return dot(queries, grad_scores, NT), dot(grads, p_ref[pair, rows, :], NT)

    def by_keys(outs, which, key_block):
        total = None
        for block in range(BLOCKS):
            place = key_block - (block + 1 - LIVE[block])
            if 0 <= place < LIVE[block]:
                part = outs[block][which][:, place * BLK : (place + 1) * BLK]
                total = part if total is None else total + part
        return total

    for pair in range(PAIRS):
        feats = pair_rows(pair)
        first = [value_grads(feats, block) for block in range(BLOCKS)]
        second = [score_grads(pair, block, first[block][1]) for block in range(BLOCKS)]
        pre_dq = dot(pre_k[:, feats], pre_ds_ref[pair], TN)
        outs = [
            out_grads(pair, feats, block, pre_dq, first[block][0], second[block])
            for block in range(BLOCKS)
        ]
        for key_block in range(BLOCKS):
            keys = slice(key_block * BLK, (key_block + 1) * BLK)
            dk_ref[feats, keys] = by_keys(outs, 0, key_block)
            dv_ref[feats, keys] = by_keys(outs, 1, key_block)


def pack_grads(dq_ref, dk_ref, dv_ref, cos, sin, packed_t):
    packed_t[:D, :] = (rope_heads(dq_ref[...], cos, -sin) * Q_BACK).astype(bf16)
    packed_t[D : 2 * D, :] = (rope_heads(dk_ref[...], cos, -sin) * K_BACK).astype(bf16)
    packed_t[2 * D :, :] = dv_ref[...].astype(bf16)


def gelu_both(before):
    cdf = 0.5 + 0.5 * lax.erf(before * (0.5**0.5))
    density = jnp.exp2(before * before * (-0.5 * LOG2E)) * (1.0 / math.sqrt(2.0 * math.pi))
    return before * cdf, cdf + before * density


FF_CHUNK = 512


def chunk_of(index):
    return slice(index * FF_CHUNK, (index + 1) * FF_CHUNK)


def feed_in(normed, w_ref, small_ref, act_ref, slope_ref, arrivals):
    for chunk in range(FF // FF_CHUNK):
        cols = chunk_of(chunk)
        wait_all(*arrivals[chunk])
        before = dot(normed, w_ref[:, cols], NN) + small_row(small_ref, B_IN + chunk)
        act, slope = gelu_both(before)
        act_ref[:, cols] = act.astype(bf16)
        slope_ref[:, cols] = slope.astype(bf16)


def layer_result(hidden, mixed_t, w_attn, act_ref, w_out, small_ref):
    attn_out = dot(jnp.transpose(mixed_t), w_attn, NN) + small_row(small_ref, B_ATTN)
    ff_out = dot(act_ref[...], w_out, NN) + small_row(small_ref, B_OUT)
    return hidden + attn_out + ff_out


def feed_back(grad, w_out, w_in, slope_ref, arrivals):
    total = jnp.zeros((SEQ, D), f32)
    for chunk in range(FF // FF_CHUNK):
        cols = chunk_of(chunk)
        wait_all(*arrivals[chunk])
        grad_act = dot(grad, w_out[cols, :], NT)
        grad_before = (grad_act * slope_ref[:, cols].astype(f32)).astype(bf16)
        total = total + dot(grad_before, w_in[:, cols], NT)
    return total


def norms_back(grad, hidden, grad_two, packed_t, w_qkv, small_ref):
    grad_one = jnp.transpose(dot(w_qkv, packed_t, NN))
    grad_hat = (
        grad_one * small_row(small_ref, G1) + grad_two * small_row(small_ref, G2)
    )
    hat, scale = normalized(hidden)
    mean_one = jnp.mean(grad_hat, axis=-1, keepdims=True)
    mean_two = jnp.mean(grad_hat * hat, axis=-1, keepdims=True)
    return grad.astype(f32) + scale * (grad_hat - mean_one - hat * mean_two)


def halves(values):
    high = values.astype(bf16)
    return high, (values - high.astype(f32)).astype(bf16)


def padded(values):
    return jnp.concatenate([values, jnp.zeros((PAD - PREFIX, values.shape[1]), f32)], axis=0)


def few_rows_dot(left, right):
    left_high, left_rest = halves(padded(left))
    right_high, right_rest = halves(right)
    both = dot(jnp.concatenate([left_high, left_rest], axis=0), right_high, NN)
    return both[:PAD] + both[PAD:] + dot(left_high, right_rest, NN)


def stacked_dot(left, right):
    left_high, left_rest = halves(padded(left))
    right_high, right_rest = halves(padded(right))
    return dot(
        jnp.concatenate([left_high, left_high, left_rest], axis=0),
        jnp.concatenate([right_high, right_rest, right_high], axis=0),
        TN,
    )


def small_kernel(gain_one, shift_one, gain_two, shift_two, attn_b, out_b, qkv_b, in_b, packed, sems):
    copies = Copies(sems)
    places = [(gain_one, 0), (shift_one, 1), (gain_two, 2), (shift_two, 3), (attn_b, 4), (out_b, 5)]
    places += [(qkv_b, 6), (in_b, 9)]
    wait_all(
        *[
            copies.start(row, packed.at[:, place * D : place * D + row.shape[1]])
            for row, place in places
        ]
    )


def small_call(*arrays):
    (packed,) = call_kernel(
        small_kernel, "small_parameters", in_hbm(*arrays), vmem([((1, SMALL), f32)]), [], 8, LATE_MIB, SMALL
    )
    return packed


def prefix_states(embed, up_w, up_b, out_w, out_b, arrivals, hidden, low, wide, up_high, up_rest):
    units = jnp.tanh(few_rows_dot(embed[...], up_w[...])[:PREFIX] + up_b[...])
    hidden[...] = units
    up_high[...], up_rest[...] = halves(jnp.transpose(up_w[...]))
    real = lax.broadcasted_iota(jnp.int32, (PAD, 1), 0) < PREFIX
    first_head = lax.rem(lax.broadcasted_iota(jnp.int32, (1, D), 1), BLK) < HD
    for part in range(4):
        cols = slice(part * D, (part + 1) * D)
        arrivals[part].wait()
        states = jnp.where(real, few_rows_dot(units, out_w[:, cols]) + out_b[:, cols], 0.0)
        low[part, :PAD, :] = jnp.where(first_head, states, 0.0).astype(bf16)
        low[part, PAD:, :] = jnp.where(first_head, 0.0, states).astype(bf16)
        wide[cols, :] = jnp.transpose(out_w[:, cols].astype(bf16))


OPENING_SHAPES = (
    ((SEQ, D), bf16),
    ((SEQ, D), f32),
    ((P_ROWS, BLK), f32),
    ((4, 2 * PAD, D), bf16),
    ((PREFIX, D), f32),
    ((4 * D, D), bf16),
    ((D, D), bf16),
    ((D, D), bf16),
    ((2 * 8, SEQ), f32),
    ((D, 3 * D), bf16),
)


def opening_kernel(x_hbm, seg_hbm, embed_hbm, up_hbm, up_b_hbm, out_hbm, out_b_hbm, tables_hbm, qkv_hbm,
                   x_ref, hat, mask, low, hidden, wide, up_high, up_rest, tables, own_qkv, seg, embed, up_w, up_b,
                   out_w, out_b, sems):
    section = lax.axis_index("pipe")
    copies = Copies(sems)
    x_copy = copies.start(x_hbm.at[section, 0], x_ref)
    seg_copy = copies.start(seg_hbm.at[section], seg)
    prefix_copies = [
        copies.start(src, dst)
        for src, dst in ((embed_hbm, embed), (up_hbm, up_w), (up_b_hbm, up_b.at[0]), (out_b_hbm, out_b.at[0]))
    ]
    parts = [
        copies.start(out_hbm.at[:, i * D : (i + 1) * D], out_w.at[:, i * D : (i + 1) * D])
        for i in range(4)
    ]
    late = [copies.start(tables_hbm, tables), copies.start(qkv_hbm.at[0], own_qkv)]
    seg_copy.wait()
    fill_mask(seg, mask)
    x_copy.wait()
    hat[...], _ = normalized(x_ref[...].astype(f32))
    wait_all(*prefix_copies)
    prefix_states(embed, up_w, up_b, out_w, out_b, parts, hidden, low, wide, up_high, up_rest)
    wait_all(*late)


def opening_call(*arrays):
    scratch = [
        ((1, SEQ), jnp.int32),
        ((PREFIX, D), f32),
        ((D, D), f32),
        ((1, D), f32),
        ((D, 4 * D), f32),
        ((1, 4 * D), f32),
    ]
    return call_kernel(
        opening_kernel, "opening", in_hbm(*arrays), vmem(OPENING_SHAPES), scratch, 12, EARLY_MIB,
        2 * 6 * PAD * D * 5 * D,
    )


HEAD_SHAPES = (
    ((D, SEQ), bf16),
    ((D, SEQ), bf16),
    ((SEQ, D), bf16),
    ((PAIRS, P_ROWS, 2 * BLK), bf16),
    ((PAIRS, 2 * PAD, SEQ), bf16),
    ((HEADS, SEQ), f32),
    ((D, SEQ), bf16),
)
FIRST_SHAPES = HEAD_SHAPES + (
    ((SEQ, D), bf16),
    ((2, 1, SMALL), f32),
    ((2, D, 3 * D), bf16),
    ((2, D, D), bf16),
    ((2, D, FF), bf16),
    ((2, FF, D), bf16),
    ((SEQ, D), bf16),
)


def first_kernel(own_small, other_small, own_qkv, other_qkv, hat_ref, mask, low, tables,
                 attn_hbm, ff_in_hbm, ff_out_hbm, cot_hbm,
                 q_t, k_t, v_m, p_ref, pp_ref, inv_ref, mixed_ref, two_ref, small, w_qkv, w_attn, w_in,
                 w_out, cot_ref, k_m, v_t, sems):
    section = lax.axis_index("pipe")
    copies = Copies(sems)
    now = [
        copies.start(own_small, small.at[section]),
        copies.start(other_small, small.at[1 - section]),
        copies.start(own_qkv, w_qkv.at[section]),
        copies.start(other_qkv.at[0], w_qkv.at[1 - section]),
    ]
    later = [
        copies.start(ff_in_hbm.at[0], w_in.at[section]),
        copies.start(attn_hbm.at[0], w_attn.at[section]),
        copies.start(ff_out_hbm.at[0], w_out.at[section]),
        copies.start(cot_hbm.at[section, 0], cot_ref),
    ]
    wait_all(*now)
    hat = hat_ref[...]
    zero = small.at[0]
    normed = (hat * small_row(zero, G1) + small_row(zero, B1)).astype(bf16)
    two_ref[...] = (hat * small_row(zero, G2) + small_row(zero, B2)).astype(bf16)
    project_heads(normed, w_qkv.at[0], zero, tables[:8, :], tables[8:, :], q_t, k_t, k_m, v_m, v_t)
    attend(q_t, k_m, v_t, low.at[0], low.at[1], mask, p_ref, pp_ref, inv_ref, mixed_ref)
    wait_all(*later)


def first_call(ready, *arrays):
    return call_kernel(
        first_kernel, "first_attention", in_vmem(*ready) + in_hbm(*arrays), vmem(FIRST_SHAPES),
        [((SEQ, D), bf16), ((D, SEQ), bf16)], 8, EARLY_MIB, 200 * SEQ * D * 3 * D,
    )


def feed_kernel(two, small, other_in, w_in_before, act_ref, slope_ref, w_in, sems):
    wait_all(Copies(sems).start(other_in.at[0], w_in.at[1 - lax.axis_index("pipe")]))
    feed_in(two[...], w_in.at[0], small.at[0], act_ref, slope_ref, NO_COPIES)


def feed_call(*arrays):
    shapes = [((SEQ, FF), bf16), ((SEQ, FF), bf16), ((2, D, FF), bf16)]
    return call_kernel(
        feed_kernel, "first_feed", in_vmem(*arrays), vmem(shapes), [], 1, LATE_MIB, 2 * SEQ * D * FF,
        {3: 2},
    )


WEIGHT_SHAPES = (((D, 3 * D), bf16), ((D, D), bf16), ((D, FF), bf16), ((FF, D), bf16))


MIDDLE_OUTS = (
    ((SEQ, D), bf16),
    ((SEQ, FF), bf16),
    ((D, SEQ), bf16),
    ((SEQ, D), f32),
    ((SEQ, D), bf16),
    ((D, SEQ), bf16),
    ((HEADS, SEQ), f32),
    ((PAIRS, 2 * PAD, SEQ), bf16),
    ((4 * PREFIX, D), f32),
    ((2, D, D), bf16),
    ((2, FF, D), bf16),
)


def middle_kernel(w_attn_before, w_out_before, q0, pp0, inv0, mixed0, small, w_qkv, w_in,
                  other_attn, other_out, cot_ref, x_ref, act_zero, low, mask, tables,
                  h_one, act_one, mixed_one, grad_one, grad_low, scaled_zero, inner_zero, pre_ds_zero,
                  prefix_grad, w_attn, w_out,
                  q_t, k_t, v_m, p_ref, pp_ref, inv_ref, scaled, inner, pre_ds, turned, slope_one, k_m, v_t,
                  dq, dk, dv, packed, sems):
    section = lax.axis_index("pipe")
    copies = Copies(sems)
    wait_all(
        copies.start(other_attn.at[0], w_attn.at[1 - section]),
        copies.start(other_out.at[0], w_out.at[1 - section]),
    )
    small_one = small.at[1]
    h_one[...] = layer_result(
        x_ref[...].astype(f32), mixed0[...], w_attn[0], act_zero, w_out[0], small.at[0]
    ).astype(bf16)

    cos, sin = tables[:8, :], tables[8:, :]
    hat, _ = normalized(h_one[...].astype(f32))
    normed = (hat * small_row(small_one, G1) + small_row(small_one, B1)).astype(bf16)
    two = (hat * small_row(small_one, G2) + small_row(small_one, B2)).astype(bf16)
    project_heads(normed, w_qkv.at[1], small_one, cos, sin, q_t, k_t, k_m, v_m, v_t)
    attend(q_t, k_m, v_t, low.at[2], low.at[3], mask, p_ref, pp_ref, inv_ref, mixed_one)
    feed_in(two, w_in.at[1], small_one, act_one, slope_one, NO_COPIES)

    grad = cot_ref[...]
    grad_two = feed_back(grad, w_out.at[1], w_in.at[1], slope_one, NO_COPIES)
    prefix_back(w_attn.at[1], grad, q_t, low.at[3], pp_ref, inv_ref, mixed_one, scaled, inner, pre_ds, turned,
                prefix_grad, 2 * PREFIX)
    attend_back(scaled, inner, pre_ds, q_t, k_t, v_m, low.at[2], p_ref, dq, dk, dv)
    pack_grads(dq, dk, dv, cos, sin, packed)
    result = norms_back(grad, h_one[...].astype(f32), grad_two, packed[...], w_qkv[1], small_one)
    grad_one[...] = result
    grad_low[...] = result.astype(bf16)

    prefix_back(w_attn.at[0], grad_low[...], q0, low.at[1], pp0, inv0, mixed0, scaled_zero, inner_zero,
                pre_ds_zero, turned, prefix_grad, 0)


def middle_call(*arrays):
    scratch = HEAD_SHAPES[:6] + (
        ((D, SEQ), bf16),
        ((HEADS, SEQ), f32),
        ((PAIRS, 2 * PAD, SEQ), bf16),
        ((D, SEQ), bf16),
        ((SEQ, FF), bf16),
        ((SEQ, D), bf16),
        ((D, SEQ), bf16),
        ((D, SEQ), f32),
        ((D, SEQ), f32),
        ((D, SEQ), f32),
        ((3 * D, SEQ), bf16),
    )
    return call_kernel(
        middle_kernel, "middle", in_vmem(*arrays), vmem(MIDDLE_OUTS), scratch, 2, MIDDLE_MIB,
        20 * SEQ * D * 6 * D, {0: 9, 1: 10},
    )


def hand_over(values, keep, send, sems):
    here = lax.axis_index("pipe") == 0
    copies = Copies(sems)
    wait_all(
        copies.of_layer(here, values[0], values[1], keep),
        copies.of_layer(here, values[1], values[0], send),
    )


def result_kernel(h_one, act, mixed, small, w_attn, w_out, keep, send, result, sems):
    result[...] = layer_result(
        h_one[...].astype(f32), mixed[...], w_attn[1], act, w_out[1], small.at[1]
    ).astype(bf16)
    hand_over((h_one, result), keep, send, sems)


def result_call(*arrays):
    return call_kernel(
        result_kernel, "layer_one_out", in_vmem(*arrays), vmem([((SEQ, D), bf16)] * 2),
        [((SEQ, D), bf16)], 2, LATE_MIB, 2 * SEQ * D * (D + FF),
    )


def heads_back_kernel(scaled, inner, pre_ds, q_t, k_t, v_m, low, p_ref, tables, packed, dq, dk, dv):
    attend_back(scaled, inner, pre_ds, q_t, k_t, v_m, low.at[0], p_ref, dq, dk, dv)
    pack_grads(dq, dk, dv, tables[:8, :], tables[8:, :], packed)


def heads_back_call(*arrays):
    return call_kernel(
        heads_back_kernel, "layer_zero_attention_back", in_vmem(*arrays), vmem([((3 * D, SEQ), bf16)]),
        [((D, SEQ), f32)] * 3, 0, LATE_MIB, 10 * SEQ * SEQ * D,
    )[0]


def feed_back_kernel(grad, slope, w_in, w_out, total):
    total[...] = feed_back(grad[...], w_out.at[0], w_in.at[0], slope, NO_COPIES)


def feed_back_call(*arrays):
    (total,) = call_kernel(
        feed_back_kernel, "layer_zero_feed_back", in_vmem(*arrays), vmem([((SEQ, D), f32)]), [], 0,
        LATE_MIB, 4 * SEQ * D * FF,
    )
    return total


def norms_kernel(x_ref, grad, two, packed, grad_one, small, w_qkv, keep, send, result, sems):
    result[...] = norms_back(
        grad[...], x_ref[...].astype(f32), two[...], packed[...], w_qkv[0], small.at[0]
    )
    hand_over((result, grad_one), keep, send, sems)


def norms_call(*arrays):
    return call_kernel(
        norms_kernel, "layer_zero_norms", in_vmem(*arrays), vmem([((SEQ, D), f32)] * 2),
        [((SEQ, D), f32)], 2, LATE_MIB, 6 * SEQ * D * D,
    )


def place_kernel(act, act_other, grad, grad_other, act_out, grad_out, sems):
    section = lax.axis_index("pipe")
    copies = Copies(sems)
    wait_all(
        *[
            copies.start(value, whole.at[0, where, 0])
            for value, whole, where in (
                (grad, grad_out, section),
                (grad_other, grad_out, 1 - section),
                (act, act_out, section),
                (act_other, act_out, 1 - section),
            )
        ]
    )


def place_call(*arrays):
    wholes = [(pltpu.HBM, (1, 2, 1, SEQ, D), bf16), (pltpu.HBM, (1, 2, 1, SEQ, D), f32)]
    return call_kernel(
        place_kernel, "place_outputs", in_vmem(*arrays), wholes, [], 4, LATE_MIB, 2 * SEQ * D
    )


def final_kernel(col_width, grads_ref, hidden, embed, wide, up_high, up_rest, *refs):
    results, (d_embed, d_up, d_up_b, d_out, d_out_b, sems) = refs[:5], refs[5:]
    section = lax.axis_index("pipe")
    shard = lax.axis_index("dp")
    copies = Copies(sems)
    placed = []
    units = hidden[...]
    both = jnp.zeros((2 * PAD, D), f32)
    for part in range(4):
        high, rest = halves(padded(grads_ref[part * PREFIX : (part + 1) * PREFIX, :]))
        both = both + dot(
            jnp.concatenate([high, rest], axis=0), wide[part * D : (part + 1) * D, :], NN
        )
    grad_units = (both[:PAD] + both[PAD:])[:PREFIX]
    grad_pre = grad_units * (1.0 - units * units)
    d_up_b[...] = jnp.sum(grad_pre, axis=0, keepdims=True)
    d_up[...] = stacked_dot(embed[...], grad_pre)
    placed += [copies.start(d_up, results[1]), copies.start(d_up_b, results[2])]
    column = section * (2 * D) + shard * col_width
    own_cols = jnp.zeros((PREFIX, col_width), f32)
    for part in range(4):
        for piece in range(D // col_width):
            here = column == part * D + piece * col_width
            cols = slice(piece * col_width, (piece + 1) * col_width)
            rows = slice(part * PREFIX, (part + 1) * PREFIX)
            own_cols = jnp.where(here, grads_ref[rows, cols], own_cols)
    d_out[...] = stacked_dot(units, own_cols)
    d_out_b[...] = jnp.sum(own_cols, axis=0, keepdims=True)
    placed += [copies.start(d_out, results[3]), copies.start(d_out_b, results[4])]
    high, rest = halves(padded(grad_pre))
    both = dot(jnp.concatenate([high, rest], axis=0), up_high[...], NN)
    both = both[:PAD] + both[PAD:] + dot(high, up_rest[...], NN)
    d_embed[...] = both[:PREFIX]
    placed.append(copies.start(d_embed, results[0]))
    wait_all(*placed)


def final_call(col_width, *arrays):
    def body(*refs):
        final_kernel(col_width, *refs)

    shapes = [((PREFIX, D), f32), ((D, D), f32), ((1, D), f32), ((D, col_width), f32), ((1, col_width), f32)]
    return call_kernel(
        body, "reparam", in_vmem(*arrays), [(pltpu.HBM, *pair) for pair in shapes], shapes, 5, LATE_MIB,
        SEQ * D * D,
    )


def swapped(array_in):
    return lax.ppermute(array_in, "pipe", [(0, 1), (1, 0)])


def hops(axis):
    size = lax.axis_size(axis)
    steps = []
    step = 1
    while step < size:
        steps.append((axis, [(i, i ^ step) for i in range(size)]))
        step *= 2
    assert step == size
    return steps


def local(
    block_input,
    cotangent,
    segments,
    ln1_gain,
    ln1_shift,
    qkv_weight,
    qkv_bias,
    attn_weight,
    attn_bias,
    ln2_gain,
    ln2_shift,
    ff_in_weight,
    ff_in_bias,
    ff_out_weight,
    ff_out_bias,
    prefix_embed,
    up_weight,
    up_bias,
    out_weight,
    out_bias,
):
    other_qkv = swapped(qkv_weight)
    small = small_call(
        ln1_gain, ln1_shift, ln2_gain, ln2_shift, attn_bias, ff_out_bias, qkv_bias, ff_in_bias
    )
    other_small = swapped(small)
    small, prefix_embed = lax.optimization_barrier((small, prefix_embed))
    tables = jnp.asarray(rope_tables())
    _, *later = lax.optimization_barrier((small, attn_weight, ff_in_weight, ff_out_weight))
    other_attn, other_in, other_out = (swapped(weight) for weight in later)
    x_zero, hat_zero, mask, low, hidden_units, wide, up_high, up_rest, tables, own_qkv = opening_call(
        block_input, segments, prefix_embed, up_weight, up_bias, out_weight, out_bias, tables, qkv_weight
    )
    q0, k0, v0, p0, pp0, inv0, mixed0, two_zero, small, w_qkv, w_attn, w_in, w_out, cot = first_call(
        (small, other_small, own_qkv, other_qkv, hat_zero, mask, low, tables),
        attn_weight, ff_in_weight, ff_out_weight, cotangent,
    )
    act_zero, slope_zero, w_in = feed_call(two_zero, small, other_in, w_in)
    (h_one, act_one, mixed_one, grad_one, grad_low, scaled_zero, inner_zero, pre_ds_zero, prefix_grad,
     w_attn, w_out) = middle_call(
        w_attn, w_out, q0, pp0, inv0, mixed0, small, w_qkv, w_in, other_attn, other_out, cot, x_zero,
        act_zero, low, mask, tables,
    )

    def layer_one_out(state):
        own, send = result_call(state["h_one"], act_one, mixed_one, small, w_attn, w_out)
        return dict(state, act_own=own, act_send=send)

    def layer_zero_attention(state):
        packed = heads_back_call(
            state["scaled"], inner_zero, pre_ds_zero, q0, k0, v0, low, p0, tables
        )
        return dict(state, packed=packed, act_other=swapped(state["act_send"]))

    def layer_zero_feed(state):
        return dict(state, two=feed_back_call(state["grad_low"], slope_zero, w_in, w_out))

    def layer_zero_norms(state):
        own, send = norms_call(x_zero, grad_low, state["two"], state["packed"], grad_one, small, w_qkv)
        return dict(state, grad_own=own, grad_send=send)

    def swap_grads(state):
        other = swapped(state["grad_send"])
        return {"wholes": place_call(state["act_own"], state["act_other"], state["grad_own"], other)}

    works = [layer_one_out, layer_zero_attention, layer_zero_feed, layer_zero_norms, swap_grads]
    state = {"h_one": h_one, "grad_low": grad_low, "scaled": scaled_zero}
    for axis, pairs in hops("pipe") + hops("dp") + hops("grp"):
        if axis == "pipe":
            moved = lax.ppermute(prefix_grad, axis, pairs)
        else:
            prefix_grad = lax.reduce_precision(prefix_grad, 8, 7)
            moved = lax.ppermute(prefix_grad.astype(bf16), axis, pairs)
        if works:
            state = works.pop(0)(state)
        prefix_grad, moved, state = lax.optimization_barrier((prefix_grad, moved, state))
        prefix_grad = prefix_grad + moved.astype(f32)
    for work in works:
        state = work(state)
    col_width = 2 * D // lax.axis_size("dp")
    grad_embed, grad_up, grad_up_b, grad_out, grad_out_b = final_call(
        col_width, prefix_grad, hidden_units, prefix_embed, wide, up_high, up_rest
    )
    activations, input_grads = state["wholes"]
    return (
        activations,
        input_grads,
        grad_embed,
        grad_up,
        grad_up_b[0],
        grad_out,
        grad_out_b[0],
    )


def solution(mesh):
    return jax.shard_map(
        local,
        mesh=mesh,
        in_specs=(
            P(None, ("grp", "dp"), None, None),
            P(None, ("grp", "dp"), None, None),
            P(None, ("grp", "dp"), None),
            P("pipe", None),
            P("pipe", None),
            P("pipe", None, None),
            P("pipe", None),
            P("pipe", None, None),
            P("pipe", None),
            P("pipe", None),
            P("pipe", None),
            P("pipe", None, None),
            P("pipe", None),
            P("pipe", None, None),
            P("pipe", None),
            P(),
            P(),
            P(),
            P(),
            P(),
        ),
        out_specs=(
            P("pipe", None, ("grp", "dp"), None, None),
            P("pipe", None, ("grp", "dp"), None, None),
            P(),
            P(),
            P(),
            P(None, ("pipe", "dp")),
            P(("pipe", "dp")),
        ),
        check_vma=False,
    )
```

```python
import math

import jax
import jax.numpy as jnp
import numpy as np
from jax import lax
from jax.experimental import pallas as pl
from jax.experimental.pallas import tpu as pltpu
from jax.sharding import PartitionSpec as P

D = 512
SEQ = 512
HEADS = 8
HD = 64
FF = 2048
ROT = 16
PREFIX = 10
PAD = 16
BLK = 128
BLOCKS = SEQ // BLK
PAIRS = HEADS // 2
LIVE = (1, 2, 3, 3)
P_ROWS = BLK * sum(LIVE)
P_START = (0, 128, 384, 768)

f32 = jnp.float32
bf16 = jnp.bfloat16
LOG2E = math.log2(math.e)
Q_SCALE = LOG2E * HD**-0.5
K_BACK = 1.0 / LOG2E
Q_BACK = HD**-0.5
NEG = -1e30

NN = (((1,), (0,)), ((), ()))
NT = (((1,), (1,)), ((), ()))
TN = (((0,), (0,)), ((), ()))

MIB = 1024 * 1024
EARLY_MIB = 24
MIDDLE_MIB = 23
LATE_MIB = 12

G1, B1, G2, B2, B_ATTN, B_OUT, B_QKV, B_IN = 0, 1, 2, 3, 4, 5, 6, 9
SMALL = 13 * D


def dot(left, right, dims):
    return lax.dot_general(left, right, dims, preferred_element_type=f32)


def call_kernel(kernel, name, ins, outs, scratch, sems, mib, cost, aliases=None):
    operands = [pltpu.with_memory_space_constraint(array, space) for array, space in ins]
    return pl.pallas_call(
        kernel,
        name=name,
        out_shape=[space(shape, dtype) for space, shape, dtype in outs],
        in_specs=[pl.BlockSpec(memory_space=space) for _, space in ins],
        out_specs=[pl.BlockSpec(memory_space=space) for space, _, _ in outs],
        scratch_shapes=[pltpu.VMEM(*pair) for pair in scratch]
        + ([pltpu.SemaphoreType.DMA((sems,))] if sems else []),
        input_output_aliases=aliases or {},
        compiler_params=pltpu.CompilerParams(vmem_limit_bytes=mib * MIB),
        cost_estimate=pl.CostEstimate(flops=cost, bytes_accessed=8 * MIB, transcendentals=0),
    )(*operands)


def in_hbm(*arrays):
    return [(array, pltpu.HBM) for array in arrays]


def anywhere(*arrays):
    return [(array, pl.ANY) for array in arrays]


def in_vmem(*arrays):
    return [(array, pltpu.VMEM) for array in arrays]


def vmem(shapes):
    return [(pltpu.VMEM, *pair) for pair in shapes]


def small_row(small_ref, place):
    return small_ref[:, place * D : (place + 1) * D]


def rope_tables():
    inv_freq = 10000.0 ** (-2.0 * np.arange(ROT // 2) / ROT)
    angles = inv_freq[:, None] * np.arange(SEQ)[None, :]
    return np.concatenate([np.cos(angles), np.sin(angles)], axis=0).astype(np.float32)


class Copies:
    def __init__(self, sems):
        self.sems = sems
        self.count = 0

    def start(self, src, dst):
        copy = pltpu.make_async_copy(src, dst, self.sems.at[self.count])
        self.count += 1
        copy.start()
        return copy

    def of_layer(self, here, own, other, dst):
        sem = self.sems.at[self.count]
        self.count += 1
        copy = pltpu.make_async_copy(own, dst, sem)

        @pl.when(here)
        def _():
            copy.start()

        @pl.when(jnp.logical_not(here))
        def _():
            pltpu.make_async_copy(other, dst, sem).start()

        return copy


def wait_all(*copies):
    for copy in copies:
        copy.wait()


def normalized(hidden):
    mean = jnp.mean(hidden, axis=-1, keepdims=True)
    centered = hidden - mean
    variance = jnp.mean(centered * centered, axis=-1, keepdims=True)
    scale = lax.rsqrt(variance + 1e-05)
    return centered * scale, scale


def rope_heads(rows, cos, sin):
    parts = []
    for head in range(rows.shape[0] // HD):
        base = head * HD
        lead = rows[base : base + 8]
        tail = rows[base + 8 : base + 16]
        parts += [lead * cos - tail * sin, tail * cos + lead * sin, rows[base + 16 : base + HD]]
    return jnp.concatenate(parts, axis=0)


def fill_mask(seg_ref, mask_ref):
    seg_row = seg_ref[...].astype(f32)
    seg_col = jnp.transpose(jnp.broadcast_to(seg_row, (8, SEQ)))[:, 0:1]
    for block in range(BLOCKS):
        for key_block in range(block + 1 - LIVE[block], block + 1):
            seen = seg_col[key_block * BLK : (key_block + 1) * BLK] == (
                seg_row[:, block * BLK : (block + 1) * BLK]
            )
            if key_block == block:
                key_pos = lax.broadcasted_iota(jnp.int32, (BLK, BLK), 0)
                query_pos = lax.broadcasted_iota(jnp.int32, (BLK, BLK), 1)
                seen = seen & (key_pos <= query_pos)
            start = P_START[block] + (key_block - (block + 1 - LIVE[block])) * BLK
            mask_ref[start : start + BLK, :] = jnp.where(seen, 0.0, NEG)


def project_heads(normed, w_ref, small_ref, cos, sin, q_t, k_t, k_m, v_m, v_t):
    bias = small_row(small_ref, B_QKV)
    rows = dot(normed, w_ref[:, :D], NN) + bias
    q_t[...] = (rope_heads(jnp.transpose(rows), cos, sin) * Q_SCALE).astype(bf16)
    bias = small_row(small_ref, B_QKV + 1)
    rows = dot(normed, w_ref[:, D : 2 * D], NN) + bias
    keys = rope_heads(jnp.transpose(rows), cos, sin).astype(bf16)
    k_t[...] = keys
    k_m[...] = jnp.transpose(keys)
    bias = small_row(small_ref, B_QKV + 2)
    values = (dot(normed, w_ref[:, 2 * D :], NN) + bias).astype(bf16)
    v_m[...] = values
    v_t[...] = jnp.transpose(values)


def block_diagonal(pair_rows):
    zeros = jnp.zeros((HD, BLK), pair_rows.dtype)
    return jnp.concatenate(
        [
            jnp.concatenate([pair_rows[:HD], zeros], axis=1),
            jnp.concatenate([zeros, pair_rows[HD:]], axis=1),
        ],
        axis=0,
    )


def from_diagonal(both):
    return jnp.concatenate([both[:HD, :BLK], both[HD:, BLK:]], axis=0)


def per_head(row, rows=HD):
    return jnp.concatenate(
        [
            jnp.broadcast_to(row[:, :BLK], (rows, BLK)),
            jnp.broadcast_to(row[:, BLK:], (rows, BLK)),
        ],
        axis=0,
    )


def geometry(block):
    live = LIVE[block] * BLK
    end = (block + 1) * BLK
    start = P_START[block]
    return slice(end - live, end), slice(block * BLK, end), slice(start, start + live)


def pair_rows(pair):
    return slice(pair * BLK, (pair + 1) * BLK)


def both_heads(rows, tokens):
    return jnp.concatenate([rows[:PAD, tokens], rows[PAD:, tokens]], axis=1)


def attend(q_t, k_m, v_t, pre_k, pre_v, mask_ref, p_ref, pp_ref, inv_ref, mixed_ref):
    real = lax.rem(lax.broadcasted_iota(jnp.int32, (2 * PAD, 1), 0), PAD) < PREFIX
    pad_mask = jnp.where(real, 0.0, NEG)

    def score(feats, block):
        keys, tokens, rows = geometry(block)
        queries = block_diagonal(q_t[feats, tokens])
        mask = mask_ref[rows, :]
        return dot(k_m[keys, feats], queries, NN) + jnp.concatenate([mask, mask], axis=1)

    def soften(pair, block, scores, pre_scores):
        _, tokens, rows = geometry(block)
        pre_scores = both_heads(pre_scores, tokens)
        peak = jnp.maximum(
            jnp.max(scores, axis=0, keepdims=True), jnp.max(pre_scores, axis=0, keepdims=True)
        )
        expo = jnp.exp2(scores - peak).astype(bf16)
        pre_expo = jnp.exp2(pre_scores - peak)
        p_ref[pair, rows, :] = expo
        pp_ref[pair, :PAD, tokens] = pre_expo[:, :BLK].astype(bf16)
        pp_ref[pair, PAD:, tokens] = pre_expo[:, BLK:].astype(bf16)
        return expo, jnp.sum(pre_expo, axis=0, keepdims=True)

    def mix(pair, block, pre_mixed, expo, pre_total):
        feats = pair_rows(pair)
        keys, tokens, _ = geometry(block)
        ones = jnp.ones((PAD, expo.shape[0]), bf16)
        mixed = dot(jnp.concatenate([v_t[feats, keys], ones], axis=0), expo, NN)
        inverse = 1.0 / (mixed[BLK : BLK + 1] + pre_total)
        inv_ref[2 * pair : 2 * pair + 1, tokens] = inverse[:, :BLK]
        inv_ref[2 * pair + 1 : 2 * pair + 2, tokens] = inverse[:, BLK:]
        mixed = from_diagonal(mixed[:BLK]) + pre_mixed[:, tokens]
        mixed_ref[feats, tokens] = (mixed * per_head(inverse)).astype(bf16)

    def score_all(pair):
        feats = pair_rows(pair)
        pre_scores = dot(pre_k[:, feats], q_t[feats, :], NN) + pad_mask
        return pre_scores, [score(feats, block) for block in range(BLOCKS)]

    def mix_all(pair, soft):
        pre_mixed = dot(pre_v[:, pair_rows(pair)], pp_ref[pair], TN)
        for block in range(BLOCKS):
            mix(pair, block, pre_mixed, *soft[block])

    ahead, behind = score_all(0), None
    for pair in range(PAIRS):
        pre_scores, scores = ahead
        if pair + 1 < PAIRS:
            ahead = score_all(pair + 1)
        soft = [soften(pair, block, scores[block], pre_scores) for block in range(BLOCKS)]
        if behind is not None:
            mix_all(*behind)
        behind = (pair, soft)
    mix_all(*behind)


def prefix_back(w_attn, grad, q_t, pre_v, pp_ref, inv_ref, mixed_ref, scaled_ref, inner_ref, pre_ds_ref, turned,
                pre_grad, pre_row):
    turned[...] = jnp.transpose(grad)

    def scale(pair):
        grad_mixed = dot(w_attn[pair_rows(pair), :], turned[...], NN)
        inner = []
        for place in range(2):
            head = 2 * pair + place
            rows = slice(head * HD, (head + 1) * HD)
            scaled = grad_mixed[place * HD : (place + 1) * HD] * inv_ref[head : head + 1, :]
            scaled = scaled.astype(bf16)
            scaled_ref[rows, :] = scaled
            products = scaled.astype(f32) * mixed_ref[rows, :].astype(f32)
            inner.append(jnp.sum(products, axis=0, keepdims=True))
            inner_ref[head : head + 1, :] = inner[-1]
        return jnp.concatenate([jnp.broadcast_to(row, (PAD, SEQ)) for row in inner], axis=0)

    pairs = range(PAIRS)
    inner = [scale(pair) for pair in pairs]
    grad_probs = [dot(pre_v[:, pair_rows(pair)], scaled_ref[pair_rows(pair), :], NN) for pair in pairs]
    for pair in pairs:
        probs = pp_ref[pair].astype(f32)
        pre_ds_ref[pair] = (probs * (grad_probs[pair] - inner[pair])).astype(bf16)
    keys = [dot(q_t[pair_rows(pair), :], pre_ds_ref[pair], NT) for pair in pairs]
    values = [dot(scaled_ref[pair_rows(pair), :], pp_ref[pair], NT) for pair in pairs]
    first_head = lax.rem(lax.broadcasted_iota(jnp.int32, (1, D), 1), BLK) < HD

    def own_head(parts):
        both = jnp.transpose(jnp.concatenate(parts, axis=0))
        return jnp.where(first_head, both[:PREFIX], both[PAD : PAD + PREFIX])

    pre_grad[pre_row : pre_row + PREFIX, :] = own_head(keys) * K_BACK
    pre_grad[pre_row + PREFIX : pre_row + 2 * PREFIX, :] = own_head(values)


def attend_back(scaled_ref, inner_ref, pre_ds_ref, q_t, k_t, v_m, pre_k, p_ref, dq_ref, dk_ref, dv_ref):
    def value_grads(feats, block):
        keys, tokens, _ = geometry(block)
        grads = block_diagonal(scaled_ref[feats, tokens])
        return grads, dot(v_m[keys, feats], grads, NN)

    def score_grads(pair, block, grad_probs):
        _, tokens, rows = geometry(block)
        inner = jnp.concatenate(
            [inner_ref[2 * pair : 2 * pair + 1, tokens], inner_ref[2 * pair + 1 : 2 * pair + 2, tokens]],
            axis=1,
        )
        return (p_ref[pair, rows, :].astype(f32) * (grad_probs - inner)).astype(bf16)

    def out_grads(pair, feats, block, pre_dq, grads, grad_scores):
        keys, tokens, rows = geometry(block)
        queries = block_diagonal(q_t[feats, tokens])
        dq_ref[feats, tokens] = (
            from_diagonal(dot(k_t[feats, keys], grad_scores, NN)) + pre_dq[:, tokens]
        )
        return dot(queries, grad_scores, NT), dot(grads, p_ref[pair, rows, :], NT)

    def by_keys(outs, which, key_block):
        total = None
        for block in range(BLOCKS):
            place = key_block - (block + 1 - LIVE[block])
            if 0 <= place < LIVE[block]:
                part = outs[block][which][:, place * BLK : (place + 1) * BLK]
                total = part if total is None else total + part
        return total

    for pair in range(PAIRS):
        feats = pair_rows(pair)
        first = [value_grads(feats, block) for block in range(BLOCKS)]
        second = [score_grads(pair, block, first[block][1]) for block in range(BLOCKS)]
        pre_dq = dot(pre_k[:, feats], pre_ds_ref[pair], TN)
        outs = [
            out_grads(pair, feats, block, pre_dq, first[block][0], second[block])
            for block in range(BLOCKS)
        ]
        for key_block in range(BLOCKS):
            keys = slice(key_block * BLK, (key_block + 1) * BLK)
            dk_ref[feats, keys] = by_keys(outs, 0, key_block)
            dv_ref[feats, keys] = by_keys(outs, 1, key_block)


def pack_grads(dq_ref, dk_ref, dv_ref, cos, sin, packed_t):
    packed_t[:D, :] = (rope_heads(dq_ref[...], cos, -sin) * Q_BACK).astype(bf16)
    packed_t[D : 2 * D, :] = (rope_heads(dk_ref[...], cos, -sin) * K_BACK).astype(bf16)
    packed_t[2 * D :, :] = dv_ref[...].astype(bf16)


ROOT_HALF = 0.5**0.5


def gelu_both(scaled):
    cdf = ROOT_HALF + ROOT_HALF * lax.erf(scaled)
    density = jnp.exp2(scaled * scaled * (-LOG2E)) * (2.0 / math.sqrt(2.0 * math.pi))
    return scaled * cdf, cdf + scaled * density


FF_CHUNK = 512
FF_ROWS = 256


def second_norm(hat, small_ref):
    gain = small_row(small_ref, G2) * ROOT_HALF
    return (hat * gain + small_row(small_ref, B2) * ROOT_HALF).astype(bf16)


def chunk_of(index):
    return slice(index * FF_CHUNK, (index + 1) * FF_CHUNK)


def feed_in(normed, w_ref, small_ref, act_ref, slope_ref):
    for chunk in range(FF // FF_CHUNK):
        cols = chunk_of(chunk)
        bias = small_row(small_ref, B_IN + chunk) * ROOT_HALF
        for start in range(0, SEQ, FF_ROWS):
            rows = slice(start, start + FF_ROWS)
            act, slope = gelu_both(dot(normed[rows], w_ref[:, cols], NN) + bias)
            act_ref[rows, cols] = act.astype(bf16)
            slope_ref[rows, cols] = slope.astype(bf16)


def feed_both(normed, grad, w_in, w_out, small_ref, act_ref):
    total = jnp.zeros((SEQ, D), f32)
    for chunk in range(FF // FF_CHUNK):
        cols = chunk_of(chunk)
        bias = small_row(small_ref, B_IN + chunk) * ROOT_HALF
        slopes = []
        for start in range(0, SEQ, FF_ROWS):
            rows = slice(start, start + FF_ROWS)
            act, slope = gelu_both(dot(normed[rows], w_in[:, cols], NN) + bias)
            act_ref[rows, cols] = act.astype(bf16)
            slopes.append(slope.astype(bf16))
        grad_act = dot(grad, w_out[cols, :], NT)
        grad_before = (grad_act * jnp.concatenate(slopes, axis=0).astype(f32)).astype(bf16)
        total = total + dot(grad_before, w_in[:, cols], NT)
    return total * ROOT_HALF


def layer_result(hidden, mixed_t, w_attn, act_ref, w_out, small_ref):
    attn_out = dot(jnp.transpose(mixed_t), w_attn, NN) + small_row(small_ref, B_ATTN)
    ff_out = dot(act_ref[...], w_out, NN) + small_row(small_ref, B_OUT)
    return hidden + attn_out + ff_out


def feed_back(grad, w_out, w_in, slope_ref):
    total = jnp.zeros((SEQ, D), f32)
    for chunk in range(FF // FF_CHUNK):
        cols = chunk_of(chunk)
        grad_act = dot(grad, w_out[cols, :], NT)
        grad_before = (grad_act * slope_ref[:, cols].astype(f32)).astype(bf16)
        total = total + dot(grad_before, w_in[:, cols], NT)
    return total * ROOT_HALF


def norms_back(grad, hat, scale, grad_two, packed_t, w_qkv, small_ref):
    grad_one = jnp.transpose(dot(w_qkv, packed_t, NN))
    grad_hat = (
        grad_one * small_row(small_ref, G1) + grad_two * small_row(small_ref, G2)
    )
    mean_one = jnp.mean(grad_hat, axis=-1, keepdims=True)
    mean_two = jnp.mean(grad_hat * hat, axis=-1, keepdims=True)
    return grad.astype(f32) + scale * (grad_hat - mean_one - hat * mean_two)


def halves(values):
    high = values.astype(bf16)
    return high, (values - high.astype(f32)).astype(bf16)


def padded(values):
    return jnp.concatenate([values, jnp.zeros((PAD - PREFIX, values.shape[1]), f32)], axis=0)


def few_rows_dot(left, right):
    left_high, left_rest = halves(padded(left))
    right_high, right_rest = halves(right)
    both = dot(jnp.concatenate([left_high, left_rest], axis=0), right_high, NN)
    return both[:PAD] + both[PAD:] + dot(left_high, right_rest, NN)


def stacked_dot(left, right):
    left_high, left_rest = halves(padded(left))
    right_high, right_rest = halves(padded(right))
    return dot(
        jnp.concatenate([left_high, left_high, left_rest], axis=0),
        jnp.concatenate([right_high, right_rest, right_high], axis=0),
        TN,
    )


def small_kernel(gain_one, shift_one, gain_two, shift_two, attn_b, out_b, qkv_b, in_b, packed, sems):
    copies = Copies(sems)
    places = [(gain_one, 0), (shift_one, 1), (gain_two, 2), (shift_two, 3), (attn_b, 4), (out_b, 5)]
    places += [(qkv_b, 6), (in_b, 9)]
    wait_all(
        *[
            copies.start(row, packed.at[:, place * D : place * D + row.shape[1]])
            for row, place in places
        ]
    )


def small_call(*arrays):
    (packed,) = call_kernel(
        small_kernel, "small_parameters", in_hbm(*arrays), vmem([((1, SMALL), f32)]), [], 8, LATE_MIB, SMALL
    )
    return packed


def prefix_states(embed, up_w, up_b, out_w, out_b, arrivals, hidden, low, wide, up_high, up_rest):
    units = jnp.tanh(few_rows_dot(embed[...], up_w[...])[:PREFIX] + up_b[...])
    hidden[...] = units
    up_high[...], up_rest[...] = halves(jnp.transpose(up_w[...]))
    real = lax.broadcasted_iota(jnp.int32, (PAD, 1), 0) < PREFIX
    first_head = lax.rem(lax.broadcasted_iota(jnp.int32, (1, D), 1), BLK) < HD
    for part in range(4):
        cols = slice(part * D, (part + 1) * D)
        arrivals[part].wait()
        states = jnp.where(real, few_rows_dot(units, out_w[:, cols]) + out_b[:, cols], 0.0)
        low[part, :PAD, :] = jnp.where(first_head, states, 0.0).astype(bf16)
        low[part, PAD:, :] = jnp.where(first_head, 0.0, states).astype(bf16)
        wide[cols, :] = jnp.transpose(out_w[:, cols].astype(bf16))


OPENING_SHAPES = (
    ((SEQ, D), bf16),
    ((SEQ, D), f32),
    ((P_ROWS, BLK), f32),
    ((4, 2 * PAD, D), bf16),
    ((PREFIX, D), f32),
    ((4 * D, D), bf16),
    ((D, D), bf16),
    ((D, D), bf16),
    ((2 * 8, SEQ), f32),
    ((D, 3 * D), bf16),
)


def opening_kernel(x_hbm, seg_hbm, embed_hbm, up_hbm, up_b_hbm, out_hbm, out_b_hbm, tables_hbm, qkv_hbm,
                   x_ref, hat, mask, low, hidden, wide, up_high, up_rest, tables, own_qkv, seg, embed, up_w, up_b,
                   out_w, out_b, sems):
    section = lax.axis_index("pipe")
    copies = Copies(sems)
    x_copy = copies.start(x_hbm.at[section, 0], x_ref)
    seg_copy = copies.start(seg_hbm.at[section], seg)
    prefix_copies = [
        copies.start(src, dst)
        for src, dst in ((embed_hbm, embed), (up_hbm, up_w), (up_b_hbm, up_b.at[0]), (out_b_hbm, out_b.at[0]))
    ]
    parts = [
        copies.start(out_hbm.at[:, i * D : (i + 1) * D], out_w.at[:, i * D : (i + 1) * D])
        for i in range(4)
    ]
    late = [copies.start(tables_hbm, tables), copies.start(qkv_hbm.at[0], own_qkv)]
    seg_copy.wait()
    fill_mask(seg, mask)
    x_copy.wait()
    hat[...], _ = normalized(x_ref[...].astype(f32))
    wait_all(*prefix_copies)
    prefix_states(embed, up_w, up_b, out_w, out_b, parts, hidden, low, wide, up_high, up_rest)
    wait_all(*late)


def opening_call(*arrays):
    scratch = [
        ((1, SEQ), jnp.int32),
        ((PREFIX, D), f32),
        ((D, D), f32),
        ((1, D), f32),
        ((D, 4 * D), f32),
        ((1, 4 * D), f32),
    ]
    return call_kernel(
        opening_kernel, "opening", in_hbm(*arrays), vmem(OPENING_SHAPES), scratch, 12, EARLY_MIB,
        2 * 6 * PAD * D * 5 * D,
    )


HEAD_SHAPES = (
    ((D, SEQ), bf16),
    ((D, SEQ), bf16),
    ((SEQ, D), bf16),
    ((PAIRS, P_ROWS, 2 * BLK), bf16),
    ((PAIRS, 2 * PAD, SEQ), bf16),
    ((HEADS, SEQ), f32),
    ((D, SEQ), bf16),
)
FIRST_SHAPES = HEAD_SHAPES + (
    ((SEQ, D), bf16),
    ((2, 1, SMALL), f32),
    ((2, D, 3 * D), bf16),
    ((2, D, D), bf16),
    ((2, D, FF), bf16),
    ((2, FF, D), bf16),
    ((SEQ, D), bf16),
)


def first_kernel(own_small, other_small, own_qkv, other_qkv, hat_ref, mask, low, tables,
                 attn_hbm, ff_in_hbm, ff_out_hbm, cot_hbm,
                 q_t, k_t, v_m, p_ref, pp_ref, inv_ref, mixed_ref, two_ref, small, w_qkv, w_attn, w_in,
                 w_out, cot_ref, k_m, v_t, sems):
    section = lax.axis_index("pipe")
    copies = Copies(sems)
    now = [
        copies.start(own_small, small.at[section]),
        copies.start(other_small, small.at[1 - section]),
        copies.start(own_qkv, w_qkv.at[section]),
        copies.start(other_qkv.at[0], w_qkv.at[1 - section]),
    ]
    later = [
        copies.start(ff_in_hbm.at[0], w_in.at[section]),
        copies.start(attn_hbm.at[0], w_attn.at[section]),
        copies.start(ff_out_hbm.at[0], w_out.at[section]),
        copies.start(cot_hbm.at[section, 0], cot_ref),
    ]
    wait_all(*now)
    hat = hat_ref[...]
    zero = small.at[0]
    normed = (hat * small_row(zero, G1) + small_row(zero, B1)).astype(bf16)
    two_ref[...] = second_norm(hat, zero)
    project_heads(normed, w_qkv.at[0], zero, tables[:8, :], tables[8:, :], q_t, k_t, k_m, v_m, v_t)
    attend(q_t, k_m, v_t, low.at[0], low.at[1], mask, p_ref, pp_ref, inv_ref, mixed_ref)
    wait_all(*later)


def first_call(ready, *arrays):
    return call_kernel(
        first_kernel, "first_attention", in_vmem(*ready) + in_hbm(*arrays), vmem(FIRST_SHAPES),
        [((SEQ, D), bf16), ((D, SEQ), bf16)], 8, EARLY_MIB, 200 * SEQ * D * 3 * D,
    )


def feed_kernel(two, small, other_in, w_in_before, act_ref, slope_ref, w_in, sems):
    wait_all(Copies(sems).start(other_in.at[0], w_in.at[1 - lax.axis_index("pipe")]))
    feed_in(two[...], w_in.at[0], small.at[0], act_ref, slope_ref)


def feed_call(*arrays):
    shapes = [((SEQ, FF), bf16), ((SEQ, FF), bf16), ((2, D, FF), bf16)]
    return call_kernel(
        feed_kernel, "first_feed", in_vmem(*arrays), vmem(shapes), [], 1, LATE_MIB, 2 * SEQ * D * FF,
        {3: 2},
    )


WEIGHT_SHAPES = (((D, 3 * D), bf16), ((D, D), bf16), ((D, FF), bf16), ((FF, D), bf16))


MIDDLE_OUTS = (
    ((SEQ, D), bf16),
    ((SEQ, FF), bf16),
    ((D, SEQ), bf16),
    ((SEQ, D), f32),
    ((SEQ, D), bf16),
    ((D, SEQ), bf16),
    ((HEADS, SEQ), f32),
    ((PAIRS, 2 * PAD, SEQ), bf16),
    ((4 * PREFIX, D), f32),
    ((2, D, D), bf16),
    ((2, FF, D), bf16),
)


def middle_kernel(w_attn_before, w_out_before, q0, pp0, inv0, mixed0, small, w_qkv, w_in,
                  other_attn, other_out, cot_ref, x_ref, act_zero, low, mask, tables,
                  h_one, act_one, mixed_one, grad_one, grad_low, scaled_zero, inner_zero, pre_ds_zero,
                  prefix_grad, w_attn, w_out,
                  q_t, k_t, v_m, p_ref, pp_ref, inv_ref, scaled, inner, pre_ds, turned, k_m, v_t,
                  dq, dk, dv, packed, sems):
    section = lax.axis_index("pipe")
    copies = Copies(sems)
    wait_all(
        copies.start(other_attn.at[0], w_attn.at[1 - section]),
        copies.start(other_out.at[0], w_out.at[1 - section]),
    )
    small_one = small.at[1]
    h_one[...] = layer_result(
        x_ref[...].astype(f32), mixed0[...], w_attn[0], act_zero, w_out[0], small.at[0]
    ).astype(bf16)

    cos, sin = tables[:8, :], tables[8:, :]
    hat, scale = normalized(h_one[...].astype(f32))
    grad_one[...] = hat
    normed = (hat * small_row(small_one, G1) + small_row(small_one, B1)).astype(bf16)
    two = second_norm(hat, small_one)
    project_heads(normed, w_qkv.at[1], small_one, cos, sin, q_t, k_t, k_m, v_m, v_t)
    attend(q_t, k_m, v_t, low.at[2], low.at[3], mask, p_ref, pp_ref, inv_ref, mixed_one)

    grad = cot_ref[...]
    grad_two = feed_both(two, grad, w_in.at[1], w_out.at[1], small_one, act_one)
    prefix_back(w_attn.at[1], grad, q_t, low.at[3], pp_ref, inv_ref, mixed_one, scaled, inner, pre_ds, turned,
                prefix_grad, 2 * PREFIX)
    attend_back(scaled, inner, pre_ds, q_t, k_t, v_m, low.at[2], p_ref, dq, dk, dv)
    pack_grads(dq, dk, dv, cos, sin, packed)
    result = norms_back(grad, grad_one[...], scale, grad_two, packed[...], w_qkv[1], small_one)
    grad_one[...] = result
    grad_low[...] = result.astype(bf16)

    prefix_back(w_attn.at[0], grad_low[...], q0, low.at[1], pp0, inv0, mixed0, scaled_zero, inner_zero,
                pre_ds_zero, turned, prefix_grad, 0)


def middle_call(*arrays):
    scratch = HEAD_SHAPES[:6] + (
        ((D, SEQ), bf16),
        ((HEADS, SEQ), f32),
        ((PAIRS, 2 * PAD, SEQ), bf16),
        ((D, SEQ), bf16),
        ((SEQ, D), bf16),
        ((D, SEQ), bf16),
        ((D, SEQ), f32),
        ((D, SEQ), f32),
        ((D, SEQ), f32),
        ((3 * D, SEQ), bf16),
    )
    return call_kernel(
        middle_kernel, "middle", in_vmem(*arrays), vmem(MIDDLE_OUTS), scratch, 2, MIDDLE_MIB,
        20 * SEQ * D * 6 * D, {0: 9, 1: 10},
    )


def hand_over(values, keep, send, sems):
    here = lax.axis_index("pipe") == 0
    copies = Copies(sems)
    wait_all(
        copies.of_layer(here, values[0], values[1], keep),
        copies.of_layer(here, values[1], values[0], send),
    )


def result_kernel(h_one, act, mixed, small, w_attn, w_out, keep, send, result, sems):
    result[...] = layer_result(
        h_one[...].astype(f32), mixed[...], w_attn[1], act, w_out[1], small.at[1]
    ).astype(bf16)
    hand_over((h_one, result), keep, send, sems)


def result_call(*arrays):
    return call_kernel(
        result_kernel, "layer_one_out", in_vmem(*arrays), vmem([((SEQ, D), bf16)] * 2),
        [((SEQ, D), bf16)], 2, LATE_MIB, 2 * SEQ * D * (D + FF),
    )


def heads_back_kernel(scaled, inner, pre_ds, q_t, k_t, v_m, low, p_ref, tables, packed, dq, dk, dv):
    attend_back(scaled, inner, pre_ds, q_t, k_t, v_m, low.at[0], p_ref, dq, dk, dv)
    pack_grads(dq, dk, dv, tables[:8, :], tables[8:, :], packed)


def heads_back_call(*arrays):
    return call_kernel(
        heads_back_kernel, "layer_zero_attention_back", in_vmem(*arrays), vmem([((3 * D, SEQ), bf16)]),
        [((D, SEQ), f32)] * 3, 0, LATE_MIB, 10 * SEQ * SEQ * D,
    )[0]


def feed_back_kernel(grad, slope, w_in, w_out, total):
    total[...] = feed_back(grad[...], w_out.at[0], w_in.at[0], slope)


def feed_back_call(*arrays):
    (total,) = call_kernel(
        feed_back_kernel, "layer_zero_feed_back", in_vmem(*arrays), vmem([((SEQ, D), f32)]), [], 0,
        LATE_MIB, 4 * SEQ * D * FF,
    )
    return total


def norms_kernel(x_ref, grad, two, packed, grad_one, small, w_qkv, keep, send, result, sems):
    hat, scale = normalized(x_ref[...].astype(f32))
    result[...] = norms_back(grad[...], hat, scale, two[...], packed[...], w_qkv[0], small.at[0])
    hand_over((result, grad_one), keep, send, sems)


def norms_call(*arrays):
    return call_kernel(
        norms_kernel, "layer_zero_norms", in_vmem(*arrays), vmem([((SEQ, D), f32)] * 2),
        [((SEQ, D), f32)], 2, LATE_MIB, 6 * SEQ * D * D,
    )


def place_kernel(act, act_other, grad, grad_other, act_out, grad_out, sems):
    section = lax.axis_index("pipe")
    copies = Copies(sems)
    wait_all(
        *[
            copies.start(value, whole.at[0, where, 0])
            for value, whole, where in (
                (grad, grad_out, section),
                (grad_other, grad_out, 1 - section),
                (act, act_out, section),
                (act_other, act_out, 1 - section),
            )
        ]
    )


def place_call(*arrays):
    wholes = [(pltpu.HBM, (1, 2, 1, SEQ, D), bf16), (pltpu.HBM, (1, 2, 1, SEQ, D), f32)]
    return call_kernel(
        place_kernel, "place_outputs", in_vmem(*arrays), wholes, [], 4, LATE_MIB, 2 * SEQ * D
    )


def final_kernel(col_width, grads_ref, hidden, embed, wide, up_high, up_rest, *refs):
    results, (d_embed, d_up, d_up_b, d_out, d_out_b, sems) = refs[:5], refs[5:]
    section = lax.axis_index("pipe")
    shard = lax.axis_index("dp")
    copies = Copies(sems)
    placed = []
    units = hidden[...]
    both = jnp.zeros((2 * PAD, D), f32)
    for part in range(4):
        high, rest = halves(padded(grads_ref[part * PREFIX : (part + 1) * PREFIX, :]))
        both = both + dot(
            jnp.concatenate([high, rest], axis=0), wide[part * D : (part + 1) * D, :], NN
        )
    grad_units = (both[:PAD] + both[PAD:])[:PREFIX]
    grad_pre = grad_units * (1.0 - units * units)
    d_up_b[...] = jnp.sum(grad_pre, axis=0, keepdims=True)
    d_up[...] = stacked_dot(embed[...], grad_pre)
    placed += [copies.start(d_up, results[1]), copies.start(d_up_b, results[2])]
    column = section * (2 * D) + shard * col_width
    own_cols = jnp.zeros((PREFIX, col_width), f32)
    for part in range(4):
        for piece in range(D // col_width):
            here = column == part * D + piece * col_width
            cols = slice(piece * col_width, (piece + 1) * col_width)
            rows = slice(part * PREFIX, (part + 1) * PREFIX)
            own_cols = jnp.where(here, grads_ref[rows, cols], own_cols)
    d_out[...] = stacked_dot(units, own_cols)
    d_out_b[...] = jnp.sum(own_cols, axis=0, keepdims=True)
    placed += [copies.start(d_out, results[3]), copies.start(d_out_b, results[4])]
    high, rest = halves(padded(grad_pre))
    both = dot(jnp.concatenate([high, rest], axis=0), up_high[...], NN)
    both = both[:PAD] + both[PAD:] + dot(high, up_rest[...], NN)
    d_embed[...] = both[:PREFIX]
    placed.append(copies.start(d_embed, results[0]))
    wait_all(*placed)


def final_call(col_width, *arrays):
    def body(*refs):
        final_kernel(col_width, *refs)

    shapes = [((PREFIX, D), f32), ((D, D), f32), ((1, D), f32), ((D, col_width), f32), ((1, col_width), f32)]
    return call_kernel(
        body, "reparam", in_vmem(*arrays), [(pltpu.HBM, *pair) for pair in shapes], shapes, 5, LATE_MIB,
        SEQ * D * D,
    )


def swapped(array_in):
    return lax.ppermute(array_in, "pipe", [(0, 1), (1, 0)])


def hops(axis):
    size = lax.axis_size(axis)
    steps = []
    step = 1
    while step < size:
        steps.append((axis, [(i, i ^ step) for i in range(size)]))
        step *= 2
    assert step == size
    return steps


def local(
    block_input,
    cotangent,
    segments,
    ln1_gain,
    ln1_shift,
    qkv_weight,
    qkv_bias,
    attn_weight,
    attn_bias,
    ln2_gain,
    ln2_shift,
    ff_in_weight,
    ff_in_bias,
    ff_out_weight,
    ff_out_bias,
    prefix_embed,
    up_weight,
    up_bias,
    out_weight,
    out_bias,
):
    other_qkv = swapped(qkv_weight)
    small = small_call(
        ln1_gain, ln1_shift, ln2_gain, ln2_shift, attn_bias, ff_out_bias, qkv_bias, ff_in_bias
    )
    other_small = swapped(small)
    small, prefix_embed = lax.optimization_barrier((small, prefix_embed))
    tables = jnp.asarray(rope_tables())
    _, *later = lax.optimization_barrier((small, attn_weight, ff_in_weight, ff_out_weight))
    other_attn, other_in, other_out = (swapped(weight) for weight in later)
    x_zero, hat_zero, mask, low, hidden_units, wide, up_high, up_rest, tables, own_qkv = opening_call(
        block_input, segments, prefix_embed, up_weight, up_bias, out_weight, out_bias, tables, qkv_weight
    )
    q0, k0, v0, p0, pp0, inv0, mixed0, two_zero, small, w_qkv, w_attn, w_in, w_out, cot = first_call(
        (small, other_small, own_qkv, other_qkv, hat_zero, mask, low, tables),
        attn_weight, ff_in_weight, ff_out_weight, cotangent,
    )
    act_zero, slope_zero, w_in = feed_call(two_zero, small, other_in, w_in)
    (h_one, act_one, mixed_one, grad_one, grad_low, scaled_zero, inner_zero, pre_ds_zero, prefix_grad,
     w_attn, w_out) = middle_call(
        w_attn, w_out, q0, pp0, inv0, mixed0, small, w_qkv, w_in, other_attn, other_out, cot, x_zero,
        act_zero, low, mask, tables,
    )

    def layer_one_out(state):
        own, send = result_call(state["h_one"], act_one, mixed_one, small, w_attn, w_out)
        return dict(state, act_own=own, act_send=send)

    def layer_zero_attention(state):
        packed = heads_back_call(
            state["scaled"], inner_zero, pre_ds_zero, q0, k0, v0, low, p0, tables
        )
        return dict(state, packed=packed, act_other=swapped(state["act_send"]))

    def layer_zero_feed(state):
        return dict(state, two=feed_back_call(state["grad_low"], slope_zero, w_in, w_out))

    def layer_zero_norms(state):
        own, send = norms_call(x_zero, grad_low, state["two"], state["packed"], grad_one, small, w_qkv)
        return dict(state, grad_own=own, grad_send=send)

    def swap_grads(state):
        other = swapped(state["grad_send"])
        return {"wholes": place_call(state["act_own"], state["act_other"], state["grad_own"], other)}

    works = [layer_one_out, layer_zero_attention, layer_zero_feed, layer_zero_norms, swap_grads]
    state = {"h_one": h_one, "grad_low": grad_low, "scaled": scaled_zero}
    for axis, pairs in hops("pipe") + hops("dp") + hops("grp"):
        if axis == "pipe":
            moved = lax.ppermute(prefix_grad, axis, pairs)
        else:
            prefix_grad = lax.reduce_precision(prefix_grad, 8, 7)
            moved = lax.ppermute(prefix_grad.astype(bf16), axis, pairs)
        if works:
            state = works.pop(0)(state)
        prefix_grad, moved, state = lax.optimization_barrier((prefix_grad, moved, state))
        prefix_grad = prefix_grad + moved.astype(f32)
    for work in works:
        state = work(state)
    col_width = 2 * D // lax.axis_size("dp")
    grad_embed, grad_up, grad_up_b, grad_out, grad_out_b = final_call(
        col_width, prefix_grad, hidden_units, prefix_embed, wide, up_high, up_rest
    )
    activations, input_grads = state["wholes"]
    return (
        activations,
        input_grads,
        grad_embed,
        grad_up,
        grad_up_b[0],
        grad_out,
        grad_out_b[0],
    )


def solution(mesh):
    return jax.shard_map(
        local,
        mesh=mesh,
        in_specs=(
            P(None, ("grp", "dp"), None, None),
            P(None, ("grp", "dp"), None, None),
            P(None, ("grp", "dp"), None),
            P("pipe", None),
            P("pipe", None),
            P("pipe", None, None),
            P("pipe", None),
            P("pipe", None, None),
            P("pipe", None),
            P("pipe", None),
            P("pipe", None),
            P("pipe", None, None),
            P("pipe", None),
            P("pipe", None, None),
            P("pipe", None),
            P(),
            P(),
            P(),
            P(),
            P(),
        ),
        out_specs=(
            P("pipe", None, ("grp", "dp"), None, None),
            P("pipe", None, ("grp", "dp"), None, None),
            P(),
            P(),
            P(),
            P(None, ("pipe", "dp")),
            P(("pipe", "dp")),
        ),
        check_vma=False,
    )
```

```python
import math

import jax
import jax.numpy as jnp
import numpy as np
from jax import lax
from jax.experimental import pallas as pl
from jax.experimental.pallas import tpu as pltpu
from jax.sharding import PartitionSpec as P

D = 512
SEQ = 512
HEADS = 8
HD = 64
FF = 2048
ROT = 16
PREFIX = 10
PAD = 16
BLK = 128
BLOCKS = SEQ // BLK
PAIRS = HEADS // 2
LIVE = (1, 2, 3, 3)
P_ROWS = BLK * sum(LIVE)
P_START = (0, 128, 384, 768)

f32 = jnp.float32
bf16 = jnp.bfloat16
LOG2E = math.log2(math.e)
Q_SCALE = LOG2E * HD**-0.5
K_BACK = 1.0 / LOG2E
Q_BACK = HD**-0.5
NEG = -1e30

NN = (((1,), (0,)), ((), ()))
NT = (((1,), (1,)), ((), ()))
TN = (((0,), (0,)), ((), ()))

MIB = 1024 * 1024
EARLY_MIB = 24
MIDDLE_MIB = 23
LATE_MIB = 12

G1, B1, G2, B2, B_ATTN, B_OUT, B_QKV, B_IN = 0, 1, 2, 3, 4, 5, 6, 9
SMALL = 13 * D


def dot(left, right, dims):
    return lax.dot_general(left, right, dims, preferred_element_type=f32)


def call_kernel(kernel, name, ins, outs, scratch, sems, mib, cost, aliases=None):
    operands = [pltpu.with_memory_space_constraint(array, space) for array, space in ins]
    return pl.pallas_call(
        kernel,
        name=name,
        out_shape=[space(shape, dtype) for space, shape, dtype in outs],
        in_specs=[pl.BlockSpec(memory_space=space) for _, space in ins],
        out_specs=[pl.BlockSpec(memory_space=space) for space, _, _ in outs],
        scratch_shapes=[pltpu.VMEM(*pair) for pair in scratch]
        + ([pltpu.SemaphoreType.DMA((sems,))] if sems else []),
        input_output_aliases=aliases or {},
        compiler_params=pltpu.CompilerParams(vmem_limit_bytes=mib * MIB),
        cost_estimate=pl.CostEstimate(flops=cost, bytes_accessed=8 * MIB, transcendentals=0),
    )(*operands)


def in_hbm(*arrays):
    return [(array, pltpu.HBM) for array in arrays]


def anywhere(*arrays):
    return [(array, pl.ANY) for array in arrays]


def in_vmem(*arrays):
    return [(array, pltpu.VMEM) for array in arrays]


def vmem(shapes):
    return [(pltpu.VMEM, *pair) for pair in shapes]


def small_row(small_ref, place):
    return small_ref[:, place * D : (place + 1) * D]


def rope_tables():
    inv_freq = 10000.0 ** (-2.0 * np.arange(ROT // 2) / ROT)
    angles = inv_freq[:, None] * np.arange(SEQ)[None, :]
    return np.concatenate([np.cos(angles), np.sin(angles)], axis=0).astype(np.float32)


class Copies:
    def __init__(self, sems):
        self.sems = sems
        self.count = 0

    def start(self, src, dst):
        copy = pltpu.make_async_copy(src, dst, self.sems.at[self.count])
        self.count += 1
        copy.start()
        return copy

    def of_layer(self, here, own, other, dst):
        sem = self.sems.at[self.count]
        self.count += 1
        copy = pltpu.make_async_copy(own, dst, sem)

        @pl.when(here)
        def _():
            copy.start()

        @pl.when(jnp.logical_not(here))
        def _():
            pltpu.make_async_copy(other, dst, sem).start()

        return copy


def wait_all(*copies):
    for copy in copies:
        copy.wait()


def normalized(hidden):
    mean = jnp.mean(hidden, axis=-1, keepdims=True)
    centered = hidden - mean
    variance = jnp.mean(centered * centered, axis=-1, keepdims=True)
    scale = lax.rsqrt(variance + 1e-05)
    return centered * scale, scale


def rope_heads(rows, cos, sin):
    parts = []
    for head in range(rows.shape[0] // HD):
        base = head * HD
        lead = rows[base : base + 8]
        tail = rows[base + 8 : base + 16]
        parts += [lead * cos - tail * sin, tail * cos + lead * sin, rows[base + 16 : base + HD]]
    return jnp.concatenate(parts, axis=0)


def fill_mask(seg_ref, mask_ref):
    seg_row = seg_ref[...].astype(f32)
    seg_col = jnp.transpose(jnp.broadcast_to(seg_row, (8, SEQ)))[:, 0:1]
    for block in range(BLOCKS):
        for key_block in range(block + 1 - LIVE[block], block + 1):
            seen = seg_col[key_block * BLK : (key_block + 1) * BLK] == (
                seg_row[:, block * BLK : (block + 1) * BLK]
            )
            if key_block == block:
                key_pos = lax.broadcasted_iota(jnp.int32, (BLK, BLK), 0)
                query_pos = lax.broadcasted_iota(jnp.int32, (BLK, BLK), 1)
                seen = seen & (key_pos <= query_pos)
            start = P_START[block] + (key_block - (block + 1 - LIVE[block])) * BLK
            mask_ref[start : start + BLK, :] = jnp.where(seen, 0.0, NEG)


def project_heads(normed, w_ref, small_ref, cos, sin, q_t, k_t, k_m, v_m, v_t):
    bias = small_row(small_ref, B_QKV)
    rows = dot(normed, w_ref[:, :D], NN) + bias
    q_t[...] = (rope_heads(jnp.transpose(rows), cos, sin) * Q_SCALE).astype(bf16)
    bias = small_row(small_ref, B_QKV + 1)
    rows = dot(normed, w_ref[:, D : 2 * D], NN) + bias
    keys = rope_heads(jnp.transpose(rows), cos, sin).astype(bf16)
    k_t[...] = keys
    k_m[...] = jnp.transpose(keys)
    bias = small_row(small_ref, B_QKV + 2)
    values = (dot(normed, w_ref[:, 2 * D :], NN) + bias).astype(bf16)
    v_m[...] = values
    v_t[...] = jnp.transpose(values)


def block_diagonal(pair_rows):
    zeros = jnp.zeros((HD, BLK), pair_rows.dtype)
    return jnp.concatenate(
        [
            jnp.concatenate([pair_rows[:HD], zeros], axis=1),
            jnp.concatenate([zeros, pair_rows[HD:]], axis=1),
        ],
        axis=0,
    )


def from_diagonal(both):
    return jnp.concatenate([both[:HD, :BLK], both[HD:, BLK:]], axis=0)


def per_head(row, rows=HD):
    return jnp.concatenate(
        [
            jnp.broadcast_to(row[:, :BLK], (rows, BLK)),
            jnp.broadcast_to(row[:, BLK:], (rows, BLK)),
        ],
        axis=0,
    )


def geometry(block):
    live = LIVE[block] * BLK
    end = (block + 1) * BLK
    start = P_START[block]
    return slice(end - live, end), slice(block * BLK, end), slice(start, start + live)


def pair_rows(pair):
    return slice(pair * BLK, (pair + 1) * BLK)


def both_heads(rows, tokens):
    return jnp.concatenate([rows[:PAD, tokens], rows[PAD:, tokens]], axis=1)


def attend(q_t, k_m, v_t, pre_k, pre_v, mask_ref, p_ref, pp_ref, inv_ref, mixed_ref):
    real = lax.rem(lax.broadcasted_iota(jnp.int32, (2 * PAD, 1), 0), PAD) < PREFIX
    pad_mask = jnp.where(real, 0.0, NEG)

    def score(feats, block):
        keys, tokens, rows = geometry(block)
        queries = block_diagonal(q_t[feats, tokens])
        mask = mask_ref[rows, :]
        return dot(k_m[keys, feats], queries, NN) + jnp.concatenate([mask, mask], axis=1)

    def soften(pair, block, scores, pre_scores):
        _, tokens, rows = geometry(block)
        pre_scores = both_heads(pre_scores, tokens)
        peak = jnp.maximum(
            jnp.max(scores, axis=0, keepdims=True), jnp.max(pre_scores, axis=0, keepdims=True)
        )
        expo = jnp.exp2(scores - peak).astype(bf16)
        pre_expo = jnp.exp2(pre_scores - peak)
        p_ref[pair, rows, :] = expo
        pp_ref[pair, :PAD, tokens] = pre_expo[:, :BLK].astype(bf16)
        pp_ref[pair, PAD:, tokens] = pre_expo[:, BLK:].astype(bf16)
        return expo, jnp.sum(pre_expo, axis=0, keepdims=True)

    def mix(pair, block, pre_mixed, expo, pre_total):
        feats = pair_rows(pair)
        keys, tokens, _ = geometry(block)
        ones = jnp.ones((PAD, expo.shape[0]), bf16)
        mixed = dot(jnp.concatenate([v_t[feats, keys], ones], axis=0), expo, NN)
        inverse = 1.0 / (mixed[BLK : BLK + 1] + pre_total)
        inv_ref[2 * pair : 2 * pair + 1, tokens] = inverse[:, :BLK]
        inv_ref[2 * pair + 1 : 2 * pair + 2, tokens] = inverse[:, BLK:]
        mixed = from_diagonal(mixed[:BLK]) + pre_mixed[:, tokens]
        mixed_ref[feats, tokens] = (mixed * per_head(inverse)).astype(bf16)

    def score_all(pair):
        feats = pair_rows(pair)
        pre_scores = dot(pre_k[:, feats], q_t[feats, :], NN) + pad_mask
        return pre_scores, [score(feats, block) for block in range(BLOCKS)]

    def mix_all(pair, soft):
        pre_mixed = dot(pre_v[:, pair_rows(pair)], pp_ref[pair], TN)
        for block in range(BLOCKS):
            mix(pair, block, pre_mixed, *soft[block])

    ahead, behind = score_all(0), None
    for pair in range(PAIRS):
        pre_scores, scores = ahead
        if pair + 1 < PAIRS:
            ahead = score_all(pair + 1)
        soft = [soften(pair, block, scores[block], pre_scores) for block in range(BLOCKS)]
        if behind is not None:
            mix_all(*behind)
        behind = (pair, soft)
    mix_all(*behind)


def prefix_back(w_attn, grad, q_t, pre_v, pp_ref, inv_ref, mixed_ref, scaled_ref, inner_ref, pre_ds_ref, turned,
                pre_grad, pre_row):
    turned[...] = jnp.transpose(grad)

    def scale(pair):
        grad_mixed = dot(w_attn[pair_rows(pair), :], turned[...], NN)
        inner = []
        for place in range(2):
            head = 2 * pair + place
            rows = slice(head * HD, (head + 1) * HD)
            scaled = grad_mixed[place * HD : (place + 1) * HD] * inv_ref[head : head + 1, :]
            scaled = scaled.astype(bf16)
            scaled_ref[rows, :] = scaled
            products = scaled.astype(f32) * mixed_ref[rows, :].astype(f32)
            inner.append(jnp.sum(products, axis=0, keepdims=True))
            inner_ref[head : head + 1, :] = inner[-1]
        return jnp.concatenate([jnp.broadcast_to(row, (PAD, SEQ)) for row in inner], axis=0)

    pairs = range(PAIRS)
    inner = [scale(pair) for pair in pairs]
    grad_probs = [dot(pre_v[:, pair_rows(pair)], scaled_ref[pair_rows(pair), :], NN) for pair in pairs]
    for pair in pairs:
        probs = pp_ref[pair].astype(f32)
        pre_ds_ref[pair] = (probs * (grad_probs[pair] - inner[pair])).astype(bf16)
    keys = [dot(q_t[pair_rows(pair), :], pre_ds_ref[pair], NT) for pair in pairs]
    values = [dot(scaled_ref[pair_rows(pair), :], pp_ref[pair], NT) for pair in pairs]
    first_head = lax.rem(lax.broadcasted_iota(jnp.int32, (1, D), 1), BLK) < HD

    def own_head(parts):
        both = jnp.transpose(jnp.concatenate(parts, axis=0))
        return jnp.where(first_head, both[:PREFIX], both[PAD : PAD + PREFIX])

    pre_grad[pre_row : pre_row + PREFIX, :] = own_head(keys) * K_BACK
    pre_grad[pre_row + PREFIX : pre_row + 2 * PREFIX, :] = own_head(values)


def attend_back(scaled_ref, inner_ref, pre_ds_ref, q_t, k_t, v_m, pre_k, p_ref, dq_ref, dk_ref, dv_ref):
    def value_grads(feats, block):
        keys, tokens, _ = geometry(block)
        grads = block_diagonal(scaled_ref[feats, tokens])
        return grads, dot(v_m[keys, feats], grads, NN)

    def score_grads(pair, block, grad_probs):
        _, tokens, rows = geometry(block)
        inner = jnp.concatenate(
            [inner_ref[2 * pair : 2 * pair + 1, tokens], inner_ref[2 * pair + 1 : 2 * pair + 2, tokens]],
            axis=1,
        )
        return (p_ref[pair, rows, :].astype(f32) * (grad_probs - inner)).astype(bf16)

    def out_grads(pair, feats, block, pre_dq, grads, grad_scores):
        keys, tokens, rows = geometry(block)
        queries = block_diagonal(q_t[feats, tokens])
        dq_ref[feats, tokens] = (
            from_diagonal(dot(k_t[feats, keys], grad_scores, NN)) + pre_dq[:, tokens]
        )
        return dot(queries, grad_scores, NT), dot(grads, p_ref[pair, rows, :], NT)

    def by_keys(outs, which, key_block):
        total = None
        for block in range(BLOCKS):
            place = key_block - (block + 1 - LIVE[block])
            if 0 <= place < LIVE[block]:
                part = outs[block][which][:, place * BLK : (place + 1) * BLK]
                total = part if total is None else total + part
        return total

    for pair in range(PAIRS):
        feats = pair_rows(pair)
        first = [value_grads(feats, block) for block in range(BLOCKS)]
        second = [score_grads(pair, block, first[block][1]) for block in range(BLOCKS)]
        pre_dq = dot(pre_k[:, feats], pre_ds_ref[pair], TN)
        outs = [
            out_grads(pair, feats, block, pre_dq, first[block][0], second[block])
            for block in range(BLOCKS)
        ]
        for key_block in range(BLOCKS):
            keys = slice(key_block * BLK, (key_block + 1) * BLK)
            dk_ref[feats, keys] = by_keys(outs, 0, key_block)
            dv_ref[feats, keys] = by_keys(outs, 1, key_block)


def pack_grads(dq_ref, dk_ref, dv_ref, cos, sin, packed_t):
    packed_t[:D, :] = (rope_heads(dq_ref[...], cos, -sin) * Q_BACK).astype(bf16)
    packed_t[D : 2 * D, :] = (rope_heads(dk_ref[...], cos, -sin) * K_BACK).astype(bf16)
    packed_t[2 * D :, :] = dv_ref[...].astype(bf16)


ROOT_HALF = 0.5**0.5


def gelu_both(scaled):
    cdf = ROOT_HALF + ROOT_HALF * lax.erf(scaled)
    density = jnp.exp2(scaled * scaled * (-LOG2E)) * (2.0 / math.sqrt(2.0 * math.pi))
    return scaled * cdf, cdf + scaled * density


FF_CHUNK = 512
FF_ROWS = 256


def second_norm(hat, small_ref):
    gain = small_row(small_ref, G2) * ROOT_HALF
    return (hat * gain + small_row(small_ref, B2) * ROOT_HALF).astype(bf16)


def chunk_of(index):
    return slice(index * FF_CHUNK, (index + 1) * FF_CHUNK)


def feed_in(normed, w_ref, small_ref, act_ref, slope_ref, between):
    for chunk in range(FF // FF_CHUNK):
        cols = chunk_of(chunk)
        bias = small_row(small_ref, B_IN + chunk) * ROOT_HALF
        between(chunk)
        for start in range(0, SEQ, FF_ROWS):
            rows = slice(start, start + FF_ROWS)
            act, slope = gelu_both(dot(normed[rows], w_ref[:, cols], NN) + bias)
            act_ref[rows, cols] = act.astype(bf16)
            slope_ref[rows, cols] = slope.astype(bf16)


def feed_both(normed, grad, w_in, w_out, small_ref, act_ref):
    total = jnp.zeros((SEQ, D), f32)
    for chunk in range(FF // FF_CHUNK):
        cols = chunk_of(chunk)
        bias = small_row(small_ref, B_IN + chunk) * ROOT_HALF
        slopes = []
        for start in range(0, SEQ, FF_ROWS):
            rows = slice(start, start + FF_ROWS)
            act, slope = gelu_both(dot(normed[rows], w_in[:, cols], NN) + bias)
            act_ref[rows, cols] = act.astype(bf16)
            slopes.append(slope.astype(bf16))
        grad_act = dot(grad, w_out[cols, :], NT)
        grad_before = (grad_act * jnp.concatenate(slopes, axis=0).astype(f32)).astype(bf16)
        total = total + dot(grad_before, w_in[:, cols], NT)
    return total * ROOT_HALF


def layer_result(hidden, mixed_t, w_attn, act_ref, w_out, small_ref):
    attn_out = dot(jnp.transpose(mixed_t), w_attn, NN) + small_row(small_ref, B_ATTN)
    ff_out = dot(act_ref[...], w_out, NN) + small_row(small_ref, B_OUT)
    return hidden + attn_out + ff_out


def feed_back(grad, w_out, w_in, slope_ref):
    total = jnp.zeros((SEQ, D), f32)
    for chunk in range(FF // FF_CHUNK):
        cols = chunk_of(chunk)
        grad_act = dot(grad, w_out[cols, :], NT)
        grad_before = (grad_act * slope_ref[:, cols].astype(f32)).astype(bf16)
        total = total + dot(grad_before, w_in[:, cols], NT)
    return total * ROOT_HALF


def norms_back(grad, hat, scale, grad_two, packed_t, w_qkv, small_ref, out_ref):
    halves_of = [slice(start, start + FF_ROWS) for start in range(0, SEQ, FF_ROWS)]
    products = [dot(w_qkv, packed_t[:, tokens], NN) for tokens in halves_of]
    for tokens, product in zip(halves_of, products):
        here = hat[tokens, :]
        grad_hat = jnp.transpose(product) * small_row(small_ref, G1)
        grad_hat = grad_hat + grad_two[tokens, :] * small_row(small_ref, G2)
        mean_one = jnp.mean(grad_hat, axis=-1, keepdims=True)
        mean_two = jnp.mean(grad_hat * here, axis=-1, keepdims=True)
        change = scale[tokens] * (grad_hat - mean_one - here * mean_two)
        out_ref[tokens, :] = grad[tokens, :].astype(f32) + change


def halves(values):
    high = values.astype(bf16)
    return high, (values - high.astype(f32)).astype(bf16)


def padded(values):
    return jnp.concatenate([values, jnp.zeros((PAD - PREFIX, values.shape[1]), f32)], axis=0)


def few_rows_dot(left, right):
    left_high, left_rest = halves(padded(left))
    right_high, right_rest = halves(right)
    both = dot(jnp.concatenate([left_high, left_rest], axis=0), right_high, NN)
    return both[:PAD] + both[PAD:] + dot(left_high, right_rest, NN)


def stacked_dot(left, right):
    left_high, left_rest = halves(padded(left))
    right_high, right_rest = halves(padded(right))
    return dot(
        jnp.concatenate([left_high, left_high, left_rest], axis=0),
        jnp.concatenate([right_high, right_rest, right_high], axis=0),
        TN,
    )


def small_kernel(gain_one, shift_one, gain_two, shift_two, attn_b, out_b, qkv_b, in_b, packed, sems):
    copies = Copies(sems)
    places = [(gain_one, 0), (shift_one, 1), (gain_two, 2), (shift_two, 3), (attn_b, 4), (out_b, 5)]
    places += [(qkv_b, 6), (in_b, 9)]
    wait_all(
        *[
            copies.start(row, packed.at[:, place * D : place * D + row.shape[1]])
            for row, place in places
        ]
    )


def small_call(*arrays):
    (packed,) = call_kernel(
        small_kernel, "small_parameters", in_hbm(*arrays), vmem([((1, SMALL), f32)]), [], 8, LATE_MIB, SMALL
    )
    return packed


def prefix_state(units, layer, part, out_w, out_b, low, wide):
    real = lax.broadcasted_iota(jnp.int32, (PAD, 1), 0) < PREFIX
    first_head = lax.rem(lax.broadcasted_iota(jnp.int32, (1, D), 1), BLK) < HD
    cols = slice(part * D, (part + 1) * D)
    bias = out_b[:, (2 * layer + part) * D : (2 * layer + part + 1) * D]
    high, rest = halves(padded(units))
    wide[:, cols] = out_w[:, cols].astype(bf16)
    both = dot(jnp.concatenate([high, rest], axis=0), wide[:, cols], NN)
    states = jnp.where(real, both[:PAD] + both[PAD:] + bias, 0.0)
    low[part, :PAD, :] = jnp.where(first_head, states, 0.0).astype(bf16)
    low[part, PAD:, :] = jnp.where(first_head, 0.0, states).astype(bf16)


def layer_parts(copies, layer, out_hbm, out_w):
    return [
        copies.start(
            out_hbm.at[:, (2 * layer + part) * D : (2 * layer + part + 1) * D],
            out_w.at[:, part * D : (part + 1) * D],
        )
        for part in range(2)
    ]


OPENING_SHAPES = (
    ((SEQ, D), bf16),
    ((SEQ, D), f32),
    ((P_ROWS, BLK), f32),
    ((2, 2 * PAD, D), bf16),
    ((PREFIX, D), f32),
    ((D, 2 * D), bf16),
    ((D, D), bf16),
    ((D, D), bf16),
    ((2 * 8, SEQ), f32),
    ((D, 3 * D), bf16),
)


def opening_kernel(x_hbm, seg_hbm, embed_hbm, up_hbm, up_b_hbm, out_hbm, out_b_hbm, tables_hbm, qkv_hbm,
                   x_ref, hat, mask, low, hidden, wide, up_high, up_rest, tables, own_qkv, seg, embed, up_w, up_b,
                   out_w, out_b, sems):
    section = lax.axis_index("pipe")
    copies = Copies(sems)
    x_copy = copies.start(x_hbm.at[section, 0], x_ref)
    seg_copy = copies.start(seg_hbm.at[section], seg)
    prefix_copies = [
        copies.start(src, dst)
        for src, dst in ((embed_hbm, embed), (up_hbm, up_w), (up_b_hbm, up_b.at[0]), (out_b_hbm, out_b.at[0]))
    ]
    parts = layer_parts(copies, 0, out_hbm, out_w)
    late = [copies.start(tables_hbm, tables), copies.start(qkv_hbm.at[0], own_qkv)]
    seg_copy.wait()
    fill_mask(seg, mask)
    x_copy.wait()
    hat[...], _ = normalized(x_ref[...].astype(f32))
    wait_all(*prefix_copies)
    units = jnp.tanh(few_rows_dot(embed[...], up_w[...])[:PREFIX] + up_b[...])
    hidden[...] = units
    up_high[...], up_rest[...] = halves(up_w[...])
    for part in range(2):
        parts[part].wait()
        prefix_state(units, 0, part, out_w, out_b, low, wide)
    wait_all(*late)


def opening_call(*arrays):
    scratch = [
        ((1, SEQ), jnp.int32),
        ((PREFIX, D), f32),
        ((D, D), f32),
        ((1, D), f32),
        ((D, 2 * D), f32),
        ((1, 4 * D), f32),
    ]
    return call_kernel(
        opening_kernel, "opening", in_hbm(*arrays), vmem(OPENING_SHAPES), scratch, 12, EARLY_MIB,
        2 * 6 * PAD * D * 5 * D,
    )


HEAD_SHAPES = (
    ((D, SEQ), bf16),
    ((D, SEQ), bf16),
    ((SEQ, D), bf16),
    ((PAIRS, P_ROWS, 2 * BLK), bf16),
    ((PAIRS, 2 * PAD, SEQ), bf16),
    ((HEADS, SEQ), f32),
    ((D, SEQ), bf16),
)
FIRST_SHAPES = HEAD_SHAPES + (
    ((SEQ, D), bf16),
    ((2, 1, SMALL), f32),
    ((2, D, 3 * D), bf16),
    ((2, D, D), bf16),
    ((2, D, FF), bf16),
    ((2, FF, D), bf16),
    ((SEQ, D), bf16),
    ((D, 2 * D), f32),
    ((1, 4 * D), f32),
)


def first_kernel(own_small, other_small, own_qkv, other_qkv, hat_ref, mask, low, tables,
                 attn_hbm, ff_in_hbm, ff_out_hbm, cot_hbm,
                 out_hbm, out_b_hbm,
                 q_t, k_t, v_m, p_ref, pp_ref, inv_ref, mixed_ref, two_ref, small, w_qkv, w_attn, w_in,
                 w_out, cot_ref, out_w, out_b, k_m, v_t, sems):
    section = lax.axis_index("pipe")
    copies = Copies(sems)
    now = [
        copies.start(own_small, small.at[section]),
        copies.start(other_small, small.at[1 - section]),
        copies.start(own_qkv, w_qkv.at[section]),
        copies.start(other_qkv.at[0], w_qkv.at[1 - section]),
    ]
    parts = layer_parts(copies, 1, out_hbm, out_w)
    later = [
        copies.start(ff_in_hbm.at[0], w_in.at[section]),
        copies.start(attn_hbm.at[0], w_attn.at[section]),
        copies.start(out_b_hbm, out_b.at[0]),
        copies.start(ff_out_hbm.at[0], w_out.at[section]),
        copies.start(cot_hbm.at[section, 0], cot_ref),
    ]
    wait_all(*now)
    hat = hat_ref[...]
    zero = small.at[0]
    normed = (hat * small_row(zero, G1) + small_row(zero, B1)).astype(bf16)
    two_ref[...] = second_norm(hat, zero)
    project_heads(normed, w_qkv.at[0], zero, tables[:8, :], tables[8:, :], q_t, k_t, k_m, v_m, v_t)
    attend(q_t, k_m, v_t, low.at[0], low.at[1], mask, p_ref, pp_ref, inv_ref, mixed_ref)
    wait_all(*later, *parts)


def first_call(ready, *arrays):
    return call_kernel(
        first_kernel, "first_attention", in_vmem(*ready) + in_hbm(*arrays), vmem(FIRST_SHAPES),
        [((SEQ, D), bf16), ((D, SEQ), bf16)], 11, EARLY_MIB, 200 * SEQ * D * 3 * D,
    )


def feed_kernel(two, small, other_in, w_in_before, hidden, out_w, out_b, act_ref, slope_ref, w_in, low_one, wide_one,
                sems):
    wait_all(Copies(sems).start(other_in.at[0], w_in.at[1 - lax.axis_index("pipe")]))

    def between(chunk):
        if chunk in (0, 2):
            prefix_state(hidden[...], 1, chunk // 2, out_w, out_b, low_one, wide_one)

    feed_in(two[...], w_in.at[0], small.at[0], act_ref, slope_ref, between)


def feed_call(*arrays):
    shapes = [((SEQ, FF), bf16), ((SEQ, FF), bf16), ((2, D, FF), bf16)]
    shapes += [((2, 2 * PAD, D), bf16), ((D, 2 * D), bf16)]
    return call_kernel(
        feed_kernel, "first_feed", in_vmem(*arrays), vmem(shapes), [], 1, LATE_MIB, 2 * SEQ * D * FF,
        {3: 2},
    )


WEIGHT_SHAPES = (((D, 3 * D), bf16), ((D, D), bf16), ((D, FF), bf16), ((FF, D), bf16))


MIDDLE_OUTS = (
    ((SEQ, D), bf16),
    ((SEQ, FF), bf16),
    ((D, SEQ), bf16),
    ((SEQ, D), f32),
    ((SEQ, D), bf16),
    ((D, SEQ), bf16),
    ((HEADS, SEQ), f32),
    ((PAIRS, 2 * PAD, SEQ), bf16),
    ((4 * PREFIX, D), f32),
    ((2, D, D), bf16),
    ((2, FF, D), bf16),
)


def middle_kernel(w_attn_before, w_out_before, q0, pp0, inv0, mixed0, small, w_qkv, w_in,
                  other_attn, other_out, cot_ref, x_ref, act_zero, low, low_one, mask, tables,
                  h_one, act_one, mixed_one, grad_one, grad_low, scaled_zero, inner_zero, pre_ds_zero,
                  prefix_grad, w_attn, w_out,
                  q_t, k_t, v_m, p_ref, pp_ref, inv_ref, scaled, inner, pre_ds, turned, k_m, v_t,
                  dq, dk, dv, packed, sems):
    section = lax.axis_index("pipe")
    copies = Copies(sems)
    wait_all(
        copies.start(other_attn.at[0], w_attn.at[1 - section]),
        copies.start(other_out.at[0], w_out.at[1 - section]),
    )
    small_one = small.at[1]
    h_one[...] = layer_result(
        x_ref[...].astype(f32), mixed0[...], w_attn[0], act_zero, w_out[0], small.at[0]
    ).astype(bf16)

    cos, sin = tables[:8, :], tables[8:, :]
    hat, scale = normalized(h_one[...].astype(f32))
    grad_one[...] = hat
    normed = (hat * small_row(small_one, G1) + small_row(small_one, B1)).astype(bf16)
    two = second_norm(hat, small_one)
    project_heads(normed, w_qkv.at[1], small_one, cos, sin, q_t, k_t, k_m, v_m, v_t)
    attend(q_t, k_m, v_t, low_one.at[0], low_one.at[1], mask, p_ref, pp_ref, inv_ref, mixed_one)

    grad = cot_ref[...]
    grad_two = feed_both(two, grad, w_in.at[1], w_out.at[1], small_one, act_one)
    prefix_back(w_attn.at[1], grad, q_t, low_one.at[1], pp_ref, inv_ref, mixed_one, scaled, inner, pre_ds, turned,
                prefix_grad, 2 * PREFIX)
    attend_back(scaled, inner, pre_ds, q_t, k_t, v_m, low_one.at[0], p_ref, dq, dk, dv)
    pack_grads(dq, dk, dv, cos, sin, packed)
    norms_back(cot_ref, grad_one, scale, grad_two, packed, w_qkv[1], small_one, grad_one)
    grad_low[...] = grad_one[...].astype(bf16)

    prefix_back(w_attn.at[0], grad_low[...], q0, low.at[1], pp0, inv0, mixed0, scaled_zero, inner_zero,
                pre_ds_zero, turned, prefix_grad, 0)


def middle_call(*arrays):
    scratch = HEAD_SHAPES[:6] + (
        ((D, SEQ), bf16),
        ((HEADS, SEQ), f32),
        ((PAIRS, 2 * PAD, SEQ), bf16),
        ((D, SEQ), bf16),
        ((SEQ, D), bf16),
        ((D, SEQ), bf16),
        ((D, SEQ), f32),
        ((D, SEQ), f32),
        ((D, SEQ), f32),
        ((3 * D, SEQ), bf16),
    )
    return call_kernel(
        middle_kernel, "middle", in_vmem(*arrays), vmem(MIDDLE_OUTS), scratch, 2, MIDDLE_MIB,
        20 * SEQ * D * 6 * D, {0: 9, 1: 10},
    )


def hand_over(values, keep, send, sems):
    here = lax.axis_index("pipe") == 0
    copies = Copies(sems)
    wait_all(
        copies.of_layer(here, values[0], values[1], keep),
        copies.of_layer(here, values[1], values[0], send),
    )


def result_kernel(h_one, act, mixed, small, w_attn, w_out, keep, send, result, sems):
    result[...] = layer_result(
        h_one[...].astype(f32), mixed[...], w_attn[1], act, w_out[1], small.at[1]
    ).astype(bf16)
    hand_over((h_one, result), keep, send, sems)


def result_call(*arrays):
    return call_kernel(
        result_kernel, "layer_one_out", in_vmem(*arrays), vmem([((SEQ, D), bf16)] * 2),
        [((SEQ, D), bf16)], 2, LATE_MIB, 2 * SEQ * D * (D + FF),
    )


def heads_back_kernel(scaled, inner, pre_ds, q_t, k_t, v_m, low, p_ref, tables, packed, dq, dk, dv):
    attend_back(scaled, inner, pre_ds, q_t, k_t, v_m, low.at[0], p_ref, dq, dk, dv)
    pack_grads(dq, dk, dv, tables[:8, :], tables[8:, :], packed)


def heads_back_call(*arrays):
    return call_kernel(
        heads_back_kernel, "layer_zero_attention_back", in_vmem(*arrays), vmem([((3 * D, SEQ), bf16)]),
        [((D, SEQ), f32)] * 3, 0, LATE_MIB, 10 * SEQ * SEQ * D,
    )[0]


def feed_back_kernel(grad, slope, w_in, w_out, total):
    total[...] = feed_back(grad[...], w_out.at[0], w_in.at[0], slope)


def feed_back_call(*arrays):
    (total,) = call_kernel(
        feed_back_kernel, "layer_zero_feed_back", in_vmem(*arrays), vmem([((SEQ, D), f32)]), [], 0,
        LATE_MIB, 4 * SEQ * D * FF,
    )
    return total


def norms_kernel(x_ref, grad, two, packed, grad_one, small, w_qkv, keep, send, result, sems):
    hat, scale = normalized(x_ref[...].astype(f32))
    norms_back(grad, hat, scale, two, packed, w_qkv[0], small.at[0], result)
    hand_over((result, grad_one), keep, send, sems)


def norms_call(*arrays):
    return call_kernel(
        norms_kernel, "layer_zero_norms", in_vmem(*arrays), vmem([((SEQ, D), f32)] * 2),
        [((SEQ, D), f32)], 2, LATE_MIB, 6 * SEQ * D * D,
    )


def place_kernel(act, act_other, grad, grad_other, wide_zero, wide_one, up_high, up_rest,
                 act_out, grad_out, wide_t, up_high_t, up_rest_t, sems):
    section = lax.axis_index("pipe")
    copies = Copies(sems)
    placed = [
        copies.start(value, whole.at[0, where, 0])
        for value, whole, where in (
            (grad, grad_out, section),
            (grad_other, grad_out, 1 - section),
            (act, act_out, section),
            (act_other, act_out, 1 - section),
        )
    ]
    for part in range(4):
        cols = slice(part % 2 * D, (part % 2 + 1) * D)
        wide_t[part * D : (part + 1) * D, :] = jnp.transpose((wide_zero, wide_one)[part // 2][:, cols])
    up_high_t[...] = jnp.transpose(up_high[...])
    up_rest_t[...] = jnp.transpose(up_rest[...])
    wait_all(*placed)


def place_call(*arrays):
    outs = [(pltpu.HBM, (1, 2, 1, SEQ, D), bf16), (pltpu.HBM, (1, 2, 1, SEQ, D), f32)]
    outs += vmem([((4 * D, D), bf16), ((D, D), bf16), ((D, D), bf16)])
    return call_kernel(
        place_kernel, "place_outputs", in_vmem(*arrays), outs, [], 4, LATE_MIB, 2 * SEQ * D
    )


def final_kernel(col_width, grads_ref, hidden, embed, wide, up_high, up_rest, *refs):
    results, (d_embed, d_up, d_up_b, d_out, d_out_b, sems) = refs[:5], refs[5:]
    section = lax.axis_index("pipe")
    shard = lax.axis_index("dp")
    copies = Copies(sems)
    placed = []
    units = hidden[...]
    both = jnp.zeros((2 * PAD, D), f32)
    for part in range(4):
        high, rest = halves(padded(grads_ref[part * PREFIX : (part + 1) * PREFIX, :]))
        both = both + dot(
            jnp.concatenate([high, rest], axis=0), wide[part * D : (part + 1) * D, :], NN
        )
    grad_units = (both[:PAD] + both[PAD:])[:PREFIX]
    grad_pre = grad_units * (1.0 - units * units)
    d_up_b[...] = jnp.sum(grad_pre, axis=0, keepdims=True)
    d_up[...] = stacked_dot(embed[...], grad_pre)
    placed += [copies.start(d_up, results[1]), copies.start(d_up_b, results[2])]
    column = section * (2 * D) + shard * col_width
    own_cols = jnp.zeros((PREFIX, col_width), f32)
    for part in range(4):
        for piece in range(D // col_width):
            here = column == part * D + piece * col_width
            cols = slice(piece * col_width, (piece + 1) * col_width)
            rows = slice(part * PREFIX, (part + 1) * PREFIX)
            own_cols = jnp.where(here, grads_ref[rows, cols], own_cols)
    d_out[...] = stacked_dot(units, own_cols)
    d_out_b[...] = jnp.sum(own_cols, axis=0, keepdims=True)
    placed += [copies.start(d_out, results[3]), copies.start(d_out_b, results[4])]
    high, rest = halves(padded(grad_pre))
    both = dot(jnp.concatenate([high, rest], axis=0), up_high[...], NN)
    both = both[:PAD] + both[PAD:] + dot(high, up_rest[...], NN)
    d_embed[...] = both[:PREFIX]
    placed.append(copies.start(d_embed, results[0]))
    wait_all(*placed)


def final_call(col_width, *arrays):
    def body(*refs):
        final_kernel(col_width, *refs)

    shapes = [((PREFIX, D), f32), ((D, D), f32), ((1, D), f32), ((D, col_width), f32), ((1, col_width), f32)]
    return call_kernel(
        body, "reparam", in_vmem(*arrays), [(pltpu.HBM, *pair) for pair in shapes], shapes, 5, LATE_MIB,
        SEQ * D * D,
    )


def swapped(array_in):
    return lax.ppermute(array_in, "pipe", [(0, 1), (1, 0)])


def hops(axis):
    size = lax.axis_size(axis)
    steps = []
    step = 1
    while step < size:
        steps.append((axis, [(i, i ^ step) for i in range(size)]))
        step *= 2
    assert step == size
    return steps


def local(
    block_input,
    cotangent,
    segments,
    ln1_gain,
    ln1_shift,
    qkv_weight,
    qkv_bias,
    attn_weight,
    attn_bias,
    ln2_gain,
    ln2_shift,
    ff_in_weight,
    ff_in_bias,
    ff_out_weight,
    ff_out_bias,
    prefix_embed,
    up_weight,
    up_bias,
    out_weight,
    out_bias,
):
    other_qkv = swapped(qkv_weight)
    small = small_call(
        ln1_gain, ln1_shift, ln2_gain, ln2_shift, attn_bias, ff_out_bias, qkv_bias, ff_in_bias
    )
    other_small = swapped(small)
    small, prefix_embed = lax.optimization_barrier((small, prefix_embed))
    tables = jnp.asarray(rope_tables())
    _, *later = lax.optimization_barrier((small, attn_weight, ff_in_weight, ff_out_weight))
    other_attn, other_in, other_out = (swapped(weight) for weight in later)
    x_zero, hat_zero, mask, low, hidden_units, wide, up_high, up_rest, tables, own_qkv = opening_call(
        block_input, segments, prefix_embed, up_weight, up_bias, out_weight, out_bias, tables, qkv_weight
    )
    q0, k0, v0, p0, pp0, inv0, mixed0, two_zero, small, w_qkv, w_attn, w_in, w_out, cot, out_w, out_b = first_call(
        (small, other_small, own_qkv, other_qkv, hat_zero, mask, low, tables),
        attn_weight, ff_in_weight, ff_out_weight, cotangent, out_weight, out_bias,
    )
    act_zero, slope_zero, w_in, low_one, wide_one = feed_call(
        two_zero, small, other_in, w_in, hidden_units, out_w, out_b
    )
    (h_one, act_one, mixed_one, grad_one, grad_low, scaled_zero, inner_zero, pre_ds_zero, prefix_grad,
     w_attn, w_out) = middle_call(
        w_attn, w_out, q0, pp0, inv0, mixed0, small, w_qkv, w_in, other_attn, other_out, cot, x_zero,
        act_zero, low, low_one, mask, tables,
    )

    def layer_one_out(state):
        own, send = result_call(state["h_one"], act_one, mixed_one, small, w_attn, w_out)
        return dict(state, act_own=own, act_send=send)

    def layer_zero_attention(state):
        packed = heads_back_call(
            state["scaled"], inner_zero, pre_ds_zero, q0, k0, v0, low, p0, tables
        )
        return dict(state, packed=packed, act_other=swapped(state["act_send"]))

    def layer_zero_feed(state):
        return dict(state, two=feed_back_call(state["grad_low"], slope_zero, w_in, w_out))

    def layer_zero_norms(state):
        own, send = norms_call(x_zero, grad_low, state["two"], state["packed"], grad_one, small, w_qkv)
        return dict(state, grad_own=own, grad_send=send)

    def swap_grads(state):
        other = swapped(state["grad_send"])
        act, grad, *turned = place_call(
            state["act_own"], state["act_other"], state["grad_own"], other, wide, wide_one, up_high, up_rest
        )
        return {"wholes": (act, grad), "turned": turned}

    works = [layer_one_out, layer_zero_attention, layer_zero_feed, layer_zero_norms, swap_grads]
    state = {"h_one": h_one, "grad_low": grad_low, "scaled": scaled_zero}
    for axis, pairs in hops("pipe") + hops("dp") + hops("grp"):
        if axis == "pipe":
            moved = lax.ppermute(prefix_grad, axis, pairs)
        else:
            prefix_grad = lax.reduce_precision(prefix_grad, 8, 7)
            moved = lax.ppermute(prefix_grad.astype(bf16), axis, pairs)
        if works:
            state = works.pop(0)(state)
        prefix_grad, moved, state = lax.optimization_barrier((prefix_grad, moved, state))
        prefix_grad = prefix_grad + moved.astype(f32)
    for work in works:
        state = work(state)
    col_width = 2 * D // lax.axis_size("dp")
    grad_embed, grad_up, grad_up_b, grad_out, grad_out_b = final_call(
        col_width, prefix_grad, hidden_units, prefix_embed, *state["turned"]
    )
    activations, input_grads = state["wholes"]
    return (
        activations,
        input_grads,
        grad_embed,
        grad_up,
        grad_up_b[0],
        grad_out,
        grad_out_b[0],
    )


def solution(mesh):
    return jax.shard_map(
        local,
        mesh=mesh,
        in_specs=(
            P(None, ("grp", "dp"), None, None),
            P(None, ("grp", "dp"), None, None),
            P(None, ("grp", "dp"), None),
            P("pipe", None),
            P("pipe", None),
            P("pipe", None, None),
            P("pipe", None),
            P("pipe", None, None),
            P("pipe", None),
            P("pipe", None),
            P("pipe", None),
            P("pipe", None, None),
            P("pipe", None),
            P("pipe", None, None),
            P("pipe", None),
            P(),
            P(),
            P(),
            P(),
            P(),
        ),
        out_specs=(
            P("pipe", None, ("grp", "dp"), None, None),
            P("pipe", None, ("grp", "dp"), None, None),
            P(),
            P(),
            P(),
            P(None, ("pipe", "dp")),
            P(("pipe", "dp")),
        ),
        check_vma=False,
    )
```

```python
import math

import jax
import jax.numpy as jnp
import numpy as np
from jax import lax
from jax.experimental import pallas as pl
from jax.experimental.pallas import tpu as pltpu
from jax.sharding import PartitionSpec as P

D = 512
SEQ = 512
HEADS = 8
HD = 64
FF = 2048
ROT = 16
PREFIX = 10
PAD = 16
BLK = 128
BLOCKS = SEQ // BLK
PAIRS = HEADS // 2
LIVE = (1, 2, 3, 3)
P_ROWS = BLK * sum(LIVE)
P_START = (0, 128, 384, 768)

f32 = jnp.float32
bf16 = jnp.bfloat16
LOG2E = math.log2(math.e)
Q_SCALE = LOG2E * HD**-0.5
K_BACK = 1.0 / LOG2E
Q_BACK = HD**-0.5
NEG = -1e30

NN = (((1,), (0,)), ((), ()))
NT = (((1,), (1,)), ((), ()))
TN = (((0,), (0,)), ((), ()))

MIB = 1024 * 1024
EARLY_MIB = 24
MIDDLE_MIB = 23
LATE_MIB = 12

G1, B1, G2, B2, B_ATTN, B_OUT, B_QKV, B_IN = 0, 1, 2, 3, 4, 5, 6, 9
SMALL = 13 * D


def dot(left, right, dims):
    return lax.dot_general(left, right, dims, preferred_element_type=f32)


def call_kernel(kernel, name, ins, outs, scratch, sems, mib, cost, aliases=None):
    operands = [pltpu.with_memory_space_constraint(array, space) for array, space in ins]
    return pl.pallas_call(
        kernel,
        name=name,
        out_shape=[space(shape, dtype) for space, shape, dtype in outs],
        in_specs=[pl.BlockSpec(memory_space=space) for _, space in ins],
        out_specs=[pl.BlockSpec(memory_space=space) for space, _, _ in outs],
        scratch_shapes=[pltpu.VMEM(*pair) for pair in scratch]
        + ([pltpu.SemaphoreType.DMA((sems,))] if sems else []),
        input_output_aliases=aliases or {},
        compiler_params=pltpu.CompilerParams(vmem_limit_bytes=mib * MIB),
        cost_estimate=pl.CostEstimate(flops=cost, bytes_accessed=8 * MIB, transcendentals=0),
    )(*operands)


def in_hbm(*arrays):
    return [(array, pltpu.HBM) for array in arrays]


def anywhere(*arrays):
    return [(array, pl.ANY) for array in arrays]


def in_vmem(*arrays):
    return [(array, pltpu.VMEM) for array in arrays]


def vmem(shapes):
    return [(pltpu.VMEM, *pair) for pair in shapes]


def small_row(small_ref, place):
    return small_ref[:, place * D : (place + 1) * D]


def rope_tables():
    inv_freq = 10000.0 ** (-2.0 * np.arange(ROT // 2) / ROT)
    angles = inv_freq[:, None] * np.arange(SEQ)[None, :]
    return np.concatenate([np.cos(angles), np.sin(angles)], axis=0).astype(np.float32)


class Copies:
    def __init__(self, sems):
        self.sems = sems
        self.count = 0

    def start(self, src, dst):
        copy = pltpu.make_async_copy(src, dst, self.sems.at[self.count])
        self.count += 1
        copy.start()
        return copy

    def of_layer(self, here, own, other, dst):
        sem = self.sems.at[self.count]
        self.count += 1
        copy = pltpu.make_async_copy(own, dst, sem)

        @pl.when(here)
        def _():
            copy.start()

        @pl.when(jnp.logical_not(here))
        def _():
            pltpu.make_async_copy(other, dst, sem).start()

        return copy


def wait_all(*copies):
    for copy in copies:
        copy.wait()


def normalized(hidden):
    mean = jnp.mean(hidden, axis=-1, keepdims=True)
    centered = hidden - mean
    variance = jnp.mean(centered * centered, axis=-1, keepdims=True)
    scale = lax.rsqrt(variance + 1e-05)
    return centered * scale, scale


def rope_heads(rows, cos, sin):
    parts = []
    for head in range(rows.shape[0] // HD):
        base = head * HD
        lead = rows[base : base + 8]
        tail = rows[base + 8 : base + 16]
        parts += [lead * cos - tail * sin, tail * cos + lead * sin, rows[base + 16 : base + HD]]
    return jnp.concatenate(parts, axis=0)


def fill_mask(seg_ref, mask_ref):
    seg_row = seg_ref[...].astype(f32)
    seg_col = jnp.transpose(jnp.broadcast_to(seg_row, (8, SEQ)))[:, 0:1]
    for block in range(BLOCKS):
        for key_block in range(block + 1 - LIVE[block], block + 1):
            seen = seg_col[key_block * BLK : (key_block + 1) * BLK] == (
                seg_row[:, block * BLK : (block + 1) * BLK]
            )
            if key_block == block:
                key_pos = lax.broadcasted_iota(jnp.int32, (BLK, BLK), 0)
                query_pos = lax.broadcasted_iota(jnp.int32, (BLK, BLK), 1)
                seen = seen & (key_pos <= query_pos)
            start = P_START[block] + (key_block - (block + 1 - LIVE[block])) * BLK
            mask_ref[start : start + BLK, :] = jnp.where(seen, 0.0, NEG)


def project_heads(normed, w_ref, small_ref, cos, sin, q_t, k_t, k_m, v_m, v_t):
    bias = small_row(small_ref, B_QKV)
    rows = dot(normed, w_ref[:, :D], NN) + bias
    q_t[...] = (rope_heads(jnp.transpose(rows), cos, sin) * Q_SCALE).astype(bf16)
    bias = small_row(small_ref, B_QKV + 1)
    rows = dot(normed, w_ref[:, D : 2 * D], NN) + bias
    keys = rope_heads(jnp.transpose(rows), cos, sin).astype(bf16)
    k_t[...] = keys
    k_m[...] = jnp.transpose(keys)
    bias = small_row(small_ref, B_QKV + 2)
    values = (dot(normed, w_ref[:, 2 * D :], NN) + bias).astype(bf16)
    v_m[...] = values
    v_t[...] = jnp.transpose(values)


def block_diagonal(pair_rows):
    zeros = jnp.zeros((HD, BLK), pair_rows.dtype)
    return jnp.concatenate(
        [
            jnp.concatenate([pair_rows[:HD], zeros], axis=1),
            jnp.concatenate([zeros, pair_rows[HD:]], axis=1),
        ],
        axis=0,
    )


def from_diagonal(both):
    return jnp.concatenate([both[:HD, :BLK], both[HD:, BLK:]], axis=0)


def per_head(row, rows=HD):
    return jnp.concatenate(
        [
            jnp.broadcast_to(row[:, :BLK], (rows, BLK)),
            jnp.broadcast_to(row[:, BLK:], (rows, BLK)),
        ],
        axis=0,
    )


def geometry(block):
    live = LIVE[block] * BLK
    end = (block + 1) * BLK
    start = P_START[block]
    return slice(end - live, end), slice(block * BLK, end), slice(start, start + live)


def pair_rows(pair):
    return slice(pair * BLK, (pair + 1) * BLK)


def both_heads(rows, tokens):
    return jnp.concatenate([rows[:PAD, tokens], rows[PAD:, tokens]], axis=1)


def attend(q_t, k_m, v_t, pre_k, pre_v, mask_ref, p_ref, pp_ref, inv_ref, mixed_ref):
    real = lax.rem(lax.broadcasted_iota(jnp.int32, (2 * PAD, 1), 0), PAD) < PREFIX
    pad_mask = jnp.where(real, 0.0, NEG)

    def score(feats, block):
        keys, tokens, rows = geometry(block)
        queries = block_diagonal(q_t[feats, tokens])
        mask = mask_ref[rows, :]
        return dot(k_m[keys, feats], queries, NN) + jnp.concatenate([mask, mask], axis=1)

    def soften(pair, block, scores, pre_scores):
        _, tokens, rows = geometry(block)
        pre_scores = both_heads(pre_scores, tokens)
        peak = jnp.maximum(
            jnp.max(scores, axis=0, keepdims=True), jnp.max(pre_scores, axis=0, keepdims=True)
        )
        expo = jnp.exp2(scores - peak).astype(bf16)
        pre_expo = jnp.exp2(pre_scores - peak)
        p_ref[pair, rows, :] = expo
        pp_ref[pair, :PAD, tokens] = pre_expo[:, :BLK].astype(bf16)
        pp_ref[pair, PAD:, tokens] = pre_expo[:, BLK:].astype(bf16)
        return expo, jnp.sum(pre_expo, axis=0, keepdims=True)

    def mix(pair, block, pre_mixed, expo, pre_total):
        feats = pair_rows(pair)
        keys, tokens, _ = geometry(block)
        ones = jnp.ones((PAD, expo.shape[0]), bf16)
        mixed = dot(jnp.concatenate([v_t[feats, keys], ones], axis=0), expo, NN)
        inverse = 1.0 / (mixed[BLK : BLK + 1] + pre_total)
        inv_ref[2 * pair : 2 * pair + 1, tokens] = inverse[:, :BLK]
        inv_ref[2 * pair + 1 : 2 * pair + 2, tokens] = inverse[:, BLK:]
        mixed = from_diagonal(mixed[:BLK]) + pre_mixed[:, tokens]
        mixed_ref[feats, tokens] = (mixed * per_head(inverse)).astype(bf16)

    def score_all(pair):
        feats = pair_rows(pair)
        pre_scores = dot(pre_k[:, feats], q_t[feats, :], NN) + pad_mask
        return pre_scores, [score(feats, block) for block in range(BLOCKS)]

    def mix_all(pair, soft):
        pre_mixed = dot(pre_v[:, pair_rows(pair)], pp_ref[pair], TN)
        for block in range(BLOCKS):
            mix(pair, block, pre_mixed, *soft[block])

    ahead, behind = score_all(0), None
    for pair in range(PAIRS):
        pre_scores, scores = ahead
        if pair + 1 < PAIRS:
            ahead = score_all(pair + 1)
        soft = [soften(pair, block, scores[block], pre_scores) for block in range(BLOCKS)]
        if behind is not None:
            mix_all(*behind)
        behind = (pair, soft)
    mix_all(*behind)


def prefix_back(w_attn, grad, q_t, pre_v, pp_ref, inv_ref, mixed_ref, scaled_ref, inner_ref, pre_ds_ref, turned,
                pre_grad, pre_row):
    turned[...] = jnp.transpose(grad)

    def scale(pair):
        grad_mixed = dot(w_attn[pair_rows(pair), :], turned[...], NN)
        inner = []
        for place in range(2):
            head = 2 * pair + place
            rows = slice(head * HD, (head + 1) * HD)
            scaled = grad_mixed[place * HD : (place + 1) * HD] * inv_ref[head : head + 1, :]
            scaled = scaled.astype(bf16)
            scaled_ref[rows, :] = scaled
            products = scaled.astype(f32) * mixed_ref[rows, :].astype(f32)
            inner.append(jnp.sum(products, axis=0, keepdims=True))
            inner_ref[head : head + 1, :] = inner[-1]
        return jnp.concatenate([jnp.broadcast_to(row, (PAD, SEQ)) for row in inner], axis=0)

    pairs = range(PAIRS)
    inner = [scale(pair) for pair in pairs]
    grad_probs = [dot(pre_v[:, pair_rows(pair)], scaled_ref[pair_rows(pair), :], NN) for pair in pairs]
    for pair in pairs:
        probs = pp_ref[pair].astype(f32)
        pre_ds_ref[pair] = (probs * (grad_probs[pair] - inner[pair])).astype(bf16)
    keys = [dot(q_t[pair_rows(pair), :], pre_ds_ref[pair], NT) for pair in pairs]
    values = [dot(scaled_ref[pair_rows(pair), :], pp_ref[pair], NT) for pair in pairs]
    first_head = lax.rem(lax.broadcasted_iota(jnp.int32, (1, D), 1), BLK) < HD

    def own_head(parts):
        both = jnp.transpose(jnp.concatenate(parts, axis=0))
        return jnp.where(first_head, both[:PREFIX], both[PAD : PAD + PREFIX])

    pre_grad[pre_row : pre_row + PREFIX, :] = own_head(keys) * K_BACK
    pre_grad[pre_row + PREFIX : pre_row + 2 * PREFIX, :] = own_head(values)


def attend_back(scaled_ref, inner_ref, pre_ds_ref, q_t, k_t, v_m, pre_k, p_ref, dq_ref, dk_ref, dv_ref):
    def value_grads(feats, block):
        keys, tokens, _ = geometry(block)
        grads = block_diagonal(scaled_ref[feats, tokens])
        return grads, dot(v_m[keys, feats], grads, NN)

    def score_grads(pair, block, grad_probs):
        _, tokens, rows = geometry(block)
        inner = jnp.concatenate(
            [inner_ref[2 * pair : 2 * pair + 1, tokens], inner_ref[2 * pair + 1 : 2 * pair + 2, tokens]],
            axis=1,
        )
        return (p_ref[pair, rows, :].astype(f32) * (grad_probs - inner)).astype(bf16)

    def out_grads(pair, feats, block, pre_dq, grads, grad_scores):
        keys, tokens, rows = geometry(block)
        queries = block_diagonal(q_t[feats, tokens])
        dq_ref[feats, tokens] = (
            from_diagonal(dot(k_t[feats, keys], grad_scores, NN)) + pre_dq[:, tokens]
        )
        return dot(queries, grad_scores, NT), dot(grads, p_ref[pair, rows, :], NT)

    def by_keys(outs, which, key_block):
        total = None
        for block in range(BLOCKS):
            place = key_block - (block + 1 - LIVE[block])
            if 0 <= place < LIVE[block]:
                part = outs[block][which][:, place * BLK : (place + 1) * BLK]
                total = part if total is None else total + part
        return total

    for pair in range(PAIRS):
        feats = pair_rows(pair)
        first = [value_grads(feats, block) for block in range(BLOCKS)]
        second = [score_grads(pair, block, first[block][1]) for block in range(BLOCKS)]
        pre_dq = dot(pre_k[:, feats], pre_ds_ref[pair], TN)
        outs = [
            out_grads(pair, feats, block, pre_dq, first[block][0], second[block])
            for block in range(BLOCKS)
        ]
        for key_block in range(BLOCKS):
            keys = slice(key_block * BLK, (key_block + 1) * BLK)
            dk_ref[feats, keys] = by_keys(outs, 0, key_block)
            dv_ref[feats, keys] = by_keys(outs, 1, key_block)


def pack_grads(dq_ref, dk_ref, dv_ref, cos, sin, packed_t):
    packed_t[:D, :] = (rope_heads(dq_ref[...], cos, -sin) * Q_BACK).astype(bf16)
    packed_t[D : 2 * D, :] = (rope_heads(dk_ref[...], cos, -sin) * K_BACK).astype(bf16)
    packed_t[2 * D :, :] = dv_ref[...].astype(bf16)


ROOT_HALF = 0.5**0.5


def gelu_both(scaled):
    cdf = ROOT_HALF + ROOT_HALF * lax.erf(scaled)
    density = jnp.exp2(scaled * scaled * (-LOG2E)) * (2.0 / math.sqrt(2.0 * math.pi))
    return scaled * cdf, cdf + scaled * density


FF_CHUNK = 512
FF_ROWS = 256


def second_norm(hat, small_ref):
    gain = small_row(small_ref, G2) * ROOT_HALF
    return (hat * gain + small_row(small_ref, B2) * ROOT_HALF).astype(bf16)


def chunk_of(index):
    return slice(index * FF_CHUNK, (index + 1) * FF_CHUNK)


def feed_in(normed, w_ref, small_ref, act_ref, slope_ref):
    for chunk in range(FF // FF_CHUNK):
        cols = chunk_of(chunk)
        bias = small_row(small_ref, B_IN + chunk) * ROOT_HALF
        for start in range(0, SEQ, FF_ROWS):
            rows = slice(start, start + FF_ROWS)
            act, slope = gelu_both(dot(normed[rows], w_ref[:, cols], NN) + bias)
            act_ref[rows, cols] = act.astype(bf16)
            slope_ref[rows, cols] = slope.astype(bf16)


def feed_both(normed, grad, w_in, w_out, small_ref, act_ref):
    total = jnp.zeros((SEQ, D), f32)
    for chunk in range(FF // FF_CHUNK):
        cols = chunk_of(chunk)
        bias = small_row(small_ref, B_IN + chunk) * ROOT_HALF
        slopes = []
        for start in range(0, SEQ, FF_ROWS):
            rows = slice(start, start + FF_ROWS)
            act, slope = gelu_both(dot(normed[rows], w_in[:, cols], NN) + bias)
            act_ref[rows, cols] = act.astype(bf16)
            slopes.append(slope.astype(bf16))
        grad_act = dot(grad, w_out[cols, :], NT)
        grad_before = (grad_act * jnp.concatenate(slopes, axis=0).astype(f32)).astype(bf16)
        total = total + dot(grad_before, w_in[:, cols], NT)
    return total * ROOT_HALF


def layer_result(hidden, mixed_t, w_attn, act_ref, w_out, small_ref):
    attn_out = dot(jnp.transpose(mixed_t), w_attn, NN) + small_row(small_ref, B_ATTN)
    ff_out = dot(act_ref[...], w_out, NN) + small_row(small_ref, B_OUT)
    return hidden + attn_out + ff_out


def feed_back(grad, w_out, w_in, slope_ref):
    total = jnp.zeros((SEQ, D), f32)
    for chunk in range(FF // FF_CHUNK):
        cols = chunk_of(chunk)
        grad_act = dot(grad, w_out[cols, :], NT)
        grad_before = (grad_act * slope_ref[:, cols].astype(f32)).astype(bf16)
        total = total + dot(grad_before, w_in[:, cols], NT)
    return total * ROOT_HALF


def norms_back(grad, hat, scale, grad_two, packed_t, w_qkv, small_ref):
    grad_one = jnp.transpose(dot(w_qkv, packed_t, NN))
    grad_hat = (
        grad_one * small_row(small_ref, G1) + grad_two * small_row(small_ref, G2)
    )
    mean_one = jnp.mean(grad_hat, axis=-1, keepdims=True)
    mean_two = jnp.mean(grad_hat * hat, axis=-1, keepdims=True)
    return grad.astype(f32) + scale * (grad_hat - mean_one - hat * mean_two)


def halves(values):
    high = values.astype(bf16)
    return high, (values - high.astype(f32)).astype(bf16)


def padded(values):
    return jnp.concatenate([values, jnp.zeros((PAD - PREFIX, values.shape[1]), f32)], axis=0)


def few_rows_dot(left, right):
    left_high, left_rest = halves(padded(left))
    right_high, right_rest = halves(right)
    both = dot(jnp.concatenate([left_high, left_rest], axis=0), right_high, NN)
    return both[:PAD] + both[PAD:] + dot(left_high, right_rest, NN)


def stacked_dot(left, right):
    left_high, left_rest = halves(padded(left))
    right_high, right_rest = halves(padded(right))
    return dot(
        jnp.concatenate([left_high, left_high, left_rest], axis=0),
        jnp.concatenate([right_high, right_rest, right_high], axis=0),
        TN,
    )


def small_kernel(gain_one, shift_one, gain_two, shift_two, attn_b, out_b, qkv_b, in_b, packed, sems):
    copies = Copies(sems)
    places = [(gain_one, 0), (shift_one, 1), (gain_two, 2), (shift_two, 3), (attn_b, 4), (out_b, 5)]
    places += [(qkv_b, 6), (in_b, 9)]
    wait_all(
        *[
            copies.start(row, packed.at[:, place * D : place * D + row.shape[1]])
            for row, place in places
        ]
    )


def small_call(*arrays):
    (packed,) = call_kernel(
        small_kernel, "small_parameters", in_hbm(*arrays), vmem([((1, SMALL), f32)]), [], 8, LATE_MIB, SMALL
    )
    return packed


def prefix_states(embed, up_w, up_b, out_w, out_b, arrivals, hidden, low, wide, up_high, up_rest):
    units = jnp.tanh(few_rows_dot(embed[...], up_w[...])[:PREFIX] + up_b[...])
    hidden[...] = units
    up_high[...], up_rest[...] = halves(jnp.transpose(up_w[...]))
    real = lax.broadcasted_iota(jnp.int32, (PAD, 1), 0) < PREFIX
    first_head = lax.rem(lax.broadcasted_iota(jnp.int32, (1, D), 1), BLK) < HD
    for part in range(4):
        cols = slice(part * D, (part + 1) * D)
        arrivals[part].wait()
        states = jnp.where(real, few_rows_dot(units, out_w[:, cols]) + out_b[:, cols], 0.0)
        low[part, :PAD, :] = jnp.where(first_head, states, 0.0).astype(bf16)
        low[part, PAD:, :] = jnp.where(first_head, 0.0, states).astype(bf16)
        wide[cols, :] = jnp.transpose(out_w[:, cols].astype(bf16))


OPENING_SHAPES = (
    ((SEQ, D), bf16),
    ((SEQ, D), f32),
    ((P_ROWS, BLK), f32),
    ((4, 2 * PAD, D), bf16),
    ((PREFIX, D), f32),
    ((4 * D, D), bf16),
    ((D, D), bf16),
    ((D, D), bf16),
    ((2 * 8, SEQ), f32),
    ((D, 3 * D), bf16),
)


def opening_kernel(x_hbm, seg_hbm, embed_hbm, up_hbm, up_b_hbm, out_hbm, out_b_hbm, tables_hbm, qkv_hbm,
                   x_ref, hat, mask, low, hidden, wide, up_high, up_rest, tables, own_qkv, seg, embed, up_w, up_b,
                   out_w, out_b, sems):
    section = lax.axis_index("pipe")
    copies = Copies(sems)
    x_copy = copies.start(x_hbm.at[section, 0], x_ref)
    seg_copy = copies.start(seg_hbm.at[section], seg)
    prefix_copies = [
        copies.start(src, dst)
        for src, dst in ((embed_hbm, embed), (up_hbm, up_w), (up_b_hbm, up_b.at[0]), (out_b_hbm, out_b.at[0]))
    ]
    parts = [
        copies.start(out_hbm.at[:, i * D : (i + 1) * D], out_w.at[:, i * D : (i + 1) * D])
        for i in range(4)
    ]
    late = [copies.start(tables_hbm, tables), copies.start(qkv_hbm.at[0], own_qkv)]
    seg_copy.wait()
    fill_mask(seg, mask)
    x_copy.wait()
    hat[...], _ = normalized(x_ref[...].astype(f32))
    wait_all(*prefix_copies)
    prefix_states(embed, up_w, up_b, out_w, out_b, parts, hidden, low, wide, up_high, up_rest)
    wait_all(*late)


def opening_call(*arrays):
    scratch = [
        ((1, SEQ), jnp.int32),
        ((PREFIX, D), f32),
        ((D, D), f32),
        ((1, D), f32),
        ((D, 4 * D), f32),
        ((1, 4 * D), f32),
    ]
    return call_kernel(
        opening_kernel, "opening", in_hbm(*arrays), vmem(OPENING_SHAPES), scratch, 12, EARLY_MIB,
        2 * 6 * PAD * D * 5 * D,
    )


HEAD_SHAPES = (
    ((D, SEQ), bf16),
    ((D, SEQ), bf16),
    ((SEQ, D), bf16),
    ((PAIRS, P_ROWS, 2 * BLK), bf16),
    ((PAIRS, 2 * PAD, SEQ), bf16),
    ((HEADS, SEQ), f32),
    ((D, SEQ), bf16),
)
FIRST_SHAPES = HEAD_SHAPES + (
    ((SEQ, D), bf16),
    ((2, 1, SMALL), f32),
    ((2, D, 3 * D), bf16),
    ((2, D, D), bf16),
    ((2, D, FF), bf16),
    ((2, FF, D), bf16),
    ((SEQ, D), bf16),
)


def first_kernel(own_small, other_small, own_qkv, other_qkv, hat_ref, mask, low, tables,
                 attn_hbm, ff_in_hbm, ff_out_hbm, cot_hbm,
                 q_t, k_t, v_m, p_ref, pp_ref, inv_ref, mixed_ref, two_ref, small, w_qkv, w_attn, w_in,
                 w_out, cot_ref, k_m, v_t, sems):
    section = lax.axis_index("pipe")
    copies = Copies(sems)
    now = [
        copies.start(own_small, small.at[section]),
        copies.start(other_small, small.at[1 - section]),
        copies.start(own_qkv, w_qkv.at[section]),
        copies.start(other_qkv.at[0], w_qkv.at[1 - section]),
    ]
    later = [
        copies.start(ff_in_hbm.at[0], w_in.at[section]),
        copies.start(attn_hbm.at[0], w_attn.at[section]),
        copies.start(ff_out_hbm.at[0], w_out.at[section]),
        copies.start(cot_hbm.at[section, 0], cot_ref),
    ]
    wait_all(*now)
    hat = hat_ref[...]
    zero = small.at[0]
    normed = (hat * small_row(zero, G1) + small_row(zero, B1)).astype(bf16)
    two_ref[...] = second_norm(hat, zero)
    project_heads(normed, w_qkv.at[0], zero, tables[:8, :], tables[8:, :], q_t, k_t, k_m, v_m, v_t)
    attend(q_t, k_m, v_t, low.at[0], low.at[1], mask, p_ref, pp_ref, inv_ref, mixed_ref)
    wait_all(*later)


def first_call(ready, *arrays):
    return call_kernel(
        first_kernel, "first_attention", in_vmem(*ready) + in_hbm(*arrays), vmem(FIRST_SHAPES),
        [((SEQ, D), bf16), ((D, SEQ), bf16)], 8, EARLY_MIB, 200 * SEQ * D * 3 * D,
    )


def feed_kernel(two, small, other_in, w_in_before, act_ref, slope_ref, w_in, sems):
    wait_all(Copies(sems).start(other_in.at[0], w_in.at[1 - lax.axis_index("pipe")]))
    feed_in(two[...], w_in.at[0], small.at[0], act_ref, slope_ref)


def feed_call(*arrays):
    shapes = [((SEQ, FF), bf16), ((SEQ, FF), bf16), ((2, D, FF), bf16)]
    return call_kernel(
        feed_kernel, "first_feed", in_vmem(*arrays), vmem(shapes), [], 1, LATE_MIB, 2 * SEQ * D * FF,
        {3: 2},
    )


WEIGHT_SHAPES = (((D, 3 * D), bf16), ((D, D), bf16), ((D, FF), bf16), ((FF, D), bf16))


MIDDLE_OUTS = (
    ((SEQ, D), bf16),
    ((SEQ, FF), bf16),
    ((D, SEQ), bf16),
    ((SEQ, D), f32),
    ((SEQ, D), bf16),
    ((D, SEQ), bf16),
    ((HEADS, SEQ), f32),
    ((PAIRS, 2 * PAD, SEQ), bf16),
    ((4 * PREFIX, D), f32),
    ((2, D, D), bf16),
    ((2, FF, D), bf16),
)


def middle_kernel(w_attn_before, w_out_before, q0, pp0, inv0, mixed0, small, w_qkv, w_in,
                  other_attn, other_out, cot_ref, x_ref, act_zero, low, mask, tables,
                  h_one, act_one, mixed_one, grad_one, grad_low, scaled_zero, inner_zero, pre_ds_zero,
                  prefix_grad, w_attn, w_out,
                  q_t, k_t, v_m, p_ref, pp_ref, inv_ref, scaled, inner, pre_ds, turned, k_m, v_t,
                  dq, dk, dv, packed, sems):
    section = lax.axis_index("pipe")
    copies = Copies(sems)
    wait_all(
        copies.start(other_attn.at[0], w_attn.at[1 - section]),
        copies.start(other_out.at[0], w_out.at[1 - section]),
    )
    small_one = small.at[1]
    h_one[...] = layer_result(
        x_ref[...].astype(f32), mixed0[...], w_attn[0], act_zero, w_out[0], small.at[0]
    ).astype(bf16)

    cos, sin = tables[:8, :], tables[8:, :]
    hat, scale = normalized(h_one[...].astype(f32))
    grad_one[...] = hat
    normed = (hat * small_row(small_one, G1) + small_row(small_one, B1)).astype(bf16)
    two = second_norm(hat, small_one)
    project_heads(normed, w_qkv.at[1], small_one, cos, sin, q_t, k_t, k_m, v_m, v_t)
    attend(q_t, k_m, v_t, low.at[2], low.at[3], mask, p_ref, pp_ref, inv_ref, mixed_one)

    grad = cot_ref[...]
    grad_two = feed_both(two, grad, w_in.at[1], w_out.at[1], small_one, act_one)
    prefix_back(w_attn.at[1], grad, q_t, low.at[3], pp_ref, inv_ref, mixed_one, scaled, inner, pre_ds, turned,
                prefix_grad, 2 * PREFIX)
    attend_back(scaled, inner, pre_ds, q_t, k_t, v_m, low.at[2], p_ref, dq, dk, dv)
    pack_grads(dq, dk, dv, cos, sin, packed)
    result = norms_back(grad, grad_one[...], scale, grad_two, packed[...], w_qkv[1], small_one)
    grad_one[...] = result
    grad_low[...] = result.astype(bf16)

    prefix_back(w_attn.at[0], grad_low[...], q0, low.at[1], pp0, inv0, mixed0, scaled_zero, inner_zero,
                pre_ds_zero, turned, prefix_grad, 0)


def middle_call(*arrays):
    scratch = HEAD_SHAPES[:6] + (
        ((D, SEQ), bf16),
        ((HEADS, SEQ), f32),
        ((PAIRS, 2 * PAD, SEQ), bf16),
        ((D, SEQ), bf16),
        ((SEQ, D), bf16),
        ((D, SEQ), bf16),
        ((D, SEQ), f32),
        ((D, SEQ), f32),
        ((D, SEQ), f32),
        ((3 * D, SEQ), bf16),
    )
    return call_kernel(
        middle_kernel, "middle", in_vmem(*arrays), vmem(MIDDLE_OUTS), scratch, 2, MIDDLE_MIB,
        20 * SEQ * D * 6 * D, {0: 9, 1: 10},
    )


def hand_over(values, keep, send, sems):
    here = lax.axis_index("pipe") == 0
    copies = Copies(sems)
    wait_all(
        copies.of_layer(here, values[0], values[1], keep),
        copies.of_layer(here, values[1], values[0], send),
    )


def result_kernel(h_one, act, mixed, small, w_attn, w_out, keep, send, result, sems):
    result[...] = layer_result(
        h_one[...].astype(f32), mixed[...], w_attn[1], act, w_out[1], small.at[1]
    ).astype(bf16)
    hand_over((h_one, result), keep, send, sems)


def result_call(*arrays):
    return call_kernel(
        result_kernel, "layer_one_out", in_vmem(*arrays), vmem([((SEQ, D), bf16)] * 2),
        [((SEQ, D), bf16)], 2, LATE_MIB, 2 * SEQ * D * (D + FF),
    )


def heads_back_kernel(scaled, inner, pre_ds, q_t, k_t, v_m, low, p_ref, tables, packed, dq, dk, dv):
    attend_back(scaled, inner, pre_ds, q_t, k_t, v_m, low.at[0], p_ref, dq, dk, dv)
    pack_grads(dq, dk, dv, tables[:8, :], tables[8:, :], packed)


def heads_back_call(*arrays):
    return call_kernel(
        heads_back_kernel, "layer_zero_attention_back", in_vmem(*arrays), vmem([((3 * D, SEQ), bf16)]),
        [((D, SEQ), f32)] * 3, 0, LATE_MIB, 10 * SEQ * SEQ * D,
    )[0]


def feed_back_kernel(grad, slope, w_in, w_out, total):
    total[...] = feed_back(grad[...], w_out.at[0], w_in.at[0], slope)


def feed_back_call(*arrays):
    (total,) = call_kernel(
        feed_back_kernel, "layer_zero_feed_back", in_vmem(*arrays), vmem([((SEQ, D), f32)]), [], 0,
        LATE_MIB, 4 * SEQ * D * FF,
    )
    return total


def norms_kernel(x_ref, grad, two, packed, grad_one, small, w_qkv, keep, send, result, sems):
    hat, scale = normalized(x_ref[...].astype(f32))
    result[...] = norms_back(grad[...], hat, scale, two[...], packed[...], w_qkv[0], small.at[0])
    hand_over((result, grad_one), keep, send, sems)


def norms_call(*arrays):
    return call_kernel(
        norms_kernel, "layer_zero_norms", in_vmem(*arrays), vmem([((SEQ, D), f32)] * 2),
        [((SEQ, D), f32)], 2, LATE_MIB, 6 * SEQ * D * D,
    )


def place_kernel(act, act_other, grad, grad_other, act_out, grad_out, sems):
    section = lax.axis_index("pipe")
    copies = Copies(sems)
    wait_all(
        *[
            copies.start(value, whole.at[0, where, 0])
            for value, whole, where in (
                (grad, grad_out, section),
                (grad_other, grad_out, 1 - section),
                (act, act_out, section),
                (act_other, act_out, 1 - section),
            )
        ]
    )


def place_call(*arrays):
    wholes = [(pltpu.HBM, (1, 2, 1, SEQ, D), bf16), (pltpu.HBM, (1, 2, 1, SEQ, D), f32)]
    return call_kernel(
        place_kernel, "place_outputs", in_vmem(*arrays), wholes, [], 4, LATE_MIB, 2 * SEQ * D
    )


QUARTER = D // 4


def final_kernel(col_width, grads_ref, hidden, embed, wide, up_high, up_rest, *refs):
    results, (d_embed, d_up, d_up_b, d_out, d_out_b, sems) = refs[:5], refs[5:]
    section = lax.axis_index("pipe")
    shard = lax.axis_index("dp")
    copies = Copies(sems)
    placed = []
    units = hidden[...]
    both = jnp.zeros((2 * PAD, D), f32)
    for part in range(4):
        high, rest = halves(padded(grads_ref[part * PREFIX : (part + 1) * PREFIX, :]))
        both = both + dot(
            jnp.concatenate([high, rest], axis=0), wide[part * D : (part + 1) * D, :], NN
        )
    grad_units = (both[:PAD] + both[PAD:])[:PREFIX]
    grad_pre = grad_units * (1.0 - units * units)
    d_up_b[...] = jnp.sum(grad_pre, axis=0, keepdims=True)
    for start in range(0, D, QUARTER):
        rows = slice(start, start + QUARTER)
        d_up[rows, :] = stacked_dot(embed[:, rows], grad_pre)
        placed.append(copies.start(d_up.at[rows], results[1].at[rows]))
    placed.append(copies.start(d_up_b, results[2]))
    column = section * (2 * D) + shard * col_width
    own_cols = jnp.zeros((PREFIX, col_width), f32)
    for part in range(4):
        for piece in range(D // col_width):
            here = column == part * D + piece * col_width
            cols = slice(piece * col_width, (piece + 1) * col_width)
            rows = slice(part * PREFIX, (part + 1) * PREFIX)
            own_cols = jnp.where(here, grads_ref[rows, cols], own_cols)
    d_out[...] = stacked_dot(units, own_cols)
    d_out_b[...] = jnp.sum(own_cols, axis=0, keepdims=True)
    placed += [copies.start(d_out, results[3]), copies.start(d_out_b, results[4])]
    high, rest = halves(padded(grad_pre))
    both = dot(jnp.concatenate([high, rest], axis=0), up_high[...], NN)
    both = both[:PAD] + both[PAD:] + dot(high, up_rest[...], NN)
    d_embed[...] = both[:PREFIX]
    placed.append(copies.start(d_embed, results[0]))
    wait_all(*placed)


def final_call(col_width, *arrays):
    def body(*refs):
        final_kernel(col_width, *refs)

    shapes = [((PREFIX, D), f32), ((D, D), f32), ((1, D), f32), ((D, col_width), f32), ((1, col_width), f32)]
    return call_kernel(
        body, "reparam", in_vmem(*arrays), [(pltpu.HBM, *pair) for pair in shapes], shapes, 8, LATE_MIB,
        SEQ * D * D,
    )


def swapped(array_in):
    return lax.ppermute(array_in, "pipe", [(0, 1), (1, 0)])


def hops(axis):
    size = lax.axis_size(axis)
    steps = []
    step = 1
    while step < size:
        steps.append((axis, [(i, i ^ step) for i in range(size)]))
        step *= 2
    assert step == size
    return steps


def local(
    block_input,
    cotangent,
    segments,
    ln1_gain,
    ln1_shift,
    qkv_weight,
    qkv_bias,
    attn_weight,
    attn_bias,
    ln2_gain,
    ln2_shift,
    ff_in_weight,
    ff_in_bias,
    ff_out_weight,
    ff_out_bias,
    prefix_embed,
    up_weight,
    up_bias,
    out_weight,
    out_bias,
):
    other_qkv = swapped(qkv_weight)
    small = small_call(
        ln1_gain, ln1_shift, ln2_gain, ln2_shift, attn_bias, ff_out_bias, qkv_bias, ff_in_bias
    )
    other_small = swapped(small)
    small, prefix_embed = lax.optimization_barrier((small, prefix_embed))
    tables = jnp.asarray(rope_tables())
    _, *later = lax.optimization_barrier((small, attn_weight, ff_in_weight, ff_out_weight))
    other_attn, other_in, other_out = (swapped(weight) for weight in later)
    x_zero, hat_zero, mask, low, hidden_units, wide, up_high, up_rest, tables, own_qkv = opening_call(
        block_input, segments, prefix_embed, up_weight, up_bias, out_weight, out_bias, tables, qkv_weight
    )
    q0, k0, v0, p0, pp0, inv0, mixed0, two_zero, small, w_qkv, w_attn, w_in, w_out, cot = first_call(
        (small, other_small, own_qkv, other_qkv, hat_zero, mask, low, tables),
        attn_weight, ff_in_weight, ff_out_weight, cotangent,
    )
    act_zero, slope_zero, w_in = feed_call(two_zero, small, other_in, w_in)
    (h_one, act_one, mixed_one, grad_one, grad_low, scaled_zero, inner_zero, pre_ds_zero, prefix_grad,
     w_attn, w_out) = middle_call(
        w_attn, w_out, q0, pp0, inv0, mixed0, small, w_qkv, w_in, other_attn, other_out, cot, x_zero,
        act_zero, low, mask, tables,
    )

    def layer_one_out(state):
        own, send = result_call(state["h_one"], act_one, mixed_one, small, w_attn, w_out)
        return dict(state, act_own=own, act_send=send)

    def layer_zero_attention(state):
        packed = heads_back_call(
            state["scaled"], inner_zero, pre_ds_zero, q0, k0, v0, low, p0, tables
        )
        return dict(state, packed=packed, act_other=swapped(state["act_send"]))

    def layer_zero_feed(state):
        return dict(state, two=feed_back_call(state["grad_low"], slope_zero, w_in, w_out))

    def layer_zero_norms(state):
        own, send = norms_call(x_zero, grad_low, state["two"], state["packed"], grad_one, small, w_qkv)
        return dict(state, grad_own=own, grad_send=send)

    def swap_grads(state):
        other = swapped(state["grad_send"])
        return {"wholes": place_call(state["act_own"], state["act_other"], state["grad_own"], other)}

    works = [layer_one_out, layer_zero_attention, layer_zero_feed, layer_zero_norms, swap_grads]
    state = {"h_one": h_one, "grad_low": grad_low, "scaled": scaled_zero}
    for axis, pairs in hops("pipe") + hops("dp") + hops("grp"):
        if axis == "pipe":
            moved = lax.ppermute(prefix_grad, axis, pairs)
        else:
            prefix_grad = lax.reduce_precision(prefix_grad, 8, 7)
            moved = lax.ppermute(prefix_grad.astype(bf16), axis, pairs)
        if works:
            state = works.pop(0)(state)
        prefix_grad, moved, state = lax.optimization_barrier((prefix_grad, moved, state))
        prefix_grad = prefix_grad + moved.astype(f32)
    for work in works:
        state = work(state)
    col_width = 2 * D // lax.axis_size("dp")
    grad_embed, grad_up, grad_up_b, grad_out, grad_out_b = final_call(
        col_width, prefix_grad, hidden_units, prefix_embed, wide, up_high, up_rest
    )
    activations, input_grads = state["wholes"]
    return (
        activations,
        input_grads,
        grad_embed,
        grad_up,
        grad_up_b[0],
        grad_out,
        grad_out_b[0],
    )


def solution(mesh):
    return jax.shard_map(
        local,
        mesh=mesh,
        in_specs=(
            P(None, ("grp", "dp"), None, None),
            P(None, ("grp", "dp"), None, None),
            P(None, ("grp", "dp"), None),
            P("pipe", None),
            P("pipe", None),
            P("pipe", None, None),
            P("pipe", None),
            P("pipe", None, None),
            P("pipe", None),
            P("pipe", None),
            P("pipe", None),
            P("pipe", None, None),
            P("pipe", None),
            P("pipe", None, None),
            P("pipe", None),
            P(),
            P(),
            P(),
            P(),
            P(),
        ),
        out_specs=(
            P("pipe", None, ("grp", "dp"), None, None),
            P("pipe", None, ("grp", "dp"), None, None),
            P(),
            P(),
            P(),
            P(None, ("pipe", "dp")),
            P(("pipe", "dp")),
        ),
        check_vma=False,
    )
```

```python
import math

import jax
import jax.numpy as jnp
import numpy as np
from jax import lax
from jax.experimental import pallas as pl
from jax.experimental.pallas import tpu as pltpu
from jax.sharding import PartitionSpec as P

D = 512
SEQ = 512
HEADS = 8
HD = 64
FF = 2048
ROT = 16
PREFIX = 10
PAD = 16
BLK = 128
BLOCKS = SEQ // BLK
PAIRS = HEADS // 2
LIVE = (1, 2, 3, 3)
P_ROWS = BLK * sum(LIVE)
P_START = (0, 128, 384, 768)

f32 = jnp.float32
bf16 = jnp.bfloat16
LOG2E = math.log2(math.e)
Q_SCALE = LOG2E * HD**-0.5
K_BACK = 1.0 / LOG2E
Q_BACK = HD**-0.5
NEG = -1e30

NN = (((1,), (0,)), ((), ()))
NT = (((1,), (1,)), ((), ()))
TN = (((0,), (0,)), ((), ()))

MIB = 1024 * 1024
EARLY_MIB = 24
MIDDLE_MIB = 23
LATE_MIB = 12

G1, B1, G2, B2, B_ATTN, B_OUT, B_QKV, B_IN = 0, 1, 2, 3, 4, 5, 6, 9
SMALL = 13 * D


def dot(left, right, dims):
    return lax.dot_general(left, right, dims, preferred_element_type=f32)


def call_kernel(kernel, name, ins, outs, scratch, sems, mib, cost, aliases=None):
    operands = [pltpu.with_memory_space_constraint(array, space) for array, space in ins]
    return pl.pallas_call(
        kernel,
        name=name,
        out_shape=[space(shape, dtype) for space, shape, dtype in outs],
        in_specs=[pl.BlockSpec(memory_space=space) for _, space in ins],
        out_specs=[pl.BlockSpec(memory_space=space) for space, _, _ in outs],
        scratch_shapes=[pltpu.VMEM(*pair) for pair in scratch]
        + ([pltpu.SemaphoreType.DMA((sems,))] if sems else []),
        input_output_aliases=aliases or {},
        compiler_params=pltpu.CompilerParams(vmem_limit_bytes=mib * MIB),
        cost_estimate=pl.CostEstimate(flops=cost, bytes_accessed=8 * MIB, transcendentals=0),
    )(*operands)


def in_hbm(*arrays):
    return [(array, pltpu.HBM) for array in arrays]


def anywhere(*arrays):
    return [(array, pl.ANY) for array in arrays]


def in_vmem(*arrays):
    return [(array, pltpu.VMEM) for array in arrays]


def vmem(shapes):
    return [(pltpu.VMEM, *pair) for pair in shapes]


def small_row(small_ref, place):
    return small_ref[:, place * D : (place + 1) * D]


def rope_tables():
    inv_freq = 10000.0 ** (-2.0 * np.arange(ROT // 2) / ROT)
    angles = inv_freq[:, None] * np.arange(SEQ)[None, :]
    return np.concatenate([np.cos(angles), np.sin(angles)], axis=0).astype(np.float32)


class Copies:
    def __init__(self, sems):
        self.sems = sems
        self.count = 0

    def start(self, src, dst):
        copy = pltpu.make_async_copy(src, dst, self.sems.at[self.count])
        self.count += 1
        copy.start()
        return copy

    def of_layer(self, here, own, other, dst):
        sem = self.sems.at[self.count]
        self.count += 1
        copy = pltpu.make_async_copy(own, dst, sem)

        @pl.when(here)
        def _():
            copy.start()

        @pl.when(jnp.logical_not(here))
        def _():
            pltpu.make_async_copy(other, dst, sem).start()

        return copy


def wait_all(*copies):
    for copy in copies:
        copy.wait()


def normalized(hidden):
    mean = jnp.mean(hidden, axis=-1, keepdims=True)
    centered = hidden - mean
    variance = jnp.mean(centered * centered, axis=-1, keepdims=True)
    scale = lax.rsqrt(variance + 1e-05)
    return centered * scale, scale


def rope_heads(rows, cos, sin):
    parts = []
    for head in range(rows.shape[0] // HD):
        base = head * HD
        lead = rows[base : base + 8]
        tail = rows[base + 8 : base + 16]
        parts += [lead * cos - tail * sin, tail * cos + lead * sin, rows[base + 16 : base + HD]]
    return jnp.concatenate(parts, axis=0)


def fill_mask(seg_ref, mask_ref):
    seg_row = seg_ref[...].astype(f32)
    seg_col = jnp.transpose(jnp.broadcast_to(seg_row, (8, SEQ)))[:, 0:1]
    for block in range(BLOCKS):
        for key_block in range(block + 1 - LIVE[block], block + 1):
            seen = seg_col[key_block * BLK : (key_block + 1) * BLK] == (
                seg_row[:, block * BLK : (block + 1) * BLK]
            )
            if key_block == block:
                key_pos = lax.broadcasted_iota(jnp.int32, (BLK, BLK), 0)
                query_pos = lax.broadcasted_iota(jnp.int32, (BLK, BLK), 1)
                seen = seen & (key_pos <= query_pos)
            start = P_START[block] + (key_block - (block + 1 - LIVE[block])) * BLK
            mask_ref[start : start + BLK, :] = jnp.where(seen, 0.0, NEG)


def project_heads(normed, w_ref, small_ref, cos, sin, q_t, k_t, k_m, v_m, v_t):
    bias = small_row(small_ref, B_QKV)
    rows = dot(normed, w_ref[:, :D], NN) + bias
    q_t[...] = (rope_heads(jnp.transpose(rows), cos, sin) * Q_SCALE).astype(bf16)
    bias = small_row(small_ref, B_QKV + 1)
    rows = dot(normed, w_ref[:, D : 2 * D], NN) + bias
    keys = rope_heads(jnp.transpose(rows), cos, sin).astype(bf16)
    k_t[...] = keys
    k_m[...] = jnp.transpose(keys)
    bias = small_row(small_ref, B_QKV + 2)
    values = (dot(normed, w_ref[:, 2 * D :], NN) + bias).astype(bf16)
    v_m[...] = values
    v_t[...] = jnp.transpose(values)


def block_diagonal(pair_rows):
    zeros = jnp.zeros((HD, BLK), pair_rows.dtype)
    return jnp.concatenate(
        [
            jnp.concatenate([pair_rows[:HD], zeros], axis=1),
            jnp.concatenate([zeros, pair_rows[HD:]], axis=1),
        ],
        axis=0,
    )


def from_diagonal(both):
    return jnp.concatenate([both[:HD, :BLK], both[HD:, BLK:]], axis=0)


def per_head(row, rows=HD):
    return jnp.concatenate(
        [
            jnp.broadcast_to(row[:, :BLK], (rows, BLK)),
            jnp.broadcast_to(row[:, BLK:], (rows, BLK)),
        ],
        axis=0,
    )


def geometry(block):
    live = LIVE[block] * BLK
    end = (block + 1) * BLK
    start = P_START[block]
    return slice(end - live, end), slice(block * BLK, end), slice(start, start + live)


def pair_rows(pair):
    return slice(pair * BLK, (pair + 1) * BLK)


def both_heads(rows, tokens):
    return jnp.concatenate([rows[:PAD, tokens], rows[PAD:, tokens]], axis=1)


def attend(q_t, k_m, v_t, pre_k, pre_v, mask_ref, p_ref, pp_ref, inv_ref, mixed_ref):
    real = lax.rem(lax.broadcasted_iota(jnp.int32, (2 * PAD, 1), 0), PAD) < PREFIX
    pad_mask = jnp.where(real, 0.0, NEG)

    def score(feats, block):
        keys, tokens, rows = geometry(block)
        queries = block_diagonal(q_t[feats, tokens])
        mask = mask_ref[rows, :]
        return dot(k_m[keys, feats], queries, NN) + jnp.concatenate([mask, mask], axis=1)

    def soften(pair, block, scores, pre_scores):
        _, tokens, rows = geometry(block)
        pre_scores = both_heads(pre_scores, tokens)
        peak = jnp.maximum(
            jnp.max(scores, axis=0, keepdims=True), jnp.max(pre_scores, axis=0, keepdims=True)
        )
        expo = jnp.exp2(scores - peak).astype(bf16)
        pre_expo = jnp.exp2(pre_scores - peak)
        p_ref[pair, rows, :] = expo
        pp_ref[pair, :PAD, tokens] = pre_expo[:, :BLK].astype(bf16)
        pp_ref[pair, PAD:, tokens] = pre_expo[:, BLK:].astype(bf16)
        return expo, jnp.sum(pre_expo, axis=0, keepdims=True)

    def mix(pair, block, pre_mixed, expo, pre_total):
        feats = pair_rows(pair)
        keys, tokens, _ = geometry(block)
        ones = jnp.ones((PAD, expo.shape[0]), bf16)
        mixed = dot(jnp.concatenate([v_t[feats, keys], ones], axis=0), expo, NN)
        inverse = 1.0 / (mixed[BLK : BLK + 1] + pre_total)
        inv_ref[2 * pair : 2 * pair + 1, tokens] = inverse[:, :BLK]
        inv_ref[2 * pair + 1 : 2 * pair + 2, tokens] = inverse[:, BLK:]
        mixed = from_diagonal(mixed[:BLK]) + pre_mixed[:, tokens]
        mixed_ref[feats, tokens] = (mixed * per_head(inverse)).astype(bf16)

    def score_all(pair):
        feats = pair_rows(pair)
        pre_scores = dot(pre_k[:, feats], q_t[feats, :], NN) + pad_mask
        return pre_scores, [score(feats, block) for block in range(BLOCKS)]

    def mix_all(pair, soft):
        pre_mixed = dot(pre_v[:, pair_rows(pair)], pp_ref[pair], TN)
        for block in range(BLOCKS):
            mix(pair, block, pre_mixed, *soft[block])

    ahead, behind = score_all(0), None
    for pair in range(PAIRS):
        pre_scores, scores = ahead
        if pair + 1 < PAIRS:
            ahead = score_all(pair + 1)
        soft = [soften(pair, block, scores[block], pre_scores) for block in range(BLOCKS)]
        if behind is not None:
            mix_all(*behind)
        behind = (pair, soft)
    mix_all(*behind)


def prefix_back(w_attn, grad, q_t, pre_v, pp_ref, inv_ref, mixed_ref, scaled_ref, inner_ref, pre_ds_ref, turned,
                pre_grad, pre_row):
    turned[...] = jnp.transpose(grad)

    def scale(pair):
        grad_mixed = dot(w_attn[pair_rows(pair), :], turned[...], NN)
        inner = []
        for place in range(2):
            head = 2 * pair + place
            rows = slice(head * HD, (head + 1) * HD)
            scaled = grad_mixed[place * HD : (place + 1) * HD] * inv_ref[head : head + 1, :]
            scaled = scaled.astype(bf16)
            scaled_ref[rows, :] = scaled
            products = scaled.astype(f32) * mixed_ref[rows, :].astype(f32)
            inner.append(jnp.sum(products, axis=0, keepdims=True))
            inner_ref[head : head + 1, :] = inner[-1]
        return jnp.concatenate([jnp.broadcast_to(row, (PAD, SEQ)) for row in inner], axis=0)

    pairs = range(PAIRS)
    inner = [scale(pair) for pair in pairs]
    grad_probs = [dot(pre_v[:, pair_rows(pair)], scaled_ref[pair_rows(pair), :], NN) for pair in pairs]
    for pair in pairs:
        probs = pp_ref[pair].astype(f32)
        pre_ds_ref[pair] = (probs * (grad_probs[pair] - inner[pair])).astype(bf16)
    keys = [dot(q_t[pair_rows(pair), :], pre_ds_ref[pair], NT) for pair in pairs]
    values = [dot(scaled_ref[pair_rows(pair), :], pp_ref[pair], NT) for pair in pairs]
    first_head = lax.rem(lax.broadcasted_iota(jnp.int32, (1, D), 1), BLK) < HD

    def own_head(parts):
        both = jnp.transpose(jnp.concatenate(parts, axis=0))
        return jnp.where(first_head, both[:PREFIX], both[PAD : PAD + PREFIX])

    pre_grad[pre_row : pre_row + PREFIX, :] = own_head(keys) * K_BACK
    pre_grad[pre_row + PREFIX : pre_row + 2 * PREFIX, :] = own_head(values)


def by_keys(outs, key_block):
    total = None
    for block in range(BLOCKS):
        place = key_block - (block + 1 - LIVE[block])
        if 0 <= place < LIVE[block]:
            part = outs[block][:, place * BLK : (place + 1) * BLK]
            total = part if total is None else total + part
    return total


def values_back(scaled_ref, p_ref, packed_v):
    for pair in range(PAIRS):
        feats = pair_rows(pair)
        outs = []
        for block in range(BLOCKS):
            _, tokens, rows = geometry(block)
            outs.append(dot(block_diagonal(scaled_ref[feats, tokens]), p_ref[pair, rows, :], NT))
        for key_block in range(BLOCKS):
            keys = slice(key_block * BLK, (key_block + 1) * BLK)
            packed_v[feats, keys] = by_keys(outs, key_block).astype(bf16)


def attend_back(scaled_ref, inner_ref, pre_ds_ref, q_t, k_t, v_m, pre_k, p_ref, dq_ref, dk_ref, dv_ref):
    def value_grads(feats, block):
        keys, tokens, _ = geometry(block)
        grads = block_diagonal(scaled_ref[feats, tokens])
        return grads, dot(v_m[keys, feats], grads, NN)

    def score_grads(pair, block, grad_probs):
        _, tokens, rows = geometry(block)
        inner = jnp.concatenate(
            [inner_ref[2 * pair : 2 * pair + 1, tokens], inner_ref[2 * pair + 1 : 2 * pair + 2, tokens]],
            axis=1,
        )
        return (p_ref[pair, rows, :].astype(f32) * (grad_probs - inner)).astype(bf16)

    def out_grads(pair, feats, block, pre_dq, grads, grad_scores):
        keys, tokens, rows = geometry(block)
        queries = block_diagonal(q_t[feats, tokens])
        dq_ref[feats, tokens] = (
            from_diagonal(dot(k_t[feats, keys], grad_scores, NN)) + pre_dq[:, tokens]
        )
        dk = dot(queries, grad_scores, NT)
        return dk, None if dv_ref is None else dot(grads, p_ref[pair, rows, :], NT)

    for pair in range(PAIRS):
        feats = pair_rows(pair)
        first = [value_grads(feats, block) for block in range(BLOCKS)]
        second = [score_grads(pair, block, first[block][1]) for block in range(BLOCKS)]
        pre_dq = dot(pre_k[:, feats], pre_ds_ref[pair], TN)
        outs = [
            out_grads(pair, feats, block, pre_dq, first[block][0], second[block])
            for block in range(BLOCKS)
        ]
        for key_block in range(BLOCKS):
            keys = slice(key_block * BLK, (key_block + 1) * BLK)
            dk_ref[feats, keys] = by_keys([out[0] for out in outs], key_block)
            if dv_ref is not None:
                dv_ref[feats, keys] = by_keys([out[1] for out in outs], key_block)


def pack_grads(dq_ref, dk_ref, cos, sin, packed_t):
    packed_t[:D, :] = (rope_heads(dq_ref[...], cos, -sin) * Q_BACK).astype(bf16)
    packed_t[D : 2 * D, :] = (rope_heads(dk_ref[...], cos, -sin) * K_BACK).astype(bf16)


ROOT_HALF = 0.5**0.5


def gelu_both(scaled):
    cdf = ROOT_HALF + ROOT_HALF * lax.erf(scaled)
    density = jnp.exp2(scaled * scaled * (-LOG2E)) * (2.0 / math.sqrt(2.0 * math.pi))
    return scaled * cdf, cdf + scaled * density


FF_CHUNK = 512
FF_ROWS = 256


def second_norm(hat, small_ref):
    gain = small_row(small_ref, G2) * ROOT_HALF
    return (hat * gain + small_row(small_ref, B2) * ROOT_HALF).astype(bf16)


def chunk_of(index):
    return slice(index * FF_CHUNK, (index + 1) * FF_CHUNK)


def feed_in(normed, w_ref, small_ref, act_ref, slope_ref, between):
    for chunk in range(FF // FF_CHUNK):
        cols = chunk_of(chunk)
        bias = small_row(small_ref, B_IN + chunk) * ROOT_HALF
        between(chunk)
        for start in range(0, SEQ, FF_ROWS):
            rows = slice(start, start + FF_ROWS)
            act, slope = gelu_both(dot(normed[rows], w_ref[:, cols], NN) + bias)
            act_ref[rows, cols] = act.astype(bf16)
            slope_ref[rows, cols] = slope.astype(bf16)


def feed_both(normed, grad, w_in, w_out, small_ref, act_ref):
    total = jnp.zeros((SEQ, D), f32)
    for chunk in range(FF // FF_CHUNK):
        cols = chunk_of(chunk)
        bias = small_row(small_ref, B_IN + chunk) * ROOT_HALF
        slopes = []
        for start in range(0, SEQ, FF_ROWS):
            rows = slice(start, start + FF_ROWS)
            act, slope = gelu_both(dot(normed[rows], w_in[:, cols], NN) + bias)
            act_ref[rows, cols] = act.astype(bf16)
            slopes.append(slope.astype(bf16))
        grad_act = dot(grad, w_out[cols, :], NT)
        grad_before = (grad_act * jnp.concatenate(slopes, axis=0).astype(f32)).astype(bf16)
        total = total + dot(grad_before, w_in[:, cols], NT)
    return total * ROOT_HALF


def layer_result(hidden, mixed_t, w_attn, act_ref, w_out, small_ref):
    attn_out = dot(jnp.transpose(mixed_t), w_attn, NN) + small_row(small_ref, B_ATTN)
    ff_out = dot(act_ref[...], w_out, NN) + small_row(small_ref, B_OUT)
    return hidden + attn_out + ff_out


def feed_back(grad, w_out, w_in, slope_ref):
    total = jnp.zeros((SEQ, D), f32)
    for chunk in range(FF // FF_CHUNK):
        cols = chunk_of(chunk)
        grad_act = dot(grad, w_out[cols, :], NT)
        grad_before = (grad_act * slope_ref[:, cols].astype(f32)).astype(bf16)
        total = total + dot(grad_before, w_in[:, cols], NT)
    return total * ROOT_HALF


def norms_back(grad, hat, scale, grad_two, packed_t, packed_v, w_qkv, small_ref, out_ref):
    halves_of = [slice(start, start + FF_ROWS) for start in range(0, SEQ, FF_ROWS)]
    products = [
        dot(w_qkv[:, : 2 * D], packed_t[:, tokens], NN) + dot(w_qkv[:, 2 * D :], packed_v[:, tokens], NN)
        for tokens in halves_of
    ]
    for tokens, product in zip(halves_of, products):
        here = hat[tokens, :]
        grad_hat = jnp.transpose(product) * small_row(small_ref, G1)
        grad_hat = grad_hat + grad_two[tokens, :] * small_row(small_ref, G2)
        mean_one = jnp.mean(grad_hat, axis=-1, keepdims=True)
        mean_two = jnp.mean(grad_hat * here, axis=-1, keepdims=True)
        change = scale[tokens] * (grad_hat - mean_one - here * mean_two)
        out_ref[tokens, :] = grad[tokens, :].astype(f32) + change


def halves(values):
    high = values.astype(bf16)
    return high, (values - high.astype(f32)).astype(bf16)


def padded(values):
    return jnp.concatenate([values, jnp.zeros((PAD - PREFIX, values.shape[1]), f32)], axis=0)


def few_rows_dot(left, right):
    left_high, left_rest = halves(padded(left))
    right_high, right_rest = halves(right)
    both = dot(jnp.concatenate([left_high, left_rest], axis=0), right_high, NN)
    return both[:PAD] + both[PAD:] + dot(left_high, right_rest, NN)


def stacked_dot(left, right):
    left_high, left_rest = halves(padded(left))
    right_high, right_rest = halves(padded(right))
    return dot(
        jnp.concatenate([left_high, left_high, left_rest], axis=0),
        jnp.concatenate([right_high, right_rest, right_high], axis=0),
        TN,
    )


def small_kernel(gain_one, shift_one, gain_two, shift_two, attn_b, out_b, qkv_b, in_b, packed, sems):
    copies = Copies(sems)
    places = [(gain_one, 0), (shift_one, 1), (gain_two, 2), (shift_two, 3), (attn_b, 4), (out_b, 5)]
    places += [(qkv_b, 6), (in_b, 9)]
    wait_all(
        *[
            copies.start(row, packed.at[:, place * D : place * D + row.shape[1]])
            for row, place in places
        ]
    )


def small_call(*arrays):
    (packed,) = call_kernel(
        small_kernel, "small_parameters", in_hbm(*arrays), vmem([((1, SMALL), f32)]), [], 8, LATE_MIB, SMALL
    )
    return packed


def prefix_state(units, layer, part, out_w, out_b, low, wide):
    real = lax.broadcasted_iota(jnp.int32, (PAD, 1), 0) < PREFIX
    first_head = lax.rem(lax.broadcasted_iota(jnp.int32, (1, D), 1), BLK) < HD
    cols = slice(part * D, (part + 1) * D)
    bias = out_b[:, (2 * layer + part) * D : (2 * layer + part + 1) * D]
    high, rest = halves(padded(units))
    wide[:, cols] = out_w[:, cols].astype(bf16)
    both = dot(jnp.concatenate([high, rest], axis=0), wide[:, cols], NN)
    states = jnp.where(real, both[:PAD] + both[PAD:] + bias, 0.0)
    low[part, :PAD, :] = jnp.where(first_head, states, 0.0).astype(bf16)
    low[part, PAD:, :] = jnp.where(first_head, 0.0, states).astype(bf16)


def layer_parts(copies, layer, out_hbm, out_w):
    return [
        copies.start(
            out_hbm.at[:, (2 * layer + part) * D : (2 * layer + part + 1) * D],
            out_w.at[:, part * D : (part + 1) * D],
        )
        for part in range(2)
    ]


OPENING_SHAPES = (
    ((SEQ, D), bf16),
    ((SEQ, D), f32),
    ((P_ROWS, BLK), f32),
    ((2, 2 * PAD, D), bf16),
    ((PREFIX, D), f32),
    ((D, 2 * D), bf16),
    ((D, D), bf16),
    ((D, D), bf16),
    ((2 * 8, SEQ), f32),
    ((D, 3 * D), bf16),
)


def opening_kernel(x_hbm, seg_hbm, embed_hbm, up_hbm, up_b_hbm, out_hbm, out_b_hbm, tables_hbm, qkv_hbm,
                   x_ref, hat, mask, low, hidden, wide, up_high, up_rest, tables, own_qkv, seg, embed, up_w, up_b,
                   out_w, out_b, sems):
    section = lax.axis_index("pipe")
    copies = Copies(sems)
    x_copy = copies.start(x_hbm.at[section, 0], x_ref)
    seg_copy = copies.start(seg_hbm.at[section], seg)
    prefix_copies = [
        copies.start(src, dst)
        for src, dst in ((embed_hbm, embed), (up_hbm, up_w), (up_b_hbm, up_b.at[0]), (out_b_hbm, out_b.at[0]))
    ]
    parts = layer_parts(copies, 0, out_hbm, out_w)
    late = [copies.start(tables_hbm, tables), copies.start(qkv_hbm.at[0], own_qkv)]
    seg_copy.wait()
    fill_mask(seg, mask)
    x_copy.wait()
    hat[...], _ = normalized(x_ref[...].astype(f32))
    wait_all(*prefix_copies)
    units = jnp.tanh(few_rows_dot(embed[...], up_w[...])[:PREFIX] + up_b[...])
    hidden[...] = units
    up_high[...], up_rest[...] = halves(up_w[...])
    for part in range(2):
        parts[part].wait()
        prefix_state(units, 0, part, out_w, out_b, low, wide)
    wait_all(*late)


def opening_call(*arrays):
    scratch = [
        ((1, SEQ), jnp.int32),
        ((PREFIX, D), f32),
        ((D, D), f32),
        ((1, D), f32),
        ((D, 2 * D), f32),
        ((1, 4 * D), f32),
    ]
    return call_kernel(
        opening_kernel, "opening", in_hbm(*arrays), vmem(OPENING_SHAPES), scratch, 12, EARLY_MIB,
        2 * 6 * PAD * D * 5 * D,
    )


HEAD_SHAPES = (
    ((D, SEQ), bf16),
    ((D, SEQ), bf16),
    ((SEQ, D), bf16),
    ((PAIRS, P_ROWS, 2 * BLK), bf16),
    ((PAIRS, 2 * PAD, SEQ), bf16),
    ((HEADS, SEQ), f32),
    ((D, SEQ), bf16),
)
FIRST_SHAPES = HEAD_SHAPES + (
    ((SEQ, D), bf16),
    ((2, 1, SMALL), f32),
    ((2, D, 3 * D), bf16),
    ((2, D, D), bf16),
    ((2, D, FF), bf16),
    ((2, FF, D), bf16),
    ((SEQ, D), bf16),
    ((D, 2 * D), f32),
    ((1, 4 * D), f32),
)


def first_kernel(own_small, other_small, own_qkv, other_qkv, hat_ref, mask, low, tables,
                 attn_hbm, ff_in_hbm, ff_out_hbm, cot_hbm,
                 out_hbm, out_b_hbm,
                 q_t, k_t, v_m, p_ref, pp_ref, inv_ref, mixed_ref, two_ref, small, w_qkv, w_attn, w_in,
                 w_out, cot_ref, out_w, out_b, k_m, v_t, sems):
    section = lax.axis_index("pipe")
    copies = Copies(sems)
    now = [
        copies.start(own_small, small.at[section]),
        copies.start(other_small, small.at[1 - section]),
        copies.start(own_qkv, w_qkv.at[section]),
        copies.start(other_qkv.at[0], w_qkv.at[1 - section]),
    ]
    parts = layer_parts(copies, 1, out_hbm, out_w)
    later = [
        copies.start(ff_in_hbm.at[0], w_in.at[section]),
        copies.start(attn_hbm.at[0], w_attn.at[section]),
        copies.start(out_b_hbm, out_b.at[0]),
        copies.start(ff_out_hbm.at[0], w_out.at[section]),
        copies.start(cot_hbm.at[section, 0], cot_ref),
    ]
    wait_all(*now)
    hat = hat_ref[...]
    zero = small.at[0]
    normed = (hat * small_row(zero, G1) + small_row(zero, B1)).astype(bf16)
    two_ref[...] = second_norm(hat, zero)
    project_heads(normed, w_qkv.at[0], zero, tables[:8, :], tables[8:, :], q_t, k_t, k_m, v_m, v_t)
    attend(q_t, k_m, v_t, low.at[0], low.at[1], mask, p_ref, pp_ref, inv_ref, mixed_ref)
    wait_all(*later, *parts)


def first_call(ready, *arrays):
    return call_kernel(
        first_kernel, "first_attention", in_vmem(*ready) + in_hbm(*arrays), vmem(FIRST_SHAPES),
        [((SEQ, D), bf16), ((D, SEQ), bf16)], 11, EARLY_MIB, 200 * SEQ * D * 3 * D,
    )


def feed_kernel(two, small, other_in, w_in_before, hidden, out_w, out_b, act_ref, slope_ref, w_in, low_one, wide_one,
                sems):
    wait_all(Copies(sems).start(other_in.at[0], w_in.at[1 - lax.axis_index("pipe")]))

    def between(chunk):
        if chunk in (0, 2):
            prefix_state(hidden[...], 1, chunk // 2, out_w, out_b, low_one, wide_one)

    feed_in(two[...], w_in.at[0], small.at[0], act_ref, slope_ref, between)


def feed_call(*arrays):
    shapes = [((SEQ, FF), bf16), ((SEQ, FF), bf16), ((2, D, FF), bf16)]
    shapes += [((2, 2 * PAD, D), bf16), ((D, 2 * D), bf16)]
    return call_kernel(
        feed_kernel, "first_feed", in_vmem(*arrays), vmem(shapes), [], 1, LATE_MIB, 2 * SEQ * D * FF,
        {3: 2},
    )


WEIGHT_SHAPES = (((D, 3 * D), bf16), ((D, D), bf16), ((D, FF), bf16), ((FF, D), bf16))


MIDDLE_OUTS = (
    ((SEQ, D), bf16),
    ((SEQ, FF), bf16),
    ((D, SEQ), bf16),
    ((SEQ, D), f32),
    ((SEQ, D), bf16),
    ((D, SEQ), bf16),
    ((HEADS, SEQ), f32),
    ((PAIRS, 2 * PAD, SEQ), bf16),
    ((4 * PREFIX, D), f32),
    ((2, D, D), bf16),
    ((2, FF, D), bf16),
)


def middle_kernel(w_attn_before, w_out_before, q0, pp0, inv0, mixed0, small, w_qkv, w_in,
                  other_attn, other_out, cot_ref, x_ref, act_zero, low, low_one, mask, tables,
                  h_one, act_one, mixed_one, grad_one, grad_low, scaled_zero, inner_zero, pre_ds_zero,
                  prefix_grad, w_attn, w_out,
                  q_t, k_t, v_m, p_ref, pp_ref, inv_ref, scaled, inner, pre_ds, turned, k_m, v_t,
                  dq, dk, dv, packed, packed_v, sems):
    section = lax.axis_index("pipe")
    copies = Copies(sems)
    wait_all(
        copies.start(other_attn.at[0], w_attn.at[1 - section]),
        copies.start(other_out.at[0], w_out.at[1 - section]),
    )
    small_one = small.at[1]
    h_one[...] = layer_result(
        x_ref[...].astype(f32), mixed0[...], w_attn[0], act_zero, w_out[0], small.at[0]
    ).astype(bf16)

    cos, sin = tables[:8, :], tables[8:, :]
    hat, scale = normalized(h_one[...].astype(f32))
    grad_one[...] = hat
    normed = (hat * small_row(small_one, G1) + small_row(small_one, B1)).astype(bf16)
    two = second_norm(hat, small_one)
    project_heads(normed, w_qkv.at[1], small_one, cos, sin, q_t, k_t, k_m, v_m, v_t)
    attend(q_t, k_m, v_t, low_one.at[0], low_one.at[1], mask, p_ref, pp_ref, inv_ref, mixed_one)

    grad = cot_ref[...]
    grad_two = feed_both(two, grad, w_in.at[1], w_out.at[1], small_one, act_one)
    prefix_back(w_attn.at[1], grad, q_t, low_one.at[1], pp_ref, inv_ref, mixed_one, scaled, inner, pre_ds, turned,
                prefix_grad, 2 * PREFIX)
    attend_back(scaled, inner, pre_ds, q_t, k_t, v_m, low_one.at[0], p_ref, dq, dk, dv)
    pack_grads(dq, dk, cos, sin, packed)
    packed_v[...] = dv[...].astype(bf16)
    norms_back(cot_ref, grad_one, scale, grad_two, packed, packed_v, w_qkv.at[1], small_one, grad_one)
    grad_low[...] = grad_one[...].astype(bf16)

    prefix_back(w_attn.at[0], grad_low[...], q0, low.at[1], pp0, inv0, mixed0, scaled_zero, inner_zero,
                pre_ds_zero, turned, prefix_grad, 0)


def middle_call(*arrays):
    scratch = HEAD_SHAPES[:6] + (
        ((D, SEQ), bf16),
        ((HEADS, SEQ), f32),
        ((PAIRS, 2 * PAD, SEQ), bf16),
        ((D, SEQ), bf16),
        ((SEQ, D), bf16),
        ((D, SEQ), bf16),
        ((D, SEQ), f32),
        ((D, SEQ), f32),
        ((D, SEQ), f32),
        ((2 * D, SEQ), bf16),
        ((D, SEQ), bf16),
    )
    return call_kernel(
        middle_kernel, "middle", in_vmem(*arrays), vmem(MIDDLE_OUTS), scratch, 2, MIDDLE_MIB,
        20 * SEQ * D * 6 * D, {0: 9, 1: 10},
    )


def hand_over(values, keep, send, sems):
    here = lax.axis_index("pipe") == 0
    copies = Copies(sems)
    wait_all(
        copies.of_layer(here, values[0], values[1], keep),
        copies.of_layer(here, values[1], values[0], send),
    )


def result_kernel(h_one, act, mixed, small, w_attn, w_out, keep, send, result, sems):
    result[...] = layer_result(
        h_one[...].astype(f32), mixed[...], w_attn[1], act, w_out[1], small.at[1]
    ).astype(bf16)
    hand_over((h_one, result), keep, send, sems)


def result_call(*arrays):
    return call_kernel(
        result_kernel, "layer_one_out", in_vmem(*arrays), vmem([((SEQ, D), bf16)] * 2),
        [((SEQ, D), bf16)], 2, LATE_MIB, 2 * SEQ * D * (D + FF),
    )


def heads_back_kernel(scaled, inner, pre_ds, q_t, k_t, v_m, low, p_ref, tables, packed, dq, dk):
    attend_back(scaled, inner, pre_ds, q_t, k_t, v_m, low.at[0], p_ref, dq, dk, None)
    pack_grads(dq, dk, tables[:8, :], tables[8:, :], packed)


def heads_back_call(*arrays):
    return call_kernel(
        heads_back_kernel, "layer_zero_attention_back", in_vmem(*arrays), vmem([((2 * D, SEQ), bf16)]),
        [((D, SEQ), f32)] * 2, 0, LATE_MIB, 10 * SEQ * SEQ * D,
    )[0]


def feed_back_kernel(grad, slope, w_in, w_out, total):
    total[...] = feed_back(grad[...], w_out.at[0], w_in.at[0], slope)


def feed_back_call(*arrays):
    (total,) = call_kernel(
        feed_back_kernel, "layer_zero_feed_back", in_vmem(*arrays), vmem([((SEQ, D), f32)]), [], 0,
        LATE_MIB, 4 * SEQ * D * FF,
    )
    return total


def norms_kernel(x_ref, grad, two, packed, scaled, p_ref, grad_one, small, w_qkv, keep, send, result, packed_v,
                 sems):
    values_back(scaled, p_ref, packed_v)
    hat, scale = normalized(x_ref[...].astype(f32))
    norms_back(grad, hat, scale, two, packed, packed_v, w_qkv.at[0], small.at[0], result)
    hand_over((result, grad_one), keep, send, sems)


def norms_call(*arrays):
    return call_kernel(
        norms_kernel, "layer_zero_norms", in_vmem(*arrays), vmem([((SEQ, D), f32)] * 2),
        [((SEQ, D), f32), ((D, SEQ), bf16)], 2, LATE_MIB, 6 * SEQ * D * D,
    )


def place_kernel(act, act_other, grad, grad_other, wide_zero, wide_one, up_high, up_rest,
                 act_out, grad_out, wide_t, up_high_t, up_rest_t, sems):
    section = lax.axis_index("pipe")
    copies = Copies(sems)
    placed = [
        copies.start(value, whole.at[0, where, 0])
        for value, whole, where in (
            (grad, grad_out, section),
            (grad_other, grad_out, 1 - section),
            (act, act_out, section),
            (act_other, act_out, 1 - section),
        )
    ]
    for part in range(4):
        cols = slice(part % 2 * D, (part % 2 + 1) * D)
        wide_t[part * D : (part + 1) * D, :] = jnp.transpose((wide_zero, wide_one)[part // 2][:, cols])
    up_high_t[...] = jnp.transpose(up_high[...])
    up_rest_t[...] = jnp.transpose(up_rest[...])
    wait_all(*placed)


def place_call(*arrays):
    outs = [(pltpu.HBM, (1, 2, 1, SEQ, D), bf16), (pltpu.HBM, (1, 2, 1, SEQ, D), f32)]
    outs += vmem([((4 * D, D), bf16), ((D, D), bf16), ((D, D), bf16)])
    return call_kernel(
        place_kernel, "place_outputs", in_vmem(*arrays), outs, [], 4, LATE_MIB, 2 * SEQ * D
    )


QUARTER = D // 4


def final_kernel(col_width, grads_ref, hidden, embed, wide, up_high, up_rest, *refs):
    results, (d_embed, d_up, d_up_b, d_out, d_out_b, sems) = refs[:5], refs[5:]
    section = lax.axis_index("pipe")
    shard = lax.axis_index("dp")
    copies = Copies(sems)
    placed = []
    units = hidden[...]
    both = jnp.zeros((2 * PAD, D), f32)
    for part in range(4):
        high, rest = halves(padded(grads_ref[part * PREFIX : (part + 1) * PREFIX, :]))
        both = both + dot(
            jnp.concatenate([high, rest], axis=0), wide[part * D : (part + 1) * D, :], NN
        )
    grad_units = (both[:PAD] + both[PAD:])[:PREFIX]
    grad_pre = grad_units * (1.0 - units * units)
    d_up_b[...] = jnp.sum(grad_pre, axis=0, keepdims=True)
    for start in range(0, D, QUARTER):
        rows = slice(start, start + QUARTER)
        d_up[rows, :] = stacked_dot(embed[:, rows], grad_pre)
        placed.append(copies.start(d_up.at[rows], results[1].at[rows]))
    placed.append(copies.start(d_up_b, results[2]))
    column = section * (2 * D) + shard * col_width
    own_cols = jnp.zeros((PREFIX, col_width), f32)
    for part in range(4):
        for piece in range(D // col_width):
            here = column == part * D + piece * col_width
            cols = slice(piece * col_width, (piece + 1) * col_width)
            rows = slice(part * PREFIX, (part + 1) * PREFIX)
            own_cols = jnp.where(here, grads_ref[rows, cols], own_cols)
    d_out[...] = stacked_dot(units, own_cols)
    d_out_b[...] = jnp.sum(own_cols, axis=0, keepdims=True)
    placed += [copies.start(d_out, results[3]), copies.start(d_out_b, results[4])]
    high, rest = halves(padded(grad_pre))
    both = dot(jnp.concatenate([high, rest], axis=0), up_high[...], NN)
    both = both[:PAD] + both[PAD:] + dot(high, up_rest[...], NN)
    d_embed[...] = both[:PREFIX]
    placed.append(copies.start(d_embed, results[0]))
    wait_all(*placed)


def final_call(col_width, *arrays):
    def body(*refs):
        final_kernel(col_width, *refs)

    shapes = [((PREFIX, D), f32), ((D, D), f32), ((1, D), f32), ((D, col_width), f32), ((1, col_width), f32)]
    return call_kernel(
        body, "reparam", in_vmem(*arrays), [(pltpu.HBM, *pair) for pair in shapes], shapes, 8, LATE_MIB,
        SEQ * D * D,
    )


def swapped(array_in):
    return lax.ppermute(array_in, "pipe", [(0, 1), (1, 0)])


def hops(axis):
    size = lax.axis_size(axis)
    steps = []
    step = 1
    while step < size:
        steps.append((axis, [(i, i ^ step) for i in range(size)]))
        step *= 2
    assert step == size
    return steps


def local(
    block_input,
    cotangent,
    segments,
    ln1_gain,
    ln1_shift,
    qkv_weight,
    qkv_bias,
    attn_weight,
    attn_bias,
    ln2_gain,
    ln2_shift,
    ff_in_weight,
    ff_in_bias,
    ff_out_weight,
    ff_out_bias,
    prefix_embed,
    up_weight,
    up_bias,
    out_weight,
    out_bias,
):
    other_qkv = swapped(qkv_weight)
    small = small_call(
        ln1_gain, ln1_shift, ln2_gain, ln2_shift, attn_bias, ff_out_bias, qkv_bias, ff_in_bias
    )
    other_small = swapped(small)
    small, prefix_embed = lax.optimization_barrier((small, prefix_embed))
    tables = jnp.asarray(rope_tables())
    _, *later = lax.optimization_barrier((small, attn_weight, ff_in_weight, ff_out_weight))
    other_attn, other_in, other_out = (swapped(weight) for weight in later)
    x_zero, hat_zero, mask, low, hidden_units, wide, up_high, up_rest, tables, own_qkv = opening_call(
        block_input, segments, prefix_embed, up_weight, up_bias, out_weight, out_bias, tables, qkv_weight
    )
    q0, k0, v0, p0, pp0, inv0, mixed0, two_zero, small, w_qkv, w_attn, w_in, w_out, cot, out_w, out_b = first_call(
        (small, other_small, own_qkv, other_qkv, hat_zero, mask, low, tables),
        attn_weight, ff_in_weight, ff_out_weight, cotangent, out_weight, out_bias,
    )
    act_zero, slope_zero, w_in, low_one, wide_one = feed_call(
        two_zero, small, other_in, w_in, hidden_units, out_w, out_b
    )
    (h_one, act_one, mixed_one, grad_one, grad_low, scaled_zero, inner_zero, pre_ds_zero, prefix_grad,
     w_attn, w_out) = middle_call(
        w_attn, w_out, q0, pp0, inv0, mixed0, small, w_qkv, w_in, other_attn, other_out, cot, x_zero,
        act_zero, low, low_one, mask, tables,
    )

    def layer_one_out(state):
        own, send = result_call(state["h_one"], act_one, mixed_one, small, w_attn, w_out)
        return dict(state, act_own=own, act_send=send)

    def layer_zero_attention(state):
        packed = heads_back_call(
            state["scaled"], inner_zero, pre_ds_zero, q0, k0, v0, low, p0, tables
        )
        return dict(state, packed=packed, act_other=swapped(state["act_send"]))

    def layer_zero_feed(state):
        return dict(state, two=feed_back_call(state["grad_low"], slope_zero, w_in, w_out))

    def layer_zero_norms(state):
        own, send = norms_call(
            x_zero, grad_low, state["two"], state["packed"], scaled_zero, p0, grad_one, small, w_qkv
        )
        return dict(state, grad_own=own, grad_send=send)

    def swap_grads(state):
        other = swapped(state["grad_send"])
        act, grad, *turned = place_call(
            state["act_own"], state["act_other"], state["grad_own"], other, wide, wide_one, up_high, up_rest
        )
        return {"wholes": (act, grad), "turned": turned}

    works = [layer_one_out, layer_zero_attention, layer_zero_feed, layer_zero_norms, swap_grads]
    state = {"h_one": h_one, "grad_low": grad_low, "scaled": scaled_zero}
    for axis, pairs in hops("pipe") + hops("dp") + hops("grp"):
        if axis == "pipe":
            moved = lax.ppermute(prefix_grad, axis, pairs)
        else:
            prefix_grad = lax.reduce_precision(prefix_grad, 8, 7)
            moved = lax.ppermute(prefix_grad.astype(bf16), axis, pairs)
        if works:
            state = works.pop(0)(state)
        prefix_grad, moved, state = lax.optimization_barrier((prefix_grad, moved, state))
        prefix_grad = prefix_grad + moved.astype(f32)
    for work in works:
        state = work(state)
    col_width = 2 * D // lax.axis_size("dp")
    grad_embed, grad_up, grad_up_b, grad_out, grad_out_b = final_call(
        col_width, prefix_grad, hidden_units, prefix_embed, *state["turned"]
    )
    activations, input_grads = state["wholes"]
    return (
        activations,
        input_grads,
        grad_embed,
        grad_up,
        grad_up_b[0],
        grad_out,
        grad_out_b[0],
    )


def solution(mesh):
    return jax.shard_map(
        local,
        mesh=mesh,
        in_specs=(
            P(None, ("grp", "dp"), None, None),
            P(None, ("grp", "dp"), None, None),
            P(None, ("grp", "dp"), None),
            P("pipe", None),
            P("pipe", None),
            P("pipe", None, None),
            P("pipe", None),
            P("pipe", None, None),
            P("pipe", None),
            P("pipe", None),
            P("pipe", None),
            P("pipe", None, None),
            P("pipe", None),
            P("pipe", None, None),
            P("pipe", None),
            P(),
            P(),
            P(),
            P(),
            P(),
        ),
        out_specs=(
            P("pipe", None, ("grp", "dp"), None, None),
            P("pipe", None, ("grp", "dp"), None, None),
            P(),
            P(),
            P(),
            P(None, ("pipe", "dp")),
            P(("pipe", "dp")),
        ),
        check_vma=False,
    )
```
